32 devices in a mesh: ctx: 8 (over z, y), fsdp: 4 (over x, core).
Axes of the slice: x: 2, y: 2, z: 4, core: 2. Of those that a mesh axis runs over, the one named last changes fastest.
Arguments:
- tokens: bfloat16 [4, 1024, 1536], P('fsdp', 'ctx'), may hold values from -6 to 6
- doc_lengths: int32 [4, 8], P('fsdp'), may hold values from 1 to 512, 1024 in all within a row
- attention_gain: bfloat16 [1536], P(('ctx', 'fsdp')), may hold values from 0.5 to 1.5
- query_weight: bfloat16 [1536, 1536], P(('ctx', 'fsdp')), may hold values from -0.21875 to 0.21875
- key_weight: bfloat16 [1536, 768], P(('ctx', 'fsdp')), may hold values from -0.21875 to 0.21875
- value_weight: bfloat16 [1536, 768], P(('ctx', 'fsdp')), may hold values from -0.15625 to 0.15625
- output_weight: bfloat16 [1536, 1536], P(('ctx', 'fsdp')), may hold values from -0.625 to 0.625
- feedforward_gain: bfloat16 [1536], P(('ctx', 'fsdp')), may hold values from 0.5 to 1.5
- gate_weight: bfloat16 [1536, 4096], P(('ctx', 'fsdp')), may hold values from -0.15625 to 0.15625
- up_weight: bfloat16 [1536, 4096], P(('ctx', 'fsdp')), may hold values from -0.15625 to 0.15625
- down_weight: bfloat16 [4096, 1536], P(('ctx', 'fsdp')), may hold values from -0.09375 to 0.09375
- cotangent: bfloat16 [4, 1024, 1536], P('fsdp', 'ctx'), may hold values from -6 to 6
Outputs:
- layer_out: bfloat16 [4, 1024, 1536], P('fsdp', 'ctx')
- tokens_grad: float32 [4, 1024, 1536], P('fsdp', 'ctx')
- attention_gain_grad: float32 [1536], P(('ctx', 'fsdp'))
- query_weight_grad: float32 [1536, 1536], P(('ctx', 'fsdp'))
- key_weight_grad: float32 [1536, 768], P(('ctx', 'fsdp'))
- value_weight_grad: float32 [1536, 768], P(('ctx', 'fsdp'))
- output_weight_grad: float32 [1536, 1536], P(('ctx', 'fsdp'))
- feedforward_gain_grad: float32 [1536], P(('ctx', 'fsdp'))
- gate_weight_grad: float32 [1536, 4096], P(('ctx', 'fsdp'))
- up_weight_grad: float32 [1536, 4096], P(('ctx', 'fsdp'))
- down_weight_grad: float32 [4096, 1536], P(('ctx', 'fsdp'))
The draws below stay inside these ranges and needn't reach their ends.
Inputs may be any that keep to these rules, and one draw needn't show every extreme that they name: `doc_lengths`: each stream's row holds the lengths of its 8 documents in order; they sum to 1024 and the longest is exactly 512.
All inputs are finite; a program needn't handle non-finite values.
Results may differ from the reference program's by a relative error of at most 0.014.
The reference program's roundings to bfloat16 on the way count: a program that leaves them out, or rounds other values in their place, can miss the bound.
Values may be sent and summed in bfloat16 or wider, within the bound.
A program may use at most 384 MiB of HBM per device.

```python
import math
import jax
import jax.numpy as jnp
import numpy as np
from jax import lax

D = 1536
H = 16
KVH = 8
HD = 96
FF = 4096
KBLK = 512
STREAMS = 4
STREAM = 1024
MAXDOC = 512
NDOC = 8
KVW = 768


def block_scale(rng, extent, split, low, top_value):
    def one(position, shards_of):
        draws = jax.random.uniform(jax.random.fold_in(jax.random.fold_in(rng, 6), position), (shards_of,), jnp.float32, low / len(split), top_value / len(split))
        return jnp.repeat(jnp.exp(draws), extent[position] // shards_of).reshape((-1,) + (1,) * (len(extent) - position - 1))

    gain = one(*split[0])
    for cut in split[1:]:
        gain = gain * one(*cut)
    return gain


def split_up(amount, total, most, skew):
    portions = [(1 << 20) // math.isqrt(standing ** skew) + 1 for standing in range(2, amount + 1)]
    spare, given = total - most - (amount - 1), [1] * (amount - 1)
    while spare > 0:
        candidates = [i for i in range(amount - 1) if given[i] < most]
        mass, left = sum([portions[i] for i in candidates]), spare
        for i in candidates:
            addition = min(most - given[i], max(1, left * portions[i] // mass), spare)
            given[i] = given[i] + addition
            spare = spare - addition
    return np.array([most] + given)


def uneven(key, number_of, total, reach, skew):
    if number_of == 2:
        one = jax.random.randint(key, (), max(1, total - reach), min(reach, total - 1) + 1)
        return jnp.stack([one, total - one])
    sizes = jnp.asarray(split_up(number_of, total, reach, skew), jnp.int32)
    pairs = (number_of - 1) // 2
    source_of, sink = sizes[1:1 + 2 * pairs:2], sizes[2:2 + 2 * pairs:2]
    margin = jnp.minimum(source_of - 1, reach - sink)
    shifted = jax.random.randint(jax.random.fold_in(key, 1), (pairs,), 0, 1 << 20) % (margin + 1)
    sizes = sizes.at[1:1 + 2 * pairs:2].set(source_of - shifted).at[2:2 + 2 * pairs:2].set(sink + shifted)
    return sizes[jax.random.permutation(jax.random.fold_in(key, 2), number_of)]


def noise(rng, dims, scale, reach, cuts=(), kind=jnp.bfloat16):
    array = jax.random.normal(rng, dims, jnp.float32) * scale
    if len(cuts) > 0:
        array = block_scale(rng, dims, cuts, -0.22, 0.18) * array
    return jnp.clip(array, min=-reach, max=reach).astype(kind)


def setup_inputs(seed: int = 0) -> dict:
    seeds = jax.random.split(jax.random.key(seed), 13)
    tokens = noise(seeds[0], (STREAMS, STREAM, D), 1.0, 6.0, ((0, 4), (1, 8)))
    doc_lengths = jax.vmap(lambda own: uneven(own, NDOC, STREAM, MAXDOC, 2))(jax.random.split(seeds[1], STREAMS)).reshape((STREAMS, NDOC)).astype(jnp.int32)
    attention_gain = jnp.clip(1.0 + 0.1 * jax.random.normal(seeds[2], (D,), jnp.float32), 0.5, 1.5).astype(jnp.bfloat16)
    query_weight = noise(seeds[3], (D, D), (D // 2) ** -0.5, 0.21875, ((0, 32),))
    key_weight = noise(seeds[4], (D, KVW), (D // 2) ** -0.5, 0.21875, ((0, 32),))
    value_weight = noise(seeds[5], (D, KVW), D ** -0.5, 0.15625, ((0, 32),))
    output_weight = noise(seeds[6], (D, D), (D // 16) ** -0.5, 0.625, ((0, 32),))
    feedforward_gain = jnp.clip(1.0 + 0.1 * jax.random.normal(seeds[7], (D,), jnp.float32), 0.5, 1.5).astype(jnp.bfloat16)
    gate_weight = noise(seeds[8], (D, FF), D ** -0.5, 0.15625, ((0, 32),))
    up_weight = noise(seeds[9], (D, FF), D ** -0.5, 0.15625, ((0, 32),))
    down_weight = noise(seeds[10], (FF, D), FF ** -0.5, 0.09375, ((0, 32),))
    cotangent = noise(seeds[11], (STREAMS, STREAM, D), 1.0, 6.0, ((0, 4), (1, 8)))
    return {"tokens": tokens, "doc_lengths": doc_lengths, "attention_gain": attention_gain, "query_weight": query_weight, "key_weight": key_weight, "value_weight": value_weight, "output_weight": output_weight, "feedforward_gain": feedforward_gain, "gate_weight": gate_weight, "up_weight": up_weight, "down_weight": down_weight, "cotangent": cotangent}


EPSILON = 1e-05
ROPE_BASE = 100000.0
MASKED_SCORE = -1e+30

@jax.custom_vjp
def low(v):
    return lax.optimization_barrier(v.astype(jnp.bfloat16)).astype(jnp.float32)

@jax.custom_vjp
def low_back(v):
    return v

def low_keep(v):
    return (low(v), None)

def low_pass(kept, grad):
    return (grad,)

def back_keep(v):
    return (v, None)

def back_low(kept, grad):
    return (low(grad),)
low.defvjp(low_keep, low_pass)
low_back.defvjp(back_keep, back_low)

def matmul_high(left, right):
    return jnp.dot(left, right, precision=lax.Precision.HIGHEST, preferred_element_type=jnp.float32)

def rms_scale(values):
    return lax.rsqrt(lax.optimization_barrier(jnp.mean(values * values, axis=-1, keepdims=True)) + EPSILON)

def document_layout(lengths, total):
    starts = (jnp.cumsum(lengths) - lengths).astype(jnp.int32)
    places = jnp.arange(total, dtype=jnp.int32)
    inside = places[:, None] >= starts[None, :]
    doc_ids = (lax.optimization_barrier(jnp.sum(inside.astype(jnp.int32), axis=1)) - 1).astype(jnp.int32)
    doc_starts = lax.optimization_barrier(jnp.max(jnp.where(inside, starts[None, :], 0), axis=1)).astype(jnp.int32)
    return (doc_ids, (places - doc_starts).astype(jnp.int32))

def rotate(values, positions, head_count, direction):
    row_count = values.shape[0]
    half_dim = HD // 2
    inverse_freq = ROPE_BASE ** (-(jnp.arange(half_dim).astype(jnp.float32) * (2.0 / HD)))
    angles = positions.astype(jnp.float32)[:, None] * inverse_freq[None, :]
    cosine = jnp.cos(angles)[:, None, :]
    sine_part = direction * jnp.sin(angles)[:, None, :]
    grouped = values.reshape(row_count, head_count, HD)
    former = grouped[:, :, :half_dim]
    latter = grouped[:, :, half_dim:]
    turned = jnp.concatenate([former * cosine - latter * sine_part, latter * cosine + former * sine_part], axis=2)
    return turned.reshape(row_count, head_count * HD)

def stream_forward(weights, inputs):
    row_tokens, doc_ids, positions = inputs
    gain_one, query_w, key_w, value_w, output_w, gain_two, gate_w, up_w, down_w = weights
    normed = low(row_tokens * rms_scale(row_tokens) * gain_one)
    queries = low_back(matmul_high(normed, query_w))
    keys_raw = low_back(matmul_high(normed, key_w))
    values_low = low(low_back(matmul_high(normed, value_w)))
    query_rot = low(rotate(queries, positions, H, 1.0))
    key_rot = low(rotate(keys_raw, positions, KVH, 1.0))
    key_pad = jnp.concatenate([jnp.zeros((MAXDOC, KVW), jnp.float32), key_rot], axis=0)
    value_pad = jnp.concatenate([jnp.zeros((MAXDOC, KVW), jnp.float32), values_low], axis=0)
    doc_pad = jnp.concatenate([jnp.full((MAXDOC,), -1, jnp.int32), doc_ids], axis=0)
    key_places = (jnp.arange(STREAM + MAXDOC) - MAXDOC).astype(jnp.int32)
    score_scale = HD ** (-0.5)
    span = MAXDOC + KBLK

    def attend(block_index):
        first_row = (block_index * KBLK).astype(jnp.int32)
        query_block = lax.dynamic_slice_in_dim(query_rot, first_row, KBLK, 0).reshape(KBLK, KVH, H // KVH, HD)
        key_block = lax.dynamic_slice_in_dim(key_pad, first_row, span, 0).reshape(span, KVH, HD)
        value_block = lax.dynamic_slice_in_dim(value_pad, first_row, span, 0).reshape(span, KVH, HD)
        query_docs = lax.dynamic_slice_in_dim(doc_ids, first_row, KBLK, 0)
        query_places = first_row + jnp.arange(KBLK, dtype=jnp.int32)
        key_docs = lax.dynamic_slice_in_dim(doc_pad, first_row, span, 0)
        key_where = lax.dynamic_slice_in_dim(key_places, first_row, span, 0)
        allowed = (key_docs[None, :] == query_docs[:, None]) & (key_where[None, :] <= query_places[:, None])
        scores = low_back(jnp.einsum('qgrd,kgd->qgrk', query_block, key_block, precision=lax.Precision.HIGHEST) * score_scale)
        scores = jnp.where(allowed[:, None, None, :], scores, MASKED_SCORE)
        row_max = lax.optimization_barrier(jnp.max(scores, axis=-1, keepdims=True))
        exponent = jnp.exp(scores - row_max)
        probabilities = low(exponent / lax.optimization_barrier(jnp.sum(exponent, axis=-1, keepdims=True)))
        mixture = jnp.einsum('qgrk,kgd->qgrd', probabilities, value_block, precision=lax.Precision.HIGHEST)
        return mixture.reshape(KBLK, D)
    blocks = lax.map(jax.checkpoint(attend), jnp.arange(STREAM // KBLK, dtype=jnp.int32))
    attended = low(low_back(blocks.reshape(STREAM, D)))
    branch = low_back(matmul_high(attended, output_w))
    middle = row_tokens + branch
    normed_two = low(middle * rms_scale(middle) * gain_two)
    gate_pre = low_back(matmul_high(normed_two, gate_w))
    up_pre = low_back(matmul_high(normed_two, up_w))
    hidden = low(jax.nn.silu(gate_pre) * up_pre)
    return middle + matmul_high(hidden, down_w)

def reference(tokens, doc_lengths, attention_gain, query_weight, key_weight, value_weight, output_weight, feedforward_gain, gate_weight, up_weight, down_weight, cotangent):
    layout_ids, layout_places = jax.vmap(lambda lengths: document_layout(lengths, STREAM))(doc_lengths)
    params = (attention_gain.astype(jnp.float32), query_weight.astype(jnp.float32), key_weight.astype(jnp.float32), value_weight.astype(jnp.float32), output_weight.astype(jnp.float32), feedforward_gain.astype(jnp.float32), gate_weight.astype(jnp.float32), up_weight.astype(jnp.float32), down_weight.astype(jnp.float32))

    def whole_layer(token_values, *weights):
        return lax.map(lambda inputs: stream_forward(weights, inputs), (token_values, layout_ids, layout_places))
    result, pullback = jax.vjp(whole_layer, tokens.astype(jnp.float32), *params)
    gradients = pullback(cotangent.astype(jnp.float32))
    return (result.astype(jnp.bfloat16), gradients[0], gradients[1], gradients[2], gradients[3], gradients[4], gradients[5], gradients[6], gradients[7], gradients[8], gradients[9])
```

```python
import jax
import jax.numpy as jnp
from jax import lax
from jax.sharding import PartitionSpec as P

D = 1536
H = 16
KVH = 8
HD = 96
KBLK = 512
DOC_MOST = 4096
KVW = 768
GAIN_PAD = 128

EPSILON = 1e-05
ROPE_BASE = 100000.0
MASKED_SCORE = -1e30
ALL = ("ctx", "fsdp")


def rms_scale(values):
    return lax.rsqrt(jnp.mean(values * values, axis=-1, keepdims=True) + EPSILON)


def document_layout(lengths, total):
    starts = jnp.cumsum(lengths) - lengths
    places = jnp.arange(total, dtype=jnp.int32)
    inside = places[:, None] >= starts[None, :]
    doc_ids = jnp.sum(inside.astype(jnp.int32), axis=1) - 1
    doc_starts = jnp.max(jnp.where(inside, starts[None, :], 0), axis=1)
    return (doc_ids, places - doc_starts)


def rotate(values, positions, head_count, direction):
    row_count = values.shape[0]
    half_dim = HD // 2
    inverse_freq = ROPE_BASE ** (-(jnp.arange(half_dim).astype(jnp.float32) * (2.0 / HD)))
    angles = positions.astype(jnp.float32)[:, None] * inverse_freq[None, :]
    cosine = jnp.cos(angles)[:, None, :]
    sine_part = direction * jnp.sin(angles)[:, None, :]
    grouped = values.reshape(row_count, head_count, HD)
    former = grouped[:, :, :half_dim]
    latter = grouped[:, :, half_dim:]
    turned = jnp.concatenate(
        [former * cosine - latter * sine_part, latter * cosine + former * sine_part], axis=2
    )
    return turned.reshape(row_count, head_count * HD)


def outer_rows(left, right):
    return lax.dot_general(
        left, right, (((0,), (0,)), ((), ())), preferred_element_type=jnp.float32
    )


def times_transposed(left, right):
    return lax.dot_general(
        left, right, (((1,), (1,)), ((), ())), preferred_element_type=jnp.float32
    )


def body(
    tokens,
    doc_lengths,
    attention_gain,
    query_weight,
    key_weight,
    value_weight,
    output_weight,
    feedforward_gain,
    gate_weight,
    up_weight,
    down_weight,
    cotangent,
):
    n_dev = lax.axis_size(ALL)
    rows = query_weight.shape[0]
    ff_rows = down_weight.shape[0]
    ff = gate_weight.shape[1]
    local_tokens = tokens[0].astype(jnp.float32)
    tok_rows = local_tokens.shape[0]
    stream_len = tok_rows * lax.axis_size("ctx")
    my_first = lax.axis_index("ctx") * tok_rows

    gain_cols = jnp.pad(
        jnp.stack([attention_gain, feedforward_gain], axis=1), ((0, 0), (0, GAIN_PAD - 2))
    )
    att_full = lax.all_gather(
        jnp.concatenate([query_weight, key_weight, value_weight, output_weight, gain_cols], axis=1),
        ALL,
        axis=0,
        tiled=True,
    )
    c_k = D
    c_v = D + KVW
    c_o = D + 2 * KVW
    c_g = 2 * D + 2 * KVW
    query_full = att_full[:, :c_k]
    key_full = att_full[:, c_k:c_v]
    value_full = att_full[:, c_v:c_o]
    qkv_full = att_full[:, :c_o]
    output_full = att_full[:, c_o:c_g]
    gain_one_f = att_full[:, c_g].astype(jnp.float32)
    gain_two_f = att_full[:, c_g + 1].astype(jnp.float32)

    key_docs_all, places_all = document_layout(doc_lengths[0], stream_len)
    query_docs = lax.dynamic_slice_in_dim(key_docs_all, my_first, tok_rows, 0)
    query_positions = lax.dynamic_slice_in_dim(places_all, my_first, tok_rows, 0)
    query_places = my_first + jnp.arange(tok_rows, dtype=jnp.int32)
    group_size = H // KVH
    score_scale = HD ** (-0.5)

    scale_one = rms_scale(local_tokens)
    normed_one = local_tokens * scale_one
    normed_low = (normed_one * gain_one_f).astype(jnp.bfloat16)
    qkv = jnp.dot(normed_low, qkv_full, preferred_element_type=jnp.float32)
    queries = qkv[:, :D]
    keys_new = qkv[:, D : D + KVW]
    values_new = qkv[:, D + KVW :]
    query_low = rotate(queries, query_positions, H, 1.0).astype(jnp.bfloat16)
    key_low = rotate(keys_new, query_positions, KVH, 1.0).astype(jnp.bfloat16)
    value_low = values_new.astype(jnp.bfloat16)

    ff_full = lax.all_gather(
        jnp.concatenate([gate_weight, up_weight, down_weight.reshape(rows, ff)], axis=1),
        ALL,
        axis=0,
        tiled=True,
    )
    kv_all = lax.all_gather(
        jnp.concatenate([key_low, value_low], axis=1), "ctx", axis=0, tiled=True
    )

    max_doc = min(DOC_MOST, KBLK * (stream_len // (2 * KBLK)))
    win = min(max_doc + tok_rows, stream_len)
    if win == stream_len:
        win_start = 0
        kv_win = kv_all
        key_docs = key_docs_all
        key_places = jnp.arange(stream_len, dtype=jnp.int32)
    else:
        win_start = jnp.clip(my_first + tok_rows - win, 0, stream_len - win)
        kv_win = lax.dynamic_slice_in_dim(kv_all, win_start, win, 0)
        key_docs = lax.dynamic_slice_in_dim(key_docs_all, win_start, win, 0)
        key_places = win_start + jnp.arange(win, dtype=jnp.int32)
    key_block = kv_win[:, :KVW].reshape(win, KVH, HD)
    value_block = kv_win[:, KVW:].reshape(win, KVH, HD)
    query_grouped = query_low.reshape(tok_rows, KVH, group_size, HD)
    allowed = (
        (key_docs[None, :] == query_docs[:, None]) & (key_places[None, :] <= query_places[:, None])
    )[:, None, None, :]
    scores = (
        jnp.einsum("qgrd,kgd->qgrk", query_grouped, key_block, preferred_element_type=jnp.float32)
        * score_scale
    )
    scores = jnp.where(allowed, scores, MASKED_SCORE)
    row_max = jnp.max(scores, axis=-1, keepdims=True)
    exponent = jnp.where(allowed, jnp.exp(scores - row_max), 0.0)
    probs = exponent / jnp.sum(exponent, axis=-1, keepdims=True)
    probs_low = probs.astype(jnp.bfloat16)
    attended_sum = jnp.einsum(
        "qgrk,kgd->qgrd", probs_low, value_block, preferred_element_type=jnp.float32
    )
    attended_low = attended_sum.reshape(tok_rows, D).astype(jnp.bfloat16)
    middle = local_tokens + jnp.dot(attended_low, output_full, preferred_element_type=jnp.float32)

    gate_up_full = ff_full[:, : 2 * ff]
    gate_full = ff_full[:, :ff]
    up_full = ff_full[:, ff : 2 * ff]
    down_full = ff_full[:, 2 * ff :].reshape(n_dev, rows, ff).reshape(n_dev * ff_rows, D)
    scale_two = rms_scale(middle)
    normed_two = middle * scale_two
    normed_two_low = (normed_two * gain_two_f).astype(jnp.bfloat16)
    gate_up = jnp.dot(normed_two_low, gate_up_full, preferred_element_type=jnp.float32)
    gate_pre = gate_up[:, :ff]
    up_pre = gate_up[:, ff:]
    sigmoid = jax.nn.sigmoid(gate_pre)
    hidden_low = (gate_pre * sigmoid * up_pre).astype(jnp.bfloat16)
    layer_out = middle + jnp.dot(hidden_low, down_full, preferred_element_type=jnp.float32)

    grad_out = cotangent[0]
    down_term = outer_rows(hidden_low, grad_out)
    hidden_grad = times_transposed(grad_out, down_full)
    gate_grad = (hidden_grad * up_pre * sigmoid * (1.0 + gate_pre * (1.0 - sigmoid))).astype(
        jnp.bfloat16
    )
    up_grad = (hidden_grad * gate_pre * sigmoid).astype(jnp.bfloat16)
    gate_up_cat = jnp.concatenate([gate_grad, up_grad], axis=1)
    gate_up_term = outer_rows(normed_two_low, gate_up_cat)
    ff_sum = lax.psum_scatter(
        jnp.concatenate(
            [
                gate_up_term.astype(jnp.bfloat16),
                down_term.reshape(n_dev, ff_rows, D).reshape(n_dev * rows, ff).astype(jnp.bfloat16),
            ],
            axis=1,
        ),
        ALL,
        scatter_dimension=0,
        tiled=True,
    )
    normed_two_grad = times_transposed(gate_up_cat, gate_up_full)
    gain_two_term = jnp.sum(normed_two_grad * normed_two, axis=0)
    scaled_two = normed_two_grad * gain_two_f
    middle_grad = grad_out.astype(jnp.float32) + scale_two * (
        scaled_two - normed_two * jnp.mean(scaled_two * normed_two, axis=-1, keepdims=True)
    )
    branch_grad = middle_grad.astype(jnp.bfloat16)
    attended_grad_low = (
        times_transposed(branch_grad, output_full)
        .astype(jnp.bfloat16)
        .reshape(tok_rows, KVH, group_size, HD)
    )
    row_delta = jnp.sum(
        attended_grad_low.astype(jnp.float32) * attended_sum, axis=-1, keepdims=True
    )
    prob_grad = jnp.einsum(
        "qgrd,kgd->qgrk", attended_grad_low, value_block, preferred_element_type=jnp.float32
    )
    score_grad = (probs * (prob_grad - row_delta)).astype(jnp.bfloat16)
    query_accum = jnp.einsum(
        "qgrk,kgd->qgrd", score_grad, key_block, preferred_element_type=jnp.float32
    )
    key_term = jnp.einsum(
        "qgrk,qgrd->kgd", score_grad, query_grouped, preferred_element_type=jnp.float32
    ).reshape(win, KVW)
    value_term = jnp.einsum(
        "qgrk,qgrd->kgd", probs_low, attended_grad_low, preferred_element_type=jnp.float32
    ).reshape(win, KVW)
    kv_term = jnp.concatenate([key_term, value_term], axis=1)
    if win != stream_len:
        kv_term = lax.dynamic_update_slice_in_dim(
            jnp.zeros((stream_len, 2 * KVW), jnp.float32), kv_term, win_start, 0
        )
    kv_sum = lax.psum_scatter(kv_term, "ctx", scatter_dimension=0, tiled=True)
    key_grad_low = rotate(kv_sum[:, :KVW] * score_scale, query_positions, KVH, -1.0).astype(
        jnp.bfloat16
    )
    value_grad_low = kv_sum[:, KVW:].astype(jnp.bfloat16)
    query_grad_low = rotate(
        query_accum.reshape(tok_rows, D) * score_scale, query_positions, H, -1.0
    ).astype(jnp.bfloat16)
    projection_cat = jnp.concatenate([query_grad_low, key_grad_low, value_grad_low], axis=1)
    normed_grad = times_transposed(projection_cat, qkv_full)
    gain_one_term = jnp.sum(normed_grad * normed_one, axis=0)
    scaled_one = normed_grad * gain_one_f
    tokens_grad = middle_grad + scale_one * (
        scaled_one - normed_one * jnp.mean(scaled_one * normed_one, axis=-1, keepdims=True)
    )
    gain_term_cols = jnp.pad(
        jnp.stack([gain_one_term, gain_two_term], axis=1), ((0, 0), (0, GAIN_PAD - 2))
    )
    attention_sum = lax.psum_scatter(
        jnp.concatenate(
            [
                outer_rows(normed_low, projection_cat).astype(jnp.bfloat16),
                outer_rows(attended_low, branch_grad).astype(jnp.bfloat16),
                gain_term_cols.astype(jnp.bfloat16),
            ],
            axis=1,
        ),
        ALL,
        scatter_dimension=0,
        tiled=True,
    ).astype(jnp.float32)
    ff_sum = ff_sum.astype(jnp.float32)
    return (
        layer_out.astype(jnp.bfloat16)[None],
        tokens_grad[None],
        attention_sum[:, c_g],
        attention_sum[:, :c_k],
        attention_sum[:, c_k:c_v],
        attention_sum[:, c_v:c_o],
        attention_sum[:, c_o:c_g],
        attention_sum[:, c_g + 1],
        ff_sum[:, :ff],
        ff_sum[:, ff : 2 * ff],
        ff_sum[:, 2 * ff :].reshape(ff_rows, D),
    )


def solution(mesh):
    weight = P(ALL, None)
    stream = P("fsdp", "ctx", None)
    return jax.shard_map(
        body,
        mesh=mesh,
        in_specs=(
            stream,
            P("fsdp", None),
            P(ALL),
            weight,
            weight,
            weight,
            weight,
            P(ALL),
            weight,
            weight,
            weight,
            stream,
        ),
        out_specs=(
            stream,
            stream,
            P(ALL),
            weight,
            weight,
            weight,
            weight,
            P(ALL),
            weight,
            weight,
            weight,
        ),
        check_vma=False,
    )
```

```python
import functools

import jax
import jax.numpy as jnp
from jax import lax
from jax.experimental import pallas as pl
from jax.experimental.pallas import tpu as pltpu
from jax.sharding import PartitionSpec as P

MESH = pl.DeviceIdType.MESH

D = 1536
H = 16
KVH = 8
HD = 96
KBLK = 512
DOC_MOST = 4096
KVW = 768
GAIN_PAD = 128

EPSILON = 1e-05
ROPE_BASE = 100000.0
MASKED_SCORE = -1e30
ALL = ("ctx", "fsdp")


def rms_scale(values):
    return lax.rsqrt(jnp.mean(values * values, axis=-1, keepdims=True) + EPSILON)


def document_layout(lengths, total):
    starts = jnp.cumsum(lengths) - lengths
    places = jnp.arange(total, dtype=jnp.int32)
    inside = places[:, None] >= starts[None, :]
    doc_ids = jnp.sum(inside.astype(jnp.int32), axis=1) - 1
    doc_starts = jnp.max(jnp.where(inside, starts[None, :], 0), axis=1)
    return (doc_ids, places - doc_starts)


def rotate(values, positions, head_count, direction):
    row_count = values.shape[0]
    half_dim = HD // 2
    inverse_freq = ROPE_BASE ** (-(jnp.arange(half_dim).astype(jnp.float32) * (2.0 / HD)))
    angles = positions.astype(jnp.float32)[:, None] * inverse_freq[None, :]
    cosine = jnp.cos(angles)[:, None, :]
    sine_part = direction * jnp.sin(angles)[:, None, :]
    grouped = values.reshape(row_count, head_count, HD)
    former = grouped[:, :, :half_dim]
    latter = grouped[:, :, half_dim:]
    turned = jnp.concatenate(
        [former * cosine - latter * sine_part, latter * cosine + former * sine_part], axis=2
    )
    return turned.reshape(row_count, head_count * HD)


def outer_rows(left, right):
    return lax.dot_general(
        left, right, (((0,), (0,)), ((), ())), preferred_element_type=jnp.float32
    )


def times_transposed(left, right):
    return lax.dot_general(
        left, right, (((1,), (1,)), ((), ())), preferred_element_type=jnp.float32
    )


def neighbour_barrier(n_ctx, back, c, f):
    barrier = pltpu.get_barrier_semaphore()
    for s in range(1, back + 1):
        for peer in ((c + s) % n_ctx, (c + n_ctx - s) % n_ctx):
            pl.semaphore_signal(barrier, inc=1, device_id=(peer, f), device_id_type=MESH)
    pl.semaphore_wait(barrier, 2 * back)


def kv_share_kernel(n_ctx, back, kv_ref, out_ref, send_sem, recv_sem):
    c = lax.axis_index("ctx")
    f = lax.axis_index("fsdp")
    neighbour_barrier(n_ctx, back, c, f)

    def copy(s, dest):
        return pltpu.make_async_remote_copy(
            src_ref=kv_ref,
            dst_ref=out_ref.at[back - s],
            send_sem=send_sem.at[s - 1],
            recv_sem=recv_sem.at[back - s],
            device_id=(dest, f),
            device_id_type=MESH,
        )

    for s in range(1, back + 1):

        @pl.when(c + s < n_ctx)
        def _():
            copy(s, c + s).start()

    out_ref[back] = kv_ref[...]
    for s in range(1, back + 1):

        @pl.when(c - s < 0)
        def _():
            out_ref[back - s] = jnp.zeros(kv_ref.shape, kv_ref.dtype)

    for s in range(1, back + 1):

        @pl.when(c + s < n_ctx)
        def _():
            copy(s, c + s).wait_send()

        @pl.when(c - s >= 0)
        def _():
            copy(s, c).wait_recv()


def kv_share(kv, n_ctx, back):
    return pl.pallas_call(
        functools.partial(kv_share_kernel, n_ctx, back),
        out_shape=jax.ShapeDtypeStruct((back + 1,) + kv.shape, kv.dtype),
        in_specs=[pl.BlockSpec(memory_space=pltpu.VMEM)],
        out_specs=pl.BlockSpec(memory_space=pltpu.VMEM),
        scratch_shapes=[pltpu.SemaphoreType.DMA((back,)), pltpu.SemaphoreType.DMA((back + 1,))],
        compiler_params=pltpu.CompilerParams(collective_id=0, has_side_effects=True),
    )(kv)


def kv_return_kernel(n_ctx, back, g_ref, out_ref, recv_buf, send_sem, recv_sem):
    c = lax.axis_index("ctx")
    f = lax.axis_index("fsdp")
    neighbour_barrier(n_ctx, back, c, f)

    def copy(s, dest):
        return pltpu.make_async_remote_copy(
            src_ref=g_ref.at[back - s],
            dst_ref=recv_buf.at[s - 1],
            send_sem=send_sem.at[s - 1],
            recv_sem=recv_sem.at[s - 1],
            device_id=(dest, f),
            device_id_type=MESH,
        )

    for s in range(1, back + 1):

        @pl.when(c - s >= 0)
        def _():
            copy(s, c - s).start()

    out_ref[...] = g_ref[back]
    for s in range(1, back + 1):

        @pl.when(c + s < n_ctx)
        def _():
            copy(s, c).wait_recv()
            out_ref[...] += recv_buf[s - 1]

    for s in range(1, back + 1):

        @pl.when(c - s >= 0)
        def _():
            copy(s, c - s).wait_send()


def kv_return(g, n_ctx, back):
    return pl.pallas_call(
        functools.partial(kv_return_kernel, n_ctx, back),
        out_shape=jax.ShapeDtypeStruct(g.shape[1:], g.dtype),
        in_specs=[pl.BlockSpec(memory_space=pltpu.VMEM)],
        out_specs=pl.BlockSpec(memory_space=pltpu.VMEM),
        scratch_shapes=[
            pltpu.VMEM((back,) + g.shape[1:], g.dtype),
            pltpu.SemaphoreType.DMA((back,)),
            pltpu.SemaphoreType.DMA((back,)),
        ],
        compiler_params=pltpu.CompilerParams(collective_id=1, has_side_effects=True),
    )(g)


def body(
    tokens,
    doc_lengths,
    attention_gain,
    query_weight,
    key_weight,
    value_weight,
    output_weight,
    feedforward_gain,
    gate_weight,
    up_weight,
    down_weight,
    cotangent,
):
    n_dev = lax.axis_size(ALL)
    rows = query_weight.shape[0]
    ff_rows = down_weight.shape[0]
    ff = gate_weight.shape[1]
    local_tokens = tokens[0].astype(jnp.float32)
    tok_rows = local_tokens.shape[0]
    stream_len = tok_rows * lax.axis_size("ctx")
    my_first = lax.axis_index("ctx") * tok_rows

    gain_cols = jnp.pad(
        jnp.stack([attention_gain, feedforward_gain], axis=1), ((0, 0), (0, GAIN_PAD - 2))
    )
    att_full = lax.all_gather(
        jnp.concatenate([query_weight, key_weight, value_weight, output_weight, gain_cols], axis=1),
        ALL,
        axis=0,
        tiled=True,
    )
    c_k = D
    c_v = D + KVW
    c_o = D + 2 * KVW
    c_g = 2 * D + 2 * KVW
    query_full = att_full[:, :c_k]
    key_full = att_full[:, c_k:c_v]
    value_full = att_full[:, c_v:c_o]
    qkv_full = att_full[:, :c_o]
    output_full = att_full[:, c_o:c_g]
    gain_one_f = att_full[:, c_g].astype(jnp.float32)
    gain_two_f = att_full[:, c_g + 1].astype(jnp.float32)

    key_docs_all, places_all = document_layout(doc_lengths[0], stream_len)
    query_docs = lax.dynamic_slice_in_dim(key_docs_all, my_first, tok_rows, 0)
    query_positions = lax.dynamic_slice_in_dim(places_all, my_first, tok_rows, 0)
    query_places = my_first + jnp.arange(tok_rows, dtype=jnp.int32)
    group_size = H // KVH
    score_scale = HD ** (-0.5)

    scale_one = rms_scale(local_tokens)
    normed_one = local_tokens * scale_one
    normed_low = (normed_one * gain_one_f).astype(jnp.bfloat16)
    qkv = jnp.dot(normed_low, qkv_full, preferred_element_type=jnp.float32)
    queries = qkv[:, :D]
    keys_new = qkv[:, D : D + KVW]
    values_new = qkv[:, D + KVW :]
    query_low = rotate(queries, query_positions, H, 1.0).astype(jnp.bfloat16)
    key_low = rotate(keys_new, query_positions, KVH, 1.0).astype(jnp.bfloat16)
    value_low = values_new.astype(jnp.bfloat16)

    ff_full = lax.all_gather(
        jnp.concatenate([gate_weight, up_weight, down_weight.reshape(rows, ff)], axis=1),
        ALL,
        axis=0,
        tiled=True,
    )
    n_ctx = lax.axis_size("ctx")
    max_doc = min(DOC_MOST, KBLK * (stream_len // (2 * KBLK)))
    back = min(-(-(max_doc - 1) // tok_rows), n_ctx - 1)
    win = (back + 1) * tok_rows
    kv_win = kv_share(
        jnp.concatenate([key_low, value_low], axis=1), n_ctx, back
    ).reshape(win, 2 * KVW)
    docs_pad = jnp.concatenate(
        [jnp.full((back * tok_rows,), -1, jnp.int32), key_docs_all.astype(jnp.int32)]
    )
    key_docs = lax.dynamic_slice_in_dim(docs_pad, my_first, win, 0)
    key_places = my_first - back * tok_rows + jnp.arange(win, dtype=jnp.int32)
    key_block = kv_win[:, :KVW].reshape(win, KVH, HD)
    value_block = kv_win[:, KVW:].reshape(win, KVH, HD)
    query_grouped = query_low.reshape(tok_rows, KVH, group_size, HD)
    allowed = (
        (key_docs[None, :] == query_docs[:, None]) & (key_places[None, :] <= query_places[:, None])
    )[:, None, None, :]
    scores = (
        jnp.einsum("qgrd,kgd->qgrk", query_grouped, key_block, preferred_element_type=jnp.float32)
        * score_scale
    )
    scores = jnp.where(allowed, scores, MASKED_SCORE)
    row_max = jnp.max(scores, axis=-1, keepdims=True)
    exponent = jnp.where(allowed, jnp.exp(scores - row_max), 0.0)
    probs = exponent / jnp.sum(exponent, axis=-1, keepdims=True)
    probs_low = probs.astype(jnp.bfloat16)
    attended_sum = jnp.einsum(
        "qgrk,kgd->qgrd", probs_low, value_block, preferred_element_type=jnp.float32
    )
    attended_low = attended_sum.reshape(tok_rows, D).astype(jnp.bfloat16)
    middle = local_tokens + jnp.dot(attended_low, output_full, preferred_element_type=jnp.float32)

    gate_up_full = ff_full[:, : 2 * ff]
    gate_full = ff_full[:, :ff]
    up_full = ff_full[:, ff : 2 * ff]
    down_full = ff_full[:, 2 * ff :].reshape(n_dev, rows, ff).reshape(n_dev * ff_rows, D)
    scale_two = rms_scale(middle)
    normed_two = middle * scale_two
    normed_two_low = (normed_two * gain_two_f).astype(jnp.bfloat16)
    gate_up = jnp.dot(normed_two_low, gate_up_full, preferred_element_type=jnp.float32)
    gate_pre = gate_up[:, :ff]
    up_pre = gate_up[:, ff:]
    sigmoid = jax.nn.sigmoid(gate_pre)
    hidden_low = (gate_pre * sigmoid * up_pre).astype(jnp.bfloat16)
    layer_out = middle + jnp.dot(hidden_low, down_full, preferred_element_type=jnp.float32)

    grad_out = cotangent[0]
    down_term = outer_rows(hidden_low, grad_out)
    hidden_grad = times_transposed(grad_out, down_full)
    gate_grad = (hidden_grad * up_pre * sigmoid * (1.0 + gate_pre * (1.0 - sigmoid))).astype(
        jnp.bfloat16
    )
    up_grad = (hidden_grad * gate_pre * sigmoid).astype(jnp.bfloat16)
    gate_up_cat = jnp.concatenate([gate_grad, up_grad], axis=1)
    gate_up_term = outer_rows(normed_two_low, gate_up_cat)
    ff_pack = jnp.concatenate(
        [
            gate_up_term.astype(jnp.bfloat16),
            down_term.reshape(n_dev, ff_rows, D).reshape(n_dev * rows, ff).astype(jnp.bfloat16),
        ],
        axis=1,
    )
    ff_pack, gate_up_cat = lax.optimization_barrier((ff_pack, gate_up_cat))
    ff_sum = lax.psum_scatter(ff_pack, ALL, scatter_dimension=0, tiled=True)
    normed_two_grad = times_transposed(gate_up_cat, gate_up_full)
    gain_two_term = jnp.sum(normed_two_grad * normed_two, axis=0)
    scaled_two = normed_two_grad * gain_two_f
    middle_grad = grad_out.astype(jnp.float32) + scale_two * (
        scaled_two - normed_two * jnp.mean(scaled_two * normed_two, axis=-1, keepdims=True)
    )
    branch_grad = middle_grad.astype(jnp.bfloat16)
    attended_grad_low = (
        times_transposed(branch_grad, output_full)
        .astype(jnp.bfloat16)
        .reshape(tok_rows, KVH, group_size, HD)
    )
    row_delta = jnp.sum(
        attended_grad_low.astype(jnp.float32) * attended_sum, axis=-1, keepdims=True
    )
    prob_grad = jnp.einsum(
        "qgrd,kgd->qgrk", attended_grad_low, value_block, preferred_element_type=jnp.float32
    )
    score_grad = (probs * (prob_grad - row_delta)).astype(jnp.bfloat16)
    query_accum = jnp.einsum(
        "qgrk,kgd->qgrd", score_grad, key_block, preferred_element_type=jnp.float32
    )
    key_term = jnp.einsum(
        "qgrk,qgrd->kgd", score_grad, query_grouped, preferred_element_type=jnp.float32
    ).reshape(win, KVW)
    value_term = jnp.einsum(
        "qgrk,qgrd->kgd", probs_low, attended_grad_low, preferred_element_type=jnp.float32
    ).reshape(win, KVW)
    kv_sum = kv_return(
        jnp.concatenate([key_term, value_term], axis=1).reshape(back + 1, tok_rows, 2 * KVW),
        n_ctx,
        back,
    )
    key_grad_low = rotate(kv_sum[:, :KVW] * score_scale, query_positions, KVH, -1.0).astype(
        jnp.bfloat16
    )
    value_grad_low = kv_sum[:, KVW:].astype(jnp.bfloat16)
    query_grad_low = rotate(
        query_accum.reshape(tok_rows, D) * score_scale, query_positions, H, -1.0
    ).astype(jnp.bfloat16)
    projection_cat = jnp.concatenate([query_grad_low, key_grad_low, value_grad_low], axis=1)
    normed_grad = times_transposed(projection_cat, qkv_full)
    gain_one_term = jnp.sum(normed_grad * normed_one, axis=0)
    scaled_one = normed_grad * gain_one_f
    tokens_grad = middle_grad + scale_one * (
        scaled_one - normed_one * jnp.mean(scaled_one * normed_one, axis=-1, keepdims=True)
    )
    gain_term_cols = jnp.pad(
        jnp.stack([gain_one_term, gain_two_term], axis=1), ((0, 0), (0, GAIN_PAD - 2))
    )
    gain_term_cols = gain_term_cols.at[0, GAIN_PAD - 1].set(ff_sum[0, 0].astype(jnp.float32) * 0.0)
    attention_sum = lax.psum_scatter(
        jnp.concatenate(
            [
                outer_rows(normed_low, projection_cat).astype(jnp.bfloat16),
                outer_rows(attended_low, branch_grad).astype(jnp.bfloat16),
                gain_term_cols.astype(jnp.bfloat16),
            ],
            axis=1,
        ),
        ALL,
        scatter_dimension=0,
        tiled=True,
    ).astype(jnp.float32)
    ff_sum = ff_sum.astype(jnp.float32)
    return (
        layer_out.astype(jnp.bfloat16)[None],
        tokens_grad[None],
        attention_sum[:, c_g],
        attention_sum[:, :c_k],
        attention_sum[:, c_k:c_v],
        attention_sum[:, c_v:c_o],
        attention_sum[:, c_o:c_g],
        attention_sum[:, c_g + 1],
        ff_sum[:, :ff],
        ff_sum[:, ff : 2 * ff],
        ff_sum[:, 2 * ff :].reshape(ff_rows, D),
    )


def solution(mesh):
    weight = P(ALL, None)
    stream = P("fsdp", "ctx", None)
    return jax.shard_map(
        body,
        mesh=mesh,
        in_specs=(
            stream,
            P("fsdp", None),
            P(ALL),
            weight,
            weight,
            weight,
            weight,
            P(ALL),
            weight,
            weight,
            weight,
            stream,
        ),
        out_specs=(
            stream,
            stream,
            P(ALL),
            weight,
            weight,
            weight,
            weight,
            P(ALL),
            weight,
            weight,
            weight,
        ),
        check_vma=False,
    )
```

```python
import functools

import jax
import jax.numpy as jnp
from jax import lax
from jax.experimental import pallas as pl
from jax.experimental.pallas import tpu as pltpu
from jax.sharding import PartitionSpec as P

MESH = pl.DeviceIdType.MESH

D = 1536
H = 16
KVH = 8
HD = 96
KBLK = 512
DOC_MOST = 4096
KVW = 768
GAIN_PAD = 128

EPSILON = 1e-05
ROPE_BASE = 100000.0
MASKED_SCORE = -1e30
ALL = ("ctx", "fsdp")


def rms_scale(values):
    return lax.rsqrt(jnp.mean(values * values, axis=-1, keepdims=True) + EPSILON)


def document_layout(lengths, total):
    starts = jnp.cumsum(lengths) - lengths
    places = jnp.arange(total, dtype=jnp.int32)
    inside = places[:, None] >= starts[None, :]
    doc_ids = jnp.sum(inside.astype(jnp.int32), axis=1) - 1
    doc_starts = jnp.max(jnp.where(inside, starts[None, :], 0), axis=1)
    return (doc_ids, places - doc_starts)


def rotate(values, positions, head_count, direction):
    row_count = values.shape[0]
    half_dim = HD // 2
    inverse_freq = ROPE_BASE ** (-(jnp.arange(half_dim).astype(jnp.float32) * (2.0 / HD)))
    angles = positions.astype(jnp.float32)[:, None] * inverse_freq[None, :]
    cosine = jnp.cos(angles)[:, None, :]
    sine_part = direction * jnp.sin(angles)[:, None, :]
    grouped = values.reshape(row_count, head_count, HD)
    former = grouped[:, :, :half_dim]
    latter = grouped[:, :, half_dim:]
    turned = jnp.concatenate(
        [former * cosine - latter * sine_part, latter * cosine + former * sine_part], axis=2
    )
    return turned.reshape(row_count, head_count * HD)


def outer_rows(left, right):
    return lax.dot_general(
        left, right, (((0,), (0,)), ((), ())), preferred_element_type=jnp.float32
    )


def times_transposed(left, right):
    return lax.dot_general(
        left, right, (((1,), (1,)), ((), ())), preferred_element_type=jnp.float32
    )


def neighbour_barrier(n_ctx, back, c, f):
    barrier = pltpu.get_barrier_semaphore()
    for s in range(1, back + 1):
        for peer in ((c + s) % n_ctx, (c + n_ctx - s) % n_ctx):
            pl.semaphore_signal(barrier, inc=1, device_id=(peer, f), device_id_type=MESH)
    pl.semaphore_wait(barrier, 2 * back)


def kv_share_kernel(n_ctx, back, kv_ref, out_ref, send_sem, recv_sem):
    c = lax.axis_index("ctx")
    f = lax.axis_index("fsdp")
    neighbour_barrier(n_ctx, back, c, f)

    def copy(s, dest):
        return pltpu.make_async_remote_copy(
            src_ref=kv_ref,
            dst_ref=out_ref.at[back - s],
            send_sem=send_sem.at[s - 1],
            recv_sem=recv_sem.at[back - s],
            device_id=(dest, f),
            device_id_type=MESH,
        )

    for s in range(1, back + 1):

        @pl.when(c + s < n_ctx)
        def _():
            copy(s, c + s).start()

    out_ref[back] = kv_ref[...]
    for s in range(1, back + 1):

        @pl.when(c - s < 0)
        def _():
            out_ref[back - s] = jnp.zeros(kv_ref.shape, kv_ref.dtype)

    for s in range(1, back + 1):

        @pl.when(c + s < n_ctx)
        def _():
            copy(s, c + s).wait_send()

        @pl.when(c - s >= 0)
        def _():
            copy(s, c).wait_recv()


def kv_share(kv, n_ctx, back):
    return pl.pallas_call(
        functools.partial(kv_share_kernel, n_ctx, back),
        out_shape=jax.ShapeDtypeStruct((back + 1,) + kv.shape, kv.dtype),
        in_specs=[pl.BlockSpec(memory_space=pltpu.VMEM)],
        out_specs=pl.BlockSpec(memory_space=pltpu.VMEM),
        scratch_shapes=[pltpu.SemaphoreType.DMA((back,)), pltpu.SemaphoreType.DMA((back + 1,))],
        compiler_params=pltpu.CompilerParams(collective_id=0, has_side_effects=True),
    )(kv)


def kv_return_kernel(n_ctx, back, own_ref, g_ref, out_ref, recv_buf, send_sem, recv_sem):
    c = lax.axis_index("ctx")
    f = lax.axis_index("fsdp")
    neighbour_barrier(n_ctx, back, c, f)

    def copy(s, dest):
        return pltpu.make_async_remote_copy(
            src_ref=g_ref.at[back - s],
            dst_ref=recv_buf.at[s - 1],
            send_sem=send_sem.at[s - 1],
            recv_sem=recv_sem.at[s - 1],
            device_id=(dest, f),
            device_id_type=MESH,
        )

    for s in range(1, back + 1):

        @pl.when(c - s >= 0)
        def _():
            copy(s, c - s).start()

    out_ref[...] = own_ref[...]
    for s in range(1, back + 1):

        @pl.when(c + s < n_ctx)
        def _():
            copy(s, c).wait_recv()
            out_ref[...] += recv_buf[s - 1].astype(jnp.float32)

    for s in range(1, back + 1):

        @pl.when(c - s >= 0)
        def _():
            copy(s, c - s).wait_send()


def kv_return(own, g, n_ctx, back):
    return pl.pallas_call(
        functools.partial(kv_return_kernel, n_ctx, back),
        out_shape=jax.ShapeDtypeStruct(own.shape, own.dtype),
        in_specs=[pl.BlockSpec(memory_space=pltpu.VMEM)] * 2,
        out_specs=pl.BlockSpec(memory_space=pltpu.VMEM),
        scratch_shapes=[
            pltpu.VMEM(g.shape, g.dtype),
            pltpu.SemaphoreType.DMA((back,)),
            pltpu.SemaphoreType.DMA((back,)),
        ],
        compiler_params=pltpu.CompilerParams(collective_id=1, has_side_effects=True),
    )(own, g)


def body(
    tokens,
    doc_lengths,
    attention_gain,
    query_weight,
    key_weight,
    value_weight,
    output_weight,
    feedforward_gain,
    gate_weight,
    up_weight,
    down_weight,
    cotangent,
):
    n_dev = lax.axis_size(ALL)
    rows = query_weight.shape[0]
    ff_rows = down_weight.shape[0]
    ff = gate_weight.shape[1]
    local_tokens = tokens[0].astype(jnp.float32)
    tok_rows = local_tokens.shape[0]
    stream_len = tok_rows * lax.axis_size("ctx")
    my_first = lax.axis_index("ctx") * tok_rows

    gain_cols = jnp.pad(
        jnp.stack([attention_gain, feedforward_gain], axis=1), ((0, 0), (0, GAIN_PAD - 2))
    )
    att_full = lax.all_gather(
        jnp.concatenate([query_weight, key_weight, value_weight, output_weight, gain_cols], axis=1),
        ALL,
        axis=0,
        tiled=True,
    )
    c_k = D
    c_v = D + KVW
    c_o = D + 2 * KVW
    c_g = 2 * D + 2 * KVW
    query_full = att_full[:, :c_k]
    key_full = att_full[:, c_k:c_v]
    value_full = att_full[:, c_v:c_o]
    qkv_full = att_full[:, :c_o]
    output_full = att_full[:, c_o:c_g]
    gain_one_f = att_full[:, c_g].astype(jnp.float32)
    gain_two_f = att_full[:, c_g + 1].astype(jnp.float32)

    key_docs_all, places_all = document_layout(doc_lengths[0], stream_len)
    query_docs = lax.dynamic_slice_in_dim(key_docs_all, my_first, tok_rows, 0)
    query_positions = lax.dynamic_slice_in_dim(places_all, my_first, tok_rows, 0)
    query_places = my_first + jnp.arange(tok_rows, dtype=jnp.int32)
    group_size = H // KVH
    score_scale = HD ** (-0.5)

    scale_one = rms_scale(local_tokens)
    normed_one = local_tokens * scale_one
    normed_low = (normed_one * gain_one_f).astype(jnp.bfloat16)
    qkv = jnp.dot(normed_low, qkv_full, preferred_element_type=jnp.float32)
    queries = qkv[:, :D]
    keys_new = qkv[:, D : D + KVW]
    values_new = qkv[:, D + KVW :]
    query_low = rotate(queries, query_positions, H, 1.0).astype(jnp.bfloat16)
    key_low = rotate(keys_new, query_positions, KVH, 1.0).astype(jnp.bfloat16)
    value_low = values_new.astype(jnp.bfloat16)

    gate_up_full = lax.all_gather(
        jnp.concatenate([gate_weight, up_weight], axis=1), ALL, axis=0, tiled=True
    )
    down_full = lax.all_gather(down_weight, ALL, axis=0, tiled=True)
    n_ctx = lax.axis_size("ctx")
    max_doc = min(DOC_MOST, KBLK * (stream_len // (2 * KBLK)))
    back = min(-(-(max_doc - 1) // tok_rows), n_ctx - 1)
    win = (back + 1) * tok_rows
    kv_win = kv_share(
        jnp.concatenate([key_low, value_low], axis=1), n_ctx, back
    ).reshape(win, 2 * KVW)
    docs_pad = jnp.concatenate(
        [jnp.full((back * tok_rows,), -1, jnp.int32), key_docs_all.astype(jnp.int32)]
    )
    key_docs = lax.dynamic_slice_in_dim(docs_pad, my_first, win, 0)
    key_places = my_first - back * tok_rows + jnp.arange(win, dtype=jnp.int32)
    key_block = kv_win[:, :KVW].reshape(win, KVH, HD)
    value_block = kv_win[:, KVW:].reshape(win, KVH, HD)
    query_grouped = query_low.reshape(tok_rows, KVH, group_size, HD)
    allowed = (
        (key_docs[None, :] == query_docs[:, None]) & (key_places[None, :] <= query_places[:, None])
    )[:, None, None, :]
    scores = (
        jnp.einsum("qgrd,kgd->qgrk", query_grouped, key_block, preferred_element_type=jnp.float32)
        * score_scale
    )
    scores = jnp.where(allowed, scores, MASKED_SCORE)
    row_max = jnp.max(scores, axis=-1, keepdims=True)
    exponent = jnp.where(allowed, jnp.exp(scores - row_max), 0.0)
    probs = exponent / jnp.sum(exponent, axis=-1, keepdims=True)
    probs_low = probs.astype(jnp.bfloat16)
    attended_sum = jnp.einsum(
        "qgrk,kgd->qgrd", probs_low, value_block, preferred_element_type=jnp.float32
    )
    attended_low = attended_sum.reshape(tok_rows, D).astype(jnp.bfloat16)
    middle = local_tokens + jnp.dot(attended_low, output_full, preferred_element_type=jnp.float32)

    scale_two = rms_scale(middle)
    normed_two = middle * scale_two
    normed_two_low = (normed_two * gain_two_f).astype(jnp.bfloat16)
    gate_up = jnp.dot(normed_two_low, gate_up_full, preferred_element_type=jnp.float32)
    gate_pre = gate_up[:, :ff]
    up_pre = gate_up[:, ff:]
    sigmoid = jax.nn.sigmoid(gate_pre)
    hidden_low = (gate_pre * sigmoid * up_pre).astype(jnp.bfloat16)
    layer_out = middle + jnp.dot(hidden_low, down_full, preferred_element_type=jnp.float32)

    grad_out = cotangent[0]
    down_sum = lax.psum_scatter(
        outer_rows(hidden_low, grad_out).astype(jnp.bfloat16), ALL, scatter_dimension=0, tiled=True
    )
    hidden_grad = times_transposed(grad_out, down_full)
    gate_grad = (hidden_grad * up_pre * sigmoid * (1.0 + gate_pre * (1.0 - sigmoid))).astype(
        jnp.bfloat16
    )
    up_grad = (hidden_grad * gate_pre * sigmoid).astype(jnp.bfloat16)
    gate_up_cat = jnp.concatenate([gate_grad, up_grad], axis=1)
    gate_up_term = outer_rows(normed_two_low, gate_up_cat)
    ff_pack, gate_up_cat = lax.optimization_barrier((gate_up_term.astype(jnp.bfloat16), gate_up_cat))
    ff_sum = lax.psum_scatter(ff_pack, ALL, scatter_dimension=0, tiled=True)
    normed_two_grad = times_transposed(gate_up_cat, gate_up_full)
    gain_two_term = jnp.sum(normed_two_grad * normed_two, axis=0)
    scaled_two = normed_two_grad * gain_two_f
    middle_grad = grad_out.astype(jnp.float32) + scale_two * (
        scaled_two - normed_two * jnp.mean(scaled_two * normed_two, axis=-1, keepdims=True)
    )
    branch_grad = middle_grad.astype(jnp.bfloat16)
    attended_grad_low = (
        times_transposed(branch_grad, output_full)
        .astype(jnp.bfloat16)
        .reshape(tok_rows, KVH, group_size, HD)
    )
    row_delta = jnp.sum(
        attended_grad_low.astype(jnp.float32) * attended_sum, axis=-1, keepdims=True
    )
    prob_grad = jnp.einsum(
        "qgrd,kgd->qgrk", attended_grad_low, value_block, preferred_element_type=jnp.float32
    )
    score_grad = (probs * (prob_grad - row_delta)).astype(jnp.bfloat16)
    query_accum = jnp.einsum(
        "qgrk,kgd->qgrd", score_grad, key_block, preferred_element_type=jnp.float32
    )
    key_term = jnp.einsum(
        "qgrk,qgrd->kgd", score_grad, query_grouped, preferred_element_type=jnp.float32
    ).reshape(win, KVW)
    value_term = jnp.einsum(
        "qgrk,qgrd->kgd", probs_low, attended_grad_low, preferred_element_type=jnp.float32
    ).reshape(win, KVW)
    kv_term = jnp.concatenate([key_term, value_term], axis=1).reshape(back + 1, tok_rows, 2 * KVW)
    kv_sum = kv_return(kv_term[back], kv_term[:back].astype(jnp.bfloat16), n_ctx, back)
    key_grad_low = rotate(kv_sum[:, :KVW] * score_scale, query_positions, KVH, -1.0).astype(
        jnp.bfloat16
    )
    value_grad_low = kv_sum[:, KVW:].astype(jnp.bfloat16)
    query_grad_low = rotate(
        query_accum.reshape(tok_rows, D) * score_scale, query_positions, H, -1.0
    ).astype(jnp.bfloat16)
    projection_cat = jnp.concatenate([query_grad_low, key_grad_low, value_grad_low], axis=1)
    normed_grad = times_transposed(projection_cat, qkv_full)
    gain_one_term = jnp.sum(normed_grad * normed_one, axis=0)
    scaled_one = normed_grad * gain_one_f
    tokens_grad = middle_grad + scale_one * (
        scaled_one - normed_one * jnp.mean(scaled_one * normed_one, axis=-1, keepdims=True)
    )
    gain_term_cols = jnp.pad(
        jnp.stack([gain_one_term, gain_two_term], axis=1), ((0, 0), (0, GAIN_PAD - 2))
    )
    gain_term_cols = gain_term_cols.at[0, GAIN_PAD - 1].set(ff_sum[0, 0].astype(jnp.float32) * 0.0)
    attention_sum = lax.psum_scatter(
        jnp.concatenate(
            [
                outer_rows(normed_low, projection_cat).astype(jnp.bfloat16),
                outer_rows(attended_low, branch_grad).astype(jnp.bfloat16),
                gain_term_cols.astype(jnp.bfloat16),
            ],
            axis=1,
        ),
        ALL,
        scatter_dimension=0,
        tiled=True,
    ).astype(jnp.float32)
    ff_sum = ff_sum.astype(jnp.float32)
    return (
        layer_out.astype(jnp.bfloat16)[None],
        tokens_grad[None],
        attention_sum[:, c_g],
        attention_sum[:, :c_k],
        attention_sum[:, c_k:c_v],
        attention_sum[:, c_v:c_o],
        attention_sum[:, c_o:c_g],
        attention_sum[:, c_g + 1],
        ff_sum[:, :ff],
        ff_sum[:, ff : 2 * ff],
        down_sum.astype(jnp.float32),
    )


def solution(mesh):
    weight = P(ALL, None)
    stream = P("fsdp", "ctx", None)
    return jax.shard_map(
        body,
        mesh=mesh,
        in_specs=(
            stream,
            P("fsdp", None),
            P(ALL),
            weight,
            weight,
            weight,
            weight,
            P(ALL),
            weight,
            weight,
            weight,
            stream,
        ),
        out_specs=(
            stream,
            stream,
            P(ALL),
            weight,
            weight,
            weight,
            weight,
            P(ALL),
            weight,
            weight,
            weight,
        ),
        check_vma=False,
    )
```

```python
import functools

import jax
import jax.numpy as jnp
from jax import lax
from jax.experimental import pallas as pl
from jax.experimental.pallas import tpu as pltpu
from jax.sharding import PartitionSpec as P

MESH = pl.DeviceIdType.MESH

D = 1536
H = 16
KVH = 8
HD = 96
KBLK = 512
DOC_MOST = 4096
KVW = 768
GAIN_PAD = 128

EPSILON = 1e-05
ROPE_BASE = 100000.0
MASKED_SCORE = -1e30
ALL = ("ctx", "fsdp")


def rms_scale(values):
    return lax.rsqrt(jnp.mean(values * values, axis=-1, keepdims=True) + EPSILON)


def document_layout(lengths, total):
    starts = jnp.cumsum(lengths) - lengths
    places = jnp.arange(total, dtype=jnp.int32)
    inside = places[:, None] >= starts[None, :]
    doc_ids = jnp.sum(inside.astype(jnp.int32), axis=1) - 1
    doc_starts = jnp.max(jnp.where(inside, starts[None, :], 0), axis=1)
    return (doc_ids, places - doc_starts)


def rotate(values, positions, head_count, direction):
    row_count = values.shape[0]
    half_dim = HD // 2
    inverse_freq = ROPE_BASE ** (-(jnp.arange(half_dim).astype(jnp.float32) * (2.0 / HD)))
    angles = positions.astype(jnp.float32)[:, None] * inverse_freq[None, :]
    cosine = jnp.cos(angles)[:, None, :]
    sine_part = direction * jnp.sin(angles)[:, None, :]
    grouped = values.reshape(row_count, head_count, HD)
    former = grouped[:, :, :half_dim]
    latter = grouped[:, :, half_dim:]
    turned = jnp.concatenate(
        [former * cosine - latter * sine_part, latter * cosine + former * sine_part], axis=2
    )
    return turned.reshape(row_count, head_count * HD)


def outer_rows(left, right):
    return lax.dot_general(
        left, right, (((0,), (0,)), ((), ())), preferred_element_type=jnp.float32
    )


def times_transposed(left, right):
    return lax.dot_general(
        left, right, (((1,), (1,)), ((), ())), preferred_element_type=jnp.float32
    )


def neighbour_barrier(n_ctx, back, c, f):
    barrier = pltpu.get_barrier_semaphore()
    for s in range(1, back + 1):
        for peer in ((c + s) % n_ctx, (c + n_ctx - s) % n_ctx):
            pl.semaphore_signal(barrier, inc=1, device_id=(peer, f), device_id_type=MESH)
    pl.semaphore_wait(barrier, 2 * back)


def kv_share_kernel(n_ctx, back, kv_ref, out_ref, send_sem, recv_sem):
    c = lax.axis_index("ctx")
    f = lax.axis_index("fsdp")
    neighbour_barrier(n_ctx, back, c, f)

    def copy(s, dest):
        return pltpu.make_async_remote_copy(
            src_ref=kv_ref,
            dst_ref=out_ref.at[back - s],
            send_sem=send_sem.at[s - 1],
            recv_sem=recv_sem.at[back - s],
            device_id=(dest, f),
            device_id_type=MESH,
        )

    for s in range(1, back + 1):

        @pl.when(c + s < n_ctx)
        def _():
            copy(s, c + s).start()

    out_ref[back] = kv_ref[...]
    for s in range(1, back + 1):

        @pl.when(c - s < 0)
        def _():
            out_ref[back - s] = jnp.zeros(kv_ref.shape, kv_ref.dtype)

    for s in range(1, back + 1):

        @pl.when(c + s < n_ctx)
        def _():
            copy(s, c + s).wait_send()

        @pl.when(c - s >= 0)
        def _():
            copy(s, c).wait_recv()


def kv_share(kv, n_ctx, back):
    return pl.pallas_call(
        functools.partial(kv_share_kernel, n_ctx, back),
        out_shape=jax.ShapeDtypeStruct((back + 1,) + kv.shape, kv.dtype),
        in_specs=[pl.BlockSpec(memory_space=pltpu.VMEM)],
        out_specs=pl.BlockSpec(memory_space=pltpu.VMEM),
        scratch_shapes=[pltpu.SemaphoreType.DMA((back,)), pltpu.SemaphoreType.DMA((back + 1,))],
        compiler_params=pltpu.CompilerParams(collective_id=0, has_side_effects=True),
    )(kv)


def kv_return_kernel(n_ctx, back, own_ref, g_ref, out_ref, recv_buf, send_sem, recv_sem):
    c = lax.axis_index("ctx")
    f = lax.axis_index("fsdp")
    neighbour_barrier(n_ctx, back, c, f)

    def copy(s, dest):
        return pltpu.make_async_remote_copy(
            src_ref=g_ref.at[back - s],
            dst_ref=recv_buf.at[s - 1],
            send_sem=send_sem.at[s - 1],
            recv_sem=recv_sem.at[s - 1],
            device_id=(dest, f),
            device_id_type=MESH,
        )

    for s in range(1, back + 1):

        @pl.when(c - s >= 0)
        def _():
            copy(s, c - s).start()

    out_ref[...] = own_ref[...]
    for s in range(1, back + 1):

        @pl.when(c + s < n_ctx)
        def _():
            copy(s, c).wait_recv()
            out_ref[...] += recv_buf[s - 1].astype(jnp.float32)

    for s in range(1, back + 1):

        @pl.when(c - s >= 0)
        def _():
            copy(s, c - s).wait_send()


def kv_return(own, g, n_ctx, back):
    return pl.pallas_call(
        functools.partial(kv_return_kernel, n_ctx, back),
        out_shape=jax.ShapeDtypeStruct(own.shape, own.dtype),
        in_specs=[pl.BlockSpec(memory_space=pltpu.VMEM)] * 2,
        out_specs=pl.BlockSpec(memory_space=pltpu.VMEM),
        scratch_shapes=[
            pltpu.VMEM(g.shape, g.dtype),
            pltpu.SemaphoreType.DMA((back,)),
            pltpu.SemaphoreType.DMA((back,)),
        ],
        compiler_params=pltpu.CompilerParams(collective_id=1, has_side_effects=True),
    )(own, g)


def peer_barrier(n_f, c, f):
    barrier = pltpu.get_barrier_semaphore()
    for k in range(1, n_f):
        pl.semaphore_signal(barrier, inc=1, device_id=(c, (f + k) % n_f), device_id_type=MESH)
    pl.semaphore_wait(barrier, n_f - 1)


def group_gather_kernel(n_f, x_ref, out_ref, send_sem, recv_sem):
    c = lax.axis_index("ctx")
    f = lax.axis_index("fsdp")
    peer_barrier(n_f, c, f)
    copies = []
    for k in range(1, n_f):
        copy = pltpu.make_async_remote_copy(
            src_ref=x_ref,
            dst_ref=out_ref.at[f],
            send_sem=send_sem.at[k - 1],
            recv_sem=recv_sem.at[k - 1],
            device_id=(c, (f + k) % n_f),
            device_id_type=MESH,
        )
        copy.start()
        copies.append(copy)
    out_ref[f] = x_ref[...]
    for k in range(1, n_f):
        pltpu.make_async_remote_copy(
            src_ref=x_ref,
            dst_ref=out_ref.at[(f + n_f - k) % n_f],
            send_sem=send_sem.at[k - 1],
            recv_sem=recv_sem.at[k - 1],
            device_id=(c, f),
            device_id_type=MESH,
        ).wait_recv()
    for copy in copies:
        copy.wait_send()


def group_gather(x, n_f):
    return pl.pallas_call(
        functools.partial(group_gather_kernel, n_f),
        out_shape=jax.ShapeDtypeStruct((n_f,) + x.shape, x.dtype),
        in_specs=[pl.BlockSpec(memory_space=pltpu.VMEM)],
        out_specs=pl.BlockSpec(memory_space=pltpu.VMEM),
        scratch_shapes=[pltpu.SemaphoreType.DMA((n_f - 1,)), pltpu.SemaphoreType.DMA((n_f - 1,))],
        compiler_params=pltpu.CompilerParams(collective_id=2, has_side_effects=True),
    )(x)


def group_reduce_kernel(n_f, p_ref, out_ref, recv_buf, send_sem, recv_sem):
    c = lax.axis_index("ctx")
    f = lax.axis_index("fsdp")
    peer_barrier(n_f, c, f)
    copies = []
    for k in range(1, n_f):
        dest = (f + k) % n_f
        copy = pltpu.make_async_remote_copy(
            src_ref=p_ref.at[dest],
            dst_ref=recv_buf.at[k - 1],
            send_sem=send_sem.at[k - 1],
            recv_sem=recv_sem.at[k - 1],
            device_id=(c, dest),
            device_id_type=MESH,
        )
        copy.start()
        copies.append(copy)
    out_ref[...] = p_ref[f]
    for k in range(1, n_f):
        copies[k - 1].wait_recv()
        out_ref[...] += recv_buf[k - 1]
    for copy in copies:
        copy.wait_send()


def group_reduce(p, n_f):
    return pl.pallas_call(
        functools.partial(group_reduce_kernel, n_f),
        out_shape=jax.ShapeDtypeStruct(p.shape[1:], p.dtype),
        in_specs=[pl.BlockSpec(memory_space=pltpu.VMEM)],
        out_specs=pl.BlockSpec(memory_space=pltpu.VMEM),
        scratch_shapes=[
            pltpu.VMEM((n_f - 1,) + p.shape[1:], p.dtype),
            pltpu.SemaphoreType.DMA((n_f - 1,)),
            pltpu.SemaphoreType.DMA((n_f - 1,)),
        ],
        compiler_params=pltpu.CompilerParams(collective_id=3, has_side_effects=True),
    )(p)


def body(
    tokens,
    doc_lengths,
    attention_gain,
    query_weight,
    key_weight,
    value_weight,
    output_weight,
    feedforward_gain,
    gate_weight,
    up_weight,
    down_weight,
    cotangent,
):
    n_dev = lax.axis_size(ALL)
    rows = query_weight.shape[0]
    ff_rows = down_weight.shape[0]
    ff = gate_weight.shape[1]
    local_tokens = tokens[0].astype(jnp.float32)
    tok_rows = local_tokens.shape[0]
    stream_len = tok_rows * lax.axis_size("ctx")
    my_first = lax.axis_index("ctx") * tok_rows

    gain_cols = jnp.pad(
        jnp.stack([attention_gain, feedforward_gain], axis=1), ((0, 0), (0, GAIN_PAD - 2))
    )
    att_full = lax.all_gather(
        jnp.concatenate([query_weight, key_weight, value_weight, output_weight, gain_cols], axis=1),
        ALL,
        axis=0,
        tiled=True,
    )
    c_k = D
    c_v = D + KVW
    c_o = D + 2 * KVW
    c_g = 2 * D + 2 * KVW
    query_full = att_full[:, :c_k]
    key_full = att_full[:, c_k:c_v]
    value_full = att_full[:, c_v:c_o]
    qkv_full = att_full[:, :c_o]
    output_full = att_full[:, c_o:c_g]
    gain_one_f = att_full[:, c_g].astype(jnp.float32)
    gain_two_f = att_full[:, c_g + 1].astype(jnp.float32)

    key_docs_all, places_all = document_layout(doc_lengths[0], stream_len)
    query_docs = lax.dynamic_slice_in_dim(key_docs_all, my_first, tok_rows, 0)
    query_positions = lax.dynamic_slice_in_dim(places_all, my_first, tok_rows, 0)
    query_places = my_first + jnp.arange(tok_rows, dtype=jnp.int32)
    group_size = H // KVH
    score_scale = HD ** (-0.5)

    scale_one = rms_scale(local_tokens)
    normed_one = local_tokens * scale_one
    normed_low = (normed_one * gain_one_f).astype(jnp.bfloat16)
    qkv = jnp.dot(normed_low, qkv_full, preferred_element_type=jnp.float32)
    queries = qkv[:, :D]
    keys_new = qkv[:, D : D + KVW]
    values_new = qkv[:, D + KVW :]
    query_low = rotate(queries, query_positions, H, 1.0).astype(jnp.bfloat16)
    key_low = rotate(keys_new, query_positions, KVH, 1.0).astype(jnp.bfloat16)
    value_low = values_new.astype(jnp.bfloat16)

    n_ctx = lax.axis_size("ctx")
    n_f = lax.axis_size("fsdp")
    chunk = ff_rows
    units = n_ctx * chunk
    gu_parts = jnp.transpose(
        jnp.stack([gate_weight, up_weight], axis=1).reshape(rows, 2, n_ctx, n_f, chunk),
        (3, 0, 1, 2, 4),
    )
    gu_parts = lax.all_to_all(gu_parts, "fsdp", 0, 0, tiled=True).reshape(n_f * rows, 2 * units)
    gate_up_tp = lax.all_gather(gu_parts, "ctx", axis=0, tiled=True)
    down_tp = lax.all_gather(down_weight, "ctx", axis=0, tiled=True)
    max_doc = min(DOC_MOST, KBLK * (stream_len // (2 * KBLK)))
    back = min(-(-(max_doc - 1) // tok_rows), n_ctx - 1)
    win = (back + 1) * tok_rows
    kv_win = kv_share(
        jnp.concatenate([key_low, value_low], axis=1), n_ctx, back
    ).reshape(win, 2 * KVW)
    docs_pad = jnp.concatenate(
        [jnp.full((back * tok_rows,), -1, jnp.int32), key_docs_all.astype(jnp.int32)]
    )
    key_docs = lax.dynamic_slice_in_dim(docs_pad, my_first, win, 0)
    key_places = my_first - back * tok_rows + jnp.arange(win, dtype=jnp.int32)
    key_block = kv_win[:, :KVW].reshape(win, KVH, HD)
    value_block = kv_win[:, KVW:].reshape(win, KVH, HD)
    query_grouped = query_low.reshape(tok_rows, KVH, group_size, HD)
    allowed = (
        (key_docs[None, :] == query_docs[:, None]) & (key_places[None, :] <= query_places[:, None])
    )[:, None, None, :]
    scores = (
        jnp.einsum("qgrd,kgd->qgrk", query_grouped, key_block, preferred_element_type=jnp.float32)
        * score_scale
    )
    scores = jnp.where(allowed, scores, MASKED_SCORE)
    row_max = jnp.max(scores, axis=-1, keepdims=True)
    exponent = jnp.where(allowed, jnp.exp(scores - row_max), 0.0)
    probs = exponent / jnp.sum(exponent, axis=-1, keepdims=True)
    probs_low = probs.astype(jnp.bfloat16)
    attended_sum = jnp.einsum(
        "qgrk,kgd->qgrd", probs_low, value_block, preferred_element_type=jnp.float32
    )
    attended_low = attended_sum.reshape(tok_rows, D).astype(jnp.bfloat16)
    middle = local_tokens + jnp.dot(attended_low, output_full, preferred_element_type=jnp.float32)

    scale_two = rms_scale(middle)
    normed_two = middle * scale_two
    normed_two_low = (normed_two * gain_two_f).astype(jnp.bfloat16)
    group_tokens = n_f * tok_rows
    xn2_all = group_gather(normed_two_low, n_f).reshape(group_tokens, D)
    gate_up = jnp.dot(xn2_all, gate_up_tp, preferred_element_type=jnp.float32)
    gate_pre = gate_up[:, :units]
    up_pre = gate_up[:, units:]
    sigmoid = jax.nn.sigmoid(gate_pre)
    hidden_low = (gate_pre * sigmoid * up_pre).astype(jnp.bfloat16)
    ff_part = jnp.dot(hidden_low, down_tp, preferred_element_type=jnp.float32)
    layer_out = middle + group_reduce(ff_part.reshape(n_f, tok_rows, D), n_f)

    grad_out = cotangent[0]
    grad_all = group_gather(grad_out, n_f).reshape(group_tokens, D)
    down_sum = lax.psum_scatter(
        outer_rows(hidden_low, grad_all).astype(jnp.bfloat16), "ctx", scatter_dimension=0, tiled=True
    )
    hidden_grad = times_transposed(grad_all, down_tp)
    gate_grad = (hidden_grad * up_pre * sigmoid * (1.0 + gate_pre * (1.0 - sigmoid))).astype(
        jnp.bfloat16
    )
    up_grad = (hidden_grad * gate_pre * sigmoid).astype(jnp.bfloat16)
    gate_up_cat = jnp.concatenate([gate_grad, up_grad], axis=1)
    gate_up_term = outer_rows(xn2_all, gate_up_cat)
    ff_pack, gate_up_cat = lax.optimization_barrier((gate_up_term.astype(jnp.bfloat16), gate_up_cat))
    gu_sum = lax.psum_scatter(ff_pack, "ctx", scatter_dimension=0, tiled=True)
    gu_sum = lax.all_to_all(gu_sum.reshape(n_f, rows, 2 * units), "fsdp", 0, 0, tiled=True)
    ff_sum = jnp.transpose(
        gu_sum.reshape(n_f, rows, 2, n_ctx, chunk), (1, 2, 3, 0, 4)
    ).reshape(rows, 2 * ff)
    normed_two_grad = group_reduce(
        times_transposed(gate_up_cat, gate_up_tp).reshape(n_f, tok_rows, D), n_f
    )
    gain_two_term = jnp.sum(normed_two_grad * normed_two, axis=0)
    scaled_two = normed_two_grad * gain_two_f
    middle_grad = grad_out.astype(jnp.float32) + scale_two * (
        scaled_two - normed_two * jnp.mean(scaled_two * normed_two, axis=-1, keepdims=True)
    )
    branch_grad = middle_grad.astype(jnp.bfloat16)
    attended_grad_low = (
        times_transposed(branch_grad, output_full)
        .astype(jnp.bfloat16)
        .reshape(tok_rows, KVH, group_size, HD)
    )
    row_delta = jnp.sum(
        attended_grad_low.astype(jnp.float32) * attended_sum, axis=-1, keepdims=True
    )
    prob_grad = jnp.einsum(
        "qgrd,kgd->qgrk", attended_grad_low, value_block, preferred_element_type=jnp.float32
    )
    score_grad = (probs * (prob_grad - row_delta)).astype(jnp.bfloat16)
    query_accum = jnp.einsum(
        "qgrk,kgd->qgrd", score_grad, key_block, preferred_element_type=jnp.float32
    )
    key_term = jnp.einsum(
        "qgrk,qgrd->kgd", score_grad, query_grouped, preferred_element_type=jnp.float32
    ).reshape(win, KVW)
    value_term = jnp.einsum(
        "qgrk,qgrd->kgd", probs_low, attended_grad_low, preferred_element_type=jnp.float32
    ).reshape(win, KVW)
    kv_term = jnp.concatenate([key_term, value_term], axis=1).reshape(back + 1, tok_rows, 2 * KVW)
    kv_sum = kv_return(kv_term[back], kv_term[:back].astype(jnp.bfloat16), n_ctx, back)
    key_grad_low = rotate(kv_sum[:, :KVW] * score_scale, query_positions, KVH, -1.0).astype(
        jnp.bfloat16
    )
    value_grad_low = kv_sum[:, KVW:].astype(jnp.bfloat16)
    query_grad_low = rotate(
        query_accum.reshape(tok_rows, D) * score_scale, query_positions, H, -1.0
    ).astype(jnp.bfloat16)
    projection_cat = jnp.concatenate([query_grad_low, key_grad_low, value_grad_low], axis=1)
    normed_grad = times_transposed(projection_cat, qkv_full)
    gain_one_term = jnp.sum(normed_grad * normed_one, axis=0)
    scaled_one = normed_grad * gain_one_f
    tokens_grad = middle_grad + scale_one * (
        scaled_one - normed_one * jnp.mean(scaled_one * normed_one, axis=-1, keepdims=True)
    )
    gain_term_cols = jnp.pad(
        jnp.stack([gain_one_term, gain_two_term], axis=1), ((0, 0), (0, GAIN_PAD - 2))
    )
    gain_term_cols = gain_term_cols.at[0, GAIN_PAD - 1].set(ff_sum[0, 0].astype(jnp.float32) * 0.0)
    attention_sum = lax.psum_scatter(
        jnp.concatenate(
            [
                outer_rows(normed_low, projection_cat).astype(jnp.bfloat16),
                outer_rows(attended_low, branch_grad).astype(jnp.bfloat16),
                gain_term_cols.astype(jnp.bfloat16),
            ],
            axis=1,
        ),
        ALL,
        scatter_dimension=0,
        tiled=True,
    ).astype(jnp.float32)
    ff_sum = ff_sum.astype(jnp.float32)
    return (
        layer_out.astype(jnp.bfloat16)[None],
        tokens_grad[None],
        attention_sum[:, c_g],
        attention_sum[:, :c_k],
        attention_sum[:, c_k:c_v],
        attention_sum[:, c_v:c_o],
        attention_sum[:, c_o:c_g],
        attention_sum[:, c_g + 1],
        ff_sum[:, :ff],
        ff_sum[:, ff : 2 * ff],
        down_sum.astype(jnp.float32),
    )


def solution(mesh):
    weight = P(ALL, None)
    stream = P("fsdp", "ctx", None)
    return jax.shard_map(
        body,
        mesh=mesh,
        in_specs=(
            stream,
            P("fsdp", None),
            P(ALL),
            weight,
            weight,
            weight,
            weight,
            P(ALL),
            weight,
            weight,
            weight,
            stream,
        ),
        out_specs=(
            stream,
            stream,
            P(ALL),
            weight,
            weight,
            weight,
            weight,
            P(ALL),
            weight,
            weight,
            weight,
        ),
        check_vma=False,
    )
```

```python
import functools

import jax
import jax.numpy as jnp
from jax import lax
from jax.experimental import pallas as pl
from jax.experimental.pallas import tpu as pltpu
from jax.sharding import PartitionSpec as P

MESH = pl.DeviceIdType.MESH

D = 1536
H = 16
KVH = 8
HD = 96
KBLK = 512
DOC_MOST = 4096
KVW = 768
GAIN_PAD = 128

EPSILON = 1e-05
ROPE_BASE = 100000.0
MASKED_SCORE = -1e30
ALL = ("ctx", "fsdp")


def rms_scale(values):
    return lax.rsqrt(jnp.mean(values * values, axis=-1, keepdims=True) + EPSILON)


def document_layout(lengths, total):
    starts = jnp.cumsum(lengths) - lengths
    places = jnp.arange(total, dtype=jnp.int32)
    inside = places[:, None] >= starts[None, :]
    doc_ids = jnp.sum(inside.astype(jnp.int32), axis=1) - 1
    doc_starts = jnp.max(jnp.where(inside, starts[None, :], 0), axis=1)
    return (doc_ids, places - doc_starts)


def rotate(values, positions, head_count, direction):
    row_count = values.shape[0]
    half_dim = HD // 2
    inverse_freq = ROPE_BASE ** (-(jnp.arange(half_dim).astype(jnp.float32) * (2.0 / HD)))
    angles = positions.astype(jnp.float32)[:, None] * inverse_freq[None, :]
    cosine = jnp.cos(angles)[:, None, :]
    sine_part = direction * jnp.sin(angles)[:, None, :]
    grouped = values.reshape(row_count, head_count, HD)
    former = grouped[:, :, :half_dim]
    latter = grouped[:, :, half_dim:]
    turned = jnp.concatenate(
        [former * cosine - latter * sine_part, latter * cosine + former * sine_part], axis=2
    )
    return turned.reshape(row_count, head_count * HD)


def outer_rows(left, right):
    return lax.dot_general(
        left, right, (((0,), (0,)), ((), ())), preferred_element_type=jnp.float32
    )


def times_transposed(left, right):
    return lax.dot_general(
        left, right, (((1,), (1,)), ((), ())), preferred_element_type=jnp.float32
    )


def neighbour_barrier(n_ctx, back, c, f):
    barrier = pltpu.get_barrier_semaphore()
    for s in range(1, back + 1):
        for peer in ((c + s) % n_ctx, (c + n_ctx - s) % n_ctx):
            pl.semaphore_signal(barrier, inc=1, device_id=(peer, f), device_id_type=MESH)
    pl.semaphore_wait(barrier, 2 * back)


def kv_share_kernel(n_ctx, back, kv_ref, out_ref, send_sem, recv_sem):
    c = lax.axis_index("ctx")
    f = lax.axis_index("fsdp")
    neighbour_barrier(n_ctx, back, c, f)

    def copy(s, dest):
        return pltpu.make_async_remote_copy(
            src_ref=kv_ref,
            dst_ref=out_ref.at[back - s],
            send_sem=send_sem.at[s - 1],
            recv_sem=recv_sem.at[back - s],
            device_id=(dest, f),
            device_id_type=MESH,
        )

    for s in range(1, back + 1):

        @pl.when(c + s < n_ctx)
        def _():
            copy(s, c + s).start()

    out_ref[back] = kv_ref[...]
    for s in range(1, back + 1):

        @pl.when(c - s < 0)
        def _():
            out_ref[back - s] = jnp.zeros(kv_ref.shape, kv_ref.dtype)

    for s in range(1, back + 1):

        @pl.when(c + s < n_ctx)
        def _():
            copy(s, c + s).wait_send()

        @pl.when(c - s >= 0)
        def _():
            copy(s, c).wait_recv()


def kv_share(kv, n_ctx, back):
    return pl.pallas_call(
        functools.partial(kv_share_kernel, n_ctx, back),
        out_shape=jax.ShapeDtypeStruct((back + 1,) + kv.shape, kv.dtype),
        in_specs=[pl.BlockSpec(memory_space=pltpu.VMEM)],
        out_specs=pl.BlockSpec(memory_space=pltpu.VMEM),
        scratch_shapes=[pltpu.SemaphoreType.DMA((back,)), pltpu.SemaphoreType.DMA((back + 1,))],
        compiler_params=pltpu.CompilerParams(collective_id=0, has_side_effects=True),
    )(kv)


def kv_return_kernel(n_ctx, back, own_ref, g_ref, out_ref, recv_buf, send_sem, recv_sem):
    c = lax.axis_index("ctx")
    f = lax.axis_index("fsdp")
    neighbour_barrier(n_ctx, back, c, f)

    def copy(s, dest):
        return pltpu.make_async_remote_copy(
            src_ref=g_ref.at[back - s],
            dst_ref=recv_buf.at[s - 1],
            send_sem=send_sem.at[s - 1],
            recv_sem=recv_sem.at[s - 1],
            device_id=(dest, f),
            device_id_type=MESH,
        )

    for s in range(1, back + 1):

        @pl.when(c - s >= 0)
        def _():
            copy(s, c - s).start()

    out_ref[...] = own_ref[...]
    for s in range(1, back + 1):

        @pl.when(c + s < n_ctx)
        def _():
            copy(s, c).wait_recv()
            out_ref[...] += recv_buf[s - 1].astype(jnp.float32)

    for s in range(1, back + 1):

        @pl.when(c - s >= 0)
        def _():
            copy(s, c - s).wait_send()


def kv_return(own, g, n_ctx, back):
    return pl.pallas_call(
        functools.partial(kv_return_kernel, n_ctx, back),
        out_shape=jax.ShapeDtypeStruct(own.shape, own.dtype),
        in_specs=[pl.BlockSpec(memory_space=pltpu.VMEM)] * 2,
        out_specs=pl.BlockSpec(memory_space=pltpu.VMEM),
        scratch_shapes=[
            pltpu.VMEM(g.shape, g.dtype),
            pltpu.SemaphoreType.DMA((back,)),
            pltpu.SemaphoreType.DMA((back,)),
        ],
        compiler_params=pltpu.CompilerParams(collective_id=1, has_side_effects=True),
    )(own, g)


def peer_barrier(n_f, c, f):
    barrier = pltpu.get_barrier_semaphore()
    for k in range(1, n_f):
        pl.semaphore_signal(barrier, inc=1, device_id=(c, (f + k) % n_f), device_id_type=MESH)
    pl.semaphore_wait(barrier, n_f - 1)


def group_gather_kernel(n_f, x_ref, out_ref, send_sem, recv_sem):
    c = lax.axis_index("ctx")
    f = lax.axis_index("fsdp")
    peer_barrier(n_f, c, f)
    copies = []
    for k in range(1, n_f):
        copy = pltpu.make_async_remote_copy(
            src_ref=x_ref,
            dst_ref=out_ref.at[f],
            send_sem=send_sem.at[k - 1],
            recv_sem=recv_sem.at[k - 1],
            device_id=(c, (f + k) % n_f),
            device_id_type=MESH,
        )
        copy.start()
        copies.append(copy)
    out_ref[f] = x_ref[...]
    for k in range(1, n_f):
        pltpu.make_async_remote_copy(
            src_ref=x_ref,
            dst_ref=out_ref.at[(f + n_f - k) % n_f],
            send_sem=send_sem.at[k - 1],
            recv_sem=recv_sem.at[k - 1],
            device_id=(c, f),
            device_id_type=MESH,
        ).wait_recv()
    for copy in copies:
        copy.wait_send()


def group_gather(x, n_f):
    return pl.pallas_call(
        functools.partial(group_gather_kernel, n_f),
        out_shape=jax.ShapeDtypeStruct((n_f,) + x.shape, x.dtype),
        in_specs=[pl.BlockSpec(memory_space=pltpu.VMEM)],
        out_specs=pl.BlockSpec(memory_space=pltpu.VMEM),
        scratch_shapes=[pltpu.SemaphoreType.DMA((n_f - 1,)), pltpu.SemaphoreType.DMA((n_f - 1,))],
        compiler_params=pltpu.CompilerParams(collective_id=2, has_side_effects=True),
    )(x)


def group_reduce_kernel(n_f, p_ref, out_ref, recv_buf, send_sem, recv_sem):
    c = lax.axis_index("ctx")
    f = lax.axis_index("fsdp")
    peer_barrier(n_f, c, f)
    copies = []
    for k in range(1, n_f):
        dest = (f + k) % n_f
        copy = pltpu.make_async_remote_copy(
            src_ref=p_ref.at[dest],
            dst_ref=recv_buf.at[k - 1],
            send_sem=send_sem.at[k - 1],
            recv_sem=recv_sem.at[k - 1],
            device_id=(c, dest),
            device_id_type=MESH,
        )
        copy.start()
        copies.append(copy)
    out_ref[...] = p_ref[f]
    for k in range(1, n_f):
        copies[k - 1].wait_recv()
        out_ref[...] += recv_buf[k - 1]
    for copy in copies:
        copy.wait_send()


def group_reduce(p, n_f):
    return pl.pallas_call(
        functools.partial(group_reduce_kernel, n_f),
        out_shape=jax.ShapeDtypeStruct(p.shape[1:], p.dtype),
        in_specs=[pl.BlockSpec(memory_space=pltpu.VMEM)],
        out_specs=pl.BlockSpec(memory_space=pltpu.VMEM),
        scratch_shapes=[
            pltpu.VMEM((n_f - 1,) + p.shape[1:], p.dtype),
            pltpu.SemaphoreType.DMA((n_f - 1,)),
            pltpu.SemaphoreType.DMA((n_f - 1,)),
        ],
        compiler_params=pltpu.CompilerParams(collective_id=3, has_side_effects=True),
    )(p)


def pair_barrier(c, partner, across):
    barrier = pltpu.get_barrier_semaphore()
    pl.semaphore_signal(barrier, inc=1, device_id=(c, partner), device_id_type=MESH)
    pl.semaphore_signal(barrier, inc=1, device_id=(c, across), device_id_type=MESH)
    pl.semaphore_wait(barrier, 2)


def quad_ids():
    c = lax.axis_index("ctx")
    f = lax.axis_index("fsdp")
    partner = f + 1 - 2 * (f % 2)
    across = (f + 2) % 4
    diagonal = (partner + 2) % 4
    return c, f, partner, across, diagonal


def quad_gather_kernel(x_ref, out_ref, send_sem, recv_sem):
    c, f, partner, across, diagonal = quad_ids()
    pair_barrier(c, partner, across)

    def copy(src, slot, dest, k):
        return pltpu.make_async_remote_copy(
            src_ref=src,
            dst_ref=out_ref.at[slot],
            send_sem=send_sem.at[k],
            recv_sem=recv_sem.at[slot],
            device_id=(c, dest),
            device_id_type=MESH,
        )

    first = copy(x_ref, f, across, 0)
    first.start()
    own = copy(x_ref, f, partner, 1)
    own.start()
    out_ref[f] = x_ref[...]
    copy(x_ref, across, f, 0).wait_recv()
    relay = copy(out_ref.at[across], across, partner, 2)
    relay.start()
    copy(x_ref, partner, f, 0).wait_recv()
    copy(x_ref, diagonal, f, 0).wait_recv()
    first.wait_send()
    own.wait_send()
    relay.wait_send()


def quad_gather(x):
    return pl.pallas_call(
        quad_gather_kernel,
        out_shape=jax.ShapeDtypeStruct((4,) + x.shape, x.dtype),
        in_specs=[pl.BlockSpec(memory_space=pltpu.VMEM)],
        out_specs=pl.BlockSpec(memory_space=pltpu.VMEM),
        scratch_shapes=[pltpu.SemaphoreType.DMA((3,)), pltpu.SemaphoreType.DMA((4,))],
        compiler_params=pltpu.CompilerParams(collective_id=4, has_side_effects=True),
    )(x)


def quad_reduce_kernel(p_ref, out_ref, near_buf, far_buf, sum_buf, send_sem, recv_sem):
    c, f, partner, across, diagonal = quad_ids()
    pair_barrier(c, partner, across)

    def copy(src, dst, dest, k):
        return pltpu.make_async_remote_copy(
            src_ref=src,
            dst_ref=dst,
            send_sem=send_sem.at[k],
            recv_sem=recv_sem.at[k],
            device_id=(c, dest),
            device_id_type=MESH,
        )

    to_partner = copy(p_ref.at[partner], near_buf.at[0], partner, 0)
    to_partner.start()
    to_diagonal = copy(p_ref.at[diagonal], near_buf.at[1], partner, 1)
    to_diagonal.start()
    to_partner.wait_recv()
    to_diagonal.wait_recv()
    sum_buf[...] = p_ref[across] + near_buf[1]
    to_across = copy(sum_buf, far_buf, across, 2)
    to_across.start()
    out_ref[...] = p_ref[f] + near_buf[0]
    to_across.wait_recv()
    out_ref[...] += far_buf[...]
    to_partner.wait_send()
    to_diagonal.wait_send()
    to_across.wait_send()


def quad_reduce(p):
    block = p.shape[1:]
    return pl.pallas_call(
        quad_reduce_kernel,
        out_shape=jax.ShapeDtypeStruct(block, p.dtype),
        in_specs=[pl.BlockSpec(memory_space=pltpu.VMEM)],
        out_specs=pl.BlockSpec(memory_space=pltpu.VMEM),
        scratch_shapes=[
            pltpu.VMEM((2,) + block, p.dtype),
            pltpu.VMEM(block, p.dtype),
            pltpu.VMEM(block, p.dtype),
            pltpu.SemaphoreType.DMA((3,)),
            pltpu.SemaphoreType.DMA((3,)),
        ],
        compiler_params=pltpu.CompilerParams(collective_id=5, has_side_effects=True),
    )(p)


def fsdp_gather(x, n_f):
    if n_f == 4:
        return quad_gather(x)
    return group_gather(x, n_f)


def fsdp_reduce(p, n_f):
    if n_f == 4:
        return quad_reduce(p)
    return group_reduce(p, n_f)


def body(
    tokens,
    doc_lengths,
    attention_gain,
    query_weight,
    key_weight,
    value_weight,
    output_weight,
    feedforward_gain,
    gate_weight,
    up_weight,
    down_weight,
    cotangent,
):
    n_dev = lax.axis_size(ALL)
    rows = query_weight.shape[0]
    ff_rows = down_weight.shape[0]
    ff = gate_weight.shape[1]
    local_tokens = tokens[0].astype(jnp.float32)
    tok_rows = local_tokens.shape[0]
    stream_len = tok_rows * lax.axis_size("ctx")
    my_first = lax.axis_index("ctx") * tok_rows

    gain_cols = jnp.pad(
        jnp.stack([attention_gain, feedforward_gain], axis=1), ((0, 0), (0, GAIN_PAD - 2))
    )
    att_full = lax.all_gather(
        jnp.concatenate([query_weight, key_weight, value_weight, output_weight, gain_cols], axis=1),
        ALL,
        axis=0,
        tiled=True,
    )
    c_k = D
    c_v = D + KVW
    c_o = D + 2 * KVW
    c_g = 2 * D + 2 * KVW
    query_full = att_full[:, :c_k]
    key_full = att_full[:, c_k:c_v]
    value_full = att_full[:, c_v:c_o]
    qkv_full = att_full[:, :c_o]
    output_full = att_full[:, c_o:c_g]
    gain_one_f = att_full[:, c_g].astype(jnp.float32)
    gain_two_f = att_full[:, c_g + 1].astype(jnp.float32)

    key_docs_all, places_all = document_layout(doc_lengths[0], stream_len)
    query_docs = lax.dynamic_slice_in_dim(key_docs_all, my_first, tok_rows, 0)
    query_positions = lax.dynamic_slice_in_dim(places_all, my_first, tok_rows, 0)
    query_places = my_first + jnp.arange(tok_rows, dtype=jnp.int32)
    group_size = H // KVH
    score_scale = HD ** (-0.5)

    scale_one = rms_scale(local_tokens)
    normed_one = local_tokens * scale_one
    normed_low = (normed_one * gain_one_f).astype(jnp.bfloat16)
    qkv = jnp.dot(normed_low, qkv_full, preferred_element_type=jnp.float32)
    queries = qkv[:, :D]
    keys_new = qkv[:, D : D + KVW]
    values_new = qkv[:, D + KVW :]
    query_low = rotate(queries, query_positions, H, 1.0).astype(jnp.bfloat16)
    key_low = rotate(keys_new, query_positions, KVH, 1.0).astype(jnp.bfloat16)
    value_low = values_new.astype(jnp.bfloat16)

    n_ctx = lax.axis_size("ctx")
    n_f = lax.axis_size("fsdp")
    chunk = ff_rows
    units = n_ctx * chunk
    gu_parts = jnp.transpose(
        jnp.stack([gate_weight, up_weight], axis=1).reshape(rows, 2, n_ctx, n_f, chunk),
        (3, 0, 1, 2, 4),
    )
    gu_parts = lax.all_to_all(gu_parts, "fsdp", 0, 0, tiled=True).reshape(n_f * rows, 2 * units)
    down_rows = D // (2 * n_ctx)
    ff_stack = lax.all_gather(
        jnp.concatenate([gu_parts, down_weight.reshape(down_rows, 2 * units)], axis=0),
        "ctx",
        axis=0,
        tiled=False,
    )
    gate_up_tp = ff_stack[:, : n_f * rows].reshape(n_ctx * n_f * rows, 2 * units)
    down_tp = ff_stack[:, n_f * rows :].reshape(n_ctx, ff_rows, D).reshape(units, D)
    max_doc = min(DOC_MOST, KBLK * (stream_len // (2 * KBLK)))
    back = min(-(-(max_doc - 1) // tok_rows), n_ctx - 1)
    win = (back + 1) * tok_rows
    kv_win = kv_share(
        jnp.concatenate([key_low, value_low], axis=1), n_ctx, back
    ).reshape(win, 2 * KVW)
    docs_pad = jnp.concatenate(
        [jnp.full((back * tok_rows,), -1, jnp.int32), key_docs_all.astype(jnp.int32)]
    )
    key_docs = lax.dynamic_slice_in_dim(docs_pad, my_first, win, 0)
    key_places = my_first - back * tok_rows + jnp.arange(win, dtype=jnp.int32)
    key_block = kv_win[:, :KVW].reshape(win, KVH, HD)
    value_block = kv_win[:, KVW:].reshape(win, KVH, HD)
    query_grouped = query_low.reshape(tok_rows, KVH, group_size, HD)
    allowed = (
        (key_docs[None, :] == query_docs[:, None]) & (key_places[None, :] <= query_places[:, None])
    )[:, None, None, :]
    scores = (
        jnp.einsum("qgrd,kgd->qgrk", query_grouped, key_block, preferred_element_type=jnp.float32)
        * score_scale
    )
    scores = jnp.where(allowed, scores, MASKED_SCORE)
    row_max = jnp.max(scores, axis=-1, keepdims=True)
    exponent = jnp.where(allowed, jnp.exp(scores - row_max), 0.0)
    probs = exponent / jnp.sum(exponent, axis=-1, keepdims=True)
    probs_low = probs.astype(jnp.bfloat16)
    attended_sum = jnp.einsum(
        "qgrk,kgd->qgrd", probs_low, value_block, preferred_element_type=jnp.float32
    )
    attended_low = attended_sum.reshape(tok_rows, D).astype(jnp.bfloat16)
    middle = local_tokens + jnp.dot(attended_low, output_full, preferred_element_type=jnp.float32)

    scale_two = rms_scale(middle)
    normed_two = middle * scale_two
    normed_two_low = (normed_two * gain_two_f).astype(jnp.bfloat16)
    group_tokens = n_f * tok_rows
    xn2_all = fsdp_gather(normed_two_low, n_f).reshape(group_tokens, D)
    gate_up = jnp.dot(xn2_all, gate_up_tp, preferred_element_type=jnp.float32)
    gate_pre = gate_up[:, :units]
    up_pre = gate_up[:, units:]
    sigmoid = jax.nn.sigmoid(gate_pre)
    hidden_low = (gate_pre * sigmoid * up_pre).astype(jnp.bfloat16)
    ff_part = jnp.dot(hidden_low, down_tp, preferred_element_type=jnp.float32)
    layer_out = middle + fsdp_reduce(ff_part.reshape(n_f, tok_rows, D), n_f)

    grad_out = cotangent[0]
    grad_all = fsdp_gather(grad_out, n_f).reshape(group_tokens, D)
    down_sum = lax.psum_scatter(
        outer_rows(hidden_low, grad_all).astype(jnp.bfloat16), "ctx", scatter_dimension=0, tiled=True
    )
    hidden_grad = times_transposed(grad_all, down_tp)
    gate_grad = (hidden_grad * up_pre * sigmoid * (1.0 + gate_pre * (1.0 - sigmoid))).astype(
        jnp.bfloat16
    )
    up_grad = (hidden_grad * gate_pre * sigmoid).astype(jnp.bfloat16)
    gate_up_cat = jnp.concatenate([gate_grad, up_grad], axis=1)
    gate_up_term = outer_rows(xn2_all, gate_up_cat)
    ff_pack, gate_up_cat = lax.optimization_barrier((gate_up_term.astype(jnp.bfloat16), gate_up_cat))
    gu_sum = lax.psum_scatter(ff_pack, "ctx", scatter_dimension=0, tiled=True)
    gu_sum = lax.all_to_all(gu_sum.reshape(n_f, rows, 2 * units), "fsdp", 0, 0, tiled=True)
    ff_sum = jnp.transpose(
        gu_sum.reshape(n_f, rows, 2, n_ctx, chunk), (1, 2, 3, 0, 4)
    ).reshape(rows, 2 * ff)
    normed_two_grad = fsdp_reduce(
        times_transposed(gate_up_cat, gate_up_tp).reshape(n_f, tok_rows, D), n_f
    )
    gain_two_term = jnp.sum(normed_two_grad * normed_two, axis=0)
    scaled_two = normed_two_grad * gain_two_f
    middle_grad = grad_out.astype(jnp.float32) + scale_two * (
        scaled_two - normed_two * jnp.mean(scaled_two * normed_two, axis=-1, keepdims=True)
    )
    branch_grad = middle_grad.astype(jnp.bfloat16)
    attended_grad_low = (
        times_transposed(branch_grad, output_full)
        .astype(jnp.bfloat16)
        .reshape(tok_rows, KVH, group_size, HD)
    )
    row_delta = jnp.sum(
        attended_grad_low.astype(jnp.float32) * attended_sum, axis=-1, keepdims=True
    )
    prob_grad = jnp.einsum(
        "qgrd,kgd->qgrk", attended_grad_low, value_block, preferred_element_type=jnp.float32
    )
    score_grad = (probs * (prob_grad - row_delta)).astype(jnp.bfloat16)
    query_accum = jnp.einsum(
        "qgrk,kgd->qgrd", score_grad, key_block, preferred_element_type=jnp.float32
    )
    key_term = jnp.einsum(
        "qgrk,qgrd->kgd", score_grad, query_grouped, preferred_element_type=jnp.float32
    ).reshape(win, KVW)
    value_term = jnp.einsum(
        "qgrk,qgrd->kgd", probs_low, attended_grad_low, preferred_element_type=jnp.float32
    ).reshape(win, KVW)
    kv_term = jnp.concatenate([key_term, value_term], axis=1).reshape(back + 1, tok_rows, 2 * KVW)
    kv_sum = kv_return(kv_term[back], kv_term[:back].astype(jnp.bfloat16), n_ctx, back)
    key_grad_low = rotate(kv_sum[:, :KVW] * score_scale, query_positions, KVH, -1.0).astype(
        jnp.bfloat16
    )
    value_grad_low = kv_sum[:, KVW:].astype(jnp.bfloat16)
    query_grad_low = rotate(
        query_accum.reshape(tok_rows, D) * score_scale, query_positions, H, -1.0
    ).astype(jnp.bfloat16)
    projection_cat = jnp.concatenate([query_grad_low, key_grad_low, value_grad_low], axis=1)
    normed_grad = times_transposed(projection_cat, qkv_full)
    gain_one_term = jnp.sum(normed_grad * normed_one, axis=0)
    scaled_one = normed_grad * gain_one_f
    tokens_grad = middle_grad + scale_one * (
        scaled_one - normed_one * jnp.mean(scaled_one * normed_one, axis=-1, keepdims=True)
    )
    gain_term_cols = jnp.pad(
        jnp.stack([gain_one_term, gain_two_term], axis=1), ((0, 0), (0, GAIN_PAD - 2))
    )
    gain_term_cols = gain_term_cols.at[0, GAIN_PAD - 1].set(ff_sum[0, 0].astype(jnp.float32) * 0.0)
    attention_sum = lax.psum_scatter(
        jnp.concatenate(
            [
                outer_rows(normed_low, projection_cat).astype(jnp.bfloat16),
                outer_rows(attended_low, branch_grad).astype(jnp.bfloat16),
                gain_term_cols.astype(jnp.bfloat16),
            ],
            axis=1,
        ),
        ALL,
        scatter_dimension=0,
        tiled=True,
    ).astype(jnp.float32)
    ff_sum = ff_sum.astype(jnp.float32)
    return (
        layer_out.astype(jnp.bfloat16)[None],
        tokens_grad[None],
        attention_sum[:, c_g],
        attention_sum[:, :c_k],
        attention_sum[:, c_k:c_v],
        attention_sum[:, c_v:c_o],
        attention_sum[:, c_o:c_g],
        attention_sum[:, c_g + 1],
        ff_sum[:, :ff],
        ff_sum[:, ff : 2 * ff],
        down_sum.astype(jnp.float32),
    )


def solution(mesh):
    weight = P(ALL, None)
    stream = P("fsdp", "ctx", None)
    return jax.shard_map(
        body,
        mesh=mesh,
        in_specs=(
            stream,
            P("fsdp", None),
            P(ALL),
            weight,
            weight,
            weight,
            weight,
            P(ALL),
            weight,
            weight,
            weight,
            stream,
        ),
        out_specs=(
            stream,
            stream,
            P(ALL),
            weight,
            weight,
            weight,
            weight,
            P(ALL),
            weight,
            weight,
            weight,
        ),
        check_vma=False,
    )
```

```python
import functools

import jax
import jax.numpy as jnp
from jax import lax
from jax.experimental import pallas as pl
from jax.experimental.pallas import tpu as pltpu
from jax.sharding import PartitionSpec as P

MESH = pl.DeviceIdType.MESH

D = 1536
H = 16
KVH = 8
HD = 96
KBLK = 512
DOC_MOST = 4096
KVW = 768
GAIN_PAD = 128

EPSILON = 1e-05
ROPE_BASE = 100000.0
MASKED_SCORE = -1e30
ALL = ("ctx", "fsdp")


def rms_scale(values):
    return lax.rsqrt(jnp.mean(values * values, axis=-1, keepdims=True) + EPSILON)


def document_layout(lengths, total):
    starts = jnp.cumsum(lengths) - lengths
    places = jnp.arange(total, dtype=jnp.int32)
    inside = places[:, None] >= starts[None, :]
    doc_ids = jnp.sum(inside.astype(jnp.int32), axis=1) - 1
    doc_starts = jnp.max(jnp.where(inside, starts[None, :], 0), axis=1)
    return (doc_ids, places - doc_starts)


def rotate(values, positions, head_count, direction):
    row_count = values.shape[0]
    half_dim = HD // 2
    inverse_freq = ROPE_BASE ** (-(jnp.arange(half_dim).astype(jnp.float32) * (2.0 / HD)))
    angles = positions.astype(jnp.float32)[:, None] * inverse_freq[None, :]
    cosine = jnp.cos(angles)[:, None, :]
    sine_part = direction * jnp.sin(angles)[:, None, :]
    grouped = values.reshape(row_count, head_count, HD)
    former = grouped[:, :, :half_dim]
    latter = grouped[:, :, half_dim:]
    turned = jnp.concatenate(
        [former * cosine - latter * sine_part, latter * cosine + former * sine_part], axis=2
    )
    return turned.reshape(row_count, head_count * HD)


def outer_rows(left, right):
    return lax.dot_general(
        left, right, (((0,), (0,)), ((), ())), preferred_element_type=jnp.float32
    )


def times_transposed(left, right):
    return lax.dot_general(
        left, right, (((1,), (1,)), ((), ())), preferred_element_type=jnp.float32
    )


def neighbour_barrier(n_ctx, back, c, f):
    barrier = pltpu.get_barrier_semaphore()
    for s in range(1, back + 1):
        for peer in ((c + s) % n_ctx, (c + n_ctx - s) % n_ctx):
            pl.semaphore_signal(barrier, inc=1, device_id=(peer, f), device_id_type=MESH)
    pl.semaphore_wait(barrier, 2 * back)


def kv_share_kernel(n_ctx, back, kv_ref, out_ref, send_sem, recv_sem):
    c = lax.axis_index("ctx")
    f = lax.axis_index("fsdp")
    neighbour_barrier(n_ctx, back, c, f)

    def copy(s, dest):
        return pltpu.make_async_remote_copy(
            src_ref=kv_ref,
            dst_ref=out_ref.at[back - s],
            send_sem=send_sem.at[s - 1],
            recv_sem=recv_sem.at[back - s],
            device_id=(dest, f),
            device_id_type=MESH,
        )

    for s in range(1, back + 1):

        @pl.when(c + s < n_ctx)
        def _():
            copy(s, c + s).start()

    out_ref[back] = kv_ref[...]
    for s in range(1, back + 1):

        @pl.when(c - s < 0)
        def _():
            out_ref[back - s] = jnp.zeros(kv_ref.shape, kv_ref.dtype)

    for s in range(1, back + 1):

        @pl.when(c + s < n_ctx)
        def _():
            copy(s, c + s).wait_send()

        @pl.when(c - s >= 0)
        def _():
            copy(s, c).wait_recv()


def kv_share(kv, n_ctx, back):
    return pl.pallas_call(
        functools.partial(kv_share_kernel, n_ctx, back),
        out_shape=jax.ShapeDtypeStruct((back + 1,) + kv.shape, kv.dtype),
        in_specs=[pl.BlockSpec(memory_space=pltpu.VMEM)],
        out_specs=pl.BlockSpec(memory_space=pltpu.VMEM),
        scratch_shapes=[pltpu.SemaphoreType.DMA((back,)), pltpu.SemaphoreType.DMA((back + 1,))],
        compiler_params=pltpu.CompilerParams(collective_id=0, has_side_effects=True),
    )(kv)


def kv_return_kernel(n_ctx, back, own_ref, g_ref, out_ref, recv_buf, send_sem, recv_sem):
    c = lax.axis_index("ctx")
    f = lax.axis_index("fsdp")
    neighbour_barrier(n_ctx, back, c, f)

    def copy(s, dest):
        return pltpu.make_async_remote_copy(
            src_ref=g_ref.at[back - s],
            dst_ref=recv_buf.at[s - 1],
            send_sem=send_sem.at[s - 1],
            recv_sem=recv_sem.at[s - 1],
            device_id=(dest, f),
            device_id_type=MESH,
        )

    for s in range(1, back + 1):

        @pl.when(c - s >= 0)
        def _():
            copy(s, c - s).start()

    out_ref[...] = own_ref[...]
    for s in range(1, back + 1):

        @pl.when(c + s < n_ctx)
        def _():
            copy(s, c).wait_recv()
            out_ref[...] += recv_buf[s - 1].astype(jnp.float32)

    for s in range(1, back + 1):

        @pl.when(c - s >= 0)
        def _():
            copy(s, c - s).wait_send()


def kv_return(own, g, n_ctx, back):
    return pl.pallas_call(
        functools.partial(kv_return_kernel, n_ctx, back),
        out_shape=jax.ShapeDtypeStruct(own.shape, own.dtype),
        in_specs=[pl.BlockSpec(memory_space=pltpu.VMEM)] * 2,
        out_specs=pl.BlockSpec(memory_space=pltpu.VMEM),
        scratch_shapes=[
            pltpu.VMEM(g.shape, g.dtype),
            pltpu.SemaphoreType.DMA((back,)),
            pltpu.SemaphoreType.DMA((back,)),
        ],
        compiler_params=pltpu.CompilerParams(collective_id=1, has_side_effects=True),
    )(own, g)


def peer_barrier(n_f, c, f):
    barrier = pltpu.get_barrier_semaphore()
    for k in range(1, n_f):
        pl.semaphore_signal(barrier, inc=1, device_id=(c, (f + k) % n_f), device_id_type=MESH)
    pl.semaphore_wait(barrier, n_f - 1)


def group_gather_kernel(n_f, x_ref, out_ref, send_sem, recv_sem):
    c = lax.axis_index("ctx")
    f = lax.axis_index("fsdp")
    peer_barrier(n_f, c, f)
    copies = []
    for k in range(1, n_f):
        copy = pltpu.make_async_remote_copy(
            src_ref=x_ref,
            dst_ref=out_ref.at[f],
            send_sem=send_sem.at[k - 1],
            recv_sem=recv_sem.at[k - 1],
            device_id=(c, (f + k) % n_f),
            device_id_type=MESH,
        )
        copy.start()
        copies.append(copy)
    out_ref[f] = x_ref[...]
    for k in range(1, n_f):
        pltpu.make_async_remote_copy(
            src_ref=x_ref,
            dst_ref=out_ref.at[(f + n_f - k) % n_f],
            send_sem=send_sem.at[k - 1],
            recv_sem=recv_sem.at[k - 1],
            device_id=(c, f),
            device_id_type=MESH,
        ).wait_recv()
    for copy in copies:
        copy.wait_send()


def group_gather(x, n_f):
    return pl.pallas_call(
        functools.partial(group_gather_kernel, n_f),
        out_shape=jax.ShapeDtypeStruct((n_f,) + x.shape, x.dtype),
        in_specs=[pl.BlockSpec(memory_space=pltpu.VMEM)],
        out_specs=pl.BlockSpec(memory_space=pltpu.VMEM),
        scratch_shapes=[pltpu.SemaphoreType.DMA((n_f - 1,)), pltpu.SemaphoreType.DMA((n_f - 1,))],
        compiler_params=pltpu.CompilerParams(collective_id=2, has_side_effects=True),
    )(x)


def group_reduce_kernel(n_f, p_ref, out_ref, recv_buf, send_sem, recv_sem):
    c = lax.axis_index("ctx")
    f = lax.axis_index("fsdp")
    peer_barrier(n_f, c, f)
    copies = []
    for k in range(1, n_f):
        dest = (f + k) % n_f
        copy = pltpu.make_async_remote_copy(
            src_ref=p_ref.at[dest],
            dst_ref=recv_buf.at[k - 1],
            send_sem=send_sem.at[k - 1],
            recv_sem=recv_sem.at[k - 1],
            device_id=(c, dest),
            device_id_type=MESH,
        )
        copy.start()
        copies.append(copy)
    out_ref[...] = p_ref[f]
    for k in range(1, n_f):
        copies[k - 1].wait_recv()
        out_ref[...] += recv_buf[k - 1]
    for copy in copies:
        copy.wait_send()


def group_reduce(p, n_f):
    return pl.pallas_call(
        functools.partial(group_reduce_kernel, n_f),
        out_shape=jax.ShapeDtypeStruct(p.shape[1:], p.dtype),
        in_specs=[pl.BlockSpec(memory_space=pltpu.VMEM)],
        out_specs=pl.BlockSpec(memory_space=pltpu.VMEM),
        scratch_shapes=[
            pltpu.VMEM((n_f - 1,) + p.shape[1:], p.dtype),
            pltpu.SemaphoreType.DMA((n_f - 1,)),
            pltpu.SemaphoreType.DMA((n_f - 1,)),
        ],
        compiler_params=pltpu.CompilerParams(collective_id=3, has_side_effects=True),
    )(p)


def pair_barrier(c, partner, across):
    barrier = pltpu.get_barrier_semaphore()
    pl.semaphore_signal(barrier, inc=1, device_id=(c, partner), device_id_type=MESH)
    pl.semaphore_signal(barrier, inc=1, device_id=(c, across), device_id_type=MESH)
    pl.semaphore_wait(barrier, 2)


def quad_ids():
    c = lax.axis_index("ctx")
    f = lax.axis_index("fsdp")
    partner = f + 1 - 2 * (f % 2)
    across = (f + 2) % 4
    diagonal = (partner + 2) % 4
    return c, f, partner, across, diagonal


def quad_gather_kernel(x_ref, out_ref, send_sem, recv_sem):
    c, f, partner, across, diagonal = quad_ids()
    pair_barrier(c, partner, across)

    def copy(src, slot, dest, k):
        return pltpu.make_async_remote_copy(
            src_ref=src,
            dst_ref=out_ref.at[slot],
            send_sem=send_sem.at[k],
            recv_sem=recv_sem.at[slot],
            device_id=(c, dest),
            device_id_type=MESH,
        )

    first = copy(x_ref, f, across, 0)
    first.start()
    own = copy(x_ref, f, partner, 1)
    own.start()
    out_ref[f] = x_ref[...]
    copy(x_ref, across, f, 0).wait_recv()
    relay = copy(out_ref.at[across], across, partner, 2)
    relay.start()
    copy(x_ref, partner, f, 0).wait_recv()
    copy(x_ref, diagonal, f, 0).wait_recv()
    first.wait_send()
    own.wait_send()
    relay.wait_send()


def quad_gather(x):
    return pl.pallas_call(
        quad_gather_kernel,
        out_shape=jax.ShapeDtypeStruct((4,) + x.shape, x.dtype),
        in_specs=[pl.BlockSpec(memory_space=pltpu.VMEM)],
        out_specs=pl.BlockSpec(memory_space=pltpu.VMEM),
        scratch_shapes=[pltpu.SemaphoreType.DMA((3,)), pltpu.SemaphoreType.DMA((4,))],
        compiler_params=pltpu.CompilerParams(collective_id=4, has_side_effects=True),
    )(x)


def quad_reduce_kernel(p_ref, out_ref, near_buf, far_buf, sum_buf, send_sem, recv_sem):
    c, f, partner, across, diagonal = quad_ids()
    pair_barrier(c, partner, across)

    def copy(src, dst, dest, k):
        return pltpu.make_async_remote_copy(
            src_ref=src,
            dst_ref=dst,
            send_sem=send_sem.at[k],
            recv_sem=recv_sem.at[k],
            device_id=(c, dest),
            device_id_type=MESH,
        )

    to_partner = copy(p_ref.at[partner], near_buf.at[0], partner, 0)
    to_partner.start()
    to_diagonal = copy(p_ref.at[diagonal], near_buf.at[1], partner, 1)
    to_diagonal.start()
    to_partner.wait_recv()
    to_diagonal.wait_recv()
    sum_buf[...] = p_ref[across] + near_buf[1]
    to_across = copy(sum_buf, far_buf, across, 2)
    to_across.start()
    out_ref[...] = p_ref[f] + near_buf[0]
    to_across.wait_recv()
    out_ref[...] += far_buf[...]
    to_partner.wait_send()
    to_diagonal.wait_send()
    to_across.wait_send()


def quad_reduce(p):
    block = p.shape[1:]
    return pl.pallas_call(
        quad_reduce_kernel,
        out_shape=jax.ShapeDtypeStruct(block, p.dtype),
        in_specs=[pl.BlockSpec(memory_space=pltpu.VMEM)],
        out_specs=pl.BlockSpec(memory_space=pltpu.VMEM),
        scratch_shapes=[
            pltpu.VMEM((2,) + block, p.dtype),
            pltpu.VMEM(block, p.dtype),
            pltpu.VMEM(block, p.dtype),
            pltpu.SemaphoreType.DMA((3,)),
            pltpu.SemaphoreType.DMA((3,)),
        ],
        compiler_params=pltpu.CompilerParams(collective_id=5, has_side_effects=True),
    )(p)


def fsdp_gather(x, n_f):
    if n_f == 4:
        return quad_gather(x)
    return group_gather(x, n_f)


def fsdp_reduce(p, n_f):
    if n_f == 4:
        return quad_reduce(p)
    return group_reduce(p, n_f)


def body(
    tokens,
    doc_lengths,
    attention_gain,
    query_weight,
    key_weight,
    value_weight,
    output_weight,
    feedforward_gain,
    gate_weight,
    up_weight,
    down_weight,
    cotangent,
):
    n_dev = lax.axis_size(ALL)
    rows = query_weight.shape[0]
    ff_rows = down_weight.shape[0]
    ff = gate_weight.shape[1]
    local_tokens = tokens[0].astype(jnp.float32)
    tok_rows = local_tokens.shape[0]
    stream_len = tok_rows * lax.axis_size("ctx")
    my_first = lax.axis_index("ctx") * tok_rows

    gain_cols = jnp.pad(
        jnp.stack([attention_gain, feedforward_gain], axis=1), ((0, 0), (0, GAIN_PAD - 2))
    )
    att_full = lax.all_gather(
        jnp.concatenate([query_weight, key_weight, value_weight, output_weight, gain_cols], axis=1),
        ALL,
        axis=0,
        tiled=True,
    )
    c_k = D
    c_v = D + KVW
    c_o = D + 2 * KVW
    c_g = 2 * D + 2 * KVW
    query_full = att_full[:, :c_k]
    key_full = att_full[:, c_k:c_v]
    value_full = att_full[:, c_v:c_o]
    qkv_full = att_full[:, :c_o]
    output_full = att_full[:, c_o:c_g]
    gain_one_f = att_full[:, c_g].astype(jnp.float32)
    gain_two_f = att_full[:, c_g + 1].astype(jnp.float32)

    key_docs_all, places_all = document_layout(doc_lengths[0], stream_len)
    query_docs = lax.dynamic_slice_in_dim(key_docs_all, my_first, tok_rows, 0)
    query_positions = lax.dynamic_slice_in_dim(places_all, my_first, tok_rows, 0)
    query_places = my_first + jnp.arange(tok_rows, dtype=jnp.int32)
    group_size = H // KVH
    score_scale = HD ** (-0.5)

    scale_one = rms_scale(local_tokens)
    normed_one = local_tokens * scale_one
    normed_low = (normed_one * gain_one_f).astype(jnp.bfloat16)
    qkv = jnp.dot(normed_low, qkv_full, preferred_element_type=jnp.float32)
    queries = qkv[:, :D]
    keys_new = qkv[:, D : D + KVW]
    values_new = qkv[:, D + KVW :]
    query_low = rotate(queries, query_positions, H, 1.0).astype(jnp.bfloat16)
    key_low = rotate(keys_new, query_positions, KVH, 1.0).astype(jnp.bfloat16)
    value_low = values_new.astype(jnp.bfloat16)

    n_ctx = lax.axis_size("ctx")
    n_f = lax.axis_size("fsdp")
    chunk = ff_rows
    units = n_ctx * chunk
    gu_parts = jnp.transpose(
        jnp.stack([gate_weight, up_weight], axis=1).reshape(rows, 2, n_ctx, n_f, chunk),
        (3, 0, 1, 2, 4),
    )
    gu_parts = lax.all_to_all(gu_parts, "fsdp", 0, 0, tiled=True).reshape(n_f * rows, 2 * units)
    down_rows = D // (2 * n_ctx)
    ff_pack = jnp.concatenate([gu_parts, down_weight.reshape(down_rows, 2 * units)], axis=0)
    ff_pack = ff_pack.at[0, 0].add(att_full[0, 0] * 0)
    ff_stack = lax.all_gather(
        ff_pack,
        "ctx",
        axis=0,
        tiled=False,
    )
    gate_up_tp = ff_stack[:, : n_f * rows].reshape(n_ctx * n_f * rows, 2 * units)
    down_tp = ff_stack[:, n_f * rows :].reshape(n_ctx, ff_rows, D).reshape(units, D)
    max_doc = min(DOC_MOST, KBLK * (stream_len // (2 * KBLK)))
    back = min(-(-(max_doc - 1) // tok_rows), n_ctx - 1)
    win = (back + 1) * tok_rows
    kv_win = kv_share(
        jnp.concatenate([key_low, value_low], axis=1), n_ctx, back
    ).reshape(win, 2 * KVW)
    docs_pad = jnp.concatenate(
        [jnp.full((back * tok_rows,), -1, jnp.int32), key_docs_all.astype(jnp.int32)]
    )
    key_docs = lax.dynamic_slice_in_dim(docs_pad, my_first, win, 0)
    key_places = my_first - back * tok_rows + jnp.arange(win, dtype=jnp.int32)
    key_block = kv_win[:, :KVW].reshape(win, KVH, HD)
    value_block = kv_win[:, KVW:].reshape(win, KVH, HD)
    query_grouped = query_low.reshape(tok_rows, KVH, group_size, HD)
    allowed = (
        (key_docs[None, :] == query_docs[:, None]) & (key_places[None, :] <= query_places[:, None])
    )[:, None, None, :]
    scores = (
        jnp.einsum("qgrd,kgd->qgrk", query_grouped, key_block, preferred_element_type=jnp.float32)
        * score_scale
    )
    scores = jnp.where(allowed, scores, MASKED_SCORE)
    row_max = jnp.max(scores, axis=-1, keepdims=True)
    exponent = jnp.where(allowed, jnp.exp(scores - row_max), 0.0)
    probs = exponent / jnp.sum(exponent, axis=-1, keepdims=True)
    probs_low = probs.astype(jnp.bfloat16)
    attended_sum = jnp.einsum(
        "qgrk,kgd->qgrd", probs_low, value_block, preferred_element_type=jnp.float32
    )
    attended_low = attended_sum.reshape(tok_rows, D).astype(jnp.bfloat16)
    middle = local_tokens + jnp.dot(attended_low, output_full, preferred_element_type=jnp.float32)

    scale_two = rms_scale(middle)
    normed_two = middle * scale_two
    normed_two_low = (normed_two * gain_two_f).astype(jnp.bfloat16)
    group_tokens = n_f * tok_rows
    xn2_all = fsdp_gather(normed_two_low, n_f).reshape(group_tokens, D)
    gate_up = jnp.dot(xn2_all, gate_up_tp, preferred_element_type=jnp.float32)
    gate_pre = gate_up[:, :units]
    up_pre = gate_up[:, units:]
    sigmoid = jax.nn.sigmoid(gate_pre)
    hidden_low = (gate_pre * sigmoid * up_pre).astype(jnp.bfloat16)
    ff_part = jnp.dot(hidden_low, down_tp, preferred_element_type=jnp.float32)
    layer_out = middle + fsdp_reduce(ff_part.reshape(n_f, tok_rows, D), n_f)

    grad_out = cotangent[0]
    grad_all = fsdp_gather(grad_out, n_f).reshape(group_tokens, D)
    down_sum = lax.psum_scatter(
        outer_rows(hidden_low, grad_all).astype(jnp.bfloat16), "ctx", scatter_dimension=0, tiled=True
    )
    hidden_grad = times_transposed(grad_all, down_tp)
    gate_grad = (hidden_grad * up_pre * sigmoid * (1.0 + gate_pre * (1.0 - sigmoid))).astype(
        jnp.bfloat16
    )
    up_grad = (hidden_grad * gate_pre * sigmoid).astype(jnp.bfloat16)
    gate_up_cat = jnp.concatenate([gate_grad, up_grad], axis=1)
    gate_up_term = outer_rows(xn2_all, gate_up_cat)
    ff_pack, gate_up_cat = lax.optimization_barrier((gate_up_term.astype(jnp.bfloat16), gate_up_cat))
    gu_sum = lax.psum_scatter(ff_pack, "ctx", scatter_dimension=0, tiled=True)
    gu_sum = lax.all_to_all(gu_sum.reshape(n_f, rows, 2 * units), "fsdp", 0, 0, tiled=True)
    ff_sum = jnp.transpose(
        gu_sum.reshape(n_f, rows, 2, n_ctx, chunk), (1, 2, 3, 0, 4)
    ).reshape(rows, 2 * ff)
    normed_two_grad = fsdp_reduce(
        times_transposed(gate_up_cat, gate_up_tp).reshape(n_f, tok_rows, D), n_f
    )
    gain_two_term = jnp.sum(normed_two_grad * normed_two, axis=0)
    scaled_two = normed_two_grad * gain_two_f
    middle_grad = grad_out.astype(jnp.float32) + scale_two * (
        scaled_two - normed_two * jnp.mean(scaled_two * normed_two, axis=-1, keepdims=True)
    )
    branch_grad = middle_grad.astype(jnp.bfloat16)
    attended_grad_low = (
        times_transposed(branch_grad, output_full)
        .astype(jnp.bfloat16)
        .reshape(tok_rows, KVH, group_size, HD)
    )
    row_delta = jnp.sum(
        attended_grad_low.astype(jnp.float32) * attended_sum, axis=-1, keepdims=True
    )
    prob_grad = jnp.einsum(
        "qgrd,kgd->qgrk", attended_grad_low, value_block, preferred_element_type=jnp.float32
    )
    score_grad = (probs * (prob_grad - row_delta)).astype(jnp.bfloat16)
    query_accum = jnp.einsum(
        "qgrk,kgd->qgrd", score_grad, key_block, preferred_element_type=jnp.float32
    )
    key_term = jnp.einsum(
        "qgrk,qgrd->kgd", score_grad, query_grouped, preferred_element_type=jnp.float32
    ).reshape(win, KVW)
    value_term = jnp.einsum(
        "qgrk,qgrd->kgd", probs_low, attended_grad_low, preferred_element_type=jnp.float32
    ).reshape(win, KVW)
    kv_term = jnp.concatenate([key_term, value_term], axis=1).reshape(back + 1, tok_rows, 2 * KVW)
    kv_sum = kv_return(kv_term[back], kv_term[:back].astype(jnp.bfloat16), n_ctx, back)
    key_grad_low = rotate(kv_sum[:, :KVW] * score_scale, query_positions, KVH, -1.0).astype(
        jnp.bfloat16
    )
    value_grad_low = kv_sum[:, KVW:].astype(jnp.bfloat16)
    query_grad_low = rotate(
        query_accum.reshape(tok_rows, D) * score_scale, query_positions, H, -1.0
    ).astype(jnp.bfloat16)
    projection_cat = jnp.concatenate([query_grad_low, key_grad_low, value_grad_low], axis=1)
    normed_grad = times_transposed(projection_cat, qkv_full)
    gain_one_term = jnp.sum(normed_grad * normed_one, axis=0)
    scaled_one = normed_grad * gain_one_f
    tokens_grad = middle_grad + scale_one * (
        scaled_one - normed_one * jnp.mean(scaled_one * normed_one, axis=-1, keepdims=True)
    )
    gain_term_cols = jnp.pad(
        jnp.stack([gain_one_term, gain_two_term], axis=1), ((0, 0), (0, GAIN_PAD - 2))
    )
    gain_term_cols = gain_term_cols.at[0, GAIN_PAD - 1].set(ff_sum[0, 0].astype(jnp.float32) * 0.0)
    attention_sum = lax.psum_scatter(
        jnp.concatenate(
            [
                outer_rows(normed_low, projection_cat).astype(jnp.bfloat16),
                outer_rows(attended_low, branch_grad).astype(jnp.bfloat16),
                gain_term_cols.astype(jnp.bfloat16),
            ],
            axis=1,
        ),
        ALL,
        scatter_dimension=0,
        tiled=True,
    ).astype(jnp.float32)
    ff_sum = ff_sum.astype(jnp.float32)
    return (
        layer_out.astype(jnp.bfloat16)[None],
        tokens_grad[None],
        attention_sum[:, c_g],
        attention_sum[:, :c_k],
        attention_sum[:, c_k:c_v],
        attention_sum[:, c_v:c_o],
        attention_sum[:, c_o:c_g],
        attention_sum[:, c_g + 1],
        ff_sum[:, :ff],
        ff_sum[:, ff : 2 * ff],
        down_sum.astype(jnp.float32),
    )


def solution(mesh):
    weight = P(ALL, None)
    stream = P("fsdp", "ctx", None)
    return jax.shard_map(
        body,
        mesh=mesh,
        in_specs=(
            stream,
            P("fsdp", None),
            P(ALL),
            weight,
            weight,
            weight,
            weight,
            P(ALL),
            weight,
            weight,
            weight,
            stream,
        ),
        out_specs=(
            stream,
            stream,
            P(ALL),
            weight,
            weight,
            weight,
            weight,
            P(ALL),
            weight,
            weight,
            weight,
        ),
        check_vma=False,
    )
```

```python
import functools

import jax
import jax.numpy as jnp
from jax import lax
from jax.experimental import pallas as pl
from jax.experimental.pallas import tpu as pltpu
from jax.sharding import PartitionSpec as P

MESH = pl.DeviceIdType.MESH

D = 1536
H = 16
KVH = 8
HD = 96
KBLK = 512
DOC_MOST = 4096
KVW = 768
GAIN_PAD = 128

EPSILON = 1e-05
ROPE_BASE = 100000.0
MASKED_SCORE = -1e30
ALL = ("ctx", "fsdp")


def rms_scale(values):
    return lax.rsqrt(jnp.mean(values * values, axis=-1, keepdims=True) + EPSILON)


def document_layout(lengths, total):
    starts = jnp.cumsum(lengths) - lengths
    places = jnp.arange(total, dtype=jnp.int32)
    inside = places[:, None] >= starts[None, :]
    doc_ids = jnp.sum(inside.astype(jnp.int32), axis=1) - 1
    doc_starts = jnp.max(jnp.where(inside, starts[None, :], 0), axis=1)
    return (doc_ids, places - doc_starts)


def rotate(values, positions, head_count, direction):
    row_count = values.shape[0]
    half_dim = HD // 2
    inverse_freq = ROPE_BASE ** (-(jnp.arange(half_dim).astype(jnp.float32) * (2.0 / HD)))
    angles = positions.astype(jnp.float32)[:, None] * inverse_freq[None, :]
    cosine = jnp.cos(angles)[:, None, :]
    sine_part = direction * jnp.sin(angles)[:, None, :]
    grouped = values.reshape(row_count, head_count, HD)
    former = grouped[:, :, :half_dim]
    latter = grouped[:, :, half_dim:]
    turned = jnp.concatenate(
        [former * cosine - latter * sine_part, latter * cosine + former * sine_part], axis=2
    )
    return turned.reshape(row_count, head_count * HD)


def outer_rows(left, right):
    return lax.dot_general(
        left, right, (((0,), (0,)), ((), ())), preferred_element_type=jnp.float32
    )


def times_transposed(left, right):
    return lax.dot_general(
        left, right, (((1,), (1,)), ((), ())), preferred_element_type=jnp.float32
    )


def neighbour_barrier(n_ctx, back, c, f):
    barrier = pltpu.get_barrier_semaphore()
    for s in range(1, back + 1):
        for peer in ((c + s) % n_ctx, (c + n_ctx - s) % n_ctx):
            pl.semaphore_signal(barrier, inc=1, device_id=(peer, f), device_id_type=MESH)
    pl.semaphore_wait(barrier, 2 * back)


def kv_share_kernel(n_ctx, back, kv_ref, out_ref, send_sem, recv_sem):
    c = lax.axis_index("ctx")
    f = lax.axis_index("fsdp")
    neighbour_barrier(n_ctx, back, c, f)

    def copy(s, dest):
        return pltpu.make_async_remote_copy(
            src_ref=kv_ref,
            dst_ref=out_ref.at[back - s],
            send_sem=send_sem.at[s - 1],
            recv_sem=recv_sem.at[back - s],
            device_id=(dest, f),
            device_id_type=MESH,
        )

    for s in range(1, back + 1):

        @pl.when(c + s < n_ctx)
        def _():
            copy(s, c + s).start()

    out_ref[back] = kv_ref[...]
    for s in range(1, back + 1):

        @pl.when(c - s < 0)
        def _():
            out_ref[back - s] = jnp.zeros(kv_ref.shape, kv_ref.dtype)

    for s in range(1, back + 1):

        @pl.when(c + s < n_ctx)
        def _():
            copy(s, c + s).wait_send()

        @pl.when(c - s >= 0)
        def _():
            copy(s, c).wait_recv()


def kv_share(kv, n_ctx, back):
    return pl.pallas_call(
        functools.partial(kv_share_kernel, n_ctx, back),
        out_shape=jax.ShapeDtypeStruct((back + 1,) + kv.shape, kv.dtype),
        in_specs=[pl.BlockSpec(memory_space=pltpu.VMEM)],
        out_specs=pl.BlockSpec(memory_space=pltpu.VMEM),
        scratch_shapes=[pltpu.SemaphoreType.DMA((back,)), pltpu.SemaphoreType.DMA((back + 1,))],
        compiler_params=pltpu.CompilerParams(collective_id=0, has_side_effects=True),
    )(kv)


def kv_return_kernel(n_ctx, back, own_ref, g_ref, out_ref, recv_buf, send_sem, recv_sem):
    c = lax.axis_index("ctx")
    f = lax.axis_index("fsdp")
    neighbour_barrier(n_ctx, back, c, f)

    def copy(s, dest):
        return pltpu.make_async_remote_copy(
            src_ref=g_ref.at[back - s],
            dst_ref=recv_buf.at[s - 1],
            send_sem=send_sem.at[s - 1],
            recv_sem=recv_sem.at[s - 1],
            device_id=(dest, f),
            device_id_type=MESH,
        )

    for s in range(1, back + 1):

        @pl.when(c - s >= 0)
        def _():
            copy(s, c - s).start()

    out_ref[...] = own_ref[...]
    for s in range(1, back + 1):

        @pl.when(c + s < n_ctx)
        def _():
            copy(s, c).wait_recv()
            out_ref[...] += recv_buf[s - 1].astype(jnp.float32)

    for s in range(1, back + 1):

        @pl.when(c - s >= 0)
        def _():
            copy(s, c - s).wait_send()


def kv_return(own, g, n_ctx, back):
    return pl.pallas_call(
        functools.partial(kv_return_kernel, n_ctx, back),
        out_shape=jax.ShapeDtypeStruct(own.shape, own.dtype),
        in_specs=[pl.BlockSpec(memory_space=pltpu.VMEM)] * 2,
        out_specs=pl.BlockSpec(memory_space=pltpu.VMEM),
        scratch_shapes=[
            pltpu.VMEM(g.shape, g.dtype),
            pltpu.SemaphoreType.DMA((back,)),
            pltpu.SemaphoreType.DMA((back,)),
        ],
        compiler_params=pltpu.CompilerParams(collective_id=1, has_side_effects=True),
    )(own, g)


def peer_barrier(n_f, c, f):
    barrier = pltpu.get_barrier_semaphore()
    for k in range(1, n_f):
        pl.semaphore_signal(barrier, inc=1, device_id=(c, (f + k) % n_f), device_id_type=MESH)
    pl.semaphore_wait(barrier, n_f - 1)


def group_gather_kernel(n_f, x_ref, out_ref, send_sem, recv_sem):
    c = lax.axis_index("ctx")
    f = lax.axis_index("fsdp")
    peer_barrier(n_f, c, f)
    copies = []
    for k in range(1, n_f):
        copy = pltpu.make_async_remote_copy(
            src_ref=x_ref,
            dst_ref=out_ref.at[f],
            send_sem=send_sem.at[k - 1],
            recv_sem=recv_sem.at[k - 1],
            device_id=(c, (f + k) % n_f),
            device_id_type=MESH,
        )
        copy.start()
        copies.append(copy)
    out_ref[f] = x_ref[...]
    for k in range(1, n_f):
        pltpu.make_async_remote_copy(
            src_ref=x_ref,
            dst_ref=out_ref.at[(f + n_f - k) % n_f],
            send_sem=send_sem.at[k - 1],
            recv_sem=recv_sem.at[k - 1],
            device_id=(c, f),
            device_id_type=MESH,
        ).wait_recv()
    for copy in copies:
        copy.wait_send()


def group_gather(x, n_f):
    return pl.pallas_call(
        functools.partial(group_gather_kernel, n_f),
        out_shape=jax.ShapeDtypeStruct((n_f,) + x.shape, x.dtype),
        in_specs=[pl.BlockSpec(memory_space=pltpu.VMEM)],
        out_specs=pl.BlockSpec(memory_space=pltpu.VMEM),
        scratch_shapes=[pltpu.SemaphoreType.DMA((n_f - 1,)), pltpu.SemaphoreType.DMA((n_f - 1,))],
        compiler_params=pltpu.CompilerParams(collective_id=2, has_side_effects=True),
    )(x)


def group_reduce_kernel(n_f, p_ref, out_ref, recv_buf, send_sem, recv_sem):
    c = lax.axis_index("ctx")
    f = lax.axis_index("fsdp")
    peer_barrier(n_f, c, f)
    copies = []
    for k in range(1, n_f):
        dest = (f + k) % n_f
        copy = pltpu.make_async_remote_copy(
            src_ref=p_ref.at[dest],
            dst_ref=recv_buf.at[k - 1],
            send_sem=send_sem.at[k - 1],
            recv_sem=recv_sem.at[k - 1],
            device_id=(c, dest),
            device_id_type=MESH,
        )
        copy.start()
        copies.append(copy)
    out_ref[...] = p_ref[f]
    for k in range(1, n_f):
        copies[k - 1].wait_recv()
        out_ref[...] += recv_buf[k - 1]
    for copy in copies:
        copy.wait_send()


def group_reduce(p, n_f):
    return pl.pallas_call(
        functools.partial(group_reduce_kernel, n_f),
        out_shape=jax.ShapeDtypeStruct(p.shape[1:], p.dtype),
        in_specs=[pl.BlockSpec(memory_space=pltpu.VMEM)],
        out_specs=pl.BlockSpec(memory_space=pltpu.VMEM),
        scratch_shapes=[
            pltpu.VMEM((n_f - 1,) + p.shape[1:], p.dtype),
            pltpu.SemaphoreType.DMA((n_f - 1,)),
            pltpu.SemaphoreType.DMA((n_f - 1,)),
        ],
        compiler_params=pltpu.CompilerParams(collective_id=3, has_side_effects=True),
    )(p)


def pair_barrier(c, partner, across):
    barrier = pltpu.get_barrier_semaphore()
    pl.semaphore_signal(barrier, inc=1, device_id=(c, partner), device_id_type=MESH)
    pl.semaphore_signal(barrier, inc=1, device_id=(c, across), device_id_type=MESH)
    pl.semaphore_wait(barrier, 2)


def quad_ids():
    c = lax.axis_index("ctx")
    f = lax.axis_index("fsdp")
    partner = f + 1 - 2 * (f % 2)
    across = (f + 2) % 4
    diagonal = (partner + 2) % 4
    return c, f, partner, across, diagonal


def quad_gather_kernel(x_ref, out_ref, send_sem, recv_sem):
    c, f, partner, across, diagonal = quad_ids()
    pair_barrier(c, partner, across)

    def copy(src, slot, dest, k):
        return pltpu.make_async_remote_copy(
            src_ref=src,
            dst_ref=out_ref.at[slot],
            send_sem=send_sem.at[k],
            recv_sem=recv_sem.at[slot],
            device_id=(c, dest),
            device_id_type=MESH,
        )

    first = copy(x_ref, f, across, 0)
    first.start()
    own = copy(x_ref, f, partner, 1)
    own.start()
    out_ref[f] = x_ref[...]
    copy(x_ref, across, f, 0).wait_recv()
    relay = copy(out_ref.at[across], across, partner, 2)
    relay.start()
    copy(x_ref, partner, f, 0).wait_recv()
    copy(x_ref, diagonal, f, 0).wait_recv()
    first.wait_send()
    own.wait_send()
    relay.wait_send()


def quad_gather(x):
    return pl.pallas_call(
        quad_gather_kernel,
        out_shape=jax.ShapeDtypeStruct((4,) + x.shape, x.dtype),
        in_specs=[pl.BlockSpec(memory_space=pltpu.VMEM)],
        out_specs=pl.BlockSpec(memory_space=pltpu.VMEM),
        scratch_shapes=[pltpu.SemaphoreType.DMA((3,)), pltpu.SemaphoreType.DMA((4,))],
        compiler_params=pltpu.CompilerParams(collective_id=4, has_side_effects=True),
    )(x)


def quad_reduce_kernel(p_ref, out_ref, near_buf, far_buf, sum_buf, send_sem, recv_sem):
    c, f, partner, across, diagonal = quad_ids()
    pair_barrier(c, partner, across)

    def copy(src, dst, dest, k):
        return pltpu.make_async_remote_copy(
            src_ref=src,
            dst_ref=dst,
            send_sem=send_sem.at[k],
            recv_sem=recv_sem.at[k],
            device_id=(c, dest),
            device_id_type=MESH,
        )

    to_partner = copy(p_ref.at[partner], near_buf.at[0], partner, 0)
    to_partner.start()
    to_diagonal = copy(p_ref.at[diagonal], near_buf.at[1], partner, 1)
    to_diagonal.start()
    to_partner.wait_recv()
    to_diagonal.wait_recv()
    sum_buf[...] = p_ref[across] + near_buf[1]
    to_across = copy(sum_buf, far_buf, across, 2)
    to_across.start()
    out_ref[...] = p_ref[f] + near_buf[0]
    to_across.wait_recv()
    out_ref[...] += far_buf[...]
    to_partner.wait_send()
    to_diagonal.wait_send()
    to_across.wait_send()


def quad_reduce(p):
    block = p.shape[1:]
    return pl.pallas_call(
        quad_reduce_kernel,
        out_shape=jax.ShapeDtypeStruct(block, p.dtype),
        in_specs=[pl.BlockSpec(memory_space=pltpu.VMEM)],
        out_specs=pl.BlockSpec(memory_space=pltpu.VMEM),
        scratch_shapes=[
            pltpu.VMEM((2,) + block, p.dtype),
            pltpu.VMEM(block, p.dtype),
            pltpu.VMEM(block, p.dtype),
            pltpu.SemaphoreType.DMA((3,)),
            pltpu.SemaphoreType.DMA((3,)),
        ],
        compiler_params=pltpu.CompilerParams(collective_id=5, has_side_effects=True),
    )(p)


def fsdp_gather(x, n_f):
    if n_f == 4:
        return quad_gather(x)
    return group_gather(x, n_f)


def fsdp_reduce(p, n_f):
    if n_f == 4:
        return quad_reduce(p)
    return group_reduce(p, n_f)


def body(
    tokens,
    doc_lengths,
    attention_gain,
    query_weight,
    key_weight,
    value_weight,
    output_weight,
    feedforward_gain,
    gate_weight,
    up_weight,
    down_weight,
    cotangent,
):
    n_dev = lax.axis_size(ALL)
    rows = query_weight.shape[0]
    ff_rows = down_weight.shape[0]
    ff = gate_weight.shape[1]
    local_tokens = tokens[0].astype(jnp.float32)
    tok_rows = local_tokens.shape[0]
    stream_len = tok_rows * lax.axis_size("ctx")
    my_first = lax.axis_index("ctx") * tok_rows

    gain_cols = jnp.pad(
        jnp.stack([attention_gain, feedforward_gain], axis=1), ((0, 0), (0, GAIN_PAD - 2))
    )
    att_full = lax.all_gather(
        jnp.concatenate([query_weight, key_weight, value_weight, output_weight, gain_cols], axis=1),
        ALL,
        axis=0,
        tiled=True,
    )
    c_k = D
    c_v = D + KVW
    c_o = D + 2 * KVW
    c_g = 2 * D + 2 * KVW
    query_full = att_full[:, :c_k]
    key_full = att_full[:, c_k:c_v]
    value_full = att_full[:, c_v:c_o]
    qkv_full = att_full[:, :c_o]
    output_full = att_full[:, c_o:c_g]
    gain_one_f = att_full[:, c_g].astype(jnp.float32)
    gain_two_f = att_full[:, c_g + 1].astype(jnp.float32)

    key_docs_all, places_all = document_layout(doc_lengths[0], stream_len)
    query_docs = lax.dynamic_slice_in_dim(key_docs_all, my_first, tok_rows, 0)
    query_positions = lax.dynamic_slice_in_dim(places_all, my_first, tok_rows, 0)
    query_places = my_first + jnp.arange(tok_rows, dtype=jnp.int32)
    group_size = H // KVH
    score_scale = HD ** (-0.5)

    scale_one = rms_scale(local_tokens)
    normed_one = local_tokens * scale_one
    normed_low = (normed_one * gain_one_f).astype(jnp.bfloat16)
    qkv = jnp.dot(normed_low, qkv_full, preferred_element_type=jnp.float32)
    queries = qkv[:, :D]
    keys_new = qkv[:, D : D + KVW]
    values_new = qkv[:, D + KVW :]
    query_low = rotate(queries, query_positions, H, 1.0).astype(jnp.bfloat16)
    key_low = rotate(keys_new, query_positions, KVH, 1.0).astype(jnp.bfloat16)
    value_low = values_new.astype(jnp.bfloat16)

    n_ctx = lax.axis_size("ctx")
    n_f = lax.axis_size("fsdp")
    chunk = ff_rows
    units = n_ctx * chunk
    gu_parts = jnp.transpose(
        jnp.stack([gate_weight, up_weight], axis=1).reshape(rows, 2, n_ctx, n_f, chunk),
        (3, 0, 1, 2, 4),
    )
    gu_parts = lax.all_to_all(gu_parts, "fsdp", 0, 0, tiled=True).reshape(n_f * rows, 2 * units)
    down_rows = D // (2 * n_ctx)
    ff_pack = jnp.concatenate([gu_parts, down_weight.reshape(down_rows, 2 * units)], axis=0)
    ff_pack = ff_pack.at[0, 0].add(att_full[0, 0] * 0)
    ff_stack = lax.all_gather(
        ff_pack,
        "ctx",
        axis=0,
        tiled=False,
    )
    gate_up_tp = ff_stack[:, : n_f * rows].reshape(n_ctx * n_f * rows, 2 * units)
    down_tp = ff_stack[:, n_f * rows :].reshape(n_ctx, ff_rows, D).reshape(units, D)
    max_doc = min(DOC_MOST, KBLK * (stream_len // (2 * KBLK)))
    back = min(-(-(max_doc - 1) // tok_rows), n_ctx - 1)
    win = (back + 1) * tok_rows
    kv_win = kv_share(
        jnp.concatenate([key_low, value_low], axis=1), n_ctx, back
    ).reshape(win, 2 * KVW)
    docs_pad = jnp.concatenate(
        [jnp.full((back * tok_rows,), -1, jnp.int32), key_docs_all.astype(jnp.int32)]
    )
    key_docs = lax.dynamic_slice_in_dim(docs_pad, my_first, win, 0)
    key_places = my_first - back * tok_rows + jnp.arange(win, dtype=jnp.int32)
    key_block = kv_win[:, :KVW].reshape(win, KVH, HD)
    value_block = kv_win[:, KVW:].reshape(win, KVH, HD)
    query_grouped = query_low.reshape(tok_rows, KVH, group_size, HD)
    allowed = (
        (key_docs[None, :] == query_docs[:, None]) & (key_places[None, :] <= query_places[:, None])
    )[:, None, None, :]
    scores = (
        jnp.einsum("qgrd,kgd->qgrk", query_grouped, key_block, preferred_element_type=jnp.float32)
        * score_scale
    )
    scores = jnp.where(allowed, scores, MASKED_SCORE)
    row_max = jnp.max(scores, axis=-1, keepdims=True)
    exponent = jnp.where(allowed, jnp.exp(scores - row_max), 0.0)
    probs = exponent / jnp.sum(exponent, axis=-1, keepdims=True)
    probs_low = probs.astype(jnp.bfloat16)
    attended_sum = jnp.einsum(
        "qgrk,kgd->qgrd", probs_low, value_block, preferred_element_type=jnp.float32
    )
    attended_low = attended_sum.reshape(tok_rows, D).astype(jnp.bfloat16)
    middle = local_tokens + jnp.dot(attended_low, output_full, preferred_element_type=jnp.float32)

    scale_two = rms_scale(middle)
    normed_two = middle * scale_two
    normed_two_low = (normed_two * gain_two_f).astype(jnp.bfloat16)
    group_tokens = n_f * tok_rows
    xn2_all = fsdp_gather(normed_two_low, n_f).reshape(group_tokens, D)
    gate_up = jnp.dot(xn2_all, gate_up_tp, preferred_element_type=jnp.float32)
    gate_pre = gate_up[:, :units]
    up_pre = gate_up[:, units:]
    sigmoid = jax.nn.sigmoid(gate_pre)
    hidden_low = (gate_pre * sigmoid * up_pre).astype(jnp.bfloat16)
    ff_part = jnp.dot(hidden_low, down_tp, preferred_element_type=jnp.float32)
    layer_out = middle + fsdp_reduce(ff_part.reshape(n_f, tok_rows, D), n_f)

    grad_out = cotangent[0]
    grad_all = fsdp_gather(grad_out, n_f).reshape(group_tokens, D)
    down_term = outer_rows(hidden_low, grad_all).astype(jnp.bfloat16)
    hidden_grad = times_transposed(grad_all, down_tp)
    gate_grad = (hidden_grad * up_pre * sigmoid * (1.0 + gate_pre * (1.0 - sigmoid))).astype(
        jnp.bfloat16
    )
    up_grad = (hidden_grad * gate_pre * sigmoid).astype(jnp.bfloat16)
    gate_up_cat = jnp.concatenate([gate_grad, up_grad], axis=1)
    gate_up_term = outer_rows(xn2_all, gate_up_cat)
    grad_pack = jnp.concatenate(
        [
            gate_up_term.astype(jnp.bfloat16).reshape(n_ctx, n_f * rows, 2 * units),
            down_term.reshape(n_ctx, down_rows, 2 * units),
        ],
        axis=1,
    ).reshape(n_ctx * (n_f * rows + down_rows), 2 * units)
    grad_pack, gate_up_cat = lax.optimization_barrier((grad_pack, gate_up_cat))
    grad_sum = lax.psum_scatter(grad_pack, "ctx", scatter_dimension=0, tiled=True)
    down_sum = grad_sum[n_f * rows :].reshape(ff_rows, D)
    gu_sum = lax.all_to_all(grad_sum[: n_f * rows].reshape(n_f, rows, 2 * units), "fsdp", 0, 0, tiled=True)
    ff_sum = jnp.transpose(
        gu_sum.reshape(n_f, rows, 2, n_ctx, chunk), (1, 2, 3, 0, 4)
    ).reshape(rows, 2 * ff)
    normed_two_grad = fsdp_reduce(
        times_transposed(gate_up_cat, gate_up_tp).reshape(n_f, tok_rows, D), n_f
    )
    gain_two_term = jnp.sum(normed_two_grad * normed_two, axis=0)
    scaled_two = normed_two_grad * gain_two_f
    middle_grad = grad_out.astype(jnp.float32) + scale_two * (
        scaled_two - normed_two * jnp.mean(scaled_two * normed_two, axis=-1, keepdims=True)
    )
    branch_grad = middle_grad.astype(jnp.bfloat16)
    attended_grad_low = (
        times_transposed(branch_grad, output_full)
        .astype(jnp.bfloat16)
        .reshape(tok_rows, KVH, group_size, HD)
    )
    row_delta = jnp.sum(
        attended_grad_low.astype(jnp.float32) * attended_sum, axis=-1, keepdims=True
    )
    prob_grad = jnp.einsum(
        "qgrd,kgd->qgrk", attended_grad_low, value_block, preferred_element_type=jnp.float32
    )
    score_grad = (probs * (prob_grad - row_delta)).astype(jnp.bfloat16)
    query_accum = jnp.einsum(
        "qgrk,kgd->qgrd", score_grad, key_block, preferred_element_type=jnp.float32
    )
    key_term = jnp.einsum(
        "qgrk,qgrd->kgd", score_grad, query_grouped, preferred_element_type=jnp.float32
    ).reshape(win, KVW)
    value_term = jnp.einsum(
        "qgrk,qgrd->kgd", probs_low, attended_grad_low, preferred_element_type=jnp.float32
    ).reshape(win, KVW)
    kv_term = jnp.concatenate([key_term, value_term], axis=1).reshape(back + 1, tok_rows, 2 * KVW)
    kv_sum = kv_return(kv_term[back], kv_term[:back].astype(jnp.bfloat16), n_ctx, back)
    key_grad_low = rotate(kv_sum[:, :KVW] * score_scale, query_positions, KVH, -1.0).astype(
        jnp.bfloat16
    )
    value_grad_low = kv_sum[:, KVW:].astype(jnp.bfloat16)
    query_grad_low = rotate(
        query_accum.reshape(tok_rows, D) * score_scale, query_positions, H, -1.0
    ).astype(jnp.bfloat16)
    projection_cat = jnp.concatenate([query_grad_low, key_grad_low, value_grad_low], axis=1)
    normed_grad = times_transposed(projection_cat, qkv_full)
    gain_one_term = jnp.sum(normed_grad * normed_one, axis=0)
    scaled_one = normed_grad * gain_one_f
    tokens_grad = middle_grad + scale_one * (
        scaled_one - normed_one * jnp.mean(scaled_one * normed_one, axis=-1, keepdims=True)
    )
    gain_term_cols = jnp.pad(
        jnp.stack([gain_one_term, gain_two_term], axis=1), ((0, 0), (0, GAIN_PAD - 2))
    )
    gain_term_cols = gain_term_cols.at[0, GAIN_PAD - 1].set(ff_sum[0, 0].astype(jnp.float32) * 0.0)
    attention_sum = lax.psum_scatter(
        jnp.concatenate(
            [
                outer_rows(normed_low, projection_cat).astype(jnp.bfloat16),
                outer_rows(attended_low, branch_grad).astype(jnp.bfloat16),
                gain_term_cols.astype(jnp.bfloat16),
            ],
            axis=1,
        ),
        ALL,
        scatter_dimension=0,
        tiled=True,
    ).astype(jnp.float32)
    ff_sum = ff_sum.astype(jnp.float32)
    return (
        layer_out.astype(jnp.bfloat16)[None],
        tokens_grad[None],
        attention_sum[:, c_g],
        attention_sum[:, :c_k],
        attention_sum[:, c_k:c_v],
        attention_sum[:, c_v:c_o],
        attention_sum[:, c_o:c_g],
        attention_sum[:, c_g + 1],
        ff_sum[:, :ff],
        ff_sum[:, ff : 2 * ff],
        down_sum.astype(jnp.float32),
    )


def solution(mesh):
    weight = P(ALL, None)
    stream = P("fsdp", "ctx", None)
    return jax.shard_map(
        body,
        mesh=mesh,
        in_specs=(
            stream,
            P("fsdp", None),
            P(ALL),
            weight,
            weight,
            weight,
            weight,
            P(ALL),
            weight,
            weight,
            weight,
            stream,
        ),
        out_specs=(
            stream,
            stream,
            P(ALL),
            weight,
            weight,
            weight,
            weight,
            P(ALL),
            weight,
            weight,
            weight,
        ),
        check_vma=False,
    )
```

```python
import functools

import jax
import jax.numpy as jnp
from jax import lax
from jax.experimental import pallas as pl
from jax.experimental.pallas import tpu as pltpu
from jax.sharding import PartitionSpec as P

MESH = pl.DeviceIdType.MESH

D = 1536
H = 16
KVH = 8
HD = 96
KBLK = 512
DOC_MOST = 4096
KVW = 768
GAIN_PAD = 128

EPSILON = 1e-05
ROPE_BASE = 100000.0
MASKED_SCORE = -1e30
ALL = ("ctx", "fsdp")


def rms_scale(values):
    return lax.rsqrt(jnp.mean(values * values, axis=-1, keepdims=True) + EPSILON)


def document_layout(lengths, total):
    starts = jnp.cumsum(lengths) - lengths
    places = jnp.arange(total, dtype=jnp.int32)
    inside = places[:, None] >= starts[None, :]
    doc_ids = jnp.sum(inside.astype(jnp.int32), axis=1) - 1
    doc_starts = jnp.max(jnp.where(inside, starts[None, :], 0), axis=1)
    return (doc_ids, places - doc_starts)


def rotate(values, positions, head_count, direction):
    row_count = values.shape[0]
    half_dim = HD // 2
    inverse_freq = ROPE_BASE ** (-(jnp.arange(half_dim).astype(jnp.float32) * (2.0 / HD)))
    angles = positions.astype(jnp.float32)[:, None] * inverse_freq[None, :]
    cosine = jnp.cos(angles)[:, None, :]
    sine_part = direction * jnp.sin(angles)[:, None, :]
    grouped = values.reshape(row_count, head_count, HD)
    former = grouped[:, :, :half_dim]
    latter = grouped[:, :, half_dim:]
    turned = jnp.concatenate(
        [former * cosine - latter * sine_part, latter * cosine + former * sine_part], axis=2
    )
    return turned.reshape(row_count, head_count * HD)


def outer_rows(left, right):
    return lax.dot_general(
        left, right, (((0,), (0,)), ((), ())), preferred_element_type=jnp.float32
    )


def times_transposed(left, right):
    return lax.dot_general(
        left, right, (((1,), (1,)), ((), ())), preferred_element_type=jnp.float32
    )


def neighbour_barrier(n_ctx, back, c, f):
    barrier = pltpu.get_barrier_semaphore()
    for s in range(1, back + 1):
        for peer in ((c + s) % n_ctx, (c + n_ctx - s) % n_ctx):
            pl.semaphore_signal(barrier, inc=1, device_id=(peer, f), device_id_type=MESH)
    pl.semaphore_wait(barrier, 2 * back)


def kv_share_kernel(n_ctx, back, kv_ref, out_ref, send_sem, recv_sem):
    c = lax.axis_index("ctx")
    f = lax.axis_index("fsdp")
    neighbour_barrier(n_ctx, back, c, f)

    def copy(s, dest):
        return pltpu.make_async_remote_copy(
            src_ref=kv_ref,
            dst_ref=out_ref.at[back - s],
            send_sem=send_sem.at[s - 1],
            recv_sem=recv_sem.at[back - s],
            device_id=(dest, f),
            device_id_type=MESH,
        )

    for s in range(1, back + 1):

        @pl.when(c + s < n_ctx)
        def _():
            copy(s, c + s).start()

    out_ref[back] = kv_ref[...]
    for s in range(1, back + 1):

        @pl.when(c - s < 0)
        def _():
            out_ref[back - s] = jnp.zeros(kv_ref.shape, kv_ref.dtype)

    for s in range(1, back + 1):

        @pl.when(c + s < n_ctx)
        def _():
            copy(s, c + s).wait_send()

        @pl.when(c - s >= 0)
        def _():
            copy(s, c).wait_recv()


def kv_share(kv, n_ctx, back):
    return pl.pallas_call(
        functools.partial(kv_share_kernel, n_ctx, back),
        out_shape=jax.ShapeDtypeStruct((back + 1,) + kv.shape, kv.dtype),
        in_specs=[pl.BlockSpec(memory_space=pltpu.VMEM)],
        out_specs=pl.BlockSpec(memory_space=pltpu.VMEM),
        scratch_shapes=[pltpu.SemaphoreType.DMA((back,)), pltpu.SemaphoreType.DMA((back + 1,))],
        compiler_params=pltpu.CompilerParams(collective_id=0, has_side_effects=True),
    )(kv)


def kv_return_kernel(n_ctx, back, own_ref, g_ref, out_ref, recv_buf, send_sem, recv_sem):
    c = lax.axis_index("ctx")
    f = lax.axis_index("fsdp")
    neighbour_barrier(n_ctx, back, c, f)

    def copy(s, dest):
        return pltpu.make_async_remote_copy(
            src_ref=g_ref.at[back - s],
            dst_ref=recv_buf.at[s - 1],
            send_sem=send_sem.at[s - 1],
            recv_sem=recv_sem.at[s - 1],
            device_id=(dest, f),
            device_id_type=MESH,
        )

    for s in range(1, back + 1):

        @pl.when(c - s >= 0)
        def _():
            copy(s, c - s).start()

    out_ref[...] = own_ref[...]
    for s in range(1, back + 1):

        @pl.when(c + s < n_ctx)
        def _():
            copy(s, c).wait_recv()
            out_ref[...] += recv_buf[s - 1].astype(jnp.float32)

    for s in range(1, back + 1):

        @pl.when(c - s >= 0)
        def _():
            copy(s, c - s).wait_send()


def kv_return(own, g, n_ctx, back):
    return pl.pallas_call(
        functools.partial(kv_return_kernel, n_ctx, back),
        out_shape=jax.ShapeDtypeStruct(own.shape, own.dtype),
        in_specs=[pl.BlockSpec(memory_space=pltpu.VMEM)] * 2,
        out_specs=pl.BlockSpec(memory_space=pltpu.VMEM),
        scratch_shapes=[
            pltpu.VMEM(g.shape, g.dtype),
            pltpu.SemaphoreType.DMA((back,)),
            pltpu.SemaphoreType.DMA((back,)),
        ],
        compiler_params=pltpu.CompilerParams(collective_id=1, has_side_effects=True),
    )(own, g)


def peer_barrier(n_f, c, f):
    barrier = pltpu.get_barrier_semaphore()
    for k in range(1, n_f):
        pl.semaphore_signal(barrier, inc=1, device_id=(c, (f + k) % n_f), device_id_type=MESH)
    pl.semaphore_wait(barrier, n_f - 1)


def group_gather_kernel(n_f, x_ref, out_ref, send_sem, recv_sem):
    c = lax.axis_index("ctx")
    f = lax.axis_index("fsdp")
    peer_barrier(n_f, c, f)
    copies = []
    for k in range(1, n_f):
        copy = pltpu.make_async_remote_copy(
            src_ref=x_ref,
            dst_ref=out_ref.at[f],
            send_sem=send_sem.at[k - 1],
            recv_sem=recv_sem.at[k - 1],
            device_id=(c, (f + k) % n_f),
            device_id_type=MESH,
        )
        copy.start()
        copies.append(copy)
    out_ref[f] = x_ref[...]
    for k in range(1, n_f):
        pltpu.make_async_remote_copy(
            src_ref=x_ref,
            dst_ref=out_ref.at[(f + n_f - k) % n_f],
            send_sem=send_sem.at[k - 1],
            recv_sem=recv_sem.at[k - 1],
            device_id=(c, f),
            device_id_type=MESH,
        ).wait_recv()
    for copy in copies:
        copy.wait_send()


def group_gather(x, n_f):
    return pl.pallas_call(
        functools.partial(group_gather_kernel, n_f),
        out_shape=jax.ShapeDtypeStruct((n_f,) + x.shape, x.dtype),
        in_specs=[pl.BlockSpec(memory_space=pltpu.VMEM)],
        out_specs=pl.BlockSpec(memory_space=pltpu.VMEM),
        scratch_shapes=[pltpu.SemaphoreType.DMA((n_f - 1,)), pltpu.SemaphoreType.DMA((n_f - 1,))],
        compiler_params=pltpu.CompilerParams(collective_id=2, has_side_effects=True),
    )(x)


def group_reduce_kernel(n_f, p_ref, out_ref, recv_buf, send_sem, recv_sem):
    c = lax.axis_index("ctx")
    f = lax.axis_index("fsdp")
    peer_barrier(n_f, c, f)
    copies = []
    for k in range(1, n_f):
        dest = (f + k) % n_f
        copy = pltpu.make_async_remote_copy(
            src_ref=p_ref.at[dest],
            dst_ref=recv_buf.at[k - 1],
            send_sem=send_sem.at[k - 1],
            recv_sem=recv_sem.at[k - 1],
            device_id=(c, dest),
            device_id_type=MESH,
        )
        copy.start()
        copies.append(copy)
    out_ref[...] = p_ref[f]
    for k in range(1, n_f):
        copies[k - 1].wait_recv()
        out_ref[...] += recv_buf[k - 1]
    for copy in copies:
        copy.wait_send()


def group_reduce(p, n_f):
    return pl.pallas_call(
        functools.partial(group_reduce_kernel, n_f),
        out_shape=jax.ShapeDtypeStruct(p.shape[1:], p.dtype),
        in_specs=[pl.BlockSpec(memory_space=pltpu.VMEM)],
        out_specs=pl.BlockSpec(memory_space=pltpu.VMEM),
        scratch_shapes=[
            pltpu.VMEM((n_f - 1,) + p.shape[1:], p.dtype),
            pltpu.SemaphoreType.DMA((n_f - 1,)),
            pltpu.SemaphoreType.DMA((n_f - 1,)),
        ],
        compiler_params=pltpu.CompilerParams(collective_id=3, has_side_effects=True),
    )(p)


def pair_barrier(c, partner, across):
    barrier = pltpu.get_barrier_semaphore()
    pl.semaphore_signal(barrier, inc=1, device_id=(c, partner), device_id_type=MESH)
    pl.semaphore_signal(barrier, inc=1, device_id=(c, across), device_id_type=MESH)
    pl.semaphore_wait(barrier, 2)


def quad_ids():
    c = lax.axis_index("ctx")
    f = lax.axis_index("fsdp")
    partner = f + 1 - 2 * (f % 2)
    across = (f + 2) % 4
    diagonal = (partner + 2) % 4
    return c, f, partner, across, diagonal


def quad_gather_kernel(x_ref, out_ref, send_sem, recv_sem):
    c, f, partner, across, diagonal = quad_ids()
    pair_barrier(c, partner, across)

    def copy(src, slot, dest, k):
        return pltpu.make_async_remote_copy(
            src_ref=src,
            dst_ref=out_ref.at[slot],
            send_sem=send_sem.at[k],
            recv_sem=recv_sem.at[slot],
            device_id=(c, dest),
            device_id_type=MESH,
        )

    first = copy(x_ref, f, across, 0)
    first.start()
    own = copy(x_ref, f, partner, 1)
    own.start()
    out_ref[f] = x_ref[...]
    copy(x_ref, across, f, 0).wait_recv()
    relay = copy(out_ref.at[across], across, partner, 2)
    relay.start()
    copy(x_ref, partner, f, 0).wait_recv()
    copy(x_ref, diagonal, f, 0).wait_recv()
    first.wait_send()
    own.wait_send()
    relay.wait_send()


def quad_gather(x):
    return pl.pallas_call(
        quad_gather_kernel,
        out_shape=jax.ShapeDtypeStruct((4,) + x.shape, x.dtype),
        in_specs=[pl.BlockSpec(memory_space=pltpu.VMEM)],
        out_specs=pl.BlockSpec(memory_space=pltpu.VMEM),
        scratch_shapes=[pltpu.SemaphoreType.DMA((3,)), pltpu.SemaphoreType.DMA((4,))],
        compiler_params=pltpu.CompilerParams(collective_id=4, has_side_effects=True),
    )(x)


def quad_reduce_kernel(p_ref, out_ref, near_buf, far_buf, sum_buf, send_sem, recv_sem):
    c, f, partner, across, diagonal = quad_ids()
    pair_barrier(c, partner, across)

    def copy(src, dst, dest, k):
        return pltpu.make_async_remote_copy(
            src_ref=src,
            dst_ref=dst,
            send_sem=send_sem.at[k],
            recv_sem=recv_sem.at[k],
            device_id=(c, dest),
            device_id_type=MESH,
        )

    to_partner = copy(p_ref.at[partner], near_buf.at[0], partner, 0)
    to_partner.start()
    to_diagonal = copy(p_ref.at[diagonal], near_buf.at[1], partner, 1)
    to_diagonal.start()
    to_partner.wait_recv()
    to_diagonal.wait_recv()
    sum_buf[...] = p_ref[across] + near_buf[1]
    to_across = copy(sum_buf, far_buf, across, 2)
    to_across.start()
    out_ref[...] = p_ref[f] + near_buf[0]
    to_across.wait_recv()
    out_ref[...] += far_buf[...]
    to_partner.wait_send()
    to_diagonal.wait_send()
    to_across.wait_send()


def quad_reduce(p):
    block = p.shape[1:]
    return pl.pallas_call(
        quad_reduce_kernel,
        out_shape=jax.ShapeDtypeStruct(block, p.dtype),
        in_specs=[pl.BlockSpec(memory_space=pltpu.VMEM)],
        out_specs=pl.BlockSpec(memory_space=pltpu.VMEM),
        scratch_shapes=[
            pltpu.VMEM((2,) + block, p.dtype),
            pltpu.VMEM(block, p.dtype),
            pltpu.VMEM(block, p.dtype),
            pltpu.SemaphoreType.DMA((3,)),
            pltpu.SemaphoreType.DMA((3,)),
        ],
        compiler_params=pltpu.CompilerParams(collective_id=5, has_side_effects=True),
    )(p)


def fsdp_gather(x, n_f):
    if n_f == 4:
        return quad_gather(x)
    return group_gather(x, n_f)


def fsdp_reduce(p, n_f):
    if n_f == 4:
        return quad_reduce(p)
    return group_reduce(p, n_f)


def body(
    tokens,
    doc_lengths,
    attention_gain,
    query_weight,
    key_weight,
    value_weight,
    output_weight,
    feedforward_gain,
    gate_weight,
    up_weight,
    down_weight,
    cotangent,
):
    n_dev = lax.axis_size(ALL)
    rows = query_weight.shape[0]
    ff_rows = down_weight.shape[0]
    ff = gate_weight.shape[1]
    local_tokens = tokens[0].astype(jnp.float32)
    tok_rows = local_tokens.shape[0]
    stream_len = tok_rows * lax.axis_size("ctx")
    my_first = lax.axis_index("ctx") * tok_rows

    gain_cols = jnp.pad(
        jnp.stack([attention_gain, feedforward_gain], axis=1), ((0, 0), (0, GAIN_PAD - 2))
    )
    att_full = lax.all_gather(
        jnp.concatenate([query_weight, key_weight, value_weight, output_weight, gain_cols], axis=1),
        ALL,
        axis=0,
        tiled=True,
    )
    c_k = D
    c_v = D + KVW
    c_o = D + 2 * KVW
    c_g = 2 * D + 2 * KVW
    query_full = att_full[:, :c_k]
    key_full = att_full[:, c_k:c_v]
    value_full = att_full[:, c_v:c_o]
    qkv_full = att_full[:, :c_o]
    output_full = att_full[:, c_o:c_g]
    gain_one_f = att_full[:, c_g].astype(jnp.float32)
    gain_two_f = att_full[:, c_g + 1].astype(jnp.float32)

    key_docs_all, places_all = document_layout(doc_lengths[0], stream_len)
    query_docs = lax.dynamic_slice_in_dim(key_docs_all, my_first, tok_rows, 0)
    query_positions = lax.dynamic_slice_in_dim(places_all, my_first, tok_rows, 0)
    query_places = my_first + jnp.arange(tok_rows, dtype=jnp.int32)
    group_size = H // KVH
    score_scale = HD ** (-0.5)

    scale_one = rms_scale(local_tokens)
    normed_one = local_tokens * scale_one
    normed_low = (normed_one * gain_one_f).astype(jnp.bfloat16)
    qkv = jnp.dot(normed_low, qkv_full, preferred_element_type=jnp.float32)
    queries = qkv[:, :D]
    keys_new = qkv[:, D : D + KVW]
    values_new = qkv[:, D + KVW :]
    query_low = rotate(queries, query_positions, H, 1.0).astype(jnp.bfloat16)
    key_low = rotate(keys_new, query_positions, KVH, 1.0).astype(jnp.bfloat16)
    value_low = values_new.astype(jnp.bfloat16)

    n_ctx = lax.axis_size("ctx")
    n_f = lax.axis_size("fsdp")
    chunk = ff_rows
    units = n_ctx * chunk
    gu_parts = jnp.transpose(
        jnp.stack([gate_weight, up_weight], axis=1).reshape(rows, 2, n_ctx, n_f, chunk),
        (3, 0, 1, 2, 4),
    )
    gu_parts = lax.all_to_all(gu_parts, "fsdp", 0, 0, tiled=True).reshape(n_f * rows, 2 * units)
    down_rows = D // (2 * n_ctx)
    ff_pack = jnp.concatenate([gu_parts, down_weight.reshape(down_rows, 2 * units)], axis=0)
    ff_pack = ff_pack.at[0, 0].add(att_full[0, 0] * 0)
    ff_stack = lax.all_gather(
        ff_pack,
        "ctx",
        axis=0,
        tiled=False,
    )
    gate_up_tp = ff_stack[:, : n_f * rows].reshape(n_ctx * n_f * rows, 2 * units)
    down_tp = ff_stack[:, n_f * rows :].reshape(n_ctx, ff_rows, D).reshape(units, D)
    max_doc = min(DOC_MOST, KBLK * (stream_len // (2 * KBLK)))
    back = min(-(-(max_doc - 1) // tok_rows), n_ctx - 1)
    win = (back + 1) * tok_rows
    kv_win = kv_share(
        jnp.concatenate([key_low, value_low], axis=1), n_ctx, back
    ).reshape(win, 2 * KVW)
    docs_pad = jnp.concatenate(
        [jnp.full((back * tok_rows,), -1, jnp.int32), key_docs_all.astype(jnp.int32)]
    )
    key_docs = lax.dynamic_slice_in_dim(docs_pad, my_first, win, 0)
    key_places = my_first - back * tok_rows + jnp.arange(win, dtype=jnp.int32)
    key_block = kv_win[:, :KVW].reshape(win, KVH, HD)
    value_block = kv_win[:, KVW:].reshape(win, KVH, HD)
    query_grouped = query_low.reshape(tok_rows, KVH, group_size, HD)
    allowed = (
        (key_docs[None, :] == query_docs[:, None]) & (key_places[None, :] <= query_places[:, None])
    )[:, None, None, :]
    scores = (
        jnp.einsum("qgrd,kgd->qgrk", query_grouped, key_block, preferred_element_type=jnp.float32)
        * score_scale
    )
    scores = jnp.where(allowed, scores, MASKED_SCORE)
    row_max = jnp.max(scores, axis=-1, keepdims=True)
    exponent = jnp.where(allowed, jnp.exp(scores - row_max), 0.0)
    probs = exponent / jnp.sum(exponent, axis=-1, keepdims=True)
    probs_low = probs.astype(jnp.bfloat16)
    attended_sum = jnp.einsum(
        "qgrk,kgd->qgrd", probs_low, value_block, preferred_element_type=jnp.float32
    )
    attended_low = attended_sum.reshape(tok_rows, D).astype(jnp.bfloat16)
    middle = local_tokens + jnp.dot(attended_low, output_full, preferred_element_type=jnp.float32)

    scale_two = rms_scale(middle)
    normed_two = middle * scale_two
    normed_two_low = (normed_two * gain_two_f).astype(jnp.bfloat16)
    group_tokens = n_f * tok_rows
    xn2_all = fsdp_gather(normed_two_low, n_f).reshape(group_tokens, D)
    gate_up = jnp.dot(xn2_all, gate_up_tp, preferred_element_type=jnp.float32)
    gate_pre = gate_up[:, :units]
    up_pre = gate_up[:, units:]
    sigmoid = jax.nn.sigmoid(gate_pre)
    hidden_low = (gate_pre * sigmoid * up_pre).astype(jnp.bfloat16)
    ff_part = jnp.dot(hidden_low, down_tp, preferred_element_type=jnp.float32)

    grad_out = cotangent[0]
    grad_all = fsdp_gather(grad_out, n_f).reshape(group_tokens, D)
    down_sum = lax.psum_scatter(
        outer_rows(hidden_low, grad_all).astype(jnp.bfloat16), "ctx", scatter_dimension=0, tiled=True
    )
    hidden_grad = times_transposed(grad_all, down_tp)
    gate_grad = (hidden_grad * up_pre * sigmoid * (1.0 + gate_pre * (1.0 - sigmoid))).astype(
        jnp.bfloat16
    )
    up_grad = (hidden_grad * gate_pre * sigmoid).astype(jnp.bfloat16)
    gate_up_cat = jnp.concatenate([gate_grad, up_grad], axis=1)
    gate_up_term = outer_rows(xn2_all, gate_up_cat)
    ff_pack, gate_up_cat = lax.optimization_barrier((gate_up_term.astype(jnp.bfloat16), gate_up_cat))
    ff_part = ff_part.at[0, 0].add(ff_pack[0, 0].astype(jnp.float32) * 0.0)
    layer_out = middle + fsdp_reduce(ff_part.reshape(n_f, tok_rows, D), n_f)
    gu_sum = lax.psum_scatter(ff_pack, "ctx", scatter_dimension=0, tiled=True)
    gu_sum = lax.all_to_all(gu_sum.reshape(n_f, rows, 2 * units), "fsdp", 0, 0, tiled=True)
    ff_sum = jnp.transpose(
        gu_sum.reshape(n_f, rows, 2, n_ctx, chunk), (1, 2, 3, 0, 4)
    ).reshape(rows, 2 * ff)
    normed_two_grad = fsdp_reduce(
        times_transposed(gate_up_cat, gate_up_tp).reshape(n_f, tok_rows, D), n_f
    )
    gain_two_term = jnp.sum(normed_two_grad * normed_two, axis=0)
    scaled_two = normed_two_grad * gain_two_f
    middle_grad = grad_out.astype(jnp.float32) + scale_two * (
        scaled_two - normed_two * jnp.mean(scaled_two * normed_two, axis=-1, keepdims=True)
    )
    branch_grad = middle_grad.astype(jnp.bfloat16)
    attended_grad_low = (
        times_transposed(branch_grad, output_full)
        .astype(jnp.bfloat16)
        .reshape(tok_rows, KVH, group_size, HD)
    )
    row_delta = jnp.sum(
        attended_grad_low.astype(jnp.float32) * attended_sum, axis=-1, keepdims=True
    )
    prob_grad = jnp.einsum(
        "qgrd,kgd->qgrk", attended_grad_low, value_block, preferred_element_type=jnp.float32
    )
    score_grad = (probs * (prob_grad - row_delta)).astype(jnp.bfloat16)
    query_accum = jnp.einsum(
        "qgrk,kgd->qgrd", score_grad, key_block, preferred_element_type=jnp.float32
    )
    key_term = jnp.einsum(
        "qgrk,qgrd->kgd", score_grad, query_grouped, preferred_element_type=jnp.float32
    ).reshape(win, KVW)
    value_term = jnp.einsum(
        "qgrk,qgrd->kgd", probs_low, attended_grad_low, preferred_element_type=jnp.float32
    ).reshape(win, KVW)
    kv_term = jnp.concatenate([key_term, value_term], axis=1).reshape(back + 1, tok_rows, 2 * KVW)
    kv_sum = kv_return(kv_term[back], kv_term[:back].astype(jnp.bfloat16), n_ctx, back)
    key_grad_low = rotate(kv_sum[:, :KVW] * score_scale, query_positions, KVH, -1.0).astype(
        jnp.bfloat16
    )
    value_grad_low = kv_sum[:, KVW:].astype(jnp.bfloat16)
    query_grad_low = rotate(
        query_accum.reshape(tok_rows, D) * score_scale, query_positions, H, -1.0
    ).astype(jnp.bfloat16)
    projection_cat = jnp.concatenate([query_grad_low, key_grad_low, value_grad_low], axis=1)
    normed_grad = times_transposed(projection_cat, qkv_full)
    gain_one_term = jnp.sum(normed_grad * normed_one, axis=0)
    scaled_one = normed_grad * gain_one_f
    tokens_grad = middle_grad + scale_one * (
        scaled_one - normed_one * jnp.mean(scaled_one * normed_one, axis=-1, keepdims=True)
    )
    gain_term_cols = jnp.pad(
        jnp.stack([gain_one_term, gain_two_term], axis=1), ((0, 0), (0, GAIN_PAD - 2))
    )
    gain_term_cols = gain_term_cols.at[0, GAIN_PAD - 1].set(ff_sum[0, 0].astype(jnp.float32) * 0.0)
    attention_sum = lax.psum_scatter(
        jnp.concatenate(
            [
                outer_rows(normed_low, projection_cat).astype(jnp.bfloat16),
                outer_rows(attended_low, branch_grad).astype(jnp.bfloat16),
                gain_term_cols.astype(jnp.bfloat16),
            ],
            axis=1,
        ),
        ALL,
        scatter_dimension=0,
        tiled=True,
    ).astype(jnp.float32)
    ff_sum = ff_sum.astype(jnp.float32)
    return (
        layer_out.astype(jnp.bfloat16)[None],
        tokens_grad[None],
        attention_sum[:, c_g],
        attention_sum[:, :c_k],
        attention_sum[:, c_k:c_v],
        attention_sum[:, c_v:c_o],
        attention_sum[:, c_o:c_g],
        attention_sum[:, c_g + 1],
        ff_sum[:, :ff],
        ff_sum[:, ff : 2 * ff],
        down_sum.astype(jnp.float32),
    )


def solution(mesh):
    weight = P(ALL, None)
    stream = P("fsdp", "ctx", None)
    return jax.shard_map(
        body,
        mesh=mesh,
        in_specs=(
            stream,
            P("fsdp", None),
            P(ALL),
            weight,
            weight,
            weight,
            weight,
            P(ALL),
            weight,
            weight,
            weight,
            stream,
        ),
        out_specs=(
            stream,
            stream,
            P(ALL),
            weight,
            weight,
            weight,
            weight,
            P(ALL),
            weight,
            weight,
            weight,
        ),
        check_vma=False,
    )
```

```python
import functools

import jax
import jax.numpy as jnp
from jax import lax
from jax.experimental import pallas as pl
from jax.experimental.pallas import tpu as pltpu
from jax.sharding import PartitionSpec as P

MESH = pl.DeviceIdType.MESH

D = 1536
H = 16
KVH = 8
HD = 96
KBLK = 512
DOC_MOST = 4096
KVW = 768
GAIN_PAD = 128

EPSILON = 1e-05
ROPE_BASE = 100000.0
MASKED_SCORE = -1e30
ALL = ("ctx", "fsdp")


def rms_scale(values):
    return lax.rsqrt(jnp.mean(values * values, axis=-1, keepdims=True) + EPSILON)


def document_layout(lengths, total):
    starts = jnp.cumsum(lengths) - lengths
    places = jnp.arange(total, dtype=jnp.int32)
    inside = places[:, None] >= starts[None, :]
    doc_ids = jnp.sum(inside.astype(jnp.int32), axis=1) - 1
    doc_starts = jnp.max(jnp.where(inside, starts[None, :], 0), axis=1)
    return (doc_ids, places - doc_starts)


def rotate(values, positions, head_count, direction):
    row_count = values.shape[0]
    half_dim = HD // 2
    inverse_freq = ROPE_BASE ** (-(jnp.arange(half_dim).astype(jnp.float32) * (2.0 / HD)))
    angles = positions.astype(jnp.float32)[:, None] * inverse_freq[None, :]
    cosine = jnp.cos(angles)[:, None, :]
    sine_part = direction * jnp.sin(angles)[:, None, :]
    grouped = values.reshape(row_count, head_count, HD)
    former = grouped[:, :, :half_dim]
    latter = grouped[:, :, half_dim:]
    turned = jnp.concatenate(
        [former * cosine - latter * sine_part, latter * cosine + former * sine_part], axis=2
    )
    return turned.reshape(row_count, head_count * HD)


def outer_rows(left, right):
    return lax.dot_general(
        left, right, (((0,), (0,)), ((), ())), preferred_element_type=jnp.float32
    )


def times_transposed(left, right):
    return lax.dot_general(
        left, right, (((1,), (1,)), ((), ())), preferred_element_type=jnp.float32
    )


def neighbour_barrier(n_ctx, back, c, f):
    barrier = pltpu.get_barrier_semaphore()
    for s in range(1, back + 1):
        for peer in ((c + s) % n_ctx, (c + n_ctx - s) % n_ctx):
            pl.semaphore_signal(barrier, inc=1, device_id=(peer, f), device_id_type=MESH)
    pl.semaphore_wait(barrier, 2 * back)


def kv_share_kernel(n_ctx, back, kv_ref, out_ref, send_sem, recv_sem):
    c = lax.axis_index("ctx")
    f = lax.axis_index("fsdp")
    neighbour_barrier(n_ctx, back, c, f)

    def copy(s, dest):
        return pltpu.make_async_remote_copy(
            src_ref=kv_ref,
            dst_ref=out_ref.at[back - s],
            send_sem=send_sem.at[s - 1],
            recv_sem=recv_sem.at[back - s],
            device_id=(dest, f),
            device_id_type=MESH,
        )

    for s in range(1, back + 1):

        @pl.when(c + s < n_ctx)
        def _():
            copy(s, c + s).start()

    out_ref[back] = kv_ref[...]
    for s in range(1, back + 1):

        @pl.when(c - s < 0)
        def _():
            out_ref[back - s] = jnp.zeros(kv_ref.shape, kv_ref.dtype)

    for s in range(1, back + 1):

        @pl.when(c + s < n_ctx)
        def _():
            copy(s, c + s).wait_send()

        @pl.when(c - s >= 0)
        def _():
            copy(s, c).wait_recv()


def kv_share(kv, n_ctx, back):
    return pl.pallas_call(
        functools.partial(kv_share_kernel, n_ctx, back),
        out_shape=jax.ShapeDtypeStruct((back + 1,) + kv.shape, kv.dtype),
        in_specs=[pl.BlockSpec(memory_space=pltpu.VMEM)],
        out_specs=pl.BlockSpec(memory_space=pltpu.VMEM),
        scratch_shapes=[pltpu.SemaphoreType.DMA((back,)), pltpu.SemaphoreType.DMA((back + 1,))],
        compiler_params=pltpu.CompilerParams(collective_id=0, has_side_effects=True),
    )(kv)


def kv_return_kernel(n_ctx, back, own_ref, g_ref, out_ref, recv_buf, send_sem, recv_sem):
    c = lax.axis_index("ctx")
    f = lax.axis_index("fsdp")
    neighbour_barrier(n_ctx, back, c, f)

    def copy(s, dest):
        return pltpu.make_async_remote_copy(
            src_ref=g_ref.at[back - s],
            dst_ref=recv_buf.at[s - 1],
            send_sem=send_sem.at[s - 1],
            recv_sem=recv_sem.at[s - 1],
            device_id=(dest, f),
            device_id_type=MESH,
        )

    for s in range(1, back + 1):

        @pl.when(c - s >= 0)
        def _():
            copy(s, c - s).start()

    out_ref[...] = own_ref[...]
    for s in range(1, back + 1):

        @pl.when(c + s < n_ctx)
        def _():
            copy(s, c).wait_recv()
            out_ref[...] += recv_buf[s - 1].astype(jnp.float32)

    for s in range(1, back + 1):

        @pl.when(c - s >= 0)
        def _():
            copy(s, c - s).wait_send()


def kv_return(own, g, n_ctx, back):
    return pl.pallas_call(
        functools.partial(kv_return_kernel, n_ctx, back),
        out_shape=jax.ShapeDtypeStruct(own.shape, own.dtype),
        in_specs=[pl.BlockSpec(memory_space=pltpu.VMEM)] * 2,
        out_specs=pl.BlockSpec(memory_space=pltpu.VMEM),
        scratch_shapes=[
            pltpu.VMEM(g.shape, g.dtype),
            pltpu.SemaphoreType.DMA((back,)),
            pltpu.SemaphoreType.DMA((back,)),
        ],
        compiler_params=pltpu.CompilerParams(collective_id=1, has_side_effects=True),
    )(own, g)


def peer_barrier(n_f, c, f):
    barrier = pltpu.get_barrier_semaphore()
    for k in range(1, n_f):
        pl.semaphore_signal(barrier, inc=1, device_id=(c, (f + k) % n_f), device_id_type=MESH)
    pl.semaphore_wait(barrier, n_f - 1)


def group_gather_kernel(n_f, x_ref, out_ref, send_sem, recv_sem):
    c = lax.axis_index("ctx")
    f = lax.axis_index("fsdp")
    peer_barrier(n_f, c, f)
    copies = []
    for k in range(1, n_f):
        copy = pltpu.make_async_remote_copy(
            src_ref=x_ref,
            dst_ref=out_ref.at[f],
            send_sem=send_sem.at[k - 1],
            recv_sem=recv_sem.at[k - 1],
            device_id=(c, (f + k) % n_f),
            device_id_type=MESH,
        )
        copy.start()
        copies.append(copy)
    out_ref[f] = x_ref[...]
    for k in range(1, n_f):
        pltpu.make_async_remote_copy(
            src_ref=x_ref,
            dst_ref=out_ref.at[(f + n_f - k) % n_f],
            send_sem=send_sem.at[k - 1],
            recv_sem=recv_sem.at[k - 1],
            device_id=(c, f),
            device_id_type=MESH,
        ).wait_recv()
    for copy in copies:
        copy.wait_send()


def group_gather(x, n_f):
    return pl.pallas_call(
        functools.partial(group_gather_kernel, n_f),
        out_shape=jax.ShapeDtypeStruct((n_f,) + x.shape, x.dtype),
        in_specs=[pl.BlockSpec(memory_space=pltpu.VMEM)],
        out_specs=pl.BlockSpec(memory_space=pltpu.VMEM),
        scratch_shapes=[pltpu.SemaphoreType.DMA((n_f - 1,)), pltpu.SemaphoreType.DMA((n_f - 1,))],
        compiler_params=pltpu.CompilerParams(collective_id=2, has_side_effects=True),
    )(x)


def group_reduce_kernel(n_f, p_ref, out_ref, recv_buf, send_sem, recv_sem):
    c = lax.axis_index("ctx")
    f = lax.axis_index("fsdp")
    peer_barrier(n_f, c, f)
    copies = []
    for k in range(1, n_f):
        dest = (f + k) % n_f
        copy = pltpu.make_async_remote_copy(
            src_ref=p_ref.at[dest],
            dst_ref=recv_buf.at[k - 1],
            send_sem=send_sem.at[k - 1],
            recv_sem=recv_sem.at[k - 1],
            device_id=(c, dest),
            device_id_type=MESH,
        )
        copy.start()
        copies.append(copy)
    out_ref[...] = p_ref[f]
    for k in range(1, n_f):
        copies[k - 1].wait_recv()
        out_ref[...] += recv_buf[k - 1]
    for copy in copies:
        copy.wait_send()


def group_reduce(p, n_f):
    return pl.pallas_call(
        functools.partial(group_reduce_kernel, n_f),
        out_shape=jax.ShapeDtypeStruct(p.shape[1:], p.dtype),
        in_specs=[pl.BlockSpec(memory_space=pltpu.VMEM)],
        out_specs=pl.BlockSpec(memory_space=pltpu.VMEM),
        scratch_shapes=[
            pltpu.VMEM((n_f - 1,) + p.shape[1:], p.dtype),
            pltpu.SemaphoreType.DMA((n_f - 1,)),
            pltpu.SemaphoreType.DMA((n_f - 1,)),
        ],
        compiler_params=pltpu.CompilerParams(collective_id=3, has_side_effects=True),
    )(p)


def pair_barrier(c, partner, across):
    barrier = pltpu.get_barrier_semaphore()
    pl.semaphore_signal(barrier, inc=1, device_id=(c, partner), device_id_type=MESH)
    pl.semaphore_signal(barrier, inc=1, device_id=(c, across), device_id_type=MESH)
    pl.semaphore_wait(barrier, 2)


def quad_ids():
    c = lax.axis_index("ctx")
    f = lax.axis_index("fsdp")
    partner = f + 1 - 2 * (f % 2)
    across = (f + 2) % 4
    diagonal = (partner + 2) % 4
    return c, f, partner, across, diagonal


def quad_gather_kernel(x_ref, out_ref, send_sem, recv_sem):
    c, f, partner, across, diagonal = quad_ids()
    pair_barrier(c, partner, across)

    def copy(src, slot, dest, k):
        return pltpu.make_async_remote_copy(
            src_ref=src,
            dst_ref=out_ref.at[slot],
            send_sem=send_sem.at[k],
            recv_sem=recv_sem.at[slot],
            device_id=(c, dest),
            device_id_type=MESH,
        )

    first = copy(x_ref, f, across, 0)
    first.start()
    own = copy(x_ref, f, partner, 1)
    own.start()
    out_ref[f] = x_ref[...]
    copy(x_ref, across, f, 0).wait_recv()
    relay = copy(out_ref.at[across], across, partner, 2)
    relay.start()
    copy(x_ref, partner, f, 0).wait_recv()
    copy(x_ref, diagonal, f, 0).wait_recv()
    first.wait_send()
    own.wait_send()
    relay.wait_send()


def quad_gather(x):
    return pl.pallas_call(
        quad_gather_kernel,
        out_shape=jax.ShapeDtypeStruct((4,) + x.shape, x.dtype),
        in_specs=[pl.BlockSpec(memory_space=pltpu.VMEM)],
        out_specs=pl.BlockSpec(memory_space=pltpu.VMEM),
        scratch_shapes=[pltpu.SemaphoreType.DMA((3,)), pltpu.SemaphoreType.DMA((4,))],
        compiler_params=pltpu.CompilerParams(collective_id=4, has_side_effects=True),
    )(x)


def quad_reduce_kernel(p_ref, out_ref, near_buf, far_buf, sum_buf, send_sem, recv_sem):
    c, f, partner, across, diagonal = quad_ids()
    pair_barrier(c, partner, across)

    def copy(src, dst, dest, k):
        return pltpu.make_async_remote_copy(
            src_ref=src,
            dst_ref=dst,
            send_sem=send_sem.at[k],
            recv_sem=recv_sem.at[k],
            device_id=(c, dest),
            device_id_type=MESH,
        )

    to_partner = copy(p_ref.at[partner], near_buf.at[0], partner, 0)
    to_partner.start()
    to_diagonal = copy(p_ref.at[diagonal], near_buf.at[1], partner, 1)
    to_diagonal.start()
    to_partner.wait_recv()
    to_diagonal.wait_recv()
    sum_buf[...] = p_ref[across] + near_buf[1]
    to_across = copy(sum_buf, far_buf, across, 2)
    to_across.start()
    out_ref[...] = p_ref[f] + near_buf[0]
    to_across.wait_recv()
    out_ref[...] += far_buf[...]
    to_partner.wait_send()
    to_diagonal.wait_send()
    to_across.wait_send()


def quad_reduce(p):
    block = p.shape[1:]
    return pl.pallas_call(
        quad_reduce_kernel,
        out_shape=jax.ShapeDtypeStruct(block, p.dtype),
        in_specs=[pl.BlockSpec(memory_space=pltpu.VMEM)],
        out_specs=pl.BlockSpec(memory_space=pltpu.VMEM),
        scratch_shapes=[
            pltpu.VMEM((2,) + block, p.dtype),
            pltpu.VMEM(block, p.dtype),
            pltpu.VMEM(block, p.dtype),
            pltpu.SemaphoreType.DMA((3,)),
            pltpu.SemaphoreType.DMA((3,)),
        ],
        compiler_params=pltpu.CompilerParams(collective_id=5, has_side_effects=True),
    )(p)


def fsdp_gather(x, n_f):
    if n_f == 4:
        return quad_gather(x)
    return group_gather(x, n_f)


def fsdp_reduce(p, n_f):
    if n_f == 4:
        return quad_reduce(p)
    return group_reduce(p, n_f)


def ring_order(n, snake):
    c = lax.axis_index("ctx")
    if snake:
        half = n // 2
        y = c % 2
        z = c // 2
        pos = (1 - y) * z + y * (n - 1 - z)

        def device_at(q):
            q = (q + n) % n
            h = q // half
            return (1 - h) * 2 * q + h * (2 * (n - 1 - q) + 1)

    else:
        pos = c

        def device_at(q):
            return (q + n) % n

    return c, pos, device_at


def ring_reduce_kernel(n, snake, part_ref, out_ref, recv_buf, send_buf, send_sem, recv_sem):
    c, pos, device_at = ring_order(n, snake)
    f = lax.axis_index("fsdp")
    nxt = device_at(pos + 1)
    prv = device_at(pos - 1)
    barrier = pltpu.get_barrier_semaphore()
    pl.semaphore_signal(barrier, inc=1, device_id=(nxt, f), device_id_type=MESH)
    pl.semaphore_signal(barrier, inc=1, device_id=(prv, f), device_id_type=MESH)
    pl.semaphore_wait(barrier, 2)
    width = part_ref.shape[2] // 2
    steps = n - 1
    directions = ((0, 1, nxt), (1, -1, prv))

    def copy(d, s, src, dest):
        return pltpu.make_async_remote_copy(
            src_ref=src,
            dst_ref=recv_buf.at[d, s],
            send_sem=send_sem.at[d, s],
            recv_sem=recv_sem.at[d, s],
            device_id=(dest, f),
            device_id_type=MESH,
        )

    sends = []
    for d, sign, dest in directions:
        cols = pl.ds(d * width, width)
        first = copy(d, 0, part_ref.at[device_at(pos - sign), :, cols], dest)
        first.start()
        sends.append(first)
    for s in range(1, steps):
        for d, sign, dest in directions:
            cols = pl.ds(d * width, width)
            copy(d, s - 1, send_buf.at[d, s], dest).wait_recv()
            block = device_at(pos - sign * (s + 1))
            send_buf[d, s] = (
                recv_buf[d, s - 1].astype(jnp.float32) + part_ref[block, :, cols].astype(jnp.float32)
            ).astype(send_buf.dtype)
            nxt_copy = copy(d, s, send_buf.at[d, s], dest)
            nxt_copy.start()
            sends.append(nxt_copy)
    for d, sign, dest in directions:
        cols = pl.ds(d * width, width)
        copy(d, steps - 1, send_buf.at[d, 0], dest).wait_recv()
        out_ref[:, cols] = recv_buf[d, steps - 1].astype(jnp.float32) + part_ref[c, :, cols].astype(
            jnp.float32
        )
    for s_copy in sends:
        s_copy.wait_send()


def ring_reduce(part, n, snake):
    _, rows_, cols_ = part.shape
    return pl.pallas_call(
        functools.partial(ring_reduce_kernel, n, snake),
        out_shape=jax.ShapeDtypeStruct((rows_, cols_), jnp.float32),
        in_specs=[pl.BlockSpec(memory_space=pltpu.VMEM)],
        out_specs=pl.BlockSpec(memory_space=pltpu.VMEM),
        scratch_shapes=[
            pltpu.VMEM((2, n - 1, rows_, cols_ // 2), part.dtype),
            pltpu.VMEM((2, n - 1, rows_, cols_ // 2), part.dtype),
            pltpu.SemaphoreType.DMA((2, n - 1)),
            pltpu.SemaphoreType.DMA((2, n - 1)),
        ],
        compiler_params=pltpu.CompilerParams(
            collective_id=6, has_side_effects=True, vmem_limit_bytes=100 * 1024 * 1024 // 2
        ),
    )(part)


def body(
    snake,
    tokens,
    doc_lengths,
    attention_gain,
    query_weight,
    key_weight,
    value_weight,
    output_weight,
    feedforward_gain,
    gate_weight,
    up_weight,
    down_weight,
    cotangent,
):
    n_dev = lax.axis_size(ALL)
    rows = query_weight.shape[0]
    ff_rows = down_weight.shape[0]
    ff = gate_weight.shape[1]
    local_tokens = tokens[0].astype(jnp.float32)
    tok_rows = local_tokens.shape[0]
    stream_len = tok_rows * lax.axis_size("ctx")
    my_first = lax.axis_index("ctx") * tok_rows

    gain_cols = jnp.pad(
        jnp.stack([attention_gain, feedforward_gain], axis=1), ((0, 0), (0, GAIN_PAD - 2))
    )
    att_full = lax.all_gather(
        jnp.concatenate([query_weight, key_weight, value_weight, output_weight, gain_cols], axis=1),
        ALL,
        axis=0,
        tiled=True,
    )
    c_k = D
    c_v = D + KVW
    c_o = D + 2 * KVW
    c_g = 2 * D + 2 * KVW
    query_full = att_full[:, :c_k]
    key_full = att_full[:, c_k:c_v]
    value_full = att_full[:, c_v:c_o]
    qkv_full = att_full[:, :c_o]
    output_full = att_full[:, c_o:c_g]
    gain_one_f = att_full[:, c_g].astype(jnp.float32)
    gain_two_f = att_full[:, c_g + 1].astype(jnp.float32)

    key_docs_all, places_all = document_layout(doc_lengths[0], stream_len)
    query_docs = lax.dynamic_slice_in_dim(key_docs_all, my_first, tok_rows, 0)
    query_positions = lax.dynamic_slice_in_dim(places_all, my_first, tok_rows, 0)
    query_places = my_first + jnp.arange(tok_rows, dtype=jnp.int32)
    group_size = H // KVH
    score_scale = HD ** (-0.5)

    scale_one = rms_scale(local_tokens)
    normed_one = local_tokens * scale_one
    normed_low = (normed_one * gain_one_f).astype(jnp.bfloat16)
    qkv = jnp.dot(normed_low, qkv_full, preferred_element_type=jnp.float32)
    queries = qkv[:, :D]
    keys_new = qkv[:, D : D + KVW]
    values_new = qkv[:, D + KVW :]
    query_low = rotate(queries, query_positions, H, 1.0).astype(jnp.bfloat16)
    key_low = rotate(keys_new, query_positions, KVH, 1.0).astype(jnp.bfloat16)
    value_low = values_new.astype(jnp.bfloat16)

    n_ctx = lax.axis_size("ctx")
    n_f = lax.axis_size("fsdp")
    chunk = ff_rows
    units = n_ctx * chunk
    gu_parts = jnp.transpose(
        jnp.stack([gate_weight, up_weight], axis=1).reshape(rows, 2, n_ctx, n_f, chunk),
        (3, 0, 1, 2, 4),
    )
    gu_parts = lax.all_to_all(gu_parts, "fsdp", 0, 0, tiled=True).reshape(n_f * rows, 2 * units)
    down_rows = D // (2 * n_ctx)
    ff_pack = jnp.concatenate([gu_parts, down_weight.reshape(down_rows, 2 * units)], axis=0)
    ff_pack = ff_pack.at[0, 0].add(att_full[0, 0] * 0)
    ff_stack = lax.all_gather(
        ff_pack,
        "ctx",
        axis=0,
        tiled=False,
    )
    gate_up_tp = ff_stack[:, : n_f * rows].reshape(n_ctx * n_f * rows, 2 * units)
    down_tp = ff_stack[:, n_f * rows :].reshape(n_ctx, ff_rows, D).reshape(units, D)
    max_doc = min(DOC_MOST, KBLK * (stream_len // (2 * KBLK)))
    back = min(-(-(max_doc - 1) // tok_rows), n_ctx - 1)
    win = (back + 1) * tok_rows
    kv_win = kv_share(
        jnp.concatenate([key_low, value_low], axis=1), n_ctx, back
    ).reshape(win, 2 * KVW)
    docs_pad = jnp.concatenate(
        [jnp.full((back * tok_rows,), -1, jnp.int32), key_docs_all.astype(jnp.int32)]
    )
    key_docs = lax.dynamic_slice_in_dim(docs_pad, my_first, win, 0)
    key_places = my_first - back * tok_rows + jnp.arange(win, dtype=jnp.int32)
    key_block = kv_win[:, :KVW].reshape(win, KVH, HD)
    value_block = kv_win[:, KVW:].reshape(win, KVH, HD)
    query_grouped = query_low.reshape(tok_rows, KVH, group_size, HD)
    allowed = (
        (key_docs[None, :] == query_docs[:, None]) & (key_places[None, :] <= query_places[:, None])
    )[:, None, None, :]
    scores = (
        jnp.einsum("qgrd,kgd->qgrk", query_grouped, key_block, preferred_element_type=jnp.float32)
        * score_scale
    )
    scores = jnp.where(allowed, scores, MASKED_SCORE)
    row_max = jnp.max(scores, axis=-1, keepdims=True)
    exponent = jnp.where(allowed, jnp.exp(scores - row_max), 0.0)
    probs = exponent / jnp.sum(exponent, axis=-1, keepdims=True)
    probs_low = probs.astype(jnp.bfloat16)
    attended_sum = jnp.einsum(
        "qgrk,kgd->qgrd", probs_low, value_block, preferred_element_type=jnp.float32
    )
    attended_low = attended_sum.reshape(tok_rows, D).astype(jnp.bfloat16)
    middle = local_tokens + jnp.dot(attended_low, output_full, preferred_element_type=jnp.float32)

    scale_two = rms_scale(middle)
    normed_two = middle * scale_two
    normed_two_low = (normed_two * gain_two_f).astype(jnp.bfloat16)
    group_tokens = n_f * tok_rows
    xn2_all = fsdp_gather(normed_two_low, n_f).reshape(group_tokens, D)
    gate_up = jnp.dot(xn2_all, gate_up_tp, preferred_element_type=jnp.float32)
    gate_pre = gate_up[:, :units]
    up_pre = gate_up[:, units:]
    sigmoid = jax.nn.sigmoid(gate_pre)
    hidden_low = (gate_pre * sigmoid * up_pre).astype(jnp.bfloat16)
    ff_part = jnp.dot(hidden_low, down_tp, preferred_element_type=jnp.float32)
    layer_out = middle + fsdp_reduce(ff_part.reshape(n_f, tok_rows, D), n_f)

    grad_out = cotangent[0]
    grad_all = fsdp_gather(grad_out, n_f).reshape(group_tokens, D)
    down_term = outer_rows(hidden_low, grad_all).astype(jnp.bfloat16)
    hidden_grad = times_transposed(grad_all, down_tp)
    gate_grad = (hidden_grad * up_pre * sigmoid * (1.0 + gate_pre * (1.0 - sigmoid))).astype(
        jnp.bfloat16
    )
    up_grad = (hidden_grad * gate_pre * sigmoid).astype(jnp.bfloat16)
    gate_up_cat = jnp.concatenate([gate_grad, up_grad], axis=1)
    gate_up_term = outer_rows(xn2_all, gate_up_cat)
    grad_pack = jnp.concatenate(
        [
            gate_up_term.astype(jnp.bfloat16).reshape(n_ctx, n_f * rows, 2 * units),
            down_term.reshape(n_ctx, down_rows, 2 * units),
        ],
        axis=1,
    )
    grad_sum = ring_reduce(grad_pack, n_ctx, snake).astype(jnp.bfloat16)
    down_sum = grad_sum[n_f * rows :].reshape(ff_rows, D)
    gu_sum = lax.all_to_all(grad_sum[: n_f * rows].reshape(n_f, rows, 2 * units), "fsdp", 0, 0, tiled=True)
    ff_sum = jnp.transpose(
        gu_sum.reshape(n_f, rows, 2, n_ctx, chunk), (1, 2, 3, 0, 4)
    ).reshape(rows, 2 * ff)
    normed_two_grad = fsdp_reduce(
        times_transposed(gate_up_cat, gate_up_tp).reshape(n_f, tok_rows, D), n_f
    )
    gain_two_term = jnp.sum(normed_two_grad * normed_two, axis=0)
    scaled_two = normed_two_grad * gain_two_f
    middle_grad = grad_out.astype(jnp.float32) + scale_two * (
        scaled_two - normed_two * jnp.mean(scaled_two * normed_two, axis=-1, keepdims=True)
    )
    branch_grad = middle_grad.astype(jnp.bfloat16)
    attended_grad_low = (
        times_transposed(branch_grad, output_full)
        .astype(jnp.bfloat16)
        .reshape(tok_rows, KVH, group_size, HD)
    )
    row_delta = jnp.sum(
        attended_grad_low.astype(jnp.float32) * attended_sum, axis=-1, keepdims=True
    )
    prob_grad = jnp.einsum(
        "qgrd,kgd->qgrk", attended_grad_low, value_block, preferred_element_type=jnp.float32
    )
    score_grad = (probs * (prob_grad - row_delta)).astype(jnp.bfloat16)
    query_accum = jnp.einsum(
        "qgrk,kgd->qgrd", score_grad, key_block, preferred_element_type=jnp.float32
    )
    key_term = jnp.einsum(
        "qgrk,qgrd->kgd", score_grad, query_grouped, preferred_element_type=jnp.float32
    ).reshape(win, KVW)
    value_term = jnp.einsum(
        "qgrk,qgrd->kgd", probs_low, attended_grad_low, preferred_element_type=jnp.float32
    ).reshape(win, KVW)
    kv_term = jnp.concatenate([key_term, value_term], axis=1).reshape(back + 1, tok_rows, 2 * KVW)
    kv_sum = kv_return(kv_term[back], kv_term[:back].astype(jnp.bfloat16), n_ctx, back)
    key_grad_low = rotate(kv_sum[:, :KVW] * score_scale, query_positions, KVH, -1.0).astype(
        jnp.bfloat16
    )
    value_grad_low = kv_sum[:, KVW:].astype(jnp.bfloat16)
    query_grad_low = rotate(
        query_accum.reshape(tok_rows, D) * score_scale, query_positions, H, -1.0
    ).astype(jnp.bfloat16)
    projection_cat = jnp.concatenate([query_grad_low, key_grad_low, value_grad_low], axis=1)
    normed_grad = times_transposed(projection_cat, qkv_full)
    gain_one_term = jnp.sum(normed_grad * normed_one, axis=0)
    scaled_one = normed_grad * gain_one_f
    tokens_grad = middle_grad + scale_one * (
        scaled_one - normed_one * jnp.mean(scaled_one * normed_one, axis=-1, keepdims=True)
    )
    gain_term_cols = jnp.pad(
        jnp.stack([gain_one_term, gain_two_term], axis=1), ((0, 0), (0, GAIN_PAD - 2))
    )
    gain_term_cols = gain_term_cols.at[0, GAIN_PAD - 1].set(ff_sum[0, 0].astype(jnp.float32) * 0.0)
    attention_sum = lax.psum_scatter(
        jnp.concatenate(
            [
                outer_rows(normed_low, projection_cat).astype(jnp.bfloat16),
                outer_rows(attended_low, branch_grad).astype(jnp.bfloat16),
                gain_term_cols.astype(jnp.bfloat16),
            ],
            axis=1,
        ),
        ALL,
        scatter_dimension=0,
        tiled=True,
    ).astype(jnp.float32)
    ff_sum = ff_sum.astype(jnp.float32)
    return (
        layer_out.astype(jnp.bfloat16)[None],
        tokens_grad[None],
        attention_sum[:, c_g],
        attention_sum[:, :c_k],
        attention_sum[:, c_k:c_v],
        attention_sum[:, c_v:c_o],
        attention_sum[:, c_o:c_g],
        attention_sum[:, c_g + 1],
        ff_sum[:, :ff],
        ff_sum[:, ff : 2 * ff],
        down_sum.astype(jnp.float32),
    )


def snake_ring(mesh):
    column = mesh.devices[:, 0]
    n = column.shape[0]
    if n % 2 or n < 4:
        return False
    return all(
        tuple(d.coords)[2] == i // 2 and tuple(d.coords)[1] == i % 2 for i, d in enumerate(column)
    )


def solution(mesh):
    weight = P(ALL, None)
    stream = P("fsdp", "ctx", None)
    return jax.shard_map(
        functools.partial(body, snake_ring(mesh)),
        mesh=mesh,
        in_specs=(
            stream,
            P("fsdp", None),
            P(ALL),
            weight,
            weight,
            weight,
            weight,
            P(ALL),
            weight,
            weight,
            weight,
            stream,
        ),
        out_specs=(
            stream,
            stream,
            P(ALL),
            weight,
            weight,
            weight,
            weight,
            P(ALL),
            weight,
            weight,
            weight,
        ),
        check_vma=False,
    )
```

```python
import functools

import jax
import jax.numpy as jnp
from jax import lax
from jax.experimental import pallas as pl
from jax.experimental.pallas import tpu as pltpu
from jax.sharding import PartitionSpec as P

MESH = pl.DeviceIdType.MESH

D = 1536
H = 16
KVH = 8
HD = 96
KBLK = 512
DOC_MOST = 4096
KVW = 768
GAIN_PAD = 128

EPSILON = 1e-05
ROPE_BASE = 100000.0
MASKED_SCORE = -1e30
ALL = ("ctx", "fsdp")


def rms_scale(values):
    return lax.rsqrt(jnp.mean(values * values, axis=-1, keepdims=True) + EPSILON)


def document_layout(lengths, total):
    starts = jnp.cumsum(lengths) - lengths
    places = jnp.arange(total, dtype=jnp.int32)
    inside = places[:, None] >= starts[None, :]
    doc_ids = jnp.sum(inside.astype(jnp.int32), axis=1) - 1
    doc_starts = jnp.max(jnp.where(inside, starts[None, :], 0), axis=1)
    return (doc_ids, places - doc_starts)


def rotate(values, positions, head_count, direction):
    row_count = values.shape[0]
    half_dim = HD // 2
    inverse_freq = ROPE_BASE ** (-(jnp.arange(half_dim).astype(jnp.float32) * (2.0 / HD)))
    angles = positions.astype(jnp.float32)[:, None] * inverse_freq[None, :]
    cosine = jnp.cos(angles)[:, None, :]
    sine_part = direction * jnp.sin(angles)[:, None, :]
    grouped = values.reshape(row_count, head_count, HD)
    former = grouped[:, :, :half_dim]
    latter = grouped[:, :, half_dim:]
    turned = jnp.concatenate(
        [former * cosine - latter * sine_part, latter * cosine + former * sine_part], axis=2
    )
    return turned.reshape(row_count, head_count * HD)


def outer_rows(left, right):
    return lax.dot_general(
        left, right, (((0,), (0,)), ((), ())), preferred_element_type=jnp.float32
    )


def times_transposed(left, right):
    return lax.dot_general(
        left, right, (((1,), (1,)), ((), ())), preferred_element_type=jnp.float32
    )


def neighbour_barrier(n_ctx, back, c, f):
    barrier = pltpu.get_barrier_semaphore()
    for s in range(1, back + 1):
        for peer in ((c + s) % n_ctx, (c + n_ctx - s) % n_ctx):
            pl.semaphore_signal(barrier, inc=1, device_id=(peer, f), device_id_type=MESH)
    pl.semaphore_wait(barrier, 2 * back)


def kv_share_kernel(n_ctx, back, kv_ref, out_ref, send_sem, recv_sem):
    c = lax.axis_index("ctx")
    f = lax.axis_index("fsdp")
    neighbour_barrier(n_ctx, back, c, f)

    def copy(s, dest):
        return pltpu.make_async_remote_copy(
            src_ref=kv_ref,
            dst_ref=out_ref.at[back - s],
            send_sem=send_sem.at[s - 1],
            recv_sem=recv_sem.at[back - s],
            device_id=(dest, f),
            device_id_type=MESH,
        )

    for s in range(1, back + 1):

        @pl.when(c + s < n_ctx)
        def _():
            copy(s, c + s).start()

    out_ref[back] = kv_ref[...]
    for s in range(1, back + 1):

        @pl.when(c - s < 0)
        def _():
            out_ref[back - s] = jnp.zeros(kv_ref.shape, kv_ref.dtype)

    for s in range(1, back + 1):

        @pl.when(c + s < n_ctx)
        def _():
            copy(s, c + s).wait_send()

        @pl.when(c - s >= 0)
        def _():
            copy(s, c).wait_recv()


def kv_share(kv, n_ctx, back):
    return pl.pallas_call(
        functools.partial(kv_share_kernel, n_ctx, back),
        out_shape=jax.ShapeDtypeStruct((back + 1,) + kv.shape, kv.dtype),
        in_specs=[pl.BlockSpec(memory_space=pltpu.VMEM)],
        out_specs=pl.BlockSpec(memory_space=pltpu.VMEM),
        scratch_shapes=[pltpu.SemaphoreType.DMA((back,)), pltpu.SemaphoreType.DMA((back + 1,))],
        compiler_params=pltpu.CompilerParams(collective_id=0, has_side_effects=True),
    )(kv)


def kv_return_kernel(n_ctx, back, own_ref, g_ref, out_ref, recv_buf, send_sem, recv_sem):
    c = lax.axis_index("ctx")
    f = lax.axis_index("fsdp")
    neighbour_barrier(n_ctx, back, c, f)

    def copy(s, dest):
        return pltpu.make_async_remote_copy(
            src_ref=g_ref.at[back - s],
            dst_ref=recv_buf.at[s - 1],
            send_sem=send_sem.at[s - 1],
            recv_sem=recv_sem.at[s - 1],
            device_id=(dest, f),
            device_id_type=MESH,
        )

    for s in range(1, back + 1):

        @pl.when(c - s >= 0)
        def _():
            copy(s, c - s).start()

    out_ref[...] = own_ref[...]
    for s in range(1, back + 1):

        @pl.when(c + s < n_ctx)
        def _():
            copy(s, c).wait_recv()
            out_ref[...] += recv_buf[s - 1].astype(jnp.float32)

    for s in range(1, back + 1):

        @pl.when(c - s >= 0)
        def _():
            copy(s, c - s).wait_send()


def kv_return(own, g, n_ctx, back):
    return pl.pallas_call(
        functools.partial(kv_return_kernel, n_ctx, back),
        out_shape=jax.ShapeDtypeStruct(own.shape, own.dtype),
        in_specs=[pl.BlockSpec(memory_space=pltpu.VMEM)] * 2,
        out_specs=pl.BlockSpec(memory_space=pltpu.VMEM),
        scratch_shapes=[
            pltpu.VMEM(g.shape, g.dtype),
            pltpu.SemaphoreType.DMA((back,)),
            pltpu.SemaphoreType.DMA((back,)),
        ],
        compiler_params=pltpu.CompilerParams(collective_id=1, has_side_effects=True),
    )(own, g)


def peer_barrier(n_f, c, f):
    barrier = pltpu.get_barrier_semaphore()
    for k in range(1, n_f):
        pl.semaphore_signal(barrier, inc=1, device_id=(c, (f + k) % n_f), device_id_type=MESH)
    pl.semaphore_wait(barrier, n_f - 1)


def group_gather_kernel(n_f, x_ref, out_ref, send_sem, recv_sem):
    c = lax.axis_index("ctx")
    f = lax.axis_index("fsdp")
    peer_barrier(n_f, c, f)
    copies = []
    for k in range(1, n_f):
        copy = pltpu.make_async_remote_copy(
            src_ref=x_ref,
            dst_ref=out_ref.at[f],
            send_sem=send_sem.at[k - 1],
            recv_sem=recv_sem.at[k - 1],
            device_id=(c, (f + k) % n_f),
            device_id_type=MESH,
        )
        copy.start()
        copies.append(copy)
    out_ref[f] = x_ref[...]
    for k in range(1, n_f):
        pltpu.make_async_remote_copy(
            src_ref=x_ref,
            dst_ref=out_ref.at[(f + n_f - k) % n_f],
            send_sem=send_sem.at[k - 1],
            recv_sem=recv_sem.at[k - 1],
            device_id=(c, f),
            device_id_type=MESH,
        ).wait_recv()
    for copy in copies:
        copy.wait_send()


def group_gather(x, n_f):
    return pl.pallas_call(
        functools.partial(group_gather_kernel, n_f),
        out_shape=jax.ShapeDtypeStruct((n_f,) + x.shape, x.dtype),
        in_specs=[pl.BlockSpec(memory_space=pltpu.VMEM)],
        out_specs=pl.BlockSpec(memory_space=pltpu.VMEM),
        scratch_shapes=[pltpu.SemaphoreType.DMA((n_f - 1,)), pltpu.SemaphoreType.DMA((n_f - 1,))],
        compiler_params=pltpu.CompilerParams(collective_id=2, has_side_effects=True),
    )(x)


def group_reduce_kernel(n_f, p_ref, out_ref, recv_buf, send_sem, recv_sem):
    c = lax.axis_index("ctx")
    f = lax.axis_index("fsdp")
    peer_barrier(n_f, c, f)
    copies = []
    for k in range(1, n_f):
        dest = (f + k) % n_f
        copy = pltpu.make_async_remote_copy(
            src_ref=p_ref.at[dest],
            dst_ref=recv_buf.at[k - 1],
            send_sem=send_sem.at[k - 1],
            recv_sem=recv_sem.at[k - 1],
            device_id=(c, dest),
            device_id_type=MESH,
        )
        copy.start()
        copies.append(copy)
    out_ref[...] = p_ref[f]
    for k in range(1, n_f):
        copies[k - 1].wait_recv()
        out_ref[...] += recv_buf[k - 1]
    for copy in copies:
        copy.wait_send()


def group_reduce(p, n_f):
    return pl.pallas_call(
        functools.partial(group_reduce_kernel, n_f),
        out_shape=jax.ShapeDtypeStruct(p.shape[1:], p.dtype),
        in_specs=[pl.BlockSpec(memory_space=pltpu.VMEM)],
        out_specs=pl.BlockSpec(memory_space=pltpu.VMEM),
        scratch_shapes=[
            pltpu.VMEM((n_f - 1,) + p.shape[1:], p.dtype),
            pltpu.SemaphoreType.DMA((n_f - 1,)),
            pltpu.SemaphoreType.DMA((n_f - 1,)),
        ],
        compiler_params=pltpu.CompilerParams(collective_id=3, has_side_effects=True),
    )(p)


def pair_barrier(c, partner, across):
    barrier = pltpu.get_barrier_semaphore()
    pl.semaphore_signal(barrier, inc=1, device_id=(c, partner), device_id_type=MESH)
    pl.semaphore_signal(barrier, inc=1, device_id=(c, across), device_id_type=MESH)
    pl.semaphore_wait(barrier, 2)


def quad_ids():
    c = lax.axis_index("ctx")
    f = lax.axis_index("fsdp")
    partner = f + 1 - 2 * (f % 2)
    across = (f + 2) % 4
    diagonal = (partner + 2) % 4
    return c, f, partner, across, diagonal


def quad_gather_kernel(x_ref, out_ref, send_sem, recv_sem):
    c, f, partner, across, diagonal = quad_ids()
    pair_barrier(c, partner, across)

    def copy(src, slot, dest, k):
        return pltpu.make_async_remote_copy(
            src_ref=src,
            dst_ref=out_ref.at[slot],
            send_sem=send_sem.at[k],
            recv_sem=recv_sem.at[slot],
            device_id=(c, dest),
            device_id_type=MESH,
        )

    first = copy(x_ref, f, across, 0)
    first.start()
    own = copy(x_ref, f, partner, 1)
    own.start()
    out_ref[f] = x_ref[...]
    copy(x_ref, across, f, 0).wait_recv()
    relay = copy(out_ref.at[across], across, partner, 2)
    relay.start()
    copy(x_ref, partner, f, 0).wait_recv()
    copy(x_ref, diagonal, f, 0).wait_recv()
    first.wait_send()
    own.wait_send()
    relay.wait_send()


def quad_gather(x):
    return pl.pallas_call(
        quad_gather_kernel,
        out_shape=jax.ShapeDtypeStruct((4,) + x.shape, x.dtype),
        in_specs=[pl.BlockSpec(memory_space=pltpu.VMEM)],
        out_specs=pl.BlockSpec(memory_space=pltpu.VMEM),
        scratch_shapes=[pltpu.SemaphoreType.DMA((3,)), pltpu.SemaphoreType.DMA((4,))],
        compiler_params=pltpu.CompilerParams(collective_id=4, has_side_effects=True),
    )(x)


def quad_reduce_kernel(p_ref, out_ref, near_buf, far_buf, sum_buf, send_sem, recv_sem):
    c, f, partner, across, diagonal = quad_ids()
    pair_barrier(c, partner, across)

    def copy(src, dst, dest, k):
        return pltpu.make_async_remote_copy(
            src_ref=src,
            dst_ref=dst,
            send_sem=send_sem.at[k],
            recv_sem=recv_sem.at[k],
            device_id=(c, dest),
            device_id_type=MESH,
        )

    to_partner = copy(p_ref.at[partner], near_buf.at[0], partner, 0)
    to_partner.start()
    to_diagonal = copy(p_ref.at[diagonal], near_buf.at[1], partner, 1)
    to_diagonal.start()
    to_partner.wait_recv()
    to_diagonal.wait_recv()
    sum_buf[...] = p_ref[across] + near_buf[1]
    to_across = copy(sum_buf, far_buf, across, 2)
    to_across.start()
    out_ref[...] = p_ref[f] + near_buf[0]
    to_across.wait_recv()
    out_ref[...] += far_buf[...]
    to_partner.wait_send()
    to_diagonal.wait_send()
    to_across.wait_send()


def quad_reduce(p):
    block = p.shape[1:]
    return pl.pallas_call(
        quad_reduce_kernel,
        out_shape=jax.ShapeDtypeStruct(block, p.dtype),
        in_specs=[pl.BlockSpec(memory_space=pltpu.VMEM)],
        out_specs=pl.BlockSpec(memory_space=pltpu.VMEM),
        scratch_shapes=[
            pltpu.VMEM((2,) + block, p.dtype),
            pltpu.VMEM(block, p.dtype),
            pltpu.VMEM(block, p.dtype),
            pltpu.SemaphoreType.DMA((3,)),
            pltpu.SemaphoreType.DMA((3,)),
        ],
        compiler_params=pltpu.CompilerParams(collective_id=5, has_side_effects=True),
    )(p)


def fsdp_gather(x, n_f):
    if n_f == 4:
        return quad_gather(x)
    return group_gather(x, n_f)


def fsdp_reduce(p, n_f):
    if n_f == 4:
        return quad_reduce(p)
    return group_reduce(p, n_f)


def ring_order(n, snake):
    c = lax.axis_index("ctx")
    if snake:
        half = n // 2
        y = c % 2
        z = c // 2
        pos = (1 - y) * z + y * (n - 1 - z)

        def device_at(q):
            q = (q + n) % n
            h = q // half
            return (1 - h) * 2 * q + h * (2 * (n - 1 - q) + 1)

    else:
        pos = c

        def device_at(q):
            return (q + n) % n

    return c, pos, device_at


def ring_reduce_kernel(n, snake, part_ref, out_ref, recv_buf, send_buf, send_sem, recv_sem):
    c, pos, device_at = ring_order(n, snake)
    f = lax.axis_index("fsdp")
    nxt = device_at(pos + 1)
    prv = device_at(pos - 1)
    barrier = pltpu.get_barrier_semaphore()
    pl.semaphore_signal(barrier, inc=1, device_id=(nxt, f), device_id_type=MESH)
    pl.semaphore_signal(barrier, inc=1, device_id=(prv, f), device_id_type=MESH)
    pl.semaphore_wait(barrier, 2)
    width = part_ref.shape[2] // 2
    steps = n - 1
    directions = ((0, 1, nxt), (1, -1, prv))

    def copy(d, s, src, dest):
        return pltpu.make_async_remote_copy(
            src_ref=src,
            dst_ref=recv_buf.at[d, s],
            send_sem=send_sem.at[d, s],
            recv_sem=recv_sem.at[d, s],
            device_id=(dest, f),
            device_id_type=MESH,
        )

    sends = []
    for d, sign, dest in directions:
        cols = pl.ds(d * width, width)
        first = copy(d, 0, part_ref.at[device_at(pos - sign), :, cols], dest)
        first.start()
        sends.append(first)
    for s in range(1, steps):
        for d, sign, dest in directions:
            cols = pl.ds(d * width, width)
            copy(d, s - 1, send_buf.at[d, s], dest).wait_recv()
            block = device_at(pos - sign * (s + 1))
            send_buf[d, s] = (
                recv_buf[d, s - 1].astype(jnp.float32) + part_ref[block, :, cols].astype(jnp.float32)
            ).astype(send_buf.dtype)
            nxt_copy = copy(d, s, send_buf.at[d, s], dest)
            nxt_copy.start()
            sends.append(nxt_copy)
    for d, sign, dest in directions:
        cols = pl.ds(d * width, width)
        copy(d, steps - 1, send_buf.at[d, 0], dest).wait_recv()
        out_ref[:, cols] = recv_buf[d, steps - 1].astype(jnp.float32) + part_ref[c, :, cols].astype(
            jnp.float32
        )
    for s_copy in sends:
        s_copy.wait_send()


def ring_reduce(part, n, snake):
    _, rows_, cols_ = part.shape
    return pl.pallas_call(
        functools.partial(ring_reduce_kernel, n, snake),
        out_shape=jax.ShapeDtypeStruct((rows_, cols_), jnp.float32),
        in_specs=[pl.BlockSpec(memory_space=pltpu.VMEM)],
        out_specs=pl.BlockSpec(memory_space=pltpu.VMEM),
        scratch_shapes=[
            pltpu.VMEM((2, n - 1, rows_, cols_ // 2), part.dtype),
            pltpu.VMEM((2, n - 1, rows_, cols_ // 2), part.dtype),
            pltpu.SemaphoreType.DMA((2, n - 1)),
            pltpu.SemaphoreType.DMA((2, n - 1)),
        ],
        compiler_params=pltpu.CompilerParams(
            collective_id=6, has_side_effects=True, vmem_limit_bytes=100 * 1024 * 1024 // 2
        ),
    )(part)


def body(
    snake,
    tokens,
    doc_lengths,
    attention_gain,
    query_weight,
    key_weight,
    value_weight,
    output_weight,
    feedforward_gain,
    gate_weight,
    up_weight,
    down_weight,
    cotangent,
):
    n_dev = lax.axis_size(ALL)
    rows = query_weight.shape[0]
    ff_rows = down_weight.shape[0]
    ff = gate_weight.shape[1]
    local_tokens = tokens[0].astype(jnp.float32)
    tok_rows = local_tokens.shape[0]
    stream_len = tok_rows * lax.axis_size("ctx")
    my_first = lax.axis_index("ctx") * tok_rows

    gain_cols = jnp.pad(
        jnp.stack([attention_gain, feedforward_gain], axis=1), ((0, 0), (0, GAIN_PAD - 2))
    )
    att_full = lax.all_gather(
        jnp.concatenate([query_weight, key_weight, value_weight, output_weight, gain_cols], axis=1),
        ALL,
        axis=0,
        tiled=True,
    )
    c_k = D
    c_v = D + KVW
    c_o = D + 2 * KVW
    c_g = 2 * D + 2 * KVW
    query_full = att_full[:, :c_k]
    key_full = att_full[:, c_k:c_v]
    value_full = att_full[:, c_v:c_o]
    qkv_full = att_full[:, :c_o]
    output_full = att_full[:, c_o:c_g]
    gain_one_f = att_full[:, c_g].astype(jnp.float32)
    gain_two_f = att_full[:, c_g + 1].astype(jnp.float32)

    key_docs_all, places_all = document_layout(doc_lengths[0], stream_len)
    query_docs = lax.dynamic_slice_in_dim(key_docs_all, my_first, tok_rows, 0)
    query_positions = lax.dynamic_slice_in_dim(places_all, my_first, tok_rows, 0)
    query_places = my_first + jnp.arange(tok_rows, dtype=jnp.int32)
    group_size = H // KVH
    score_scale = HD ** (-0.5)

    scale_one = rms_scale(local_tokens)
    normed_one = local_tokens * scale_one
    normed_low = (normed_one * gain_one_f).astype(jnp.bfloat16)
    qkv = jnp.dot(normed_low, qkv_full, preferred_element_type=jnp.float32)
    queries = qkv[:, :D]
    keys_new = qkv[:, D : D + KVW]
    values_new = qkv[:, D + KVW :]
    query_low = rotate(queries, query_positions, H, 1.0).astype(jnp.bfloat16)
    key_low = rotate(keys_new, query_positions, KVH, 1.0).astype(jnp.bfloat16)
    value_low = values_new.astype(jnp.bfloat16)

    n_ctx = lax.axis_size("ctx")
    n_f = lax.axis_size("fsdp")
    chunk = ff_rows
    units = n_ctx * chunk
    gu_parts = jnp.transpose(
        jnp.stack([gate_weight, up_weight], axis=1).reshape(rows, 2, n_ctx, n_f, chunk),
        (3, 0, 1, 2, 4),
    )
    gu_parts = lax.all_to_all(gu_parts, "fsdp", 0, 0, tiled=True).reshape(n_f * rows, 2 * units)
    down_rows = D // (2 * n_ctx)
    ff_pack = jnp.concatenate([gu_parts, down_weight.reshape(down_rows, 2 * units)], axis=0)
    ff_pack = ff_pack.at[0, 0].add(att_full[0, 0] * 0)
    ff_stack = lax.all_gather(
        ff_pack,
        "ctx",
        axis=0,
        tiled=False,
    )
    gate_up_tp = ff_stack[:, : n_f * rows].reshape(n_ctx * n_f * rows, 2 * units)
    down_tp = ff_stack[:, n_f * rows :].reshape(n_ctx, ff_rows, D).reshape(units, D)
    max_doc = min(DOC_MOST, KBLK * (stream_len // (2 * KBLK)))
    back = min(-(-(max_doc - 1) // tok_rows), n_ctx - 1)
    win = (back + 1) * tok_rows
    kv_win = kv_share(
        jnp.concatenate([key_low, value_low], axis=1), n_ctx, back
    ).reshape(win, 2 * KVW)
    docs_pad = jnp.concatenate(
        [jnp.full((back * tok_rows,), -1, jnp.int32), key_docs_all.astype(jnp.int32)]
    )
    key_docs = lax.dynamic_slice_in_dim(docs_pad, my_first, win, 0)
    key_places = my_first - back * tok_rows + jnp.arange(win, dtype=jnp.int32)
    key_block = kv_win[:, :KVW].reshape(win, KVH, HD)
    value_block = kv_win[:, KVW:].reshape(win, KVH, HD)
    query_grouped = query_low.reshape(tok_rows, KVH, group_size, HD)
    allowed = (
        (key_docs[None, :] == query_docs[:, None]) & (key_places[None, :] <= query_places[:, None])
    )[:, None, None, :]
    scores = (
        jnp.einsum("qgrd,kgd->qgrk", query_grouped, key_block, preferred_element_type=jnp.float32)
        * score_scale
    )
    scores = jnp.where(allowed, scores, MASKED_SCORE)
    row_max = jnp.max(scores, axis=-1, keepdims=True)
    exponent = jnp.where(allowed, jnp.exp(scores - row_max), 0.0)
    probs = exponent / jnp.sum(exponent, axis=-1, keepdims=True)
    probs_low = probs.astype(jnp.bfloat16)
    attended_sum = jnp.einsum(
        "qgrk,kgd->qgrd", probs_low, value_block, preferred_element_type=jnp.float32
    )
    attended_low = attended_sum.reshape(tok_rows, D).astype(jnp.bfloat16)
    middle = local_tokens + jnp.dot(attended_low, output_full, preferred_element_type=jnp.float32)

    scale_two = rms_scale(middle)
    normed_two = middle * scale_two
    normed_two_low = (normed_two * gain_two_f).astype(jnp.bfloat16)
    group_tokens = n_f * tok_rows
    xn2_all = fsdp_gather(normed_two_low, n_f).reshape(group_tokens, D)
    gate_up = jnp.dot(xn2_all, gate_up_tp, preferred_element_type=jnp.float32)
    gate_pre = gate_up[:, :units]
    up_pre = gate_up[:, units:]
    sigmoid = jax.nn.sigmoid(gate_pre)
    hidden_low = (gate_pre * sigmoid * up_pre).astype(jnp.bfloat16)
    ff_part = jnp.dot(hidden_low, down_tp, preferred_element_type=jnp.float32)
    layer_out = middle + fsdp_reduce(ff_part.reshape(n_f, tok_rows, D), n_f)

    grad_out = cotangent[0]
    grad_all = fsdp_gather(grad_out, n_f).reshape(group_tokens, D)
    down_term = outer_rows(hidden_low, grad_all).astype(jnp.bfloat16)
    hidden_grad = times_transposed(grad_all, down_tp)
    gate_grad = (hidden_grad * up_pre * sigmoid * (1.0 + gate_pre * (1.0 - sigmoid))).astype(
        jnp.bfloat16
    )
    up_grad = (hidden_grad * gate_pre * sigmoid).astype(jnp.bfloat16)
    gate_up_cat = jnp.concatenate([gate_grad, up_grad], axis=1)
    gate_up_term = outer_rows(xn2_all, gate_up_cat)
    grad_pack = jnp.concatenate(
        [
            gate_up_term.astype(jnp.bfloat16).reshape(n_ctx, n_f * rows, 2 * units),
            down_term.reshape(n_ctx, down_rows, 2 * units),
        ],
        axis=1,
    )
    normed_two_grad = fsdp_reduce(
        times_transposed(gate_up_cat, gate_up_tp).reshape(n_f, tok_rows, D), n_f
    )
    gain_two_term = jnp.sum(normed_two_grad * normed_two, axis=0)
    scaled_two = normed_two_grad * gain_two_f
    middle_grad = grad_out.astype(jnp.float32) + scale_two * (
        scaled_two - normed_two * jnp.mean(scaled_two * normed_two, axis=-1, keepdims=True)
    )
    branch_grad = middle_grad.astype(jnp.bfloat16)
    attended_grad_low = (
        times_transposed(branch_grad, output_full)
        .astype(jnp.bfloat16)
        .reshape(tok_rows, KVH, group_size, HD)
    )
    row_delta = jnp.sum(
        attended_grad_low.astype(jnp.float32) * attended_sum, axis=-1, keepdims=True
    )
    prob_grad = jnp.einsum(
        "qgrd,kgd->qgrk", attended_grad_low, value_block, preferred_element_type=jnp.float32
    )
    score_grad = (probs * (prob_grad - row_delta)).astype(jnp.bfloat16)
    query_accum = jnp.einsum(
        "qgrk,kgd->qgrd", score_grad, key_block, preferred_element_type=jnp.float32
    )
    key_term = jnp.einsum(
        "qgrk,qgrd->kgd", score_grad, query_grouped, preferred_element_type=jnp.float32
    ).reshape(win, KVW)
    value_term = jnp.einsum(
        "qgrk,qgrd->kgd", probs_low, attended_grad_low, preferred_element_type=jnp.float32
    ).reshape(win, KVW)
    kv_term = jnp.concatenate([key_term, value_term], axis=1).reshape(back + 1, tok_rows, 2 * KVW)
    query_grad_low = rotate(
        query_accum.reshape(tok_rows, D) * score_scale, query_positions, H, -1.0
    ).astype(jnp.bfloat16)
    first_pack = jnp.concatenate(
        [
            outer_rows(normed_low, query_grad_low).astype(jnp.bfloat16),
            outer_rows(attended_low, branch_grad).astype(jnp.bfloat16),
        ],
        axis=1,
    )
    first_pack, grad_pack = lax.optimization_barrier((first_pack, grad_pack))
    first_sum = lax.psum_scatter(first_pack, ALL, scatter_dimension=0, tiled=True).astype(jnp.float32)
    grad_sum = ring_reduce(grad_pack, n_ctx, snake).astype(jnp.bfloat16)
    down_sum = grad_sum[n_f * rows :].reshape(ff_rows, D)
    gu_sum = lax.all_to_all(grad_sum[: n_f * rows].reshape(n_f, rows, 2 * units), "fsdp", 0, 0, tiled=True)
    ff_sum = jnp.transpose(
        gu_sum.reshape(n_f, rows, 2, n_ctx, chunk), (1, 2, 3, 0, 4)
    ).reshape(rows, 2 * ff)
    kv_own = kv_term[back].at[0, 0].add(
        (grad_sum[0, 0].astype(jnp.float32) + first_sum[0, 0]) * 0.0
    )
    kv_sum = kv_return(kv_own, kv_term[:back].astype(jnp.bfloat16), n_ctx, back)
    key_grad_low = rotate(kv_sum[:, :KVW] * score_scale, query_positions, KVH, -1.0).astype(
        jnp.bfloat16
    )
    value_grad_low = kv_sum[:, KVW:].astype(jnp.bfloat16)
    kv_grad_cat = jnp.concatenate([key_grad_low, value_grad_low], axis=1)
    projection_cat = jnp.concatenate([query_grad_low, kv_grad_cat], axis=1)
    normed_grad = times_transposed(projection_cat, qkv_full)
    gain_one_term = jnp.sum(normed_grad * normed_one, axis=0)
    scaled_one = normed_grad * gain_one_f
    tokens_grad = middle_grad + scale_one * (
        scaled_one - normed_one * jnp.mean(scaled_one * normed_one, axis=-1, keepdims=True)
    )
    gain_term_cols = jnp.pad(
        jnp.stack([gain_one_term, gain_two_term], axis=1), ((0, 0), (0, GAIN_PAD - 2))
    )
    second_sum = lax.psum_scatter(
        jnp.concatenate(
            [
                outer_rows(normed_low, kv_grad_cat).astype(jnp.bfloat16),
                gain_term_cols.astype(jnp.bfloat16),
            ],
            axis=1,
        ),
        ALL,
        scatter_dimension=0,
        tiled=True,
    ).astype(jnp.float32)
    ff_sum = ff_sum.astype(jnp.float32)
    return (
        layer_out.astype(jnp.bfloat16)[None],
        tokens_grad[None],
        second_sum[:, 2 * KVW],
        first_sum[:, :D],
        second_sum[:, :KVW],
        second_sum[:, KVW : 2 * KVW],
        first_sum[:, D:],
        second_sum[:, 2 * KVW + 1],
        ff_sum[:, :ff],
        ff_sum[:, ff : 2 * ff],
        down_sum.astype(jnp.float32),
    )


def snake_ring(mesh):
    column = mesh.devices[:, 0]
    n = column.shape[0]
    if n % 2 or n < 4:
        return False
    return all(
        tuple(d.coords)[2] == i // 2 and tuple(d.coords)[1] == i % 2 for i, d in enumerate(column)
    )


def solution(mesh):
    weight = P(ALL, None)
    stream = P("fsdp", "ctx", None)
    return jax.shard_map(
        functools.partial(body, snake_ring(mesh)),
        mesh=mesh,
        in_specs=(
            stream,
            P("fsdp", None),
            P(ALL),
            weight,
            weight,
            weight,
            weight,
            P(ALL),
            weight,
            weight,
            weight,
            stream,
        ),
        out_specs=(
            stream,
            stream,
            P(ALL),
            weight,
            weight,
            weight,
            weight,
            P(ALL),
            weight,
            weight,
            weight,
        ),
        check_vma=False,
    )
```

```python
import functools

import jax
import jax.numpy as jnp
from jax import lax
from jax.experimental import pallas as pl
from jax.experimental.pallas import tpu as pltpu
from jax.sharding import PartitionSpec as P

MESH = pl.DeviceIdType.MESH

D = 1536
H = 16
KVH = 8
HD = 96
KBLK = 512
DOC_MOST = 4096
KVW = 768
GAIN_PAD = 128

EPSILON = 1e-05
ROPE_BASE = 100000.0
MASKED_SCORE = -1e30
ALL = ("ctx", "fsdp")


def rms_scale(values):
    return lax.rsqrt(jnp.mean(values * values, axis=-1, keepdims=True) + EPSILON)


def document_layout(lengths, total):
    starts = jnp.cumsum(lengths) - lengths
    places = jnp.arange(total, dtype=jnp.int32)
    inside = places[:, None] >= starts[None, :]
    doc_ids = jnp.sum(inside.astype(jnp.int32), axis=1) - 1
    doc_starts = jnp.max(jnp.where(inside, starts[None, :], 0), axis=1)
    return (doc_ids, places - doc_starts)


def rotate(values, positions, head_count, direction):
    row_count = values.shape[0]
    half_dim = HD // 2
    inverse_freq = ROPE_BASE ** (-(jnp.arange(half_dim).astype(jnp.float32) * (2.0 / HD)))
    angles = positions.astype(jnp.float32)[:, None] * inverse_freq[None, :]
    cosine = jnp.cos(angles)[:, None, :]
    sine_part = direction * jnp.sin(angles)[:, None, :]
    grouped = values.reshape(row_count, head_count, HD)
    former = grouped[:, :, :half_dim]
    latter = grouped[:, :, half_dim:]
    turned = jnp.concatenate(
        [former * cosine - latter * sine_part, latter * cosine + former * sine_part], axis=2
    )
    return turned.reshape(row_count, head_count * HD)


def outer_rows(left, right):
    return lax.dot_general(
        left, right, (((0,), (0,)), ((), ())), preferred_element_type=jnp.float32
    )


def times_transposed(left, right):
    return lax.dot_general(
        left, right, (((1,), (1,)), ((), ())), preferred_element_type=jnp.float32
    )


def neighbour_barrier(n_ctx, back, c, f):
    barrier = pltpu.get_barrier_semaphore()
    for s in range(1, back + 1):
        for peer in ((c + s) % n_ctx, (c + n_ctx - s) % n_ctx):
            pl.semaphore_signal(barrier, inc=1, device_id=(peer, f), device_id_type=MESH)
    pl.semaphore_wait(barrier, 2 * back)


def kv_share_kernel(n_ctx, back, kv_ref, out_ref, send_sem, recv_sem):
    c = lax.axis_index("ctx")
    f = lax.axis_index("fsdp")
    neighbour_barrier(n_ctx, back, c, f)

    def copy(s, dest):
        return pltpu.make_async_remote_copy(
            src_ref=kv_ref,
            dst_ref=out_ref.at[back - s],
            send_sem=send_sem.at[s - 1],
            recv_sem=recv_sem.at[back - s],
            device_id=(dest, f),
            device_id_type=MESH,
        )

    for s in range(1, back + 1):

        @pl.when(c + s < n_ctx)
        def _():
            copy(s, c + s).start()

    out_ref[back] = kv_ref[...]
    for s in range(1, back + 1):

        @pl.when(c - s < 0)
        def _():
            out_ref[back - s] = jnp.zeros(kv_ref.shape, kv_ref.dtype)

    for s in range(1, back + 1):

        @pl.when(c + s < n_ctx)
        def _():
            copy(s, c + s).wait_send()

        @pl.when(c - s >= 0)
        def _():
            copy(s, c).wait_recv()


def kv_share(kv, n_ctx, back):
    return pl.pallas_call(
        functools.partial(kv_share_kernel, n_ctx, back),
        out_shape=jax.ShapeDtypeStruct((back + 1,) + kv.shape, kv.dtype),
        in_specs=[pl.BlockSpec(memory_space=pltpu.VMEM)],
        out_specs=pl.BlockSpec(memory_space=pltpu.VMEM),
        scratch_shapes=[pltpu.SemaphoreType.DMA((back,)), pltpu.SemaphoreType.DMA((back + 1,))],
        compiler_params=pltpu.CompilerParams(collective_id=0, has_side_effects=True),
    )(kv)


def kv_return_kernel(n_ctx, back, own_ref, g_ref, out_ref, recv_buf, send_sem, recv_sem):
    c = lax.axis_index("ctx")
    f = lax.axis_index("fsdp")
    neighbour_barrier(n_ctx, back, c, f)

    def copy(s, dest):
        return pltpu.make_async_remote_copy(
            src_ref=g_ref.at[back - s],
            dst_ref=recv_buf.at[s - 1],
            send_sem=send_sem.at[s - 1],
            recv_sem=recv_sem.at[s - 1],
            device_id=(dest, f),
            device_id_type=MESH,
        )

    for s in range(1, back + 1):

        @pl.when(c - s >= 0)
        def _():
            copy(s, c - s).start()

    out_ref[...] = own_ref[...]
    for s in range(1, back + 1):

        @pl.when(c + s < n_ctx)
        def _():
            copy(s, c).wait_recv()
            out_ref[...] += recv_buf[s - 1].astype(jnp.float32)

    for s in range(1, back + 1):

        @pl.when(c - s >= 0)
        def _():
            copy(s, c - s).wait_send()


def kv_return(own, g, n_ctx, back):
    return pl.pallas_call(
        functools.partial(kv_return_kernel, n_ctx, back),
        out_shape=jax.ShapeDtypeStruct(own.shape, own.dtype),
        in_specs=[pl.BlockSpec(memory_space=pltpu.VMEM)] * 2,
        out_specs=pl.BlockSpec(memory_space=pltpu.VMEM),
        scratch_shapes=[
            pltpu.VMEM(g.shape, g.dtype),
            pltpu.SemaphoreType.DMA((back,)),
            pltpu.SemaphoreType.DMA((back,)),
        ],
        compiler_params=pltpu.CompilerParams(collective_id=1, has_side_effects=True),
    )(own, g)


def peer_barrier(n_f, c, f):
    barrier = pltpu.get_barrier_semaphore()
    for k in range(1, n_f):
        pl.semaphore_signal(barrier, inc=1, device_id=(c, (f + k) % n_f), device_id_type=MESH)
    pl.semaphore_wait(barrier, n_f - 1)


def group_gather_kernel(n_f, x_ref, out_ref, send_sem, recv_sem):
    c = lax.axis_index("ctx")
    f = lax.axis_index("fsdp")
    peer_barrier(n_f, c, f)
    copies = []
    for k in range(1, n_f):
        copy = pltpu.make_async_remote_copy(
            src_ref=x_ref,
            dst_ref=out_ref.at[f],
            send_sem=send_sem.at[k - 1],
            recv_sem=recv_sem.at[k - 1],
            device_id=(c, (f + k) % n_f),
            device_id_type=MESH,
        )
        copy.start()
        copies.append(copy)
    out_ref[f] = x_ref[...]
    for k in range(1, n_f):
        pltpu.make_async_remote_copy(
            src_ref=x_ref,
            dst_ref=out_ref.at[(f + n_f - k) % n_f],
            send_sem=send_sem.at[k - 1],
            recv_sem=recv_sem.at[k - 1],
            device_id=(c, f),
            device_id_type=MESH,
        ).wait_recv()
    for copy in copies:
        copy.wait_send()


def group_gather(x, n_f):
    return pl.pallas_call(
        functools.partial(group_gather_kernel, n_f),
        out_shape=jax.ShapeDtypeStruct((n_f,) + x.shape, x.dtype),
        in_specs=[pl.BlockSpec(memory_space=pltpu.VMEM)],
        out_specs=pl.BlockSpec(memory_space=pltpu.VMEM),
        scratch_shapes=[pltpu.SemaphoreType.DMA((n_f - 1,)), pltpu.SemaphoreType.DMA((n_f - 1,))],
        compiler_params=pltpu.CompilerParams(collective_id=2, has_side_effects=True),
    )(x)


def group_reduce_kernel(n_f, p_ref, out_ref, recv_buf, send_sem, recv_sem):
    c = lax.axis_index("ctx")
    f = lax.axis_index("fsdp")
    peer_barrier(n_f, c, f)
    copies = []
    for k in range(1, n_f):
        dest = (f + k) % n_f
        copy = pltpu.make_async_remote_copy(
            src_ref=p_ref.at[dest],
            dst_ref=recv_buf.at[k - 1],
            send_sem=send_sem.at[k - 1],
            recv_sem=recv_sem.at[k - 1],
            device_id=(c, dest),
            device_id_type=MESH,
        )
        copy.start()
        copies.append(copy)
    out_ref[...] = p_ref[f]
    for k in range(1, n_f):
        copies[k - 1].wait_recv()
        out_ref[...] += recv_buf[k - 1]
    for copy in copies:
        copy.wait_send()


def group_reduce(p, n_f):
    return pl.pallas_call(
        functools.partial(group_reduce_kernel, n_f),
        out_shape=jax.ShapeDtypeStruct(p.shape[1:], p.dtype),
        in_specs=[pl.BlockSpec(memory_space=pltpu.VMEM)],
        out_specs=pl.BlockSpec(memory_space=pltpu.VMEM),
        scratch_shapes=[
            pltpu.VMEM((n_f - 1,) + p.shape[1:], p.dtype),
            pltpu.SemaphoreType.DMA((n_f - 1,)),
            pltpu.SemaphoreType.DMA((n_f - 1,)),
        ],
        compiler_params=pltpu.CompilerParams(collective_id=3, has_side_effects=True),
    )(p)


def pair_barrier(c, partner, across):
    barrier = pltpu.get_barrier_semaphore()
    pl.semaphore_signal(barrier, inc=1, device_id=(c, partner), device_id_type=MESH)
    pl.semaphore_signal(barrier, inc=1, device_id=(c, across), device_id_type=MESH)
    pl.semaphore_wait(barrier, 2)


def quad_ids():
    c = lax.axis_index("ctx")
    f = lax.axis_index("fsdp")
    partner = f + 1 - 2 * (f % 2)
    across = (f + 2) % 4
    diagonal = (partner + 2) % 4
    return c, f, partner, across, diagonal


def quad_gather_kernel(x_ref, out_ref, send_sem, recv_sem):
    c, f, partner, across, diagonal = quad_ids()
    pair_barrier(c, partner, across)

    def copy(src, slot, dest, k):
        return pltpu.make_async_remote_copy(
            src_ref=src,
            dst_ref=out_ref.at[slot],
            send_sem=send_sem.at[k],
            recv_sem=recv_sem.at[slot],
            device_id=(c, dest),
            device_id_type=MESH,
        )

    first = copy(x_ref, f, across, 0)
    first.start()
    own = copy(x_ref, f, partner, 1)
    own.start()
    out_ref[f] = x_ref[...]
    copy(x_ref, across, f, 0).wait_recv()
    relay = copy(out_ref.at[across], across, partner, 2)
    relay.start()
    copy(x_ref, partner, f, 0).wait_recv()
    copy(x_ref, diagonal, f, 0).wait_recv()
    first.wait_send()
    own.wait_send()
    relay.wait_send()


def quad_gather(x):
    return pl.pallas_call(
        quad_gather_kernel,
        out_shape=jax.ShapeDtypeStruct((4,) + x.shape, x.dtype),
        in_specs=[pl.BlockSpec(memory_space=pltpu.VMEM)],
        out_specs=pl.BlockSpec(memory_space=pltpu.VMEM),
        scratch_shapes=[pltpu.SemaphoreType.DMA((3,)), pltpu.SemaphoreType.DMA((4,))],
        compiler_params=pltpu.CompilerParams(collective_id=4, has_side_effects=True),
    )(x)


def quad_reduce_kernel(p_ref, out_ref, near_buf, far_buf, sum_buf, send_sem, recv_sem):
    c, f, partner, across, diagonal = quad_ids()
    pair_barrier(c, partner, across)

    def copy(src, dst, dest, k):
        return pltpu.make_async_remote_copy(
            src_ref=src,
            dst_ref=dst,
            send_sem=send_sem.at[k],
            recv_sem=recv_sem.at[k],
            device_id=(c, dest),
            device_id_type=MESH,
        )

    to_partner = copy(p_ref.at[partner], near_buf.at[0], partner, 0)
    to_partner.start()
    to_diagonal = copy(p_ref.at[diagonal], near_buf.at[1], partner, 1)
    to_diagonal.start()
    to_partner.wait_recv()
    to_diagonal.wait_recv()
    sum_buf[...] = p_ref[across] + near_buf[1]
    to_across = copy(sum_buf, far_buf, across, 2)
    to_across.start()
    out_ref[...] = p_ref[f] + near_buf[0]
    to_across.wait_recv()
    out_ref[...] += far_buf[...]
    to_partner.wait_send()
    to_diagonal.wait_send()
    to_across.wait_send()


def quad_reduce(p):
    block = p.shape[1:]
    return pl.pallas_call(
        quad_reduce_kernel,
        out_shape=jax.ShapeDtypeStruct(block, p.dtype),
        in_specs=[pl.BlockSpec(memory_space=pltpu.VMEM)],
        out_specs=pl.BlockSpec(memory_space=pltpu.VMEM),
        scratch_shapes=[
            pltpu.VMEM((2,) + block, p.dtype),
            pltpu.VMEM(block, p.dtype),
            pltpu.VMEM(block, p.dtype),
            pltpu.SemaphoreType.DMA((3,)),
            pltpu.SemaphoreType.DMA((3,)),
        ],
        compiler_params=pltpu.CompilerParams(collective_id=5, has_side_effects=True),
    )(p)


def fsdp_gather(x, n_f):
    if n_f == 4:
        return quad_gather(x)
    return group_gather(x, n_f)


def fsdp_reduce(p, n_f):
    if n_f == 4:
        return quad_reduce(p)
    return group_reduce(p, n_f)


def body(
    tokens,
    doc_lengths,
    attention_gain,
    query_weight,
    key_weight,
    value_weight,
    output_weight,
    feedforward_gain,
    gate_weight,
    up_weight,
    down_weight,
    cotangent,
):
    n_dev = lax.axis_size(ALL)
    rows = query_weight.shape[0]
    ff_rows = down_weight.shape[0]
    ff = gate_weight.shape[1]
    local_tokens = tokens[0].astype(jnp.float32)
    tok_rows = local_tokens.shape[0]
    stream_len = tok_rows * lax.axis_size("ctx")
    my_first = lax.axis_index("ctx") * tok_rows

    gain_cols = jnp.pad(
        jnp.stack([attention_gain, feedforward_gain], axis=1), ((0, 0), (0, GAIN_PAD - 2))
    )
    att_full = lax.all_gather(
        jnp.concatenate([query_weight, key_weight, value_weight, output_weight, gain_cols], axis=1),
        ALL,
        axis=0,
        tiled=True,
    )
    c_k = D
    c_v = D + KVW
    c_o = D + 2 * KVW
    c_g = 2 * D + 2 * KVW
    query_full = att_full[:, :c_k]
    key_full = att_full[:, c_k:c_v]
    value_full = att_full[:, c_v:c_o]
    qkv_full = att_full[:, :c_o]
    output_full = att_full[:, c_o:c_g]
    gain_one_f = att_full[:, c_g].astype(jnp.float32)
    gain_two_f = att_full[:, c_g + 1].astype(jnp.float32)

    key_docs_all, places_all = document_layout(doc_lengths[0], stream_len)
    query_docs = lax.dynamic_slice_in_dim(key_docs_all, my_first, tok_rows, 0)
    query_positions = lax.dynamic_slice_in_dim(places_all, my_first, tok_rows, 0)
    query_places = my_first + jnp.arange(tok_rows, dtype=jnp.int32)
    group_size = H // KVH
    score_scale = HD ** (-0.5)

    scale_one = rms_scale(local_tokens)
    normed_one = local_tokens * scale_one
    normed_low = (normed_one * gain_one_f).astype(jnp.bfloat16)
    qkv = jnp.dot(normed_low, qkv_full, preferred_element_type=jnp.float32)
    queries = qkv[:, :D]
    keys_new = qkv[:, D : D + KVW]
    values_new = qkv[:, D + KVW :]
    query_low = rotate(queries, query_positions, H, 1.0).astype(jnp.bfloat16)
    key_low = rotate(keys_new, query_positions, KVH, 1.0).astype(jnp.bfloat16)
    value_low = values_new.astype(jnp.bfloat16)

    n_ctx = lax.axis_size("ctx")
    n_f = lax.axis_size("fsdp")
    chunk = ff_rows
    units = n_ctx * chunk
    gu_parts = jnp.transpose(
        jnp.stack([gate_weight, up_weight], axis=1).reshape(rows, 2, n_ctx, n_f, chunk),
        (3, 0, 1, 2, 4),
    )
    gu_parts = lax.all_to_all(gu_parts, "fsdp", 0, 0, tiled=True).reshape(n_f * rows, 2 * units)
    down_rows = D // (2 * n_ctx)
    ff_pack = jnp.concatenate([gu_parts, down_weight.reshape(down_rows, 2 * units)], axis=0)
    ff_pack = ff_pack.at[0, 0].add(att_full[0, 0] * 0)
    ff_stack = lax.all_gather(
        ff_pack,
        "ctx",
        axis=0,
        tiled=False,
    )
    gate_up_tp = ff_stack[:, : n_f * rows].reshape(n_ctx * n_f * rows, 2 * units)
    down_tp = ff_stack[:, n_f * rows :].reshape(n_ctx, ff_rows, D).reshape(units, D)
    max_doc = min(DOC_MOST, KBLK * (stream_len // (2 * KBLK)))
    back = min(-(-(max_doc - 1) // tok_rows), n_ctx - 1)
    win = (back + 1) * tok_rows
    kv_win = kv_share(
        jnp.concatenate([key_low, value_low], axis=1), n_ctx, back
    ).reshape(win, 2 * KVW)
    docs_pad = jnp.concatenate(
        [jnp.full((back * tok_rows,), -1, jnp.int32), key_docs_all.astype(jnp.int32)]
    )
    key_docs = lax.dynamic_slice_in_dim(docs_pad, my_first, win, 0)
    key_places = my_first - back * tok_rows + jnp.arange(win, dtype=jnp.int32)
    key_block = kv_win[:, :KVW].reshape(win, KVH, HD)
    value_block = kv_win[:, KVW:].reshape(win, KVH, HD)
    query_grouped = query_low.reshape(tok_rows, KVH, group_size, HD)
    allowed = (
        (key_docs[None, :] == query_docs[:, None]) & (key_places[None, :] <= query_places[:, None])
    )[:, None, None, :]
    scores = (
        jnp.einsum("qgrd,kgd->qgrk", query_grouped, key_block, preferred_element_type=jnp.float32)
        * score_scale
    )
    scores = jnp.where(allowed, scores, MASKED_SCORE)
    row_max = jnp.max(scores, axis=-1, keepdims=True)
    exponent = jnp.where(allowed, jnp.exp(scores - row_max), 0.0)
    probs = exponent / jnp.sum(exponent, axis=-1, keepdims=True)
    probs_low = probs.astype(jnp.bfloat16)
    attended_sum = jnp.einsum(
        "qgrk,kgd->qgrd", probs_low, value_block, preferred_element_type=jnp.float32
    )
    attended_low = attended_sum.reshape(tok_rows, D).astype(jnp.bfloat16)
    middle = local_tokens + jnp.dot(attended_low, output_full, preferred_element_type=jnp.float32)

    scale_two = rms_scale(middle)
    normed_two = middle * scale_two
    normed_two_low = (normed_two * gain_two_f).astype(jnp.bfloat16)
    group_tokens = n_f * tok_rows
    xn2_all = fsdp_gather(normed_two_low, n_f).reshape(group_tokens, D)
    gate_up = jnp.dot(xn2_all, gate_up_tp, preferred_element_type=jnp.float32)
    gate_pre = gate_up[:, :units]
    up_pre = gate_up[:, units:]
    sigmoid = jax.nn.sigmoid(gate_pre)
    hidden_low = (gate_pre * sigmoid * up_pre).astype(jnp.bfloat16)
    ff_part = jnp.dot(hidden_low, down_tp, preferred_element_type=jnp.float32)

    grad_out = cotangent[0]
    grad_all = fsdp_gather(grad_out, n_f).reshape(group_tokens, D)
    down_sum = lax.psum_scatter(
        outer_rows(hidden_low, grad_all).astype(jnp.bfloat16), "ctx", scatter_dimension=0, tiled=True
    )
    hidden_grad = times_transposed(grad_all, down_tp)
    gate_grad = (hidden_grad * up_pre * sigmoid * (1.0 + gate_pre * (1.0 - sigmoid))).astype(
        jnp.bfloat16
    )
    up_grad = (hidden_grad * gate_pre * sigmoid).astype(jnp.bfloat16)
    gate_up_cat = jnp.concatenate([gate_grad, up_grad], axis=1)
    gate_up_term = outer_rows(xn2_all, gate_up_cat)
    ff_pack, gate_up_cat = lax.optimization_barrier((gate_up_term.astype(jnp.bfloat16), gate_up_cat))
    gu_sum = lax.psum_scatter(ff_pack, "ctx", scatter_dimension=0, tiled=True)
    gu_sum = lax.all_to_all(gu_sum.reshape(n_f, rows, 2 * units), "fsdp", 0, 0, tiled=True)
    ff_sum = jnp.transpose(
        gu_sum.reshape(n_f, rows, 2, n_ctx, chunk), (1, 2, 3, 0, 4)
    ).reshape(rows, 2 * ff)
    normed_two_grad = fsdp_reduce(
        times_transposed(gate_up_cat, gate_up_tp).reshape(n_f, tok_rows, D), n_f
    )
    gain_two_term = jnp.sum(normed_two_grad * normed_two, axis=0)
    scaled_two = normed_two_grad * gain_two_f
    middle_grad = grad_out.astype(jnp.float32) + scale_two * (
        scaled_two - normed_two * jnp.mean(scaled_two * normed_two, axis=-1, keepdims=True)
    )
    branch_grad = middle_grad.astype(jnp.bfloat16)
    attended_grad_low = (
        times_transposed(branch_grad, output_full)
        .astype(jnp.bfloat16)
        .reshape(tok_rows, KVH, group_size, HD)
    )
    row_delta = jnp.sum(
        attended_grad_low.astype(jnp.float32) * attended_sum, axis=-1, keepdims=True
    )
    prob_grad = jnp.einsum(
        "qgrd,kgd->qgrk", attended_grad_low, value_block, preferred_element_type=jnp.float32
    )
    score_grad = (probs * (prob_grad - row_delta)).astype(jnp.bfloat16)
    query_accum = jnp.einsum(
        "qgrk,kgd->qgrd", score_grad, key_block, preferred_element_type=jnp.float32
    )
    key_term = jnp.einsum(
        "qgrk,qgrd->kgd", score_grad, query_grouped, preferred_element_type=jnp.float32
    ).reshape(win, KVW)
    value_term = jnp.einsum(
        "qgrk,qgrd->kgd", probs_low, attended_grad_low, preferred_element_type=jnp.float32
    ).reshape(win, KVW)
    kv_term = jnp.concatenate([key_term, value_term], axis=1).reshape(back + 1, tok_rows, 2 * KVW)
    kv_sum = kv_return(kv_term[back], kv_term[:back].astype(jnp.bfloat16), n_ctx, back)
    key_grad_low = rotate(kv_sum[:, :KVW] * score_scale, query_positions, KVH, -1.0).astype(
        jnp.bfloat16
    )
    value_grad_low = kv_sum[:, KVW:].astype(jnp.bfloat16)
    query_grad_low = rotate(
        query_accum.reshape(tok_rows, D) * score_scale, query_positions, H, -1.0
    ).astype(jnp.bfloat16)
    projection_cat = jnp.concatenate([query_grad_low, key_grad_low, value_grad_low], axis=1)
    normed_grad = times_transposed(projection_cat, qkv_full)
    gain_one_term = jnp.sum(normed_grad * normed_one, axis=0)
    scaled_one = normed_grad * gain_one_f
    tokens_grad = middle_grad + scale_one * (
        scaled_one - normed_one * jnp.mean(scaled_one * normed_one, axis=-1, keepdims=True)
    )
    gain_term_cols = jnp.pad(
        jnp.stack([gain_one_term, gain_two_term], axis=1), ((0, 0), (0, GAIN_PAD - 2))
    )
    gain_term_cols = gain_term_cols.at[0, GAIN_PAD - 1].set(ff_sum[0, 0].astype(jnp.float32) * 0.0)
    attention_pack = jnp.concatenate(
        [
            outer_rows(normed_low, projection_cat).astype(jnp.bfloat16),
            outer_rows(attended_low, branch_grad).astype(jnp.bfloat16),
            gain_term_cols.astype(jnp.bfloat16),
        ],
        axis=1,
    )
    attention_sum = lax.psum_scatter(
        attention_pack, ALL, scatter_dimension=0, tiled=True
    ).astype(jnp.float32)
    ff_part = ff_part.at[0, 0].add(attention_pack[0, 0].astype(jnp.float32) * 0.0)
    layer_out = middle + fsdp_reduce(ff_part.reshape(n_f, tok_rows, D), n_f)
    ff_sum = ff_sum.astype(jnp.float32)
    return (
        layer_out.astype(jnp.bfloat16)[None],
        tokens_grad[None],
        attention_sum[:, c_g],
        attention_sum[:, :c_k],
        attention_sum[:, c_k:c_v],
        attention_sum[:, c_v:c_o],
        attention_sum[:, c_o:c_g],
        attention_sum[:, c_g + 1],
        ff_sum[:, :ff],
        ff_sum[:, ff : 2 * ff],
        down_sum.astype(jnp.float32),
    )


def solution(mesh):
    weight = P(ALL, None)
    stream = P("fsdp", "ctx", None)
    return jax.shard_map(
        body,
        mesh=mesh,
        in_specs=(
            stream,
            P("fsdp", None),
            P(ALL),
            weight,
            weight,
            weight,
            weight,
            P(ALL),
            weight,
            weight,
            weight,
            stream,
        ),
        out_specs=(
            stream,
            stream,
            P(ALL),
            weight,
            weight,
            weight,
            weight,
            P(ALL),
            weight,
            weight,
            weight,
        ),
        check_vma=False,
    )
```

```python
import functools

import jax
import jax.numpy as jnp
from jax import lax
from jax.experimental import pallas as pl
from jax.experimental.pallas import tpu as pltpu
from jax.sharding import PartitionSpec as P

MESH = pl.DeviceIdType.MESH

D = 1536
H = 16
KVH = 8
HD = 96
KBLK = 512
DOC_MOST = 4096
KVW = 768
GAIN_PAD = 128

EPSILON = 1e-05
ROPE_BASE = 100000.0
MASKED_SCORE = -1e30
ALL = ("ctx", "fsdp")


def rms_scale(values):
    return lax.rsqrt(jnp.mean(values * values, axis=-1, keepdims=True) + EPSILON)


def document_layout(lengths, total):
    starts = jnp.cumsum(lengths) - lengths
    places = jnp.arange(total, dtype=jnp.int32)
    inside = places[:, None] >= starts[None, :]
    doc_ids = jnp.sum(inside.astype(jnp.int32), axis=1) - 1
    doc_starts = jnp.max(jnp.where(inside, starts[None, :], 0), axis=1)
    return (doc_ids, places - doc_starts)


def rotate(values, positions, head_count, direction):
    row_count = values.shape[0]
    half_dim = HD // 2
    inverse_freq = ROPE_BASE ** (-(jnp.arange(half_dim).astype(jnp.float32) * (2.0 / HD)))
    angles = positions.astype(jnp.float32)[:, None] * inverse_freq[None, :]
    cosine = jnp.cos(angles)[:, None, :]
    sine_part = direction * jnp.sin(angles)[:, None, :]
    grouped = values.reshape(row_count, head_count, HD)
    former = grouped[:, :, :half_dim]
    latter = grouped[:, :, half_dim:]
    turned = jnp.concatenate(
        [former * cosine - latter * sine_part, latter * cosine + former * sine_part], axis=2
    )
    return turned.reshape(row_count, head_count * HD)


def outer_rows(left, right):
    return lax.dot_general(
        left, right, (((0,), (0,)), ((), ())), preferred_element_type=jnp.float32
    )


def times_transposed(left, right):
    return lax.dot_general(
        left, right, (((1,), (1,)), ((), ())), preferred_element_type=jnp.float32
    )


def neighbour_barrier(n_ctx, back, c, f):
    barrier = pltpu.get_barrier_semaphore()
    for s in range(1, back + 1):
        for peer in ((c + s) % n_ctx, (c + n_ctx - s) % n_ctx):
            pl.semaphore_signal(barrier, inc=1, device_id=(peer, f), device_id_type=MESH)
    pl.semaphore_wait(barrier, 2 * back)


def kv_share_kernel(n_ctx, back, kv_ref, out_ref, send_sem, recv_sem):
    c = lax.axis_index("ctx")
    f = lax.axis_index("fsdp")
    neighbour_barrier(n_ctx, back, c, f)

    def copy(s, dest):
        return pltpu.make_async_remote_copy(
            src_ref=kv_ref,
            dst_ref=out_ref.at[back - s],
            send_sem=send_sem.at[s - 1],
            recv_sem=recv_sem.at[back - s],
            device_id=(dest, f),
            device_id_type=MESH,
        )

    for s in range(1, back + 1):

        @pl.when(c + s < n_ctx)
        def _():
            copy(s, c + s).start()

    out_ref[back] = kv_ref[...]
    for s in range(1, back + 1):

        @pl.when(c - s < 0)
        def _():
            out_ref[back - s] = jnp.zeros(kv_ref.shape, kv_ref.dtype)

    for s in range(1, back + 1):

        @pl.when(c + s < n_ctx)
        def _():
            copy(s, c + s).wait_send()

        @pl.when(c - s >= 0)
        def _():
            copy(s, c).wait_recv()


def kv_share(kv, n_ctx, back):
    return pl.pallas_call(
        functools.partial(kv_share_kernel, n_ctx, back),
        out_shape=jax.ShapeDtypeStruct((back + 1,) + kv.shape, kv.dtype),
        in_specs=[pl.BlockSpec(memory_space=pltpu.VMEM)],
        out_specs=pl.BlockSpec(memory_space=pltpu.VMEM),
        scratch_shapes=[pltpu.SemaphoreType.DMA((back,)), pltpu.SemaphoreType.DMA((back + 1,))],
        compiler_params=pltpu.CompilerParams(collective_id=0, has_side_effects=True),
    )(kv)


def kv_return_kernel(n_ctx, back, own_ref, g_ref, out_ref, recv_buf, send_sem, recv_sem):
    c = lax.axis_index("ctx")
    f = lax.axis_index("fsdp")
    neighbour_barrier(n_ctx, back, c, f)

    def copy(s, dest):
        return pltpu.make_async_remote_copy(
            src_ref=g_ref.at[back - s],
            dst_ref=recv_buf.at[s - 1],
            send_sem=send_sem.at[s - 1],
            recv_sem=recv_sem.at[s - 1],
            device_id=(dest, f),
            device_id_type=MESH,
        )

    for s in range(1, back + 1):

        @pl.when(c - s >= 0)
        def _():
            copy(s, c - s).start()

    out_ref[...] = own_ref[...]
    for s in range(1, back + 1):

        @pl.when(c + s < n_ctx)
        def _():
            copy(s, c).wait_recv()
            out_ref[...] += recv_buf[s - 1].astype(jnp.float32)

    for s in range(1, back + 1):

        @pl.when(c - s >= 0)
        def _():
            copy(s, c - s).wait_send()


def kv_return(own, g, n_ctx, back):
    return pl.pallas_call(
        functools.partial(kv_return_kernel, n_ctx, back),
        out_shape=jax.ShapeDtypeStruct(own.shape, own.dtype),
        in_specs=[pl.BlockSpec(memory_space=pltpu.VMEM)] * 2,
        out_specs=pl.BlockSpec(memory_space=pltpu.VMEM),
        scratch_shapes=[
            pltpu.VMEM(g.shape, g.dtype),
            pltpu.SemaphoreType.DMA((back,)),
            pltpu.SemaphoreType.DMA((back,)),
        ],
        compiler_params=pltpu.CompilerParams(collective_id=1, has_side_effects=True),
    )(own, g)


def peer_barrier(n_f, c, f):
    barrier = pltpu.get_barrier_semaphore()
    for k in range(1, n_f):
        pl.semaphore_signal(barrier, inc=1, device_id=(c, (f + k) % n_f), device_id_type=MESH)
    pl.semaphore_wait(barrier, n_f - 1)


def group_gather_kernel(n_f, x_ref, out_ref, send_sem, recv_sem):
    c = lax.axis_index("ctx")
    f = lax.axis_index("fsdp")
    peer_barrier(n_f, c, f)
    copies = []
    for k in range(1, n_f):
        copy = pltpu.make_async_remote_copy(
            src_ref=x_ref,
            dst_ref=out_ref.at[f],
            send_sem=send_sem.at[k - 1],
            recv_sem=recv_sem.at[k - 1],
            device_id=(c, (f + k) % n_f),
            device_id_type=MESH,
        )
        copy.start()
        copies.append(copy)
    out_ref[f] = x_ref[...]
    for k in range(1, n_f):
        pltpu.make_async_remote_copy(
            src_ref=x_ref,
            dst_ref=out_ref.at[(f + n_f - k) % n_f],
            send_sem=send_sem.at[k - 1],
            recv_sem=recv_sem.at[k - 1],
            device_id=(c, f),
            device_id_type=MESH,
        ).wait_recv()
    for copy in copies:
        copy.wait_send()


def group_gather(x, n_f):
    return pl.pallas_call(
        functools.partial(group_gather_kernel, n_f),
        out_shape=jax.ShapeDtypeStruct((n_f,) + x.shape, x.dtype),
        in_specs=[pl.BlockSpec(memory_space=pltpu.VMEM)],
        out_specs=pl.BlockSpec(memory_space=pltpu.VMEM),
        scratch_shapes=[pltpu.SemaphoreType.DMA((n_f - 1,)), pltpu.SemaphoreType.DMA((n_f - 1,))],
        compiler_params=pltpu.CompilerParams(collective_id=2, has_side_effects=True),
    )(x)


def group_reduce_kernel(n_f, p_ref, out_ref, recv_buf, send_sem, recv_sem):
    c = lax.axis_index("ctx")
    f = lax.axis_index("fsdp")
    peer_barrier(n_f, c, f)
    copies = []
    for k in range(1, n_f):
        dest = (f + k) % n_f
        copy = pltpu.make_async_remote_copy(
            src_ref=p_ref.at[dest],
            dst_ref=recv_buf.at[k - 1],
            send_sem=send_sem.at[k - 1],
            recv_sem=recv_sem.at[k - 1],
            device_id=(c, dest),
            device_id_type=MESH,
        )
        copy.start()
        copies.append(copy)
    out_ref[...] = p_ref[f]
    for k in range(1, n_f):
        copies[k - 1].wait_recv()
        out_ref[...] += recv_buf[k - 1]
    for copy in copies:
        copy.wait_send()


def group_reduce(p, n_f):
    return pl.pallas_call(
        functools.partial(group_reduce_kernel, n_f),
        out_shape=jax.ShapeDtypeStruct(p.shape[1:], p.dtype),
        in_specs=[pl.BlockSpec(memory_space=pltpu.VMEM)],
        out_specs=pl.BlockSpec(memory_space=pltpu.VMEM),
        scratch_shapes=[
            pltpu.VMEM((n_f - 1,) + p.shape[1:], p.dtype),
            pltpu.SemaphoreType.DMA((n_f - 1,)),
            pltpu.SemaphoreType.DMA((n_f - 1,)),
        ],
        compiler_params=pltpu.CompilerParams(collective_id=3, has_side_effects=True),
    )(p)


def pair_barrier(c, partner, across):
    barrier = pltpu.get_barrier_semaphore()
    pl.semaphore_signal(barrier, inc=1, device_id=(c, partner), device_id_type=MESH)
    pl.semaphore_signal(barrier, inc=1, device_id=(c, across), device_id_type=MESH)
    pl.semaphore_wait(barrier, 2)


def quad_ids():
    c = lax.axis_index("ctx")
    f = lax.axis_index("fsdp")
    partner = f + 1 - 2 * (f % 2)
    across = (f + 2) % 4
    diagonal = (partner + 2) % 4
    return c, f, partner, across, diagonal


def quad_gather_kernel(x_ref, out_ref, send_sem, recv_sem):
    c, f, partner, across, diagonal = quad_ids()
    pair_barrier(c, partner, across)

    def copy(src, slot, dest, k):
        return pltpu.make_async_remote_copy(
            src_ref=src,
            dst_ref=out_ref.at[slot],
            send_sem=send_sem.at[k],
            recv_sem=recv_sem.at[slot],
            device_id=(c, dest),
            device_id_type=MESH,
        )

    first = copy(x_ref, f, across, 0)
    first.start()
    own = copy(x_ref, f, partner, 1)
    own.start()
    out_ref[f] = x_ref[...]
    copy(x_ref, across, f, 0).wait_recv()
    relay = copy(out_ref.at[across], across, partner, 2)
    relay.start()
    copy(x_ref, partner, f, 0).wait_recv()
    copy(x_ref, diagonal, f, 0).wait_recv()
    first.wait_send()
    own.wait_send()
    relay.wait_send()


def quad_gather(x):
    return pl.pallas_call(
        quad_gather_kernel,
        out_shape=jax.ShapeDtypeStruct((4,) + x.shape, x.dtype),
        in_specs=[pl.BlockSpec(memory_space=pltpu.VMEM)],
        out_specs=pl.BlockSpec(memory_space=pltpu.VMEM),
        scratch_shapes=[pltpu.SemaphoreType.DMA((3,)), pltpu.SemaphoreType.DMA((4,))],
        compiler_params=pltpu.CompilerParams(collective_id=4, has_side_effects=True),
    )(x)


def quad_reduce_kernel(p_ref, out_ref, near_buf, far_buf, sum_buf, send_sem, recv_sem):
    c, f, partner, across, diagonal = quad_ids()
    pair_barrier(c, partner, across)

    def copy(src, dst, dest, k):
        return pltpu.make_async_remote_copy(
            src_ref=src,
            dst_ref=dst,
            send_sem=send_sem.at[k],
            recv_sem=recv_sem.at[k],
            device_id=(c, dest),
            device_id_type=MESH,
        )

    to_partner = copy(p_ref.at[partner], near_buf.at[0], partner, 0)
    to_partner.start()
    to_diagonal = copy(p_ref.at[diagonal], near_buf.at[1], partner, 1)
    to_diagonal.start()
    to_partner.wait_recv()
    to_diagonal.wait_recv()
    sum_buf[...] = p_ref[across] + near_buf[1]
    to_across = copy(sum_buf, far_buf, across, 2)
    to_across.start()
    out_ref[...] = p_ref[f] + near_buf[0]
    to_across.wait_recv()
    out_ref[...] += far_buf[...]
    to_partner.wait_send()
    to_diagonal.wait_send()
    to_across.wait_send()


def quad_reduce(p):
    block = p.shape[1:]
    return pl.pallas_call(
        quad_reduce_kernel,
        out_shape=jax.ShapeDtypeStruct(block, p.dtype),
        in_specs=[pl.BlockSpec(memory_space=pltpu.VMEM)],
        out_specs=pl.BlockSpec(memory_space=pltpu.VMEM),
        scratch_shapes=[
            pltpu.VMEM((2,) + block, p.dtype),
            pltpu.VMEM(block, p.dtype),
            pltpu.VMEM(block, p.dtype),
            pltpu.SemaphoreType.DMA((3,)),
            pltpu.SemaphoreType.DMA((3,)),
        ],
        compiler_params=pltpu.CompilerParams(collective_id=5, has_side_effects=True),
    )(p)


def fsdp_gather(x, n_f):
    if n_f == 4:
        return quad_gather(x)
    return group_gather(x, n_f)


def fsdp_reduce(p, n_f):
    if n_f == 4:
        return quad_reduce(p)
    return group_reduce(p, n_f)


def body(
    tokens,
    doc_lengths,
    attention_gain,
    query_weight,
    key_weight,
    value_weight,
    output_weight,
    feedforward_gain,
    gate_weight,
    up_weight,
    down_weight,
    cotangent,
):
    n_dev = lax.axis_size(ALL)
    rows = query_weight.shape[0]
    ff_rows = down_weight.shape[0]
    ff = gate_weight.shape[1]
    local_tokens = tokens[0].astype(jnp.float32)
    tok_rows = local_tokens.shape[0]
    stream_len = tok_rows * lax.axis_size("ctx")
    my_first = lax.axis_index("ctx") * tok_rows

    gain_cols = jnp.pad(
        jnp.stack([attention_gain, feedforward_gain], axis=1), ((0, 0), (0, GAIN_PAD - 2))
    )
    att_full = lax.all_gather(
        jnp.concatenate([query_weight, key_weight, value_weight, output_weight, gain_cols], axis=1),
        ALL,
        axis=0,
        tiled=True,
    )
    c_k = D
    c_v = D + KVW
    c_o = D + 2 * KVW
    c_g = 2 * D + 2 * KVW
    query_full = att_full[:, :c_k]
    key_full = att_full[:, c_k:c_v]
    value_full = att_full[:, c_v:c_o]
    qkv_full = att_full[:, :c_o]
    output_full = att_full[:, c_o:c_g]
    gain_one_f = att_full[:, c_g].astype(jnp.float32)
    gain_two_f = att_full[:, c_g + 1].astype(jnp.float32)

    key_docs_all, places_all = document_layout(doc_lengths[0], stream_len)
    query_docs = lax.dynamic_slice_in_dim(key_docs_all, my_first, tok_rows, 0)
    query_positions = lax.dynamic_slice_in_dim(places_all, my_first, tok_rows, 0)
    query_places = my_first + jnp.arange(tok_rows, dtype=jnp.int32)
    group_size = H // KVH
    score_scale = HD ** (-0.5)

    scale_one = rms_scale(local_tokens)
    normed_one = local_tokens * scale_one
    normed_low = (normed_one * gain_one_f).astype(jnp.bfloat16)
    qkv = jnp.dot(normed_low, qkv_full, preferred_element_type=jnp.float32)
    queries = qkv[:, :D]
    keys_new = qkv[:, D : D + KVW]
    values_new = qkv[:, D + KVW :]
    query_low = rotate(queries, query_positions, H, 1.0).astype(jnp.bfloat16)
    key_low = rotate(keys_new, query_positions, KVH, 1.0).astype(jnp.bfloat16)
    value_low = values_new.astype(jnp.bfloat16)

    n_ctx = lax.axis_size("ctx")
    n_f = lax.axis_size("fsdp")
    chunk = ff_rows
    units = n_ctx * chunk
    gu_parts = jnp.transpose(
        jnp.stack([gate_weight, up_weight], axis=1).reshape(rows, 2, n_ctx, n_f, chunk),
        (3, 0, 1, 2, 4),
    )
    gu_parts = lax.all_to_all(gu_parts, "fsdp", 0, 0, tiled=True).reshape(n_f * rows, 2 * units)
    down_rows = D // (2 * n_ctx)
    ff_pack = jnp.concatenate([gu_parts, down_weight.reshape(down_rows, 2 * units)], axis=0)
    ff_pack = ff_pack.at[0, 0].add(att_full[0, 0] * 0)
    ff_stack = lax.all_gather(
        ff_pack,
        "ctx",
        axis=0,
        tiled=False,
    )
    gate_up_tp = ff_stack[:, : n_f * rows].reshape(n_ctx * n_f * rows, 2 * units)
    down_tp = ff_stack[:, n_f * rows :].reshape(n_ctx, ff_rows, D).reshape(units, D)
    max_doc = min(DOC_MOST, KBLK * (stream_len // (2 * KBLK)))
    back = min(-(-(max_doc - 1) // tok_rows), n_ctx - 1)
    win = (back + 1) * tok_rows
    kv_win = kv_share(
        jnp.concatenate([key_low, value_low], axis=1), n_ctx, back
    ).reshape(win, 2 * KVW)
    docs_pad = jnp.concatenate(
        [jnp.full((back * tok_rows,), -1, jnp.int32), key_docs_all.astype(jnp.int32)]
    )
    key_docs = lax.dynamic_slice_in_dim(docs_pad, my_first, win, 0)
    key_places = my_first - back * tok_rows + jnp.arange(win, dtype=jnp.int32)
    key_block = kv_win[:, :KVW].reshape(win, KVH, HD)
    value_block = kv_win[:, KVW:].reshape(win, KVH, HD)
    query_grouped = query_low.reshape(tok_rows, KVH, group_size, HD)
    allowed = (
        (key_docs[None, :] == query_docs[:, None]) & (key_places[None, :] <= query_places[:, None])
    )[:, None, None, :]
    scores = (
        jnp.einsum("qgrd,kgd->qgrk", query_grouped, key_block, preferred_element_type=jnp.float32)
        * score_scale
    )
    scores = jnp.where(allowed, scores, MASKED_SCORE)
    row_max = jnp.max(scores, axis=-1, keepdims=True)
    exponent = jnp.where(allowed, jnp.exp(scores - row_max), 0.0)
    probs = exponent / jnp.sum(exponent, axis=-1, keepdims=True)
    probs_low = probs.astype(jnp.bfloat16)
    attended_sum = jnp.einsum(
        "qgrk,kgd->qgrd", probs_low, value_block, preferred_element_type=jnp.float32
    )
    attended_low = attended_sum.reshape(tok_rows, D).astype(jnp.bfloat16)
    middle = local_tokens + jnp.dot(attended_low, output_full, preferred_element_type=jnp.float32)

    scale_two = rms_scale(middle)
    normed_two = middle * scale_two
    normed_two_low = (normed_two * gain_two_f).astype(jnp.bfloat16)
    group_tokens = n_f * tok_rows
    xn2_all = fsdp_gather(normed_two_low, n_f).reshape(group_tokens, D)
    gate_up = jnp.dot(xn2_all, gate_up_tp, preferred_element_type=jnp.float32)
    gate_pre = gate_up[:, :units]
    up_pre = gate_up[:, units:]
    sigmoid = jax.nn.sigmoid(gate_pre)
    hidden_low = (gate_pre * sigmoid * up_pre).astype(jnp.bfloat16)
    ff_part = jnp.dot(hidden_low, down_tp, preferred_element_type=jnp.float32)

    grad_out = cotangent[0]
    grad_all = fsdp_gather(grad_out, n_f).reshape(group_tokens, D)
    down_term = outer_rows(hidden_low, grad_all).astype(jnp.bfloat16)
    hidden_grad = times_transposed(grad_all, down_tp)
    gate_grad = (hidden_grad * up_pre * sigmoid * (1.0 + gate_pre * (1.0 - sigmoid))).astype(
        jnp.bfloat16
    )
    up_grad = (hidden_grad * gate_pre * sigmoid).astype(jnp.bfloat16)
    gate_up_cat = jnp.concatenate([gate_grad, up_grad], axis=1)
    gate_up_term = outer_rows(xn2_all, gate_up_cat)
    grad_pack = jnp.concatenate(
        [
            gate_up_term.astype(jnp.bfloat16).reshape(n_ctx, n_f * rows, 2 * units),
            down_term.reshape(n_ctx, down_rows, 2 * units),
        ],
        axis=1,
    ).reshape(n_ctx * (n_f * rows + down_rows), 2 * units)
    grad_pack, gate_up_cat = lax.optimization_barrier((grad_pack, gate_up_cat))
    grad_sum = lax.psum_scatter(grad_pack, "ctx", scatter_dimension=0, tiled=True)
    down_sum = grad_sum[n_f * rows :].reshape(ff_rows, D)
    gu_sum = lax.all_to_all(grad_sum[: n_f * rows].reshape(n_f, rows, 2 * units), "fsdp", 0, 0, tiled=True)
    ff_sum = jnp.transpose(
        gu_sum.reshape(n_f, rows, 2, n_ctx, chunk), (1, 2, 3, 0, 4)
    ).reshape(rows, 2 * ff)
    normed_two_grad = fsdp_reduce(
        times_transposed(gate_up_cat, gate_up_tp).reshape(n_f, tok_rows, D), n_f
    )
    gain_two_term = jnp.sum(normed_two_grad * normed_two, axis=0)
    scaled_two = normed_two_grad * gain_two_f
    middle_grad = grad_out.astype(jnp.float32) + scale_two * (
        scaled_two - normed_two * jnp.mean(scaled_two * normed_two, axis=-1, keepdims=True)
    )
    branch_grad = middle_grad.astype(jnp.bfloat16)
    attended_grad_low = (
        times_transposed(branch_grad, output_full)
        .astype(jnp.bfloat16)
        .reshape(tok_rows, KVH, group_size, HD)
    )
    row_delta = jnp.sum(
        attended_grad_low.astype(jnp.float32) * attended_sum, axis=-1, keepdims=True
    )
    prob_grad = jnp.einsum(
        "qgrd,kgd->qgrk", attended_grad_low, value_block, preferred_element_type=jnp.float32
    )
    score_grad = (probs * (prob_grad - row_delta)).astype(jnp.bfloat16)
    query_accum = jnp.einsum(
        "qgrk,kgd->qgrd", score_grad, key_block, preferred_element_type=jnp.float32
    )
    key_term = jnp.einsum(
        "qgrk,qgrd->kgd", score_grad, query_grouped, preferred_element_type=jnp.float32
    ).reshape(win, KVW)
    value_term = jnp.einsum(
        "qgrk,qgrd->kgd", probs_low, attended_grad_low, preferred_element_type=jnp.float32
    ).reshape(win, KVW)
    kv_term = jnp.concatenate([key_term, value_term], axis=1).reshape(back + 1, tok_rows, 2 * KVW)
    kv_sum = kv_return(kv_term[back], kv_term[:back].astype(jnp.bfloat16), n_ctx, back)
    key_grad_low = rotate(kv_sum[:, :KVW] * score_scale, query_positions, KVH, -1.0).astype(
        jnp.bfloat16
    )
    value_grad_low = kv_sum[:, KVW:].astype(jnp.bfloat16)
    query_grad_low = rotate(
        query_accum.reshape(tok_rows, D) * score_scale, query_positions, H, -1.0
    ).astype(jnp.bfloat16)
    projection_cat = jnp.concatenate([query_grad_low, key_grad_low, value_grad_low], axis=1)
    normed_grad = times_transposed(projection_cat, qkv_full)
    gain_one_term = jnp.sum(normed_grad * normed_one, axis=0)
    scaled_one = normed_grad * gain_one_f
    tokens_grad = middle_grad + scale_one * (
        scaled_one - normed_one * jnp.mean(scaled_one * normed_one, axis=-1, keepdims=True)
    )
    gain_term_cols = jnp.pad(
        jnp.stack([gain_one_term, gain_two_term], axis=1), ((0, 0), (0, GAIN_PAD - 2))
    )
    gain_term_cols = gain_term_cols.at[0, GAIN_PAD - 1].set(ff_sum[0, 0].astype(jnp.float32) * 0.0)
    attention_pack = jnp.concatenate(
        [
            outer_rows(normed_low, projection_cat).astype(jnp.bfloat16),
            outer_rows(attended_low, branch_grad).astype(jnp.bfloat16),
            gain_term_cols.astype(jnp.bfloat16),
        ],
        axis=1,
    )
    attention_sum = lax.psum_scatter(
        attention_pack, ALL, scatter_dimension=0, tiled=True
    ).astype(jnp.float32)
    ff_part = ff_part.at[0, 0].add(attention_pack[0, 0].astype(jnp.float32) * 0.0)
    layer_out = middle + fsdp_reduce(ff_part.reshape(n_f, tok_rows, D), n_f)
    ff_sum = ff_sum.astype(jnp.float32)
    return (
        layer_out.astype(jnp.bfloat16)[None],
        tokens_grad[None],
        attention_sum[:, c_g],
        attention_sum[:, :c_k],
        attention_sum[:, c_k:c_v],
        attention_sum[:, c_v:c_o],
        attention_sum[:, c_o:c_g],
        attention_sum[:, c_g + 1],
        ff_sum[:, :ff],
        ff_sum[:, ff : 2 * ff],
        down_sum.astype(jnp.float32),
    )


def solution(mesh):
    weight = P(ALL, None)
    stream = P("fsdp", "ctx", None)
    return jax.shard_map(
        body,
        mesh=mesh,
        in_specs=(
            stream,
            P("fsdp", None),
            P(ALL),
            weight,
            weight,
            weight,
            weight,
            P(ALL),
            weight,
            weight,
            weight,
            stream,
        ),
        out_specs=(
            stream,
            stream,
            P(ALL),
            weight,
            weight,
            weight,
            weight,
            P(ALL),
            weight,
            weight,
            weight,
        ),
        check_vma=False,
    )
```

```python
import functools

import jax
import jax.numpy as jnp
from jax import lax
from jax.experimental import pallas as pl
from jax.experimental.pallas import tpu as pltpu
from jax.sharding import PartitionSpec as P

MESH = pl.DeviceIdType.MESH

D = 1536
H = 16
KVH = 8
HD = 96
KBLK = 512
DOC_MOST = 4096
KVW = 768
GAIN_PAD = 128

EPSILON = 1e-05
ROPE_BASE = 100000.0
MASKED_SCORE = -1e30
ALL = ("ctx", "fsdp")


def rms_scale(values):
    return lax.rsqrt(jnp.mean(values * values, axis=-1, keepdims=True) + EPSILON)


def document_layout(lengths, total):
    starts = jnp.cumsum(lengths) - lengths
    places = jnp.arange(total, dtype=jnp.int32)
    inside = places[:, None] >= starts[None, :]
    doc_ids = jnp.sum(inside.astype(jnp.int32), axis=1) - 1
    doc_starts = jnp.max(jnp.where(inside, starts[None, :], 0), axis=1)
    return (doc_ids, places - doc_starts)


def rotate(values, positions, head_count, direction):
    row_count = values.shape[0]
    half_dim = HD // 2
    inverse_freq = ROPE_BASE ** (-(jnp.arange(half_dim).astype(jnp.float32) * (2.0 / HD)))
    angles = positions.astype(jnp.float32)[:, None] * inverse_freq[None, :]
    cosine = jnp.cos(angles)[:, None, :]
    sine_part = direction * jnp.sin(angles)[:, None, :]
    grouped = values.reshape(row_count, head_count, HD)
    former = grouped[:, :, :half_dim]
    latter = grouped[:, :, half_dim:]
    turned = jnp.concatenate(
        [former * cosine - latter * sine_part, latter * cosine + former * sine_part], axis=2
    )
    return turned.reshape(row_count, head_count * HD)


def outer_rows(left, right):
    return lax.dot_general(
        left, right, (((0,), (0,)), ((), ())), preferred_element_type=jnp.float32
    )


def times_transposed(left, right):
    return lax.dot_general(
        left, right, (((1,), (1,)), ((), ())), preferred_element_type=jnp.float32
    )


def neighbour_barrier(n_ctx, back, c, f):
    barrier = pltpu.get_barrier_semaphore()
    for s in range(1, back + 1):
        for peer in ((c + s) % n_ctx, (c + n_ctx - s) % n_ctx):
            pl.semaphore_signal(barrier, inc=1, device_id=(peer, f), device_id_type=MESH)
    pl.semaphore_wait(barrier, 2 * back)


def kv_share_kernel(n_ctx, back, kv_ref, out_ref, send_sem, recv_sem):
    c = lax.axis_index("ctx")
    f = lax.axis_index("fsdp")
    neighbour_barrier(n_ctx, back, c, f)

    def copy(s, dest):
        return pltpu.make_async_remote_copy(
            src_ref=kv_ref,
            dst_ref=out_ref.at[back - s],
            send_sem=send_sem.at[s - 1],
            recv_sem=recv_sem.at[back - s],
            device_id=(dest, f),
            device_id_type=MESH,
        )

    for s in range(1, back + 1):

        @pl.when(c + s < n_ctx)
        def _():
            copy(s, c + s).start()

    out_ref[back] = kv_ref[...]
    for s in range(1, back + 1):

        @pl.when(c - s < 0)
        def _():
            out_ref[back - s] = jnp.zeros(kv_ref.shape, kv_ref.dtype)

    for s in range(1, back + 1):

        @pl.when(c + s < n_ctx)
        def _():
            copy(s, c + s).wait_send()

        @pl.when(c - s >= 0)
        def _():
            copy(s, c).wait_recv()


def kv_share(kv, n_ctx, back):
    return pl.pallas_call(
        functools.partial(kv_share_kernel, n_ctx, back),
        out_shape=jax.ShapeDtypeStruct((back + 1,) + kv.shape, kv.dtype),
        in_specs=[pl.BlockSpec(memory_space=pltpu.VMEM)],
        out_specs=pl.BlockSpec(memory_space=pltpu.VMEM),
        scratch_shapes=[pltpu.SemaphoreType.DMA((back,)), pltpu.SemaphoreType.DMA((back + 1,))],
        compiler_params=pltpu.CompilerParams(collective_id=0, has_side_effects=True),
    )(kv)


def kv_return_kernel(n_ctx, back, own_ref, g_ref, out_ref, recv_buf, send_sem, recv_sem):
    c = lax.axis_index("ctx")
    f = lax.axis_index("fsdp")
    neighbour_barrier(n_ctx, back, c, f)

    def copy(s, dest):
        return pltpu.make_async_remote_copy(
            src_ref=g_ref.at[back - s],
            dst_ref=recv_buf.at[s - 1],
            send_sem=send_sem.at[s - 1],
            recv_sem=recv_sem.at[s - 1],
            device_id=(dest, f),
            device_id_type=MESH,
        )

    for s in range(1, back + 1):

        @pl.when(c - s >= 0)
        def _():
            copy(s, c - s).start()

    out_ref[...] = own_ref[...]
    for s in range(1, back + 1):

        @pl.when(c + s < n_ctx)
        def _():
            copy(s, c).wait_recv()
            out_ref[...] += recv_buf[s - 1].astype(jnp.float32)

    for s in range(1, back + 1):

        @pl.when(c - s >= 0)
        def _():
            copy(s, c - s).wait_send()


def kv_return(own, g, n_ctx, back):
    return pl.pallas_call(
        functools.partial(kv_return_kernel, n_ctx, back),
        out_shape=jax.ShapeDtypeStruct(own.shape, own.dtype),
        in_specs=[pl.BlockSpec(memory_space=pltpu.VMEM)] * 2,
        out_specs=pl.BlockSpec(memory_space=pltpu.VMEM),
        scratch_shapes=[
            pltpu.VMEM(g.shape, g.dtype),
            pltpu.SemaphoreType.DMA((back,)),
            pltpu.SemaphoreType.DMA((back,)),
        ],
        compiler_params=pltpu.CompilerParams(collective_id=1, has_side_effects=True),
    )(own, g)


def peer_barrier(n_f, c, f):
    barrier = pltpu.get_barrier_semaphore()
    for k in range(1, n_f):
        pl.semaphore_signal(barrier, inc=1, device_id=(c, (f + k) % n_f), device_id_type=MESH)
    pl.semaphore_wait(barrier, n_f - 1)


def group_gather_kernel(n_f, x_ref, out_ref, send_sem, recv_sem):
    c = lax.axis_index("ctx")
    f = lax.axis_index("fsdp")
    peer_barrier(n_f, c, f)
    copies = []
    for k in range(1, n_f):
        copy = pltpu.make_async_remote_copy(
            src_ref=x_ref,
            dst_ref=out_ref.at[f],
            send_sem=send_sem.at[k - 1],
            recv_sem=recv_sem.at[k - 1],
            device_id=(c, (f + k) % n_f),
            device_id_type=MESH,
        )
        copy.start()
        copies.append(copy)
    out_ref[f] = x_ref[...]
    for k in range(1, n_f):
        pltpu.make_async_remote_copy(
            src_ref=x_ref,
            dst_ref=out_ref.at[(f + n_f - k) % n_f],
            send_sem=send_sem.at[k - 1],
            recv_sem=recv_sem.at[k - 1],
            device_id=(c, f),
            device_id_type=MESH,
        ).wait_recv()
    for copy in copies:
        copy.wait_send()


def group_gather(x, n_f):
    return pl.pallas_call(
        functools.partial(group_gather_kernel, n_f),
        out_shape=jax.ShapeDtypeStruct((n_f,) + x.shape, x.dtype),
        in_specs=[pl.BlockSpec(memory_space=pltpu.VMEM)],
        out_specs=pl.BlockSpec(memory_space=pltpu.VMEM),
        scratch_shapes=[pltpu.SemaphoreType.DMA((n_f - 1,)), pltpu.SemaphoreType.DMA((n_f - 1,))],
        compiler_params=pltpu.CompilerParams(collective_id=2, has_side_effects=True),
    )(x)


def group_reduce_kernel(n_f, p_ref, out_ref, recv_buf, send_sem, recv_sem):
    c = lax.axis_index("ctx")
    f = lax.axis_index("fsdp")
    peer_barrier(n_f, c, f)
    copies = []
    for k in range(1, n_f):
        dest = (f + k) % n_f
        copy = pltpu.make_async_remote_copy(
            src_ref=p_ref.at[dest],
            dst_ref=recv_buf.at[k - 1],
            send_sem=send_sem.at[k - 1],
            recv_sem=recv_sem.at[k - 1],
            device_id=(c, dest),
            device_id_type=MESH,
        )
        copy.start()
        copies.append(copy)
    out_ref[...] = p_ref[f]
    for k in range(1, n_f):
        copies[k - 1].wait_recv()
        out_ref[...] += recv_buf[k - 1]
    for copy in copies:
        copy.wait_send()


def group_reduce(p, n_f):
    return pl.pallas_call(
        functools.partial(group_reduce_kernel, n_f),
        out_shape=jax.ShapeDtypeStruct(p.shape[1:], p.dtype),
        in_specs=[pl.BlockSpec(memory_space=pltpu.VMEM)],
        out_specs=pl.BlockSpec(memory_space=pltpu.VMEM),
        scratch_shapes=[
            pltpu.VMEM((n_f - 1,) + p.shape[1:], p.dtype),
            pltpu.SemaphoreType.DMA((n_f - 1,)),
            pltpu.SemaphoreType.DMA((n_f - 1,)),
        ],
        compiler_params=pltpu.CompilerParams(collective_id=3, has_side_effects=True),
    )(p)


def pair_barrier(c, partner, across):
    barrier = pltpu.get_barrier_semaphore()
    pl.semaphore_signal(barrier, inc=1, device_id=(c, partner), device_id_type=MESH)
    pl.semaphore_signal(barrier, inc=1, device_id=(c, across), device_id_type=MESH)
    pl.semaphore_wait(barrier, 2)


def quad_ids():
    c = lax.axis_index("ctx")
    f = lax.axis_index("fsdp")
    partner = f + 1 - 2 * (f % 2)
    across = (f + 2) % 4
    diagonal = (partner + 2) % 4
    return c, f, partner, across, diagonal


def quad_gather_kernel(x_ref, out_ref, send_sem, recv_sem):
    c, f, partner, across, diagonal = quad_ids()
    pair_barrier(c, partner, across)

    def copy(src, slot, dest, k):
        return pltpu.make_async_remote_copy(
            src_ref=src,
            dst_ref=out_ref.at[slot],
            send_sem=send_sem.at[k],
            recv_sem=recv_sem.at[slot],
            device_id=(c, dest),
            device_id_type=MESH,
        )

    first = copy(x_ref, f, across, 0)
    first.start()
    own = copy(x_ref, f, partner, 1)
    own.start()
    out_ref[f] = x_ref[...]
    copy(x_ref, across, f, 0).wait_recv()
    relay = copy(out_ref.at[across], across, partner, 2)
    relay.start()
    copy(x_ref, partner, f, 0).wait_recv()
    copy(x_ref, diagonal, f, 0).wait_recv()
    first.wait_send()
    own.wait_send()
    relay.wait_send()


def quad_gather(x):
    return pl.pallas_call(
        quad_gather_kernel,
        out_shape=jax.ShapeDtypeStruct((4,) + x.shape, x.dtype),
        in_specs=[pl.BlockSpec(memory_space=pltpu.VMEM)],
        out_specs=pl.BlockSpec(memory_space=pltpu.VMEM),
        scratch_shapes=[pltpu.SemaphoreType.DMA((3,)), pltpu.SemaphoreType.DMA((4,))],
        compiler_params=pltpu.CompilerParams(collective_id=4, has_side_effects=True),
    )(x)


def quad_reduce_kernel(p_ref, out_ref, near_buf, far_buf, sum_buf, send_sem, recv_sem):
    c, f, partner, across, diagonal = quad_ids()
    pair_barrier(c, partner, across)

    def copy(src, dst, dest, k):
        return pltpu.make_async_remote_copy(
            src_ref=src,
            dst_ref=dst,
            send_sem=send_sem.at[k],
            recv_sem=recv_sem.at[k],
            device_id=(c, dest),
            device_id_type=MESH,
        )

    to_partner = copy(p_ref.at[partner], near_buf.at[0], partner, 0)
    to_partner.start()
    to_diagonal = copy(p_ref.at[diagonal], near_buf.at[1], partner, 1)
    to_diagonal.start()
    to_partner.wait_recv()
    to_diagonal.wait_recv()
    sum_buf[...] = p_ref[across] + near_buf[1]
    to_across = copy(sum_buf, far_buf, across, 2)
    to_across.start()
    out_ref[...] = p_ref[f] + near_buf[0]
    to_across.wait_recv()
    out_ref[...] += far_buf[...]
    to_partner.wait_send()
    to_diagonal.wait_send()
    to_across.wait_send()


def quad_reduce(p):
    block = p.shape[1:]
    return pl.pallas_call(
        quad_reduce_kernel,
        out_shape=jax.ShapeDtypeStruct(block, p.dtype),
        in_specs=[pl.BlockSpec(memory_space=pltpu.VMEM)],
        out_specs=pl.BlockSpec(memory_space=pltpu.VMEM),
        scratch_shapes=[
            pltpu.VMEM((2,) + block, p.dtype),
            pltpu.VMEM(block, p.dtype),
            pltpu.VMEM(block, p.dtype),
            pltpu.SemaphoreType.DMA((3,)),
            pltpu.SemaphoreType.DMA((3,)),
        ],
        compiler_params=pltpu.CompilerParams(collective_id=5, has_side_effects=True),
    )(p)


def fsdp_gather(x, n_f):
    if n_f == 4:
        return quad_gather(x)
    return group_gather(x, n_f)


def fsdp_reduce(p, n_f):
    if n_f == 4:
        return quad_reduce(p)
    return group_reduce(p, n_f)


def body(
    tokens,
    doc_lengths,
    attention_gain,
    query_weight,
    key_weight,
    value_weight,
    output_weight,
    feedforward_gain,
    gate_weight,
    up_weight,
    down_weight,
    cotangent,
):
    n_dev = lax.axis_size(ALL)
    rows = query_weight.shape[0]
    ff_rows = down_weight.shape[0]
    ff = gate_weight.shape[1]
    local_tokens = tokens[0].astype(jnp.float32)
    tok_rows = local_tokens.shape[0]
    stream_len = tok_rows * lax.axis_size("ctx")
    my_first = lax.axis_index("ctx") * tok_rows

    gain_cols = jnp.pad(
        jnp.stack([attention_gain, feedforward_gain], axis=1), ((0, 0), (0, GAIN_PAD - 2))
    )
    att_full = lax.all_gather(
        jnp.concatenate([query_weight, key_weight, value_weight, output_weight, gain_cols], axis=1),
        ALL,
        axis=0,
        tiled=True,
    )
    c_k = D
    c_v = D + KVW
    c_o = D + 2 * KVW
    c_g = 2 * D + 2 * KVW
    query_full = att_full[:, :c_k]
    key_full = att_full[:, c_k:c_v]
    value_full = att_full[:, c_v:c_o]
    qkv_full = att_full[:, :c_o]
    output_full = att_full[:, c_o:c_g]
    gain_one_f = att_full[:, c_g].astype(jnp.float32)
    gain_two_f = att_full[:, c_g + 1].astype(jnp.float32)

    key_docs_all, places_all = document_layout(doc_lengths[0], stream_len)
    query_docs = lax.dynamic_slice_in_dim(key_docs_all, my_first, tok_rows, 0)
    query_positions = lax.dynamic_slice_in_dim(places_all, my_first, tok_rows, 0)
    query_places = my_first + jnp.arange(tok_rows, dtype=jnp.int32)
    group_size = H // KVH
    score_scale = HD ** (-0.5)

    scale_one = rms_scale(local_tokens)
    normed_one = local_tokens * scale_one
    normed_low = (normed_one * gain_one_f).astype(jnp.bfloat16)
    qkv = jnp.dot(normed_low, qkv_full, preferred_element_type=jnp.float32)
    queries = qkv[:, :D]
    keys_new = qkv[:, D : D + KVW]
    values_new = qkv[:, D + KVW :]
    query_low = rotate(queries, query_positions, H, 1.0).astype(jnp.bfloat16)
    key_low = rotate(keys_new, query_positions, KVH, 1.0).astype(jnp.bfloat16)
    value_low = values_new.astype(jnp.bfloat16)

    n_ctx = lax.axis_size("ctx")
    n_f = lax.axis_size("fsdp")
    chunk = ff_rows
    units = n_ctx * chunk
    gu_parts = jnp.transpose(
        jnp.stack([gate_weight, up_weight], axis=1).reshape(rows, 2, n_ctx, n_f, chunk),
        (3, 0, 1, 2, 4),
    )
    gu_parts = lax.all_to_all(gu_parts, "fsdp", 0, 0, tiled=True).reshape(n_f * rows, 2 * units)
    down_rows = D // (2 * n_ctx)
    ff_pack = jnp.concatenate([gu_parts, down_weight.reshape(down_rows, 2 * units)], axis=0)
    ff_pack = ff_pack.at[0, 0].add(att_full[0, 0] * 0)
    ff_stack = lax.all_gather(
        ff_pack,
        "ctx",
        axis=0,
        tiled=False,
    )
    gate_up_tp = ff_stack[:, : n_f * rows].reshape(n_ctx * n_f * rows, 2 * units)
    down_tp = ff_stack[:, n_f * rows :].reshape(n_ctx, ff_rows, D).reshape(units, D)
    max_doc = min(DOC_MOST, KBLK * (stream_len // (2 * KBLK)))
    back = min(-(-(max_doc - 1) // tok_rows), n_ctx - 1)
    win = (back + 1) * tok_rows
    kv_win = kv_share(
        jnp.concatenate([key_low, value_low], axis=1), n_ctx, back
    ).reshape(win, 2 * KVW)
    docs_pad = jnp.concatenate(
        [jnp.full((back * tok_rows,), -1, jnp.int32), key_docs_all.astype(jnp.int32)]
    )
    key_docs = lax.dynamic_slice_in_dim(docs_pad, my_first, win, 0)
    key_places = my_first - back * tok_rows + jnp.arange(win, dtype=jnp.int32)
    key_block = kv_win[:, :KVW].reshape(win, KVH, HD)
    value_block = kv_win[:, KVW:].reshape(win, KVH, HD)
    query_grouped = query_low.reshape(tok_rows, KVH, group_size, HD)
    allowed = (
        (key_docs[None, :] == query_docs[:, None]) & (key_places[None, :] <= query_places[:, None])
    )[:, None, None, :]
    scores = (
        jnp.einsum("qgrd,kgd->qgrk", query_grouped, key_block, preferred_element_type=jnp.float32)
        * score_scale
    )
    scores = jnp.where(allowed, scores, MASKED_SCORE)
    row_max = jnp.max(scores, axis=-1, keepdims=True)
    exponent = jnp.where(allowed, jnp.exp(scores - row_max), 0.0)
    probs = exponent / jnp.sum(exponent, axis=-1, keepdims=True)
    probs_low = probs.astype(jnp.bfloat16)
    attended_sum = jnp.einsum(
        "qgrk,kgd->qgrd", probs_low, value_block, preferred_element_type=jnp.float32
    )
    attended_low = attended_sum.reshape(tok_rows, D).astype(jnp.bfloat16)
    middle = local_tokens + jnp.dot(attended_low, output_full, preferred_element_type=jnp.float32)

    scale_two = rms_scale(middle)
    normed_two = middle * scale_two
    normed_two_low = (normed_two * gain_two_f).astype(jnp.bfloat16)
    group_tokens = n_f * tok_rows
    xn2_all = fsdp_gather(normed_two_low, n_f).reshape(group_tokens, D)
    gate_up = jnp.dot(xn2_all, gate_up_tp, preferred_element_type=jnp.float32)
    gate_pre = gate_up[:, :units]
    up_pre = gate_up[:, units:]
    sigmoid = jax.nn.sigmoid(gate_pre)
    hidden_low = (gate_pre * sigmoid * up_pre).astype(jnp.bfloat16)
    ff_part = jnp.dot(hidden_low, down_tp, preferred_element_type=jnp.float32)

    grad_out = cotangent[0]
    grad_all = fsdp_gather(grad_out, n_f).reshape(group_tokens, D)
    down_term, grad_all = lax.optimization_barrier(
        (outer_rows(hidden_low, grad_all).astype(jnp.bfloat16), grad_all)
    )
    down_sum = lax.psum_scatter(down_term, "ctx", scatter_dimension=0, tiled=True)
    hidden_grad = times_transposed(grad_all, down_tp)
    gate_grad = (hidden_grad * up_pre * sigmoid * (1.0 + gate_pre * (1.0 - sigmoid))).astype(
        jnp.bfloat16
    )
    up_grad = (hidden_grad * gate_pre * sigmoid).astype(jnp.bfloat16)
    gate_up_cat = jnp.concatenate([gate_grad, up_grad], axis=1)
    gate_up_term = outer_rows(xn2_all, gate_up_cat)
    ff_pack, gate_up_cat = lax.optimization_barrier((gate_up_term.astype(jnp.bfloat16), gate_up_cat))
    gu_sum = lax.psum_scatter(ff_pack, "ctx", scatter_dimension=0, tiled=True)
    gu_sum = lax.all_to_all(gu_sum.reshape(n_f, rows, 2 * units), "fsdp", 0, 0, tiled=True)
    ff_sum = jnp.transpose(
        gu_sum.reshape(n_f, rows, 2, n_ctx, chunk), (1, 2, 3, 0, 4)
    ).reshape(rows, 2 * ff)
    normed_two_grad = fsdp_reduce(
        times_transposed(gate_up_cat, gate_up_tp).reshape(n_f, tok_rows, D), n_f
    )
    gain_two_term = jnp.sum(normed_two_grad * normed_two, axis=0)
    scaled_two = normed_two_grad * gain_two_f
    middle_grad = grad_out.astype(jnp.float32) + scale_two * (
        scaled_two - normed_two * jnp.mean(scaled_two * normed_two, axis=-1, keepdims=True)
    )
    branch_grad = middle_grad.astype(jnp.bfloat16)
    attended_grad_low = (
        times_transposed(branch_grad, output_full)
        .astype(jnp.bfloat16)
        .reshape(tok_rows, KVH, group_size, HD)
    )
    row_delta = jnp.sum(
        attended_grad_low.astype(jnp.float32) * attended_sum, axis=-1, keepdims=True
    )
    prob_grad = jnp.einsum(
        "qgrd,kgd->qgrk", attended_grad_low, value_block, preferred_element_type=jnp.float32
    )
    score_grad = (probs * (prob_grad - row_delta)).astype(jnp.bfloat16)
    query_accum = jnp.einsum(
        "qgrk,kgd->qgrd", score_grad, key_block, preferred_element_type=jnp.float32
    )
    key_term = jnp.einsum(
        "qgrk,qgrd->kgd", score_grad, query_grouped, preferred_element_type=jnp.float32
    ).reshape(win, KVW)
    value_term = jnp.einsum(
        "qgrk,qgrd->kgd", probs_low, attended_grad_low, preferred_element_type=jnp.float32
    ).reshape(win, KVW)
    kv_term = jnp.concatenate([key_term, value_term], axis=1).reshape(back + 1, tok_rows, 2 * KVW)
    kv_own = kv_term[back].at[0, 0].add(down_sum[0, 0].astype(jnp.float32) * 0.0)
    kv_sum = kv_return(kv_own, kv_term[:back].astype(jnp.bfloat16), n_ctx, back)
    key_grad_low = rotate(kv_sum[:, :KVW] * score_scale, query_positions, KVH, -1.0).astype(
        jnp.bfloat16
    )
    value_grad_low = kv_sum[:, KVW:].astype(jnp.bfloat16)
    query_grad_low = rotate(
        query_accum.reshape(tok_rows, D) * score_scale, query_positions, H, -1.0
    ).astype(jnp.bfloat16)
    projection_cat = jnp.concatenate([query_grad_low, key_grad_low, value_grad_low], axis=1)
    normed_grad = times_transposed(projection_cat, qkv_full)
    gain_one_term = jnp.sum(normed_grad * normed_one, axis=0)
    scaled_one = normed_grad * gain_one_f
    tokens_grad = middle_grad + scale_one * (
        scaled_one - normed_one * jnp.mean(scaled_one * normed_one, axis=-1, keepdims=True)
    )
    gain_term_cols = jnp.pad(
        jnp.stack([gain_one_term, gain_two_term], axis=1), ((0, 0), (0, GAIN_PAD - 2))
    )
    gain_term_cols = gain_term_cols.at[0, GAIN_PAD - 1].set(ff_sum[0, 0].astype(jnp.float32) * 0.0)
    attention_pack = jnp.concatenate(
        [
            outer_rows(normed_low, projection_cat).astype(jnp.bfloat16),
            outer_rows(attended_low, branch_grad).astype(jnp.bfloat16),
            gain_term_cols.astype(jnp.bfloat16),
        ],
        axis=1,
    )
    attention_sum = lax.psum_scatter(
        attention_pack, ALL, scatter_dimension=0, tiled=True
    ).astype(jnp.float32)
    ff_part = ff_part.at[0, 0].add(attention_pack[0, 0].astype(jnp.float32) * 0.0)
    layer_out = middle + fsdp_reduce(ff_part.reshape(n_f, tok_rows, D), n_f)
    ff_sum = ff_sum.astype(jnp.float32)
    return (
        layer_out.astype(jnp.bfloat16)[None],
        tokens_grad[None],
        attention_sum[:, c_g],
        attention_sum[:, :c_k],
        attention_sum[:, c_k:c_v],
        attention_sum[:, c_v:c_o],
        attention_sum[:, c_o:c_g],
        attention_sum[:, c_g + 1],
        ff_sum[:, :ff],
        ff_sum[:, ff : 2 * ff],
        down_sum.astype(jnp.float32),
    )


def solution(mesh):
    weight = P(ALL, None)
    stream = P("fsdp", "ctx", None)
    return jax.shard_map(
        body,
        mesh=mesh,
        in_specs=(
            stream,
            P("fsdp", None),
            P(ALL),
            weight,
            weight,
            weight,
            weight,
            P(ALL),
            weight,
            weight,
            weight,
            stream,
        ),
        out_specs=(
            stream,
            stream,
            P(ALL),
            weight,
            weight,
            weight,
            weight,
            P(ALL),
            weight,
            weight,
            weight,
        ),
        check_vma=False,
    )
```

```python
import functools

import jax
import jax.numpy as jnp
from jax import lax
from jax.experimental import pallas as pl
from jax.experimental.pallas import tpu as pltpu
from jax.sharding import PartitionSpec as P

MESH = pl.DeviceIdType.MESH

D = 1536
H = 16
KVH = 8
HD = 96
KBLK = 512
DOC_MOST = 4096
KVW = 768
GAIN_PAD = 128

EPSILON = 1e-05
ROPE_BASE = 100000.0
MASKED_SCORE = -1e30
ALL = ("ctx", "fsdp")


def rms_scale(values):
    return lax.rsqrt(jnp.mean(values * values, axis=-1, keepdims=True) + EPSILON)


def document_layout(lengths, total):
    starts = jnp.cumsum(lengths) - lengths
    places = jnp.arange(total, dtype=jnp.int32)
    inside = places[:, None] >= starts[None, :]
    doc_ids = jnp.sum(inside.astype(jnp.int32), axis=1) - 1
    doc_starts = jnp.max(jnp.where(inside, starts[None, :], 0), axis=1)
    return (doc_ids, places - doc_starts)


def rotate(values, positions, head_count, direction):
    row_count = values.shape[0]
    half_dim = HD // 2
    inverse_freq = ROPE_BASE ** (-(jnp.arange(half_dim).astype(jnp.float32) * (2.0 / HD)))
    angles = positions.astype(jnp.float32)[:, None] * inverse_freq[None, :]
    cosine = jnp.cos(angles)[:, None, :]
    sine_part = direction * jnp.sin(angles)[:, None, :]
    grouped = values.reshape(row_count, head_count, HD)
    former = grouped[:, :, :half_dim]
    latter = grouped[:, :, half_dim:]
    turned = jnp.concatenate(
        [former * cosine - latter * sine_part, latter * cosine + former * sine_part], axis=2
    )
    return turned.reshape(row_count, head_count * HD)


def outer_rows(left, right):
    return lax.dot_general(
        left, right, (((0,), (0,)), ((), ())), preferred_element_type=jnp.float32
    )


def times_transposed(left, right):
    return lax.dot_general(
        left, right, (((1,), (1,)), ((), ())), preferred_element_type=jnp.float32
    )


def neighbour_barrier(n_ctx, back, c, f):
    barrier = pltpu.get_barrier_semaphore()
    for s in range(1, back + 1):
        for peer in ((c + s) % n_ctx, (c + n_ctx - s) % n_ctx):
            pl.semaphore_signal(barrier, inc=1, device_id=(peer, f), device_id_type=MESH)
    pl.semaphore_wait(barrier, 2 * back)


def kv_share_kernel(n_ctx, back, kv_ref, out_ref, send_sem, recv_sem):
    c = lax.axis_index("ctx")
    f = lax.axis_index("fsdp")
    neighbour_barrier(n_ctx, back, c, f)

    def copy(s, dest):
        return pltpu.make_async_remote_copy(
            src_ref=kv_ref,
            dst_ref=out_ref.at[back - s],
            send_sem=send_sem.at[s - 1],
            recv_sem=recv_sem.at[back - s],
            device_id=(dest, f),
            device_id_type=MESH,
        )

    for s in range(1, back + 1):

        @pl.when(c + s < n_ctx)
        def _():
            copy(s, c + s).start()

    out_ref[back] = kv_ref[...]
    for s in range(1, back + 1):

        @pl.when(c - s < 0)
        def _():
            out_ref[back - s] = jnp.zeros(kv_ref.shape, kv_ref.dtype)

    for s in range(1, back + 1):

        @pl.when(c + s < n_ctx)
        def _():
            copy(s, c + s).wait_send()

        @pl.when(c - s >= 0)
        def _():
            copy(s, c).wait_recv()


def kv_share(kv, n_ctx, back):
    return pl.pallas_call(
        functools.partial(kv_share_kernel, n_ctx, back),
        out_shape=jax.ShapeDtypeStruct((back + 1,) + kv.shape, kv.dtype),
        in_specs=[pl.BlockSpec(memory_space=pltpu.VMEM)],
        out_specs=pl.BlockSpec(memory_space=pltpu.VMEM),
        scratch_shapes=[pltpu.SemaphoreType.DMA((back,)), pltpu.SemaphoreType.DMA((back + 1,))],
        compiler_params=pltpu.CompilerParams(collective_id=0, has_side_effects=True),
    )(kv)


def kv_return_kernel(n_ctx, back, own_ref, g_ref, out_ref, recv_buf, send_sem, recv_sem):
    c = lax.axis_index("ctx")
    f = lax.axis_index("fsdp")
    neighbour_barrier(n_ctx, back, c, f)

    def copy(s, dest):
        return pltpu.make_async_remote_copy(
            src_ref=g_ref.at[back - s],
            dst_ref=recv_buf.at[s - 1],
            send_sem=send_sem.at[s - 1],
            recv_sem=recv_sem.at[s - 1],
            device_id=(dest, f),
            device_id_type=MESH,
        )

    for s in range(1, back + 1):

        @pl.when(c - s >= 0)
        def _():
            copy(s, c - s).start()

    out_ref[...] = own_ref[...]
    for s in range(1, back + 1):

        @pl.when(c + s < n_ctx)
        def _():
            copy(s, c).wait_recv()
            out_ref[...] += recv_buf[s - 1].astype(jnp.float32)

    for s in range(1, back + 1):

        @pl.when(c - s >= 0)
        def _():
            copy(s, c - s).wait_send()


def kv_return(own, g, n_ctx, back):
    return pl.pallas_call(
        functools.partial(kv_return_kernel, n_ctx, back),
        out_shape=jax.ShapeDtypeStruct(own.shape, own.dtype),
        in_specs=[pl.BlockSpec(memory_space=pltpu.VMEM)] * 2,
        out_specs=pl.BlockSpec(memory_space=pltpu.VMEM),
        scratch_shapes=[
            pltpu.VMEM(g.shape, g.dtype),
            pltpu.SemaphoreType.DMA((back,)),
            pltpu.SemaphoreType.DMA((back,)),
        ],
        compiler_params=pltpu.CompilerParams(collective_id=1, has_side_effects=True),
    )(own, g)


def peer_barrier(n_f, c, f):
    barrier = pltpu.get_barrier_semaphore()
    for k in range(1, n_f):
        pl.semaphore_signal(barrier, inc=1, device_id=(c, (f + k) % n_f), device_id_type=MESH)
    pl.semaphore_wait(barrier, n_f - 1)


def group_gather_kernel(n_f, x_ref, out_ref, send_sem, recv_sem):
    c = lax.axis_index("ctx")
    f = lax.axis_index("fsdp")
    peer_barrier(n_f, c, f)
    copies = []
    for k in range(1, n_f):
        copy = pltpu.make_async_remote_copy(
            src_ref=x_ref,
            dst_ref=out_ref.at[f],
            send_sem=send_sem.at[k - 1],
            recv_sem=recv_sem.at[k - 1],
            device_id=(c, (f + k) % n_f),
            device_id_type=MESH,
        )
        copy.start()
        copies.append(copy)
    out_ref[f] = x_ref[...]
    for k in range(1, n_f):
        pltpu.make_async_remote_copy(
            src_ref=x_ref,
            dst_ref=out_ref.at[(f + n_f - k) % n_f],
            send_sem=send_sem.at[k - 1],
            recv_sem=recv_sem.at[k - 1],
            device_id=(c, f),
            device_id_type=MESH,
        ).wait_recv()
    for copy in copies:
        copy.wait_send()


def group_gather(x, n_f):
    return pl.pallas_call(
        functools.partial(group_gather_kernel, n_f),
        out_shape=jax.ShapeDtypeStruct((n_f,) + x.shape, x.dtype),
        in_specs=[pl.BlockSpec(memory_space=pltpu.VMEM)],
        out_specs=pl.BlockSpec(memory_space=pltpu.VMEM),
        scratch_shapes=[pltpu.SemaphoreType.DMA((n_f - 1,)), pltpu.SemaphoreType.DMA((n_f - 1,))],
        compiler_params=pltpu.CompilerParams(collective_id=2, has_side_effects=True),
    )(x)


def group_reduce_kernel(n_f, p_ref, out_ref, recv_buf, send_sem, recv_sem):
    c = lax.axis_index("ctx")
    f = lax.axis_index("fsdp")
    peer_barrier(n_f, c, f)
    copies = []
    for k in range(1, n_f):
        dest = (f + k) % n_f
        copy = pltpu.make_async_remote_copy(
            src_ref=p_ref.at[dest],
            dst_ref=recv_buf.at[k - 1],
            send_sem=send_sem.at[k - 1],
            recv_sem=recv_sem.at[k - 1],
            device_id=(c, dest),
            device_id_type=MESH,
        )
        copy.start()
        copies.append(copy)
    out_ref[...] = p_ref[f]
    for k in range(1, n_f):
        copies[k - 1].wait_recv()
        out_ref[...] += recv_buf[k - 1]
    for copy in copies:
        copy.wait_send()


def group_reduce(p, n_f):
    return pl.pallas_call(
        functools.partial(group_reduce_kernel, n_f),
        out_shape=jax.ShapeDtypeStruct(p.shape[1:], p.dtype),
        in_specs=[pl.BlockSpec(memory_space=pltpu.VMEM)],
        out_specs=pl.BlockSpec(memory_space=pltpu.VMEM),
        scratch_shapes=[
            pltpu.VMEM((n_f - 1,) + p.shape[1:], p.dtype),
            pltpu.SemaphoreType.DMA((n_f - 1,)),
            pltpu.SemaphoreType.DMA((n_f - 1,)),
        ],
        compiler_params=pltpu.CompilerParams(collective_id=3, has_side_effects=True),
    )(p)


def pair_barrier(c, partner, across):
    barrier = pltpu.get_barrier_semaphore()
    pl.semaphore_signal(barrier, inc=1, device_id=(c, partner), device_id_type=MESH)
    pl.semaphore_signal(barrier, inc=1, device_id=(c, across), device_id_type=MESH)
    pl.semaphore_wait(barrier, 2)


def quad_ids():
    c = lax.axis_index("ctx")
    f = lax.axis_index("fsdp")
    partner = f + 1 - 2 * (f % 2)
    across = (f + 2) % 4
    diagonal = (partner + 2) % 4
    return c, f, partner, across, diagonal


def quad_gather_kernel(x_ref, out_ref, send_sem, recv_sem):
    c, f, partner, across, diagonal = quad_ids()
    pair_barrier(c, partner, across)

    def copy(src, slot, dest, k):
        return pltpu.make_async_remote_copy(
            src_ref=src,
            dst_ref=out_ref.at[slot],
            send_sem=send_sem.at[k],
            recv_sem=recv_sem.at[slot],
            device_id=(c, dest),
            device_id_type=MESH,
        )

    first = copy(x_ref, f, across, 0)
    first.start()
    own = copy(x_ref, f, partner, 1)
    own.start()
    out_ref[f] = x_ref[...]
    copy(x_ref, across, f, 0).wait_recv()
    relay = copy(out_ref.at[across], across, partner, 2)
    relay.start()
    copy(x_ref, partner, f, 0).wait_recv()
    copy(x_ref, diagonal, f, 0).wait_recv()
    first.wait_send()
    own.wait_send()
    relay.wait_send()


def quad_gather(x):
    return pl.pallas_call(
        quad_gather_kernel,
        out_shape=jax.ShapeDtypeStruct((4,) + x.shape, x.dtype),
        in_specs=[pl.BlockSpec(memory_space=pltpu.VMEM)],
        out_specs=pl.BlockSpec(memory_space=pltpu.VMEM),
        scratch_shapes=[pltpu.SemaphoreType.DMA((3,)), pltpu.SemaphoreType.DMA((4,))],
        compiler_params=pltpu.CompilerParams(collective_id=4, has_side_effects=True),
    )(x)


def quad_reduce_kernel(p_ref, out_ref, near_buf, far_buf, sum_buf, send_sem, recv_sem):
    c, f, partner, across, diagonal = quad_ids()
    pair_barrier(c, partner, across)

    def copy(src, dst, dest, k):
        return pltpu.make_async_remote_copy(
            src_ref=src,
            dst_ref=dst,
            send_sem=send_sem.at[k],
            recv_sem=recv_sem.at[k],
            device_id=(c, dest),
            device_id_type=MESH,
        )

    to_partner = copy(p_ref.at[partner], near_buf.at[0], partner, 0)
    to_partner.start()
    to_diagonal = copy(p_ref.at[diagonal], near_buf.at[1], partner, 1)
    to_diagonal.start()
    to_partner.wait_recv()
    to_diagonal.wait_recv()
    sum_buf[...] = p_ref[across] + near_buf[1]
    to_across = copy(sum_buf, far_buf, across, 2)
    to_across.start()
    out_ref[...] = p_ref[f] + near_buf[0]
    to_across.wait_recv()
    out_ref[...] += far_buf[...]
    to_partner.wait_send()
    to_diagonal.wait_send()
    to_across.wait_send()


def quad_reduce(p):
    block = p.shape[1:]
    return pl.pallas_call(
        quad_reduce_kernel,
        out_shape=jax.ShapeDtypeStruct(block, p.dtype),
        in_specs=[pl.BlockSpec(memory_space=pltpu.VMEM)],
        out_specs=pl.BlockSpec(memory_space=pltpu.VMEM),
        scratch_shapes=[
            pltpu.VMEM((2,) + block, p.dtype),
            pltpu.VMEM(block, p.dtype),
            pltpu.VMEM(block, p.dtype),
            pltpu.SemaphoreType.DMA((3,)),
            pltpu.SemaphoreType.DMA((3,)),
        ],
        compiler_params=pltpu.CompilerParams(collective_id=5, has_side_effects=True),
    )(p)


def fsdp_gather(x, n_f):
    if n_f == 4:
        return quad_gather(x)
    return group_gather(x, n_f)


def fsdp_reduce(p, n_f):
    if n_f == 4:
        return quad_reduce(p)
    return group_reduce(p, n_f)


def body(
    tokens,
    doc_lengths,
    attention_gain,
    query_weight,
    key_weight,
    value_weight,
    output_weight,
    feedforward_gain,
    gate_weight,
    up_weight,
    down_weight,
    cotangent,
):
    n_dev = lax.axis_size(ALL)
    rows = query_weight.shape[0]
    ff_rows = down_weight.shape[0]
    ff = gate_weight.shape[1]
    local_tokens = tokens[0].astype(jnp.float32)
    tok_rows = local_tokens.shape[0]
    stream_len = tok_rows * lax.axis_size("ctx")
    my_first = lax.axis_index("ctx") * tok_rows

    gain_cols = jnp.pad(
        jnp.stack([attention_gain, feedforward_gain], axis=1), ((0, 0), (0, GAIN_PAD - 2))
    )
    att_full = lax.all_gather(
        jnp.concatenate([query_weight, key_weight, value_weight, output_weight, gain_cols], axis=1),
        ALL,
        axis=0,
        tiled=True,
    )
    c_k = D
    c_v = D + KVW
    c_o = D + 2 * KVW
    c_g = 2 * D + 2 * KVW
    query_full = att_full[:, :c_k]
    key_full = att_full[:, c_k:c_v]
    value_full = att_full[:, c_v:c_o]
    qkv_full = att_full[:, :c_o]
    output_full = att_full[:, c_o:c_g]
    gain_one_f = att_full[:, c_g].astype(jnp.float32)
    gain_two_f = att_full[:, c_g + 1].astype(jnp.float32)

    key_docs_all, places_all = document_layout(doc_lengths[0], stream_len)
    query_docs = lax.dynamic_slice_in_dim(key_docs_all, my_first, tok_rows, 0)
    query_positions = lax.dynamic_slice_in_dim(places_all, my_first, tok_rows, 0)
    query_places = my_first + jnp.arange(tok_rows, dtype=jnp.int32)
    group_size = H // KVH
    score_scale = HD ** (-0.5)

    scale_one = rms_scale(local_tokens)
    normed_one = local_tokens * scale_one
    normed_low = (normed_one * gain_one_f).astype(jnp.bfloat16)
    qkv = jnp.dot(normed_low, qkv_full, preferred_element_type=jnp.float32)
    queries = qkv[:, :D]
    keys_new = qkv[:, D : D + KVW]
    values_new = qkv[:, D + KVW :]
    query_low = rotate(queries, query_positions, H, 1.0).astype(jnp.bfloat16)
    key_low = rotate(keys_new, query_positions, KVH, 1.0).astype(jnp.bfloat16)
    value_low = values_new.astype(jnp.bfloat16)

    n_ctx = lax.axis_size("ctx")
    n_f = lax.axis_size("fsdp")
    chunk = ff_rows
    units = n_ctx * chunk
    gu_parts = jnp.transpose(
        jnp.stack([gate_weight, up_weight], axis=1).reshape(rows, 2, n_ctx, n_f, chunk),
        (3, 0, 1, 2, 4),
    )
    gu_parts = lax.all_to_all(gu_parts, "fsdp", 0, 0, tiled=True).reshape(n_f * rows, 2 * units)
    down_rows = D // (2 * n_ctx)
    ff_pack = jnp.concatenate([gu_parts, down_weight.reshape(down_rows, 2 * units)], axis=0)
    ff_pack = ff_pack.at[0, 0].add(att_full[0, 0] * 0)
    ff_stack = lax.all_gather(
        ff_pack,
        "ctx",
        axis=0,
        tiled=False,
    )
    gate_up_tp = ff_stack[:, : n_f * rows].reshape(n_ctx * n_f * rows, 2 * units)
    down_tp = ff_stack[:, n_f * rows :].reshape(n_ctx, ff_rows, D).reshape(units, D)
    max_doc = min(DOC_MOST, KBLK * (stream_len // (2 * KBLK)))
    back = min(-(-(max_doc - 1) // tok_rows), n_ctx - 1)
    win = (back + 1) * tok_rows
    kv_win = kv_share(
        jnp.concatenate([key_low, value_low], axis=1), n_ctx, back
    ).reshape(win, 2 * KVW)
    docs_pad = jnp.concatenate(
        [jnp.full((back * tok_rows,), -1, jnp.int32), key_docs_all.astype(jnp.int32)]
    )
    key_docs = lax.dynamic_slice_in_dim(docs_pad, my_first, win, 0)
    key_places = my_first - back * tok_rows + jnp.arange(win, dtype=jnp.int32)
    key_block = kv_win[:, :KVW].reshape(win, KVH, HD)
    value_block = kv_win[:, KVW:].reshape(win, KVH, HD)
    query_grouped = query_low.reshape(tok_rows, KVH, group_size, HD)
    allowed = (
        (key_docs[None, :] == query_docs[:, None]) & (key_places[None, :] <= query_places[:, None])
    )[:, None, None, :]
    scores = (
        jnp.einsum("qgrd,kgd->qgrk", query_grouped, key_block, preferred_element_type=jnp.float32)
        * score_scale
    )
    scores = jnp.where(allowed, scores, MASKED_SCORE)
    row_max = jnp.max(scores, axis=-1, keepdims=True)
    exponent = jnp.where(allowed, jnp.exp(scores - row_max), 0.0)
    probs = exponent / jnp.sum(exponent, axis=-1, keepdims=True)
    probs_low = probs.astype(jnp.bfloat16)
    attended_sum = jnp.einsum(
        "qgrk,kgd->qgrd", probs_low, value_block, preferred_element_type=jnp.float32
    )
    attended_low = attended_sum.reshape(tok_rows, D).astype(jnp.bfloat16)
    middle = local_tokens + jnp.dot(attended_low, output_full, preferred_element_type=jnp.float32)

    scale_two = rms_scale(middle)
    normed_two = middle * scale_two
    normed_two_low = (normed_two * gain_two_f).astype(jnp.bfloat16)
    group_tokens = n_f * tok_rows
    xn2_all = fsdp_gather(normed_two_low, n_f).reshape(group_tokens, D)
    gate_up = jnp.dot(xn2_all, gate_up_tp, preferred_element_type=jnp.float32)
    gate_pre = gate_up[:, :units]
    up_pre = gate_up[:, units:]
    sigmoid = jax.nn.sigmoid(gate_pre)
    hidden_low = (gate_pre * sigmoid * up_pre).astype(jnp.bfloat16)
    ff_part = jnp.dot(hidden_low, down_tp, preferred_element_type=jnp.float32)

    grad_out = cotangent[0]
    grad_all = fsdp_gather(grad_out, n_f).reshape(group_tokens, D)
    down_term, grad_all = lax.optimization_barrier(
        (outer_rows(hidden_low, grad_all).astype(jnp.bfloat16), grad_all)
    )
    down_sum = lax.psum_scatter(down_term, "ctx", scatter_dimension=0, tiled=True)
    hidden_grad = times_transposed(grad_all, down_tp)
    gate_grad = (hidden_grad * up_pre * sigmoid * (1.0 + gate_pre * (1.0 - sigmoid))).astype(
        jnp.bfloat16
    )
    up_grad = (hidden_grad * gate_pre * sigmoid).astype(jnp.bfloat16)
    gate_up_cat = jnp.concatenate([gate_grad, up_grad], axis=1)
    gate_up_term = outer_rows(xn2_all, gate_up_cat)
    ff_pack, gate_up_cat = lax.optimization_barrier((gate_up_term.astype(jnp.bfloat16), gate_up_cat))
    gu_sum = lax.psum_scatter(ff_pack, "ctx", scatter_dimension=0, tiled=True)
    gu_sum = lax.all_to_all(gu_sum.reshape(n_f, rows, 2 * units), "fsdp", 0, 0, tiled=True)
    ff_sum = jnp.transpose(
        gu_sum.reshape(n_f, rows, 2, n_ctx, chunk), (1, 2, 3, 0, 4)
    ).reshape(rows, 2 * ff)
    normed_two_grad = fsdp_reduce(
        times_transposed(gate_up_cat, gate_up_tp).reshape(n_f, tok_rows, D), n_f
    )
    gain_two_term = jnp.sum(normed_two_grad * normed_two, axis=0)
    scaled_two = normed_two_grad * gain_two_f
    middle_grad = grad_out.astype(jnp.float32) + scale_two * (
        scaled_two - normed_two * jnp.mean(scaled_two * normed_two, axis=-1, keepdims=True)
    )
    branch_grad = middle_grad.astype(jnp.bfloat16)
    attended_grad_low = (
        times_transposed(branch_grad, output_full)
        .astype(jnp.bfloat16)
        .reshape(tok_rows, KVH, group_size, HD)
    )
    row_delta = jnp.sum(
        attended_grad_low.astype(jnp.float32) * attended_sum, axis=-1, keepdims=True
    )
    prob_grad = jnp.einsum(
        "qgrd,kgd->qgrk", attended_grad_low, value_block, preferred_element_type=jnp.float32
    )
    score_grad = (probs * (prob_grad - row_delta)).astype(jnp.bfloat16)
    query_accum = jnp.einsum(
        "qgrk,kgd->qgrd", score_grad, key_block, preferred_element_type=jnp.float32
    )
    key_term = jnp.einsum(
        "qgrk,qgrd->kgd", score_grad, query_grouped, preferred_element_type=jnp.float32
    ).reshape(win, KVW)
    value_term = jnp.einsum(
        "qgrk,qgrd->kgd", probs_low, attended_grad_low, preferred_element_type=jnp.float32
    ).reshape(win, KVW)
    kv_term = jnp.concatenate([key_term, value_term], axis=1).reshape(back + 1, tok_rows, 2 * KVW)
    kv_own = kv_term[back].at[0, 0].add(down_sum[0, 0].astype(jnp.float32) * 0.0)
    kv_sum = kv_return(kv_own, kv_term[:back].astype(jnp.bfloat16), n_ctx, back)
    key_grad_low = rotate(kv_sum[:, :KVW] * score_scale, query_positions, KVH, -1.0).astype(
        jnp.bfloat16
    )
    value_grad_low = kv_sum[:, KVW:].astype(jnp.bfloat16)
    query_grad_low = rotate(
        query_accum.reshape(tok_rows, D) * score_scale, query_positions, H, -1.0
    ).astype(jnp.bfloat16)
    projection_cat = jnp.concatenate([query_grad_low, key_grad_low, value_grad_low], axis=1)
    normed_grad = times_transposed(projection_cat, qkv_full)
    gain_one_term = jnp.sum(normed_grad * normed_one, axis=0)
    scaled_one = normed_grad * gain_one_f
    tokens_grad = middle_grad + scale_one * (
        scaled_one - normed_one * jnp.mean(scaled_one * normed_one, axis=-1, keepdims=True)
    )
    gain_term_cols = jnp.pad(
        jnp.stack([gain_one_term, gain_two_term], axis=1), ((0, 0), (0, GAIN_PAD - 2))
    )
    attention_pack = jnp.concatenate(
        [
            outer_rows(normed_low, projection_cat).astype(jnp.bfloat16),
            outer_rows(attended_low, branch_grad).astype(jnp.bfloat16),
            gain_term_cols.astype(jnp.bfloat16),
        ],
        axis=1,
    )
    attention_sum = lax.psum_scatter(
        attention_pack, ALL, scatter_dimension=0, tiled=True
    ).astype(jnp.float32)
    ff_part = ff_part.at[0, 0].add(attention_pack[0, 0].astype(jnp.float32) * 0.0)
    layer_out = middle + fsdp_reduce(ff_part.reshape(n_f, tok_rows, D), n_f)
    ff_sum = ff_sum.astype(jnp.float32)
    return (
        layer_out.astype(jnp.bfloat16)[None],
        tokens_grad[None],
        attention_sum[:, c_g],
        attention_sum[:, :c_k],
        attention_sum[:, c_k:c_v],
        attention_sum[:, c_v:c_o],
        attention_sum[:, c_o:c_g],
        attention_sum[:, c_g + 1],
        ff_sum[:, :ff],
        ff_sum[:, ff : 2 * ff],
        down_sum.astype(jnp.float32),
    )


def solution(mesh):
    weight = P(ALL, None)
    stream = P("fsdp", "ctx", None)
    return jax.shard_map(
        body,
        mesh=mesh,
        in_specs=(
            stream,
            P("fsdp", None),
            P(ALL),
            weight,
            weight,
            weight,
            weight,
            P(ALL),
            weight,
            weight,
            weight,
            stream,
        ),
        out_specs=(
            stream,
            stream,
            P(ALL),
            weight,
            weight,
            weight,
            weight,
            P(ALL),
            weight,
            weight,
            weight,
        ),
        check_vma=False,
    )
```

```python
import functools

import jax
import jax.numpy as jnp
from jax import lax
from jax.experimental import pallas as pl
from jax.experimental.pallas import tpu as pltpu
from jax.sharding import PartitionSpec as P

MESH = pl.DeviceIdType.MESH

D = 1536
H = 16
KVH = 8
HD = 96
KBLK = 512
DOC_MOST = 4096
KVW = 768
GAIN_PAD = 128

EPSILON = 1e-05
ROPE_BASE = 100000.0
MASKED_SCORE = -1e30
ALL = ("ctx", "fsdp")


def rms_scale(values):
    return lax.rsqrt(jnp.mean(values * values, axis=-1, keepdims=True) + EPSILON)


def document_layout(lengths, total):
    starts = jnp.cumsum(lengths) - lengths
    places = jnp.arange(total, dtype=jnp.int32)
    inside = places[:, None] >= starts[None, :]
    doc_ids = jnp.sum(inside.astype(jnp.int32), axis=1) - 1
    doc_starts = jnp.max(jnp.where(inside, starts[None, :], 0), axis=1)
    return (doc_ids, places - doc_starts)


def rotate(values, positions, head_count, direction):
    row_count = values.shape[0]
    half_dim = HD // 2
    inverse_freq = ROPE_BASE ** (-(jnp.arange(half_dim).astype(jnp.float32) * (2.0 / HD)))
    angles = positions.astype(jnp.float32)[:, None] * inverse_freq[None, :]
    cosine = jnp.cos(angles)[:, None, :]
    sine_part = direction * jnp.sin(angles)[:, None, :]
    grouped = values.reshape(row_count, head_count, HD)
    former = grouped[:, :, :half_dim]
    latter = grouped[:, :, half_dim:]
    turned = jnp.concatenate(
        [former * cosine - latter * sine_part, latter * cosine + former * sine_part], axis=2
    )
    return turned.reshape(row_count, head_count * HD)


def outer_rows(left, right):
    return lax.dot_general(
        left, right, (((0,), (0,)), ((), ())), preferred_element_type=jnp.float32
    )


def times_transposed(left, right):
    return lax.dot_general(
        left, right, (((1,), (1,)), ((), ())), preferred_element_type=jnp.float32
    )


def neighbour_barrier(n_ctx, back, c, f):
    barrier = pltpu.get_barrier_semaphore()
    for s in range(1, back + 1):
        for peer in ((c + s) % n_ctx, (c + n_ctx - s) % n_ctx):
            pl.semaphore_signal(barrier, inc=1, device_id=(peer, f), device_id_type=MESH)
    pl.semaphore_wait(barrier, 2 * back)


def kv_share_kernel(n_ctx, back, kv_ref, out_ref, send_sem, recv_sem):
    c = lax.axis_index("ctx")
    f = lax.axis_index("fsdp")
    neighbour_barrier(n_ctx, back, c, f)

    def copy(s, dest):
        return pltpu.make_async_remote_copy(
            src_ref=kv_ref,
            dst_ref=out_ref.at[back - s],
            send_sem=send_sem.at[s - 1],
            recv_sem=recv_sem.at[back - s],
            device_id=(dest, f),
            device_id_type=MESH,
        )

    for s in range(1, back + 1):

        @pl.when(c + s < n_ctx)
        def _():
            copy(s, c + s).start()

    out_ref[back] = kv_ref[...]
    for s in range(1, back + 1):

        @pl.when(c - s < 0)
        def _():
            out_ref[back - s] = jnp.zeros(kv_ref.shape, kv_ref.dtype)

    for s in range(1, back + 1):

        @pl.when(c + s < n_ctx)
        def _():
            copy(s, c + s).wait_send()

        @pl.when(c - s >= 0)
        def _():
            copy(s, c).wait_recv()


def kv_share(kv, n_ctx, back):
    return pl.pallas_call(
        functools.partial(kv_share_kernel, n_ctx, back),
        out_shape=jax.ShapeDtypeStruct((back + 1,) + kv.shape, kv.dtype),
        in_specs=[pl.BlockSpec(memory_space=pltpu.VMEM)],
        out_specs=pl.BlockSpec(memory_space=pltpu.VMEM),
        scratch_shapes=[pltpu.SemaphoreType.DMA((back,)), pltpu.SemaphoreType.DMA((back + 1,))],
        compiler_params=pltpu.CompilerParams(collective_id=0, has_side_effects=True),
    )(kv)


def kv_return_kernel(n_ctx, back, own_ref, g_ref, out_ref, recv_buf, send_sem, recv_sem):
    c = lax.axis_index("ctx")
    f = lax.axis_index("fsdp")
    neighbour_barrier(n_ctx, back, c, f)

    def copy(s, dest):
        return pltpu.make_async_remote_copy(
            src_ref=g_ref.at[back - s],
            dst_ref=recv_buf.at[s - 1],
            send_sem=send_sem.at[s - 1],
            recv_sem=recv_sem.at[s - 1],
            device_id=(dest, f),
            device_id_type=MESH,
        )

    for s in range(1, back + 1):

        @pl.when(c - s >= 0)
        def _():
            copy(s, c - s).start()

    out_ref[...] = own_ref[...]
    for s in range(1, back + 1):

        @pl.when(c + s < n_ctx)
        def _():
            copy(s, c).wait_recv()
            out_ref[...] += recv_buf[s - 1].astype(jnp.float32)

    for s in range(1, back + 1):

        @pl.when(c - s >= 0)
        def _():
            copy(s, c - s).wait_send()


def kv_return(own, g, n_ctx, back):
    return pl.pallas_call(
        functools.partial(kv_return_kernel, n_ctx, back),
        out_shape=jax.ShapeDtypeStruct(own.shape, own.dtype),
        in_specs=[pl.BlockSpec(memory_space=pltpu.VMEM)] * 2,
        out_specs=pl.BlockSpec(memory_space=pltpu.VMEM),
        scratch_shapes=[
            pltpu.VMEM(g.shape, g.dtype),
            pltpu.SemaphoreType.DMA((back,)),
            pltpu.SemaphoreType.DMA((back,)),
        ],
        compiler_params=pltpu.CompilerParams(collective_id=1, has_side_effects=True),
    )(own, g)


def peer_barrier(n_f, c, f):
    barrier = pltpu.get_barrier_semaphore()
    for k in range(1, n_f):
        pl.semaphore_signal(barrier, inc=1, device_id=(c, (f + k) % n_f), device_id_type=MESH)
    pl.semaphore_wait(barrier, n_f - 1)


def group_gather_kernel(n_f, x_ref, out_ref, send_sem, recv_sem):
    c = lax.axis_index("ctx")
    f = lax.axis_index("fsdp")
    peer_barrier(n_f, c, f)
    copies = []
    for k in range(1, n_f):
        copy = pltpu.make_async_remote_copy(
            src_ref=x_ref,
            dst_ref=out_ref.at[f],
            send_sem=send_sem.at[k - 1],
            recv_sem=recv_sem.at[k - 1],
            device_id=(c, (f + k) % n_f),
            device_id_type=MESH,
        )
        copy.start()
        copies.append(copy)
    out_ref[f] = x_ref[...]
    for k in range(1, n_f):
        pltpu.make_async_remote_copy(
            src_ref=x_ref,
            dst_ref=out_ref.at[(f + n_f - k) % n_f],
            send_sem=send_sem.at[k - 1],
            recv_sem=recv_sem.at[k - 1],
            device_id=(c, f),
            device_id_type=MESH,
        ).wait_recv()
    for copy in copies:
        copy.wait_send()


def group_gather(x, n_f):
    return pl.pallas_call(
        functools.partial(group_gather_kernel, n_f),
        out_shape=jax.ShapeDtypeStruct((n_f,) + x.shape, x.dtype),
        in_specs=[pl.BlockSpec(memory_space=pltpu.VMEM)],
        out_specs=pl.BlockSpec(memory_space=pltpu.VMEM),
        scratch_shapes=[pltpu.SemaphoreType.DMA((n_f - 1,)), pltpu.SemaphoreType.DMA((n_f - 1,))],
        compiler_params=pltpu.CompilerParams(collective_id=2, has_side_effects=True),
    )(x)


def group_reduce_kernel(n_f, p_ref, out_ref, recv_buf, send_sem, recv_sem):
    c = lax.axis_index("ctx")
    f = lax.axis_index("fsdp")
    peer_barrier(n_f, c, f)
    copies = []
    for k in range(1, n_f):
        dest = (f + k) % n_f
        copy = pltpu.make_async_remote_copy(
            src_ref=p_ref.at[dest],
            dst_ref=recv_buf.at[k - 1],
            send_sem=send_sem.at[k - 1],
            recv_sem=recv_sem.at[k - 1],
            device_id=(c, dest),
            device_id_type=MESH,
        )
        copy.start()
        copies.append(copy)
    out_ref[...] = p_ref[f]
    for k in range(1, n_f):
        copies[k - 1].wait_recv()
        out_ref[...] += recv_buf[k - 1]
    for copy in copies:
        copy.wait_send()


def group_reduce(p, n_f):
    return pl.pallas_call(
        functools.partial(group_reduce_kernel, n_f),
        out_shape=jax.ShapeDtypeStruct(p.shape[1:], p.dtype),
        in_specs=[pl.BlockSpec(memory_space=pltpu.VMEM)],
        out_specs=pl.BlockSpec(memory_space=pltpu.VMEM),
        scratch_shapes=[
            pltpu.VMEM((n_f - 1,) + p.shape[1:], p.dtype),
            pltpu.SemaphoreType.DMA((n_f - 1,)),
            pltpu.SemaphoreType.DMA((n_f - 1,)),
        ],
        compiler_params=pltpu.CompilerParams(collective_id=3, has_side_effects=True),
    )(p)


def pair_barrier(c, partner, across):
    barrier = pltpu.get_barrier_semaphore()
    pl.semaphore_signal(barrier, inc=1, device_id=(c, partner), device_id_type=MESH)
    pl.semaphore_signal(barrier, inc=1, device_id=(c, across), device_id_type=MESH)
    pl.semaphore_wait(barrier, 2)


def quad_ids():
    c = lax.axis_index("ctx")
    f = lax.axis_index("fsdp")
    partner = f + 1 - 2 * (f % 2)
    across = (f + 2) % 4
    diagonal = (partner + 2) % 4
    return c, f, partner, across, diagonal


def quad_gather_kernel(x_ref, out_ref, send_sem, recv_sem):
    c, f, partner, across, diagonal = quad_ids()
    pair_barrier(c, partner, across)

    def copy(src, slot, dest, k):
        return pltpu.make_async_remote_copy(
            src_ref=src,
            dst_ref=out_ref.at[slot],
            send_sem=send_sem.at[k],
            recv_sem=recv_sem.at[slot],
            device_id=(c, dest),
            device_id_type=MESH,
        )

    first = copy(x_ref, f, across, 0)
    first.start()
    own = copy(x_ref, f, partner, 1)
    own.start()
    out_ref[f] = x_ref[...]
    copy(x_ref, across, f, 0).wait_recv()
    relay = copy(out_ref.at[across], across, partner, 2)
    relay.start()
    copy(x_ref, partner, f, 0).wait_recv()
    copy(x_ref, diagonal, f, 0).wait_recv()
    first.wait_send()
    own.wait_send()
    relay.wait_send()


def quad_gather(x):
    return pl.pallas_call(
        quad_gather_kernel,
        out_shape=jax.ShapeDtypeStruct((4,) + x.shape, x.dtype),
        in_specs=[pl.BlockSpec(memory_space=pltpu.VMEM)],
        out_specs=pl.BlockSpec(memory_space=pltpu.VMEM),
        scratch_shapes=[pltpu.SemaphoreType.DMA((3,)), pltpu.SemaphoreType.DMA((4,))],
        compiler_params=pltpu.CompilerParams(collective_id=4, has_side_effects=True),
    )(x)


def quad_reduce_kernel(p_ref, out_ref, near_buf, far_buf, sum_buf, send_sem, recv_sem):
    c, f, partner, across, diagonal = quad_ids()
    pair_barrier(c, partner, across)

    def copy(src, dst, dest, k):
        return pltpu.make_async_remote_copy(
            src_ref=src,
            dst_ref=dst,
            send_sem=send_sem.at[k],
            recv_sem=recv_sem.at[k],
            device_id=(c, dest),
            device_id_type=MESH,
        )

    to_partner = copy(p_ref.at[partner], near_buf.at[0], partner, 0)
    to_partner.start()
    to_diagonal = copy(p_ref.at[diagonal], near_buf.at[1], partner, 1)
    to_diagonal.start()
    to_partner.wait_recv()
    to_diagonal.wait_recv()
    sum_buf[...] = (p_ref[across] + near_buf[1]).astype(sum_buf.dtype)
    to_across = copy(sum_buf, far_buf, across, 2)
    to_across.start()
    out_ref[...] = p_ref[f] + near_buf[0]
    to_across.wait_recv()
    out_ref[...] += far_buf[...].astype(out_ref.dtype)
    to_partner.wait_send()
    to_diagonal.wait_send()
    to_across.wait_send()


def quad_reduce(p):
    block = p.shape[1:]
    return pl.pallas_call(
        quad_reduce_kernel,
        out_shape=jax.ShapeDtypeStruct(block, p.dtype),
        in_specs=[pl.BlockSpec(memory_space=pltpu.VMEM)],
        out_specs=pl.BlockSpec(memory_space=pltpu.VMEM),
        scratch_shapes=[
            pltpu.VMEM((2,) + block, p.dtype),
            pltpu.VMEM(block, jnp.bfloat16),
            pltpu.VMEM(block, jnp.bfloat16),
            pltpu.SemaphoreType.DMA((3,)),
            pltpu.SemaphoreType.DMA((3,)),
        ],
        compiler_params=pltpu.CompilerParams(collective_id=5, has_side_effects=True),
    )(p)


def fsdp_gather(x, n_f):
    if n_f == 4:
        return quad_gather(x)
    return group_gather(x, n_f)


def fsdp_reduce(p, n_f):
    if n_f == 4:
        return quad_reduce(p)
    return group_reduce(p, n_f)


def body(
    tokens,
    doc_lengths,
    attention_gain,
    query_weight,
    key_weight,
    value_weight,
    output_weight,
    feedforward_gain,
    gate_weight,
    up_weight,
    down_weight,
    cotangent,
):
    n_dev = lax.axis_size(ALL)
    rows = query_weight.shape[0]
    ff_rows = down_weight.shape[0]
    ff = gate_weight.shape[1]
    local_tokens = tokens[0].astype(jnp.float32)
    tok_rows = local_tokens.shape[0]
    stream_len = tok_rows * lax.axis_size("ctx")
    my_first = lax.axis_index("ctx") * tok_rows

    gain_cols = jnp.pad(
        jnp.stack([attention_gain, feedforward_gain], axis=1), ((0, 0), (0, GAIN_PAD - 2))
    )
    att_full = lax.all_gather(
        jnp.concatenate([query_weight, key_weight, value_weight, output_weight, gain_cols], axis=1),
        ALL,
        axis=0,
        tiled=True,
    )
    c_k = D
    c_v = D + KVW
    c_o = D + 2 * KVW
    c_g = 2 * D + 2 * KVW
    query_full = att_full[:, :c_k]
    key_full = att_full[:, c_k:c_v]
    value_full = att_full[:, c_v:c_o]
    qkv_full = att_full[:, :c_o]
    output_full = att_full[:, c_o:c_g]
    gain_one_f = att_full[:, c_g].astype(jnp.float32)
    gain_two_f = att_full[:, c_g + 1].astype(jnp.float32)

    key_docs_all, places_all = document_layout(doc_lengths[0], stream_len)
    query_docs = lax.dynamic_slice_in_dim(key_docs_all, my_first, tok_rows, 0)
    query_positions = lax.dynamic_slice_in_dim(places_all, my_first, tok_rows, 0)
    query_places = my_first + jnp.arange(tok_rows, dtype=jnp.int32)
    group_size = H // KVH
    score_scale = HD ** (-0.5)

    scale_one = rms_scale(local_tokens)
    normed_one = local_tokens * scale_one
    normed_low = (normed_one * gain_one_f).astype(jnp.bfloat16)
    qkv = jnp.dot(normed_low, qkv_full, preferred_element_type=jnp.float32)
    queries = qkv[:, :D]
    keys_new = qkv[:, D : D + KVW]
    values_new = qkv[:, D + KVW :]
    query_low = rotate(queries, query_positions, H, 1.0).astype(jnp.bfloat16)
    key_low = rotate(keys_new, query_positions, KVH, 1.0).astype(jnp.bfloat16)
    value_low = values_new.astype(jnp.bfloat16)

    n_ctx = lax.axis_size("ctx")
    n_f = lax.axis_size("fsdp")
    chunk = ff_rows
    units = n_ctx * chunk
    gu_parts = jnp.transpose(
        jnp.stack([gate_weight, up_weight], axis=1).reshape(rows, 2, n_ctx, n_f, chunk),
        (3, 0, 1, 2, 4),
    )
    gu_parts = lax.all_to_all(gu_parts, "fsdp", 0, 0, tiled=True).reshape(n_f * rows, 2 * units)
    down_rows = D // (2 * n_ctx)
    ff_pack = jnp.concatenate([gu_parts, down_weight.reshape(down_rows, 2 * units)], axis=0)
    ff_pack = ff_pack.at[0, 0].add(att_full[0, 0] * 0)
    ff_stack = lax.all_gather(
        ff_pack,
        "ctx",
        axis=0,
        tiled=False,
    )
    gate_up_tp = ff_stack[:, : n_f * rows].reshape(n_ctx * n_f * rows, 2 * units)
    down_tp = ff_stack[:, n_f * rows :].reshape(n_ctx, ff_rows, D).reshape(units, D)
    max_doc = min(DOC_MOST, KBLK * (stream_len // (2 * KBLK)))
    back = min(-(-(max_doc - 1) // tok_rows), n_ctx - 1)
    win = (back + 1) * tok_rows
    kv_win = kv_share(
        jnp.concatenate([key_low, value_low], axis=1), n_ctx, back
    ).reshape(win, 2 * KVW)
    docs_pad = jnp.concatenate(
        [jnp.full((back * tok_rows,), -1, jnp.int32), key_docs_all.astype(jnp.int32)]
    )
    key_docs = lax.dynamic_slice_in_dim(docs_pad, my_first, win, 0)
    key_places = my_first - back * tok_rows + jnp.arange(win, dtype=jnp.int32)
    key_block = kv_win[:, :KVW].reshape(win, KVH, HD)
    value_block = kv_win[:, KVW:].reshape(win, KVH, HD)
    query_grouped = query_low.reshape(tok_rows, KVH, group_size, HD)
    allowed = (
        (key_docs[None, :] == query_docs[:, None]) & (key_places[None, :] <= query_places[:, None])
    )[:, None, None, :]
    scores = (
        jnp.einsum("qgrd,kgd->qgrk", query_grouped, key_block, preferred_element_type=jnp.float32)
        * score_scale
    )
    scores = jnp.where(allowed, scores, MASKED_SCORE)
    row_max = jnp.max(scores, axis=-1, keepdims=True)
    exponent = jnp.where(allowed, jnp.exp(scores - row_max), 0.0)
    probs = exponent / jnp.sum(exponent, axis=-1, keepdims=True)
    probs_low = probs.astype(jnp.bfloat16)
    attended_sum = jnp.einsum(
        "qgrk,kgd->qgrd", probs_low, value_block, preferred_element_type=jnp.float32
    )
    attended_low = attended_sum.reshape(tok_rows, D).astype(jnp.bfloat16)
    middle = local_tokens + jnp.dot(attended_low, output_full, preferred_element_type=jnp.float32)

    scale_two = rms_scale(middle)
    normed_two = middle * scale_two
    normed_two_low = (normed_two * gain_two_f).astype(jnp.bfloat16)
    group_tokens = n_f * tok_rows
    xn2_all = fsdp_gather(normed_two_low, n_f).reshape(group_tokens, D)
    gate_up = jnp.dot(xn2_all, gate_up_tp, preferred_element_type=jnp.float32)
    gate_pre = gate_up[:, :units]
    up_pre = gate_up[:, units:]
    sigmoid = jax.nn.sigmoid(gate_pre)
    hidden_low = (gate_pre * sigmoid * up_pre).astype(jnp.bfloat16)
    ff_part = jnp.dot(hidden_low, down_tp, preferred_element_type=jnp.float32)

    grad_out = cotangent[0]
    grad_all = fsdp_gather(grad_out, n_f).reshape(group_tokens, D)
    down_term, grad_all = lax.optimization_barrier(
        (outer_rows(hidden_low, grad_all).astype(jnp.bfloat16), grad_all)
    )
    down_sum = lax.psum_scatter(down_term, "ctx", scatter_dimension=0, tiled=True)
    hidden_grad = times_transposed(grad_all, down_tp)
    gate_grad = (hidden_grad * up_pre * sigmoid * (1.0 + gate_pre * (1.0 - sigmoid))).astype(
        jnp.bfloat16
    )
    up_grad = (hidden_grad * gate_pre * sigmoid).astype(jnp.bfloat16)
    gate_up_cat = jnp.concatenate([gate_grad, up_grad], axis=1)
    gate_up_term = outer_rows(xn2_all, gate_up_cat)
    ff_pack, gate_up_cat = lax.optimization_barrier((gate_up_term.astype(jnp.bfloat16), gate_up_cat))
    gu_sum = lax.psum_scatter(ff_pack, "ctx", scatter_dimension=0, tiled=True)
    gu_sum = lax.all_to_all(gu_sum.reshape(n_f, rows, 2 * units), "fsdp", 0, 0, tiled=True)
    ff_sum = jnp.transpose(
        gu_sum.reshape(n_f, rows, 2, n_ctx, chunk), (1, 2, 3, 0, 4)
    ).reshape(rows, 2 * ff)
    normed_two_grad = fsdp_reduce(
        times_transposed(gate_up_cat, gate_up_tp).reshape(n_f, tok_rows, D), n_f
    )
    gain_two_term = jnp.sum(normed_two_grad * normed_two, axis=0)
    scaled_two = normed_two_grad * gain_two_f
    middle_grad = grad_out.astype(jnp.float32) + scale_two * (
        scaled_two - normed_two * jnp.mean(scaled_two * normed_two, axis=-1, keepdims=True)
    )
    branch_grad = middle_grad.astype(jnp.bfloat16)
    attended_grad_low = (
        times_transposed(branch_grad, output_full)
        .astype(jnp.bfloat16)
        .reshape(tok_rows, KVH, group_size, HD)
    )
    row_delta = jnp.sum(
        attended_grad_low.astype(jnp.float32) * attended_sum, axis=-1, keepdims=True
    )
    prob_grad = jnp.einsum(
        "qgrd,kgd->qgrk", attended_grad_low, value_block, preferred_element_type=jnp.float32
    )
    score_grad = (probs * (prob_grad - row_delta)).astype(jnp.bfloat16)
    query_accum = jnp.einsum(
        "qgrk,kgd->qgrd", score_grad, key_block, preferred_element_type=jnp.float32
    )
    key_term = jnp.einsum(
        "qgrk,qgrd->kgd", score_grad, query_grouped, preferred_element_type=jnp.float32
    ).reshape(win, KVW)
    value_term = jnp.einsum(
        "qgrk,qgrd->kgd", probs_low, attended_grad_low, preferred_element_type=jnp.float32
    ).reshape(win, KVW)
    kv_term = jnp.concatenate([key_term, value_term], axis=1).reshape(back + 1, tok_rows, 2 * KVW)
    kv_own = kv_term[back].at[0, 0].add(down_sum[0, 0].astype(jnp.float32) * 0.0)
    kv_sum = kv_return(kv_own, kv_term[:back].astype(jnp.bfloat16), n_ctx, back)
    key_grad_low = rotate(kv_sum[:, :KVW] * score_scale, query_positions, KVH, -1.0).astype(
        jnp.bfloat16
    )
    value_grad_low = kv_sum[:, KVW:].astype(jnp.bfloat16)
    query_grad_low = rotate(
        query_accum.reshape(tok_rows, D) * score_scale, query_positions, H, -1.0
    ).astype(jnp.bfloat16)
    projection_cat = jnp.concatenate([query_grad_low, key_grad_low, value_grad_low], axis=1)
    normed_grad = times_transposed(projection_cat, qkv_full)
    gain_one_term = jnp.sum(normed_grad * normed_one, axis=0)
    scaled_one = normed_grad * gain_one_f
    tokens_grad = middle_grad + scale_one * (
        scaled_one - normed_one * jnp.mean(scaled_one * normed_one, axis=-1, keepdims=True)
    )
    gain_term_cols = jnp.pad(
        jnp.stack([gain_one_term, gain_two_term], axis=1), ((0, 0), (0, GAIN_PAD - 2))
    )
    attention_pack = jnp.concatenate(
        [
            outer_rows(normed_low, projection_cat).astype(jnp.bfloat16),
            outer_rows(attended_low, branch_grad).astype(jnp.bfloat16),
            gain_term_cols.astype(jnp.bfloat16),
        ],
        axis=1,
    )
    attention_sum = lax.psum_scatter(
        attention_pack, ALL, scatter_dimension=0, tiled=True
    ).astype(jnp.float32)
    ff_part = ff_part.at[0, 0].add(attention_pack[0, 0].astype(jnp.float32) * 0.0)
    layer_out = middle + fsdp_reduce(ff_part.reshape(n_f, tok_rows, D), n_f)
    ff_sum = ff_sum.astype(jnp.float32)
    return (
        layer_out.astype(jnp.bfloat16)[None],
        tokens_grad[None],
        attention_sum[:, c_g],
        attention_sum[:, :c_k],
        attention_sum[:, c_k:c_v],
        attention_sum[:, c_v:c_o],
        attention_sum[:, c_o:c_g],
        attention_sum[:, c_g + 1],
        ff_sum[:, :ff],
        ff_sum[:, ff : 2 * ff],
        down_sum.astype(jnp.float32),
    )


def solution(mesh):
    weight = P(ALL, None)
    stream = P("fsdp", "ctx", None)
    return jax.shard_map(
        body,
        mesh=mesh,
        in_specs=(
            stream,
            P("fsdp", None),
            P(ALL),
            weight,
            weight,
            weight,
            weight,
            P(ALL),
            weight,
            weight,
            weight,
            stream,
        ),
        out_specs=(
            stream,
            stream,
            P(ALL),
            weight,
            weight,
            weight,
            weight,
            P(ALL),
            weight,
            weight,
            weight,
        ),
        check_vma=False,
    )
```

```python
import functools

import jax
import jax.numpy as jnp
from jax import lax
from jax.experimental import pallas as pl
from jax.experimental.pallas import tpu as pltpu
from jax.sharding import PartitionSpec as P

MESH = pl.DeviceIdType.MESH

D = 1536
H = 16
KVH = 8
HD = 96
KBLK = 512
DOC_MOST = 4096
KVW = 768
GAIN_PAD = 128

EPSILON = 1e-05
ROPE_BASE = 100000.0
MASKED_SCORE = -1e30
ALL = ("ctx", "fsdp")


def rms_scale(values):
    return lax.rsqrt(jnp.mean(values * values, axis=-1, keepdims=True) + EPSILON)


def document_layout(lengths, total):
    starts = jnp.cumsum(lengths) - lengths
    places = jnp.arange(total, dtype=jnp.int32)
    inside = places[:, None] >= starts[None, :]
    doc_ids = jnp.sum(inside.astype(jnp.int32), axis=1) - 1
    doc_starts = jnp.max(jnp.where(inside, starts[None, :], 0), axis=1)
    return (doc_ids, places - doc_starts)


def rotate(values, positions, head_count, direction):
    row_count = values.shape[0]
    half_dim = HD // 2
    inverse_freq = ROPE_BASE ** (-(jnp.arange(half_dim).astype(jnp.float32) * (2.0 / HD)))
    angles = positions.astype(jnp.float32)[:, None] * inverse_freq[None, :]
    cosine = jnp.cos(angles)[:, None, :]
    sine_part = direction * jnp.sin(angles)[:, None, :]
    grouped = values.reshape(row_count, head_count, HD)
    former = grouped[:, :, :half_dim]
    latter = grouped[:, :, half_dim:]
    turned = jnp.concatenate(
        [former * cosine - latter * sine_part, latter * cosine + former * sine_part], axis=2
    )
    return turned.reshape(row_count, head_count * HD)


def outer_rows(left, right):
    return lax.dot_general(
        left, right, (((0,), (0,)), ((), ())), preferred_element_type=jnp.float32
    )


def times_transposed(left, right):
    return lax.dot_general(
        left, right, (((1,), (1,)), ((), ())), preferred_element_type=jnp.float32
    )


def neighbour_barrier(n_ctx, back, c, f):
    barrier = pltpu.get_barrier_semaphore()
    for s in range(1, back + 1):
        for peer in ((c + s) % n_ctx, (c + n_ctx - s) % n_ctx):
            pl.semaphore_signal(barrier, inc=1, device_id=(peer, f), device_id_type=MESH)
    pl.semaphore_wait(barrier, 2 * back)


def kv_share_kernel(n_ctx, back, kv_ref, out_ref, send_sem, recv_sem):
    c = lax.axis_index("ctx")
    f = lax.axis_index("fsdp")
    neighbour_barrier(n_ctx, back, c, f)

    def copy(s, dest):
        return pltpu.make_async_remote_copy(
            src_ref=kv_ref,
            dst_ref=out_ref.at[back - s],
            send_sem=send_sem.at[s - 1],
            recv_sem=recv_sem.at[back - s],
            device_id=(dest, f),
            device_id_type=MESH,
        )

    for s in range(1, back + 1):

        @pl.when(c + s < n_ctx)
        def _():
            copy(s, c + s).start()

    out_ref[back] = kv_ref[...]
    for s in range(1, back + 1):

        @pl.when(c - s < 0)
        def _():
            out_ref[back - s] = jnp.zeros(kv_ref.shape, kv_ref.dtype)

    for s in range(1, back + 1):

        @pl.when(c + s < n_ctx)
        def _():
            copy(s, c + s).wait_send()

        @pl.when(c - s >= 0)
        def _():
            copy(s, c).wait_recv()


def kv_share(kv, n_ctx, back):
    return pl.pallas_call(
        functools.partial(kv_share_kernel, n_ctx, back),
        out_shape=jax.ShapeDtypeStruct((back + 1,) + kv.shape, kv.dtype),
        in_specs=[pl.BlockSpec(memory_space=pltpu.VMEM)],
        out_specs=pl.BlockSpec(memory_space=pltpu.VMEM),
        scratch_shapes=[pltpu.SemaphoreType.DMA((back,)), pltpu.SemaphoreType.DMA((back + 1,))],
        compiler_params=pltpu.CompilerParams(collective_id=0, has_side_effects=True),
    )(kv)


def kv_return_kernel(n_ctx, back, own_ref, g_ref, out_ref, recv_buf, send_sem, recv_sem):
    c = lax.axis_index("ctx")
    f = lax.axis_index("fsdp")
    neighbour_barrier(n_ctx, back, c, f)

    def copy(s, dest):
        return pltpu.make_async_remote_copy(
            src_ref=g_ref.at[back - s],
            dst_ref=recv_buf.at[s - 1],
            send_sem=send_sem.at[s - 1],
            recv_sem=recv_sem.at[s - 1],
            device_id=(dest, f),
            device_id_type=MESH,
        )

    for s in range(1, back + 1):

        @pl.when(c - s >= 0)
        def _():
            copy(s, c - s).start()

    out_ref[...] = own_ref[...]
    for s in range(1, back + 1):

        @pl.when(c + s < n_ctx)
        def _():
            copy(s, c).wait_recv()
            out_ref[...] += recv_buf[s - 1].astype(jnp.float32)

    for s in range(1, back + 1):

        @pl.when(c - s >= 0)
        def _():
            copy(s, c - s).wait_send()


def kv_return(own, g, n_ctx, back):
    return pl.pallas_call(
        functools.partial(kv_return_kernel, n_ctx, back),
        out_shape=jax.ShapeDtypeStruct(own.shape, own.dtype),
        in_specs=[pl.BlockSpec(memory_space=pltpu.VMEM)] * 2,
        out_specs=pl.BlockSpec(memory_space=pltpu.VMEM),
        scratch_shapes=[
            pltpu.VMEM(g.shape, g.dtype),
            pltpu.SemaphoreType.DMA((back,)),
            pltpu.SemaphoreType.DMA((back,)),
        ],
        compiler_params=pltpu.CompilerParams(collective_id=1, has_side_effects=True),
    )(own, g)


def peer_barrier(n_f, c, f):
    barrier = pltpu.get_barrier_semaphore()
    for k in range(1, n_f):
        pl.semaphore_signal(barrier, inc=1, device_id=(c, (f + k) % n_f), device_id_type=MESH)
    pl.semaphore_wait(barrier, n_f - 1)


def group_gather_kernel(n_f, x_ref, out_ref, send_sem, recv_sem):
    c = lax.axis_index("ctx")
    f = lax.axis_index("fsdp")
    peer_barrier(n_f, c, f)
    copies = []
    for k in range(1, n_f):
        copy = pltpu.make_async_remote_copy(
            src_ref=x_ref,
            dst_ref=out_ref.at[f],
            send_sem=send_sem.at[k - 1],
            recv_sem=recv_sem.at[k - 1],
            device_id=(c, (f + k) % n_f),
            device_id_type=MESH,
        )
        copy.start()
        copies.append(copy)
    out_ref[f] = x_ref[...]
    for k in range(1, n_f):
        pltpu.make_async_remote_copy(
            src_ref=x_ref,
            dst_ref=out_ref.at[(f + n_f - k) % n_f],
            send_sem=send_sem.at[k - 1],
            recv_sem=recv_sem.at[k - 1],
            device_id=(c, f),
            device_id_type=MESH,
        ).wait_recv()
    for copy in copies:
        copy.wait_send()


def group_gather(x, n_f):
    return pl.pallas_call(
        functools.partial(group_gather_kernel, n_f),
        out_shape=jax.ShapeDtypeStruct((n_f,) + x.shape, x.dtype),
        in_specs=[pl.BlockSpec(memory_space=pltpu.VMEM)],
        out_specs=pl.BlockSpec(memory_space=pltpu.VMEM),
        scratch_shapes=[pltpu.SemaphoreType.DMA((n_f - 1,)), pltpu.SemaphoreType.DMA((n_f - 1,))],
        compiler_params=pltpu.CompilerParams(collective_id=2, has_side_effects=True),
    )(x)


def group_reduce_kernel(n_f, p_ref, out_ref, recv_buf, send_sem, recv_sem):
    c = lax.axis_index("ctx")
    f = lax.axis_index("fsdp")
    peer_barrier(n_f, c, f)
    copies = []
    for k in range(1, n_f):
        dest = (f + k) % n_f
        copy = pltpu.make_async_remote_copy(
            src_ref=p_ref.at[dest],
            dst_ref=recv_buf.at[k - 1],
            send_sem=send_sem.at[k - 1],
            recv_sem=recv_sem.at[k - 1],
            device_id=(c, dest),
            device_id_type=MESH,
        )
        copy.start()
        copies.append(copy)
    out_ref[...] = p_ref[f]
    for k in range(1, n_f):
        copies[k - 1].wait_recv()
        out_ref[...] += recv_buf[k - 1]
    for copy in copies:
        copy.wait_send()


def group_reduce(p, n_f):
    return pl.pallas_call(
        functools.partial(group_reduce_kernel, n_f),
        out_shape=jax.ShapeDtypeStruct(p.shape[1:], p.dtype),
        in_specs=[pl.BlockSpec(memory_space=pltpu.VMEM)],
        out_specs=pl.BlockSpec(memory_space=pltpu.VMEM),
        scratch_shapes=[
            pltpu.VMEM((n_f - 1,) + p.shape[1:], p.dtype),
            pltpu.SemaphoreType.DMA((n_f - 1,)),
            pltpu.SemaphoreType.DMA((n_f - 1,)),
        ],
        compiler_params=pltpu.CompilerParams(collective_id=3, has_side_effects=True),
    )(p)


def pair_barrier(c, partner, across):
    barrier = pltpu.get_barrier_semaphore()
    pl.semaphore_signal(barrier, inc=1, device_id=(c, partner), device_id_type=MESH)
    pl.semaphore_signal(barrier, inc=1, device_id=(c, across), device_id_type=MESH)
    pl.semaphore_wait(barrier, 2)


def quad_ids():
    c = lax.axis_index("ctx")
    f = lax.axis_index("fsdp")
    partner = f + 1 - 2 * (f % 2)
    across = (f + 2) % 4
    diagonal = (partner + 2) % 4
    return c, f, partner, across, diagonal


def quad_gather_kernel(x_ref, out_ref, send_sem, recv_sem):
    c, f, partner, across, diagonal = quad_ids()
    pair_barrier(c, partner, across)

    def copy(src, slot, dest, k):
        return pltpu.make_async_remote_copy(
            src_ref=src,
            dst_ref=out_ref.at[slot],
            send_sem=send_sem.at[k],
            recv_sem=recv_sem.at[slot],
            device_id=(c, dest),
            device_id_type=MESH,
        )

    first = copy(x_ref, f, across, 0)
    first.start()
    own = copy(x_ref, f, partner, 1)
    own.start()
    out_ref[f] = x_ref[...]
    copy(x_ref, across, f, 0).wait_recv()
    relay = copy(out_ref.at[across], across, partner, 2)
    relay.start()
    copy(x_ref, partner, f, 0).wait_recv()
    copy(x_ref, diagonal, f, 0).wait_recv()
    first.wait_send()
    own.wait_send()
    relay.wait_send()


def quad_gather(x):
    return pl.pallas_call(
        quad_gather_kernel,
        out_shape=jax.ShapeDtypeStruct((4,) + x.shape, x.dtype),
        in_specs=[pl.BlockSpec(memory_space=pltpu.VMEM)],
        out_specs=pl.BlockSpec(memory_space=pltpu.VMEM),
        scratch_shapes=[pltpu.SemaphoreType.DMA((3,)), pltpu.SemaphoreType.DMA((4,))],
        compiler_params=pltpu.CompilerParams(collective_id=4, has_side_effects=True),
    )(x)


def quad_reduce_kernel(p_ref, out_ref, near_buf, far_buf, sum_buf, send_sem, recv_sem):
    c, f, partner, across, diagonal = quad_ids()
    pair_barrier(c, partner, across)

    def copy(src, dst, dest, k):
        return pltpu.make_async_remote_copy(
            src_ref=src,
            dst_ref=dst,
            send_sem=send_sem.at[k],
            recv_sem=recv_sem.at[k],
            device_id=(c, dest),
            device_id_type=MESH,
        )

    to_partner = copy(p_ref.at[partner], near_buf.at[0], partner, 0)
    to_partner.start()
    to_diagonal = copy(p_ref.at[diagonal], near_buf.at[1], partner, 1)
    to_diagonal.start()
    to_partner.wait_recv()
    to_diagonal.wait_recv()
    sum_buf[...] = p_ref[across] + near_buf[1]
    to_across = copy(sum_buf, far_buf, across, 2)
    to_across.start()
    out_ref[...] = p_ref[f] + near_buf[0]
    to_across.wait_recv()
    out_ref[...] += far_buf[...]
    to_partner.wait_send()
    to_diagonal.wait_send()
    to_across.wait_send()


def quad_reduce(p):
    block = p.shape[1:]
    return pl.pallas_call(
        quad_reduce_kernel,
        out_shape=jax.ShapeDtypeStruct(block, p.dtype),
        in_specs=[pl.BlockSpec(memory_space=pltpu.VMEM)],
        out_specs=pl.BlockSpec(memory_space=pltpu.VMEM),
        scratch_shapes=[
            pltpu.VMEM((2,) + block, p.dtype),
            pltpu.VMEM(block, p.dtype),
            pltpu.VMEM(block, p.dtype),
            pltpu.SemaphoreType.DMA((3,)),
            pltpu.SemaphoreType.DMA((3,)),
        ],
        compiler_params=pltpu.CompilerParams(collective_id=5, has_side_effects=True),
    )(p)


def fsdp_gather(x, n_f):
    if n_f == 4:
        return quad_gather(x)
    return group_gather(x, n_f)


def fsdp_reduce(p, n_f):
    if n_f == 4:
        return quad_reduce(p)
    return group_reduce(p, n_f)


def body(
    tokens,
    doc_lengths,
    attention_gain,
    query_weight,
    key_weight,
    value_weight,
    output_weight,
    feedforward_gain,
    gate_weight,
    up_weight,
    down_weight,
    cotangent,
):
    n_dev = lax.axis_size(ALL)
    rows = query_weight.shape[0]
    ff_rows = down_weight.shape[0]
    ff = gate_weight.shape[1]
    local_tokens = tokens[0].astype(jnp.float32)
    tok_rows = local_tokens.shape[0]
    stream_len = tok_rows * lax.axis_size("ctx")
    my_first = lax.axis_index("ctx") * tok_rows

    gain_cols = jnp.pad(
        jnp.stack([attention_gain, feedforward_gain], axis=1), ((0, 0), (0, GAIN_PAD - 2))
    )
    att_full = lax.all_gather(
        jnp.concatenate([query_weight, key_weight, value_weight, output_weight, gain_cols], axis=1),
        ALL,
        axis=0,
        tiled=True,
    )
    c_k = D
    c_v = D + KVW
    c_o = D + 2 * KVW
    c_g = 2 * D + 2 * KVW
    query_full = att_full[:, :c_k]
    key_full = att_full[:, c_k:c_v]
    value_full = att_full[:, c_v:c_o]
    qkv_full = att_full[:, :c_o]
    output_full = att_full[:, c_o:c_g]
    gain_one_f = att_full[:, c_g].astype(jnp.float32)
    gain_two_f = att_full[:, c_g + 1].astype(jnp.float32)

    key_docs_all, places_all = document_layout(doc_lengths[0], stream_len)
    query_docs = lax.dynamic_slice_in_dim(key_docs_all, my_first, tok_rows, 0)
    query_positions = lax.dynamic_slice_in_dim(places_all, my_first, tok_rows, 0)
    query_places = my_first + jnp.arange(tok_rows, dtype=jnp.int32)
    group_size = H // KVH
    score_scale = HD ** (-0.5)

    scale_one = rms_scale(local_tokens)
    normed_one = local_tokens * scale_one
    normed_low = (normed_one * gain_one_f).astype(jnp.bfloat16)
    qkv = jnp.dot(normed_low, qkv_full, preferred_element_type=jnp.float32)
    queries = qkv[:, :D]
    keys_new = qkv[:, D : D + KVW]
    values_new = qkv[:, D + KVW :]
    query_low = rotate(queries, query_positions, H, 1.0).astype(jnp.bfloat16)
    key_low = rotate(keys_new, query_positions, KVH, 1.0).astype(jnp.bfloat16)
    value_low = values_new.astype(jnp.bfloat16)

    n_ctx = lax.axis_size("ctx")
    n_f = lax.axis_size("fsdp")
    chunk = ff_rows
    units = n_ctx * chunk
    gu_parts = jnp.transpose(
        jnp.stack([gate_weight, up_weight], axis=1).reshape(rows, 2, n_ctx, n_f, chunk),
        (3, 0, 1, 2, 4),
    )
    gu_parts = lax.all_to_all(gu_parts, "fsdp", 0, 0, tiled=True).reshape(n_f * rows, 2 * units)
    down_rows = D // (2 * n_ctx)
    ff_pack = jnp.concatenate([gu_parts, down_weight.reshape(down_rows, 2 * units)], axis=0)
    ff_pack = ff_pack.at[0, 0].add(att_full[0, 0] * 0)
    ff_stack = lax.all_gather(
        ff_pack,
        "ctx",
        axis=0,
        tiled=False,
    )
    gate_up_tp = ff_stack[:, : n_f * rows].reshape(n_ctx * n_f * rows, 2 * units)
    down_tp = ff_stack[:, n_f * rows :].reshape(n_ctx, ff_rows, D).reshape(units, D)
    max_doc = min(DOC_MOST, KBLK * (stream_len // (2 * KBLK)))
    back = min(-(-(max_doc - 1) // tok_rows), n_ctx - 1)
    win = (back + 1) * tok_rows
    kv_win = kv_share(
        jnp.concatenate([key_low, value_low], axis=1), n_ctx, back
    ).reshape(win, 2 * KVW)
    docs_pad = jnp.concatenate(
        [jnp.full((back * tok_rows,), -1, jnp.int32), key_docs_all.astype(jnp.int32)]
    )
    key_docs = lax.dynamic_slice_in_dim(docs_pad, my_first, win, 0)
    key_places = my_first - back * tok_rows + jnp.arange(win, dtype=jnp.int32)
    key_block = kv_win[:, :KVW].reshape(win, KVH, HD)
    value_block = kv_win[:, KVW:].reshape(win, KVH, HD)
    query_grouped = query_low.reshape(tok_rows, KVH, group_size, HD)
    allowed = (
        (key_docs[None, :] == query_docs[:, None]) & (key_places[None, :] <= query_places[:, None])
    )[:, None, None, :]
    scores = (
        jnp.einsum("qgrd,kgd->qgrk", query_grouped, key_block, preferred_element_type=jnp.float32)
        * score_scale
    )
    scores = jnp.where(allowed, scores, MASKED_SCORE)
    row_max = jnp.max(scores, axis=-1, keepdims=True)
    exponent = jnp.where(allowed, jnp.exp(scores - row_max), 0.0)
    probs = exponent / jnp.sum(exponent, axis=-1, keepdims=True)
    probs_low = probs.astype(jnp.bfloat16)
    attended_sum = jnp.einsum(
        "qgrk,kgd->qgrd", probs_low, value_block, preferred_element_type=jnp.float32
    )
    attended_low = attended_sum.reshape(tok_rows, D).astype(jnp.bfloat16)
    middle = local_tokens + jnp.dot(attended_low, output_full, preferred_element_type=jnp.float32)

    scale_two = rms_scale(middle)
    normed_two = middle * scale_two
    normed_two_low = (normed_two * gain_two_f).astype(jnp.bfloat16)
    group_tokens = n_f * tok_rows
    xn2_all = fsdp_gather(normed_two_low, n_f).reshape(group_tokens, D)
    gate_up = jnp.dot(xn2_all, gate_up_tp, preferred_element_type=jnp.float32)
    gate_pre = gate_up[:, :units]
    up_pre = gate_up[:, units:]
    sigmoid = jax.nn.sigmoid(gate_pre)
    hidden_low = (gate_pre * sigmoid * up_pre).astype(jnp.bfloat16)
    ff_part = jnp.dot(hidden_low, down_tp, preferred_element_type=jnp.float32)

    grad_out = cotangent[0]
    grad_all = fsdp_gather(grad_out, n_f).reshape(group_tokens, D)
    down_term = outer_rows(hidden_low, grad_all).astype(jnp.bfloat16)
    hidden_grad = times_transposed(grad_all, down_tp)
    gate_grad = (hidden_grad * up_pre * sigmoid * (1.0 + gate_pre * (1.0 - sigmoid))).astype(
        jnp.bfloat16
    )
    up_grad = (hidden_grad * gate_pre * sigmoid).astype(jnp.bfloat16)
    gate_up_cat = jnp.concatenate([gate_grad, up_grad], axis=1)
    gate_up_term = outer_rows(xn2_all, gate_up_cat)
    grad_pack = jnp.concatenate(
        [
            gate_up_term.astype(jnp.bfloat16).reshape(n_ctx, n_f * rows, 2 * units),
            down_term.reshape(n_ctx, down_rows, 2 * units),
        ],
        axis=1,
    ).reshape(n_ctx * (n_f * rows + down_rows), 2 * units)
    grad_pack, gate_up_cat = lax.optimization_barrier((grad_pack, gate_up_cat))
    grad_sum = lax.psum_scatter(grad_pack, "ctx", scatter_dimension=0, tiled=True)
    down_sum = grad_sum[n_f * rows :].reshape(ff_rows, D)
    gu_sum = lax.all_to_all(grad_sum[: n_f * rows].reshape(n_f, rows, 2 * units), "fsdp", 0, 0, tiled=True)
    ff_sum = jnp.transpose(
        gu_sum.reshape(n_f, rows, 2, n_ctx, chunk), (1, 2, 3, 0, 4)
    ).reshape(rows, 2 * ff)
    normed_two_grad = fsdp_reduce(
        times_transposed(gate_up_cat, gate_up_tp).reshape(n_f, tok_rows, D), n_f
    )
    gain_two_term = jnp.sum(normed_two_grad * normed_two, axis=0)
    scaled_two = normed_two_grad * gain_two_f
    middle_grad = grad_out.astype(jnp.float32) + scale_two * (
        scaled_two - normed_two * jnp.mean(scaled_two * normed_two, axis=-1, keepdims=True)
    )
    branch_grad = middle_grad.astype(jnp.bfloat16)
    attended_grad_low = (
        times_transposed(branch_grad, output_full)
        .astype(jnp.bfloat16)
        .reshape(tok_rows, KVH, group_size, HD)
    )
    row_delta = jnp.sum(
        attended_grad_low.astype(jnp.float32) * attended_sum, axis=-1, keepdims=True
    )
    prob_grad = jnp.einsum(
        "qgrd,kgd->qgrk", attended_grad_low, value_block, preferred_element_type=jnp.float32
    )
    score_grad = (probs * (prob_grad - row_delta)).astype(jnp.bfloat16)
    query_accum = jnp.einsum(
        "qgrk,kgd->qgrd", score_grad, key_block, preferred_element_type=jnp.float32
    )
    key_term = jnp.einsum(
        "qgrk,qgrd->kgd", score_grad, query_grouped, preferred_element_type=jnp.float32
    ).reshape(win, KVW)
    value_term = jnp.einsum(
        "qgrk,qgrd->kgd", probs_low, attended_grad_low, preferred_element_type=jnp.float32
    ).reshape(win, KVW)
    kv_term = jnp.concatenate([key_term, value_term], axis=1).reshape(back + 1, tok_rows, 2 * KVW)
    kv_sum = kv_return(kv_term[back], kv_term[:back].astype(jnp.bfloat16), n_ctx, back)
    key_grad_low = rotate(kv_sum[:, :KVW] * score_scale, query_positions, KVH, -1.0).astype(
        jnp.bfloat16
    )
    value_grad_low = kv_sum[:, KVW:].astype(jnp.bfloat16)
    query_grad_low = rotate(
        query_accum.reshape(tok_rows, D) * score_scale, query_positions, H, -1.0
    ).astype(jnp.bfloat16)
    projection_cat = jnp.concatenate([query_grad_low, key_grad_low, value_grad_low], axis=1)
    normed_grad = times_transposed(projection_cat, qkv_full)
    gain_one_term = jnp.sum(normed_grad * normed_one, axis=0)
    scaled_one = normed_grad * gain_one_f
    tokens_grad = middle_grad + scale_one * (
        scaled_one - normed_one * jnp.mean(scaled_one * normed_one, axis=-1, keepdims=True)
    )
    gain_term_cols = jnp.pad(
        jnp.stack([gain_one_term, gain_two_term], axis=1), ((0, 0), (0, GAIN_PAD - 2))
    )
    attention_pack = jnp.concatenate(
        [
            outer_rows(normed_low, projection_cat).astype(jnp.bfloat16),
            outer_rows(attended_low, branch_grad).astype(jnp.bfloat16),
            gain_term_cols.astype(jnp.bfloat16),
        ],
        axis=1,
    )
    attention_sum = lax.psum_scatter(
        attention_pack, ALL, scatter_dimension=0, tiled=True
    ).astype(jnp.float32)
    ff_part = ff_part.at[0, 0].add(attention_pack[0, 0].astype(jnp.float32) * 0.0)
    layer_out = middle + fsdp_reduce(ff_part.reshape(n_f, tok_rows, D), n_f)
    ff_sum = ff_sum.astype(jnp.float32)
    return (
        layer_out.astype(jnp.bfloat16)[None],
        tokens_grad[None],
        attention_sum[:, c_g],
        attention_sum[:, :c_k],
        attention_sum[:, c_k:c_v],
        attention_sum[:, c_v:c_o],
        attention_sum[:, c_o:c_g],
        attention_sum[:, c_g + 1],
        ff_sum[:, :ff],
        ff_sum[:, ff : 2 * ff],
        down_sum.astype(jnp.float32),
    )


def solution(mesh):
    weight = P(ALL, None)
    stream = P("fsdp", "ctx", None)
    return jax.shard_map(
        body,
        mesh=mesh,
        in_specs=(
            stream,
            P("fsdp", None),
            P(ALL),
            weight,
            weight,
            weight,
            weight,
            P(ALL),
            weight,
            weight,
            weight,
            stream,
        ),
        out_specs=(
            stream,
            stream,
            P(ALL),
            weight,
            weight,
            weight,
            weight,
            P(ALL),
            weight,
            weight,
            weight,
        ),
        check_vma=False,
    )
```

```python
import functools

import jax
import jax.numpy as jnp
from jax import lax
from jax.experimental import pallas as pl
from jax.experimental.pallas import tpu as pltpu
from jax.sharding import PartitionSpec as P

MESH = pl.DeviceIdType.MESH

D = 1536
H = 16
KVH = 8
HD = 96
KBLK = 512
DOC_MOST = 4096
KVW = 768
GAIN_PAD = 128

EPSILON = 1e-05
ROPE_BASE = 100000.0
MASKED_SCORE = -1e30
ALL = ("ctx", "fsdp")


def rms_scale(values):
    return lax.rsqrt(jnp.mean(values * values, axis=-1, keepdims=True) + EPSILON)


def document_layout(lengths, total):
    starts = jnp.cumsum(lengths) - lengths
    places = jnp.arange(total, dtype=jnp.int32)
    inside = places[:, None] >= starts[None, :]
    doc_ids = jnp.sum(inside.astype(jnp.int32), axis=1) - 1
    doc_starts = jnp.max(jnp.where(inside, starts[None, :], 0), axis=1)
    return (doc_ids, places - doc_starts)


def rotate(values, positions, head_count, direction):
    row_count = values.shape[0]
    half_dim = HD // 2
    inverse_freq = ROPE_BASE ** (-(jnp.arange(half_dim).astype(jnp.float32) * (2.0 / HD)))
    angles = positions.astype(jnp.float32)[:, None] * inverse_freq[None, :]
    cosine = jnp.cos(angles)[:, None, :]
    sine_part = direction * jnp.sin(angles)[:, None, :]
    grouped = values.reshape(row_count, head_count, HD)
    former = grouped[:, :, :half_dim]
    latter = grouped[:, :, half_dim:]
    turned = jnp.concatenate(
        [former * cosine - latter * sine_part, latter * cosine + former * sine_part], axis=2
    )
    return turned.reshape(row_count, head_count * HD)


def outer_rows(left, right):
    return lax.dot_general(
        left, right, (((0,), (0,)), ((), ())), preferred_element_type=jnp.float32
    )


def times_transposed(left, right):
    return lax.dot_general(
        left, right, (((1,), (1,)), ((), ())), preferred_element_type=jnp.float32
    )


def neighbour_barrier(n_ctx, back, c, f):
    barrier = pltpu.get_barrier_semaphore()
    for s in range(1, back + 1):
        for peer in ((c + s) % n_ctx, (c + n_ctx - s) % n_ctx):
            pl.semaphore_signal(barrier, inc=1, device_id=(peer, f), device_id_type=MESH)
    pl.semaphore_wait(barrier, 2 * back)


def kv_share_kernel(n_ctx, back, kv_ref, out_ref, send_sem, recv_sem):
    c = lax.axis_index("ctx")
    f = lax.axis_index("fsdp")
    neighbour_barrier(n_ctx, back, c, f)

    def copy(s, dest):
        return pltpu.make_async_remote_copy(
            src_ref=kv_ref,
            dst_ref=out_ref.at[back - s],
            send_sem=send_sem.at[s - 1],
            recv_sem=recv_sem.at[back - s],
            device_id=(dest, f),
            device_id_type=MESH,
        )

    for s in range(1, back + 1):

        @pl.when(c + s < n_ctx)
        def _():
            copy(s, c + s).start()

    out_ref[back] = kv_ref[...]
    for s in range(1, back + 1):

        @pl.when(c - s < 0)
        def _():
            out_ref[back - s] = jnp.zeros(kv_ref.shape, kv_ref.dtype)

    for s in range(1, back + 1):

        @pl.when(c + s < n_ctx)
        def _():
            copy(s, c + s).wait_send()

        @pl.when(c - s >= 0)
        def _():
            copy(s, c).wait_recv()


def kv_share(kv, n_ctx, back):
    return pl.pallas_call(
        functools.partial(kv_share_kernel, n_ctx, back),
        out_shape=jax.ShapeDtypeStruct((back + 1,) + kv.shape, kv.dtype),
        in_specs=[pl.BlockSpec(memory_space=pltpu.VMEM)],
        out_specs=pl.BlockSpec(memory_space=pltpu.VMEM),
        scratch_shapes=[pltpu.SemaphoreType.DMA((back,)), pltpu.SemaphoreType.DMA((back + 1,))],
        compiler_params=pltpu.CompilerParams(collective_id=0, has_side_effects=True),
    )(kv)


def kv_return_kernel(n_ctx, back, own_ref, g_ref, out_ref, recv_buf, send_sem, recv_sem):
    c = lax.axis_index("ctx")
    f = lax.axis_index("fsdp")
    neighbour_barrier(n_ctx, back, c, f)

    def copy(s, dest):
        return pltpu.make_async_remote_copy(
            src_ref=g_ref.at[back - s],
            dst_ref=recv_buf.at[s - 1],
            send_sem=send_sem.at[s - 1],
            recv_sem=recv_sem.at[s - 1],
            device_id=(dest, f),
            device_id_type=MESH,
        )

    for s in range(1, back + 1):

        @pl.when(c - s >= 0)
        def _():
            copy(s, c - s).start()

    out_ref[...] = own_ref[...]
    for s in range(1, back + 1):

        @pl.when(c + s < n_ctx)
        def _():
            copy(s, c).wait_recv()
            out_ref[...] += recv_buf[s - 1].astype(jnp.float32)

    for s in range(1, back + 1):

        @pl.when(c - s >= 0)
        def _():
            copy(s, c - s).wait_send()


def kv_return(own, g, n_ctx, back):
    return pl.pallas_call(
        functools.partial(kv_return_kernel, n_ctx, back),
        out_shape=jax.ShapeDtypeStruct(own.shape, own.dtype),
        in_specs=[pl.BlockSpec(memory_space=pltpu.VMEM)] * 2,
        out_specs=pl.BlockSpec(memory_space=pltpu.VMEM),
        scratch_shapes=[
            pltpu.VMEM(g.shape, g.dtype),
            pltpu.SemaphoreType.DMA((back,)),
            pltpu.SemaphoreType.DMA((back,)),
        ],
        compiler_params=pltpu.CompilerParams(collective_id=1, has_side_effects=True),
    )(own, g)


def peer_barrier(n_f, c, f):
    barrier = pltpu.get_barrier_semaphore()
    for k in range(1, n_f):
        pl.semaphore_signal(barrier, inc=1, device_id=(c, (f + k) % n_f), device_id_type=MESH)
    pl.semaphore_wait(barrier, n_f - 1)


def group_gather_kernel(n_f, x_ref, out_ref, send_sem, recv_sem):
    c = lax.axis_index("ctx")
    f = lax.axis_index("fsdp")
    peer_barrier(n_f, c, f)
    copies = []
    for k in range(1, n_f):
        copy = pltpu.make_async_remote_copy(
            src_ref=x_ref,
            dst_ref=out_ref.at[f],
            send_sem=send_sem.at[k - 1],
            recv_sem=recv_sem.at[k - 1],
            device_id=(c, (f + k) % n_f),
            device_id_type=MESH,
        )
        copy.start()
        copies.append(copy)
    out_ref[f] = x_ref[...]
    for k in range(1, n_f):
        pltpu.make_async_remote_copy(
            src_ref=x_ref,
            dst_ref=out_ref.at[(f + n_f - k) % n_f],
            send_sem=send_sem.at[k - 1],
            recv_sem=recv_sem.at[k - 1],
            device_id=(c, f),
            device_id_type=MESH,
        ).wait_recv()
    for copy in copies:
        copy.wait_send()


def group_gather(x, n_f):
    return pl.pallas_call(
        functools.partial(group_gather_kernel, n_f),
        out_shape=jax.ShapeDtypeStruct((n_f,) + x.shape, x.dtype),
        in_specs=[pl.BlockSpec(memory_space=pltpu.VMEM)],
        out_specs=pl.BlockSpec(memory_space=pltpu.VMEM),
        scratch_shapes=[pltpu.SemaphoreType.DMA((n_f - 1,)), pltpu.SemaphoreType.DMA((n_f - 1,))],
        compiler_params=pltpu.CompilerParams(collective_id=2, has_side_effects=True),
    )(x)


def group_reduce_kernel(n_f, p_ref, out_ref, recv_buf, send_sem, recv_sem):
    c = lax.axis_index("ctx")
    f = lax.axis_index("fsdp")
    peer_barrier(n_f, c, f)
    copies = []
    for k in range(1, n_f):
        dest = (f + k) % n_f
        copy = pltpu.make_async_remote_copy(
            src_ref=p_ref.at[dest],
            dst_ref=recv_buf.at[k - 1],
            send_sem=send_sem.at[k - 1],
            recv_sem=recv_sem.at[k - 1],
            device_id=(c, dest),
            device_id_type=MESH,
        )
        copy.start()
        copies.append(copy)
    out_ref[...] = p_ref[f]
    for k in range(1, n_f):
        copies[k - 1].wait_recv()
        out_ref[...] += recv_buf[k - 1]
    for copy in copies:
        copy.wait_send()


def group_reduce(p, n_f):
    return pl.pallas_call(
        functools.partial(group_reduce_kernel, n_f),
        out_shape=jax.ShapeDtypeStruct(p.shape[1:], p.dtype),
        in_specs=[pl.BlockSpec(memory_space=pltpu.VMEM)],
        out_specs=pl.BlockSpec(memory_space=pltpu.VMEM),
        scratch_shapes=[
            pltpu.VMEM((n_f - 1,) + p.shape[1:], p.dtype),
            pltpu.SemaphoreType.DMA((n_f - 1,)),
            pltpu.SemaphoreType.DMA((n_f - 1,)),
        ],
        compiler_params=pltpu.CompilerParams(collective_id=3, has_side_effects=True),
    )(p)


def pair_barrier(c, partner, across):
    barrier = pltpu.get_barrier_semaphore()
    pl.semaphore_signal(barrier, inc=1, device_id=(c, partner), device_id_type=MESH)
    pl.semaphore_signal(barrier, inc=1, device_id=(c, across), device_id_type=MESH)
    pl.semaphore_wait(barrier, 2)


def quad_ids():
    c = lax.axis_index("ctx")
    f = lax.axis_index("fsdp")
    partner = f + 1 - 2 * (f % 2)
    across = (f + 2) % 4
    diagonal = (partner + 2) % 4
    return c, f, partner, across, diagonal


def quad_gather_kernel(x_ref, out_ref, send_sem, recv_sem):
    c, f, partner, across, diagonal = quad_ids()
    pair_barrier(c, partner, across)

    def copy(src, slot, dest, k):
        return pltpu.make_async_remote_copy(
            src_ref=src,
            dst_ref=out_ref.at[slot],
            send_sem=send_sem.at[k],
            recv_sem=recv_sem.at[slot],
            device_id=(c, dest),
            device_id_type=MESH,
        )

    first = copy(x_ref, f, across, 0)
    first.start()
    own = copy(x_ref, f, partner, 1)
    own.start()
    out_ref[f] = x_ref[...]
    copy(x_ref, across, f, 0).wait_recv()
    relay = copy(out_ref.at[across], across, partner, 2)
    relay.start()
    copy(x_ref, partner, f, 0).wait_recv()
    copy(x_ref, diagonal, f, 0).wait_recv()
    first.wait_send()
    own.wait_send()
    relay.wait_send()


def quad_gather(x):
    return pl.pallas_call(
        quad_gather_kernel,
        out_shape=jax.ShapeDtypeStruct((4,) + x.shape, x.dtype),
        in_specs=[pl.BlockSpec(memory_space=pltpu.VMEM)],
        out_specs=pl.BlockSpec(memory_space=pltpu.VMEM),
        scratch_shapes=[pltpu.SemaphoreType.DMA((3,)), pltpu.SemaphoreType.DMA((4,))],
        compiler_params=pltpu.CompilerParams(collective_id=4, has_side_effects=True),
    )(x)


def quad_reduce_kernel(p_ref, out_ref, near_buf, far_buf, sum_buf, send_sem, recv_sem):
    c, f, partner, across, diagonal = quad_ids()
    pair_barrier(c, partner, across)

    def copy(src, dst, dest, k):
        return pltpu.make_async_remote_copy(
            src_ref=src,
            dst_ref=dst,
            send_sem=send_sem.at[k],
            recv_sem=recv_sem.at[k],
            device_id=(c, dest),
            device_id_type=MESH,
        )

    to_partner = copy(p_ref.at[partner], near_buf.at[0], partner, 0)
    to_partner.start()
    to_diagonal = copy(p_ref.at[diagonal], near_buf.at[1], partner, 1)
    to_diagonal.start()
    to_partner.wait_recv()
    to_diagonal.wait_recv()
    sum_buf[...] = (p_ref[across] + near_buf[1]).astype(sum_buf.dtype)
    to_across = copy(sum_buf, far_buf, across, 2)
    to_across.start()
    out_ref[...] = p_ref[f] + near_buf[0]
    to_across.wait_recv()
    out_ref[...] += far_buf[...].astype(out_ref.dtype)
    to_partner.wait_send()
    to_diagonal.wait_send()
    to_across.wait_send()


def quad_reduce(p):
    block = p.shape[1:]
    return pl.pallas_call(
        quad_reduce_kernel,
        out_shape=jax.ShapeDtypeStruct(block, p.dtype),
        in_specs=[pl.BlockSpec(memory_space=pltpu.VMEM)],
        out_specs=pl.BlockSpec(memory_space=pltpu.VMEM),
        scratch_shapes=[
            pltpu.VMEM((2,) + block, p.dtype),
            pltpu.VMEM(block, jnp.bfloat16),
            pltpu.VMEM(block, jnp.bfloat16),
            pltpu.SemaphoreType.DMA((3,)),
            pltpu.SemaphoreType.DMA((3,)),
        ],
        compiler_params=pltpu.CompilerParams(collective_id=5, has_side_effects=True),
    )(p)


def fsdp_gather(x, n_f):
    if n_f == 4:
        return quad_gather(x)
    return group_gather(x, n_f)


def fsdp_reduce(p, n_f):
    if n_f == 4:
        return quad_reduce(p)
    return group_reduce(p, n_f)


def body(
    tokens,
    doc_lengths,
    attention_gain,
    query_weight,
    key_weight,
    value_weight,
    output_weight,
    feedforward_gain,
    gate_weight,
    up_weight,
    down_weight,
    cotangent,
):
    n_dev = lax.axis_size(ALL)
    rows = query_weight.shape[0]
    ff_rows = down_weight.shape[0]
    ff = gate_weight.shape[1]
    local_tokens = tokens[0].astype(jnp.float32)
    tok_rows = local_tokens.shape[0]
    stream_len = tok_rows * lax.axis_size("ctx")
    my_first = lax.axis_index("ctx") * tok_rows

    gain_cols = jnp.pad(
        jnp.stack([attention_gain, feedforward_gain], axis=1), ((0, 0), (0, GAIN_PAD - 2))
    )
    att_full = lax.all_gather(
        jnp.concatenate([query_weight, key_weight, value_weight, output_weight, gain_cols], axis=1),
        ALL,
        axis=0,
        tiled=True,
    )
    c_k = D
    c_v = D + KVW
    c_o = D + 2 * KVW
    c_g = 2 * D + 2 * KVW
    query_full = att_full[:, :c_k]
    key_full = att_full[:, c_k:c_v]
    value_full = att_full[:, c_v:c_o]
    qkv_full = att_full[:, :c_o]
    output_full = att_full[:, c_o:c_g]
    gain_one_f = att_full[:, c_g].astype(jnp.float32)
    gain_two_f = att_full[:, c_g + 1].astype(jnp.float32)

    key_docs_all, places_all = document_layout(doc_lengths[0], stream_len)
    query_docs = lax.dynamic_slice_in_dim(key_docs_all, my_first, tok_rows, 0)
    query_positions = lax.dynamic_slice_in_dim(places_all, my_first, tok_rows, 0)
    query_places = my_first + jnp.arange(tok_rows, dtype=jnp.int32)
    group_size = H // KVH
    score_scale = HD ** (-0.5)

    scale_one = rms_scale(local_tokens)
    normed_one = local_tokens * scale_one
    normed_low = (normed_one * gain_one_f).astype(jnp.bfloat16)
    qkv = jnp.dot(normed_low, qkv_full, preferred_element_type=jnp.float32)
    queries = qkv[:, :D]
    keys_new = qkv[:, D : D + KVW]
    values_new = qkv[:, D + KVW :]
    query_low = rotate(queries, query_positions, H, 1.0).astype(jnp.bfloat16)
    key_low = rotate(keys_new, query_positions, KVH, 1.0).astype(jnp.bfloat16)
    value_low = values_new.astype(jnp.bfloat16)

    n_ctx = lax.axis_size("ctx")
    n_f = lax.axis_size("fsdp")
    chunk = ff_rows
    units = n_ctx * chunk
    gu_parts = jnp.transpose(
        jnp.stack([gate_weight, up_weight], axis=1).reshape(rows, 2, n_ctx, n_f, chunk),
        (3, 0, 1, 2, 4),
    )
    gu_parts = lax.all_to_all(gu_parts, "fsdp", 0, 0, tiled=True).reshape(n_f * rows, 2 * units)
    down_rows = D // (2 * n_ctx)
    ff_pack = jnp.concatenate([gu_parts, down_weight.reshape(down_rows, 2 * units)], axis=0)
    ff_pack = ff_pack.at[0, 0].add(att_full[0, 0] * 0)
    ff_stack = lax.all_gather(
        ff_pack,
        "ctx",
        axis=0,
        tiled=False,
    )
    gate_up_tp = ff_stack[:, : n_f * rows].reshape(n_ctx * n_f * rows, 2 * units)
    down_tp = ff_stack[:, n_f * rows :].reshape(n_ctx, ff_rows, D).reshape(units, D)
    max_doc = min(DOC_MOST, KBLK * (stream_len // (2 * KBLK)))
    back = min(-(-(max_doc - 1) // tok_rows), n_ctx - 1)
    win = (back + 1) * tok_rows
    kv_win = kv_share(
        jnp.concatenate([key_low, value_low], axis=1), n_ctx, back
    ).reshape(win, 2 * KVW)
    docs_pad = jnp.concatenate(
        [jnp.full((back * tok_rows,), -1, jnp.int32), key_docs_all.astype(jnp.int32)]
    )
    key_docs = lax.dynamic_slice_in_dim(docs_pad, my_first, win, 0)
    key_places = my_first - back * tok_rows + jnp.arange(win, dtype=jnp.int32)
    key_block = kv_win[:, :KVW].reshape(win, KVH, HD)
    value_block = kv_win[:, KVW:].reshape(win, KVH, HD)
    query_grouped = query_low.reshape(tok_rows, KVH, group_size, HD)
    allowed = (
        (key_docs[None, :] == query_docs[:, None]) & (key_places[None, :] <= query_places[:, None])
    )[:, None, None, :]
    scores = (
        jnp.einsum("qgrd,kgd->qgrk", query_grouped, key_block, preferred_element_type=jnp.float32)
        * score_scale
    )
    scores = jnp.where(allowed, scores, MASKED_SCORE)
    row_max = jnp.max(scores, axis=-1, keepdims=True)
    exponent = jnp.where(allowed, jnp.exp(scores - row_max), 0.0)
    probs = exponent / jnp.sum(exponent, axis=-1, keepdims=True)
    probs_low = probs.astype(jnp.bfloat16)
    attended_sum = jnp.einsum(
        "qgrk,kgd->qgrd", probs_low, value_block, preferred_element_type=jnp.float32
    )
    attended_low = attended_sum.reshape(tok_rows, D).astype(jnp.bfloat16)
    middle = local_tokens + jnp.dot(attended_low, output_full, preferred_element_type=jnp.float32)

    scale_two = rms_scale(middle)
    normed_two = middle * scale_two
    normed_two_low = (normed_two * gain_two_f).astype(jnp.bfloat16)
    group_tokens = n_f * tok_rows
    xn2_all = fsdp_gather(normed_two_low, n_f).reshape(group_tokens, D)
    gate_up = jnp.dot(xn2_all, gate_up_tp, preferred_element_type=jnp.float32)
    gate_pre = gate_up[:, :units]
    up_pre = gate_up[:, units:]
    sigmoid = jax.nn.sigmoid(gate_pre)
    hidden_low = (gate_pre * sigmoid * up_pre).astype(jnp.bfloat16)
    ff_part = jnp.dot(hidden_low, down_tp, preferred_element_type=jnp.float32)

    grad_out = cotangent[0]
    grad_all = fsdp_gather(grad_out, n_f).reshape(group_tokens, D)
    down_term = outer_rows(hidden_low, grad_all).astype(jnp.bfloat16)
    hidden_grad = times_transposed(grad_all, down_tp)
    gate_grad = (hidden_grad * up_pre * sigmoid * (1.0 + gate_pre * (1.0 - sigmoid))).astype(
        jnp.bfloat16
    )
    up_grad = (hidden_grad * gate_pre * sigmoid).astype(jnp.bfloat16)
    gate_up_cat = jnp.concatenate([gate_grad, up_grad], axis=1)
    gate_up_term = outer_rows(xn2_all, gate_up_cat)
    grad_pack = jnp.concatenate(
        [
            gate_up_term.astype(jnp.bfloat16).reshape(n_ctx, n_f * rows, 2 * units),
            down_term.reshape(n_ctx, down_rows, 2 * units),
        ],
        axis=1,
    ).reshape(n_ctx * (n_f * rows + down_rows), 2 * units)
    grad_pack, gate_up_cat = lax.optimization_barrier((grad_pack, gate_up_cat))
    grad_sum = lax.psum_scatter(grad_pack, "ctx", scatter_dimension=0, tiled=True)
    down_sum = grad_sum[n_f * rows :].reshape(ff_rows, D)
    gu_sum = lax.all_to_all(grad_sum[: n_f * rows].reshape(n_f, rows, 2 * units), "fsdp", 0, 0, tiled=True)
    ff_sum = jnp.transpose(
        gu_sum.reshape(n_f, rows, 2, n_ctx, chunk), (1, 2, 3, 0, 4)
    ).reshape(rows, 2 * ff)
    normed_two_grad = fsdp_reduce(
        times_transposed(gate_up_cat, gate_up_tp).reshape(n_f, tok_rows, D), n_f
    )
    gain_two_term = jnp.sum(normed_two_grad * normed_two, axis=0)
    scaled_two = normed_two_grad * gain_two_f
    middle_grad = grad_out.astype(jnp.float32) + scale_two * (
        scaled_two - normed_two * jnp.mean(scaled_two * normed_two, axis=-1, keepdims=True)
    )
    branch_grad = middle_grad.astype(jnp.bfloat16)
    attended_grad_low = (
        times_transposed(branch_grad, output_full)
        .astype(jnp.bfloat16)
        .reshape(tok_rows, KVH, group_size, HD)
    )
    row_delta = jnp.sum(
        attended_grad_low.astype(jnp.float32) * attended_sum, axis=-1, keepdims=True
    )
    prob_grad = jnp.einsum(
        "qgrd,kgd->qgrk", attended_grad_low, value_block, preferred_element_type=jnp.float32
    )
    score_grad = (probs * (prob_grad - row_delta)).astype(jnp.bfloat16)
    query_accum = jnp.einsum(
        "qgrk,kgd->qgrd", score_grad, key_block, preferred_element_type=jnp.float32
    )
    key_term = jnp.einsum(
        "qgrk,qgrd->kgd", score_grad, query_grouped, preferred_element_type=jnp.float32
    ).reshape(win, KVW)
    value_term = jnp.einsum(
        "qgrk,qgrd->kgd", probs_low, attended_grad_low, preferred_element_type=jnp.float32
    ).reshape(win, KVW)
    kv_term = jnp.concatenate([key_term, value_term], axis=1).reshape(back + 1, tok_rows, 2 * KVW)
    kv_sum = kv_return(kv_term[back], kv_term[:back].astype(jnp.bfloat16), n_ctx, back)
    key_grad_low = rotate(kv_sum[:, :KVW] * score_scale, query_positions, KVH, -1.0).astype(
        jnp.bfloat16
    )
    value_grad_low = kv_sum[:, KVW:].astype(jnp.bfloat16)
    query_grad_low = rotate(
        query_accum.reshape(tok_rows, D) * score_scale, query_positions, H, -1.0
    ).astype(jnp.bfloat16)
    projection_cat = jnp.concatenate([query_grad_low, key_grad_low, value_grad_low], axis=1)
    normed_grad = times_transposed(projection_cat, qkv_full)
    gain_one_term = jnp.sum(normed_grad * normed_one, axis=0)
    scaled_one = normed_grad * gain_one_f
    tokens_grad = middle_grad + scale_one * (
        scaled_one - normed_one * jnp.mean(scaled_one * normed_one, axis=-1, keepdims=True)
    )
    gain_term_cols = jnp.pad(
        jnp.stack([gain_one_term, gain_two_term], axis=1), ((0, 0), (0, GAIN_PAD - 2))
    )
    attention_pack = jnp.concatenate(
        [
            outer_rows(normed_low, projection_cat).astype(jnp.bfloat16),
            outer_rows(attended_low, branch_grad).astype(jnp.bfloat16),
            gain_term_cols.astype(jnp.bfloat16),
        ],
        axis=1,
    )
    attention_sum = lax.psum_scatter(
        attention_pack, ALL, scatter_dimension=0, tiled=True
    ).astype(jnp.float32)
    ff_part = ff_part.at[0, 0].add(attention_pack[0, 0].astype(jnp.float32) * 0.0)
    layer_out = middle + fsdp_reduce(ff_part.reshape(n_f, tok_rows, D), n_f)
    ff_sum = ff_sum.astype(jnp.float32)
    return (
        layer_out.astype(jnp.bfloat16)[None],
        tokens_grad[None],
        attention_sum[:, c_g],
        attention_sum[:, :c_k],
        attention_sum[:, c_k:c_v],
        attention_sum[:, c_v:c_o],
        attention_sum[:, c_o:c_g],
        attention_sum[:, c_g + 1],
        ff_sum[:, :ff],
        ff_sum[:, ff : 2 * ff],
        down_sum.astype(jnp.float32),
    )


def solution(mesh):
    weight = P(ALL, None)
    stream = P("fsdp", "ctx", None)
    return jax.shard_map(
        body,
        mesh=mesh,
        in_specs=(
            stream,
            P("fsdp", None),
            P(ALL),
            weight,
            weight,
            weight,
            weight,
            P(ALL),
            weight,
            weight,
            weight,
            stream,
        ),
        out_specs=(
            stream,
            stream,
            P(ALL),
            weight,
            weight,
            weight,
            weight,
            P(ALL),
            weight,
            weight,
            weight,
        ),
        check_vma=False,
    )
```

```python
import functools

import jax
import jax.numpy as jnp
from jax import lax
from jax.experimental import pallas as pl
from jax.experimental.pallas import tpu as pltpu
from jax.sharding import PartitionSpec as P

MESH = pl.DeviceIdType.MESH

D = 1536
H = 16
KVH = 8
HD = 96
KBLK = 512
DOC_MOST = 4096
KVW = 768
GAIN_PAD = 128

EPSILON = 1e-05
ROPE_BASE = 100000.0
MASKED_SCORE = -1e30
ALL = ("ctx", "fsdp")


def rms_scale(values):
    return lax.rsqrt(jnp.mean(values * values, axis=-1, keepdims=True) + EPSILON)


def document_layout(lengths, total):
    starts = jnp.cumsum(lengths) - lengths
    places = jnp.arange(total, dtype=jnp.int32)
    inside = places[:, None] >= starts[None, :]
    doc_ids = jnp.sum(inside.astype(jnp.int32), axis=1) - 1
    doc_starts = jnp.max(jnp.where(inside, starts[None, :], 0), axis=1)
    return (doc_ids, places - doc_starts)


def rotate(values, positions, head_count, direction):
    row_count = values.shape[0]
    half_dim = HD // 2
    inverse_freq = ROPE_BASE ** (-(jnp.arange(half_dim).astype(jnp.float32) * (2.0 / HD)))
    angles = positions.astype(jnp.float32)[:, None] * inverse_freq[None, :]
    cosine = jnp.cos(angles)[:, None, :]
    sine_part = direction * jnp.sin(angles)[:, None, :]
    grouped = values.reshape(row_count, head_count, HD)
    former = grouped[:, :, :half_dim]
    latter = grouped[:, :, half_dim:]
    turned = jnp.concatenate(
        [former * cosine - latter * sine_part, latter * cosine + former * sine_part], axis=2
    )
    return turned.reshape(row_count, head_count * HD)


def outer_rows(left, right):
    return lax.dot_general(
        left, right, (((0,), (0,)), ((), ())), preferred_element_type=jnp.float32
    )


def times_transposed(left, right):
    return lax.dot_general(
        left, right, (((1,), (1,)), ((), ())), preferred_element_type=jnp.float32
    )


def neighbour_barrier(n_ctx, back, c, f):
    barrier = pltpu.get_barrier_semaphore()
    for s in range(1, back + 1):
        for peer in ((c + s) % n_ctx, (c + n_ctx - s) % n_ctx):
            pl.semaphore_signal(barrier, inc=1, device_id=(peer, f), device_id_type=MESH)
    pl.semaphore_wait(barrier, 2 * back)


def kv_share_kernel(n_ctx, back, kv_ref, out_ref, send_sem, recv_sem):
    c = lax.axis_index("ctx")
    f = lax.axis_index("fsdp")
    neighbour_barrier(n_ctx, back, c, f)

    def copy(s, dest):
        return pltpu.make_async_remote_copy(
            src_ref=kv_ref,
            dst_ref=out_ref.at[back - s],
            send_sem=send_sem.at[s - 1],
            recv_sem=recv_sem.at[back - s],
            device_id=(dest, f),
            device_id_type=MESH,
        )

    for s in range(1, back + 1):

        @pl.when(c + s < n_ctx)
        def _():
            copy(s, c + s).start()

    out_ref[back] = kv_ref[...]
    for s in range(1, back + 1):

        @pl.when(c - s < 0)
        def _():
            out_ref[back - s] = jnp.zeros(kv_ref.shape, kv_ref.dtype)

    for s in range(1, back + 1):

        @pl.when(c + s < n_ctx)
        def _():
            copy(s, c + s).wait_send()

        @pl.when(c - s >= 0)
        def _():
            copy(s, c).wait_recv()


def kv_share(kv, n_ctx, back):
    return pl.pallas_call(
        functools.partial(kv_share_kernel, n_ctx, back),
        out_shape=jax.ShapeDtypeStruct((back + 1,) + kv.shape, kv.dtype),
        in_specs=[pl.BlockSpec(memory_space=pltpu.VMEM)],
        out_specs=pl.BlockSpec(memory_space=pltpu.VMEM),
        scratch_shapes=[pltpu.SemaphoreType.DMA((back,)), pltpu.SemaphoreType.DMA((back + 1,))],
        compiler_params=pltpu.CompilerParams(collective_id=0, has_side_effects=True),
    )(kv)


def kv_return_kernel(n_ctx, back, own_ref, g_ref, out_ref, recv_buf, send_sem, recv_sem):
    c = lax.axis_index("ctx")
    f = lax.axis_index("fsdp")
    neighbour_barrier(n_ctx, back, c, f)

    def copy(s, dest):
        return pltpu.make_async_remote_copy(
            src_ref=g_ref.at[back - s],
            dst_ref=recv_buf.at[s - 1],
            send_sem=send_sem.at[s - 1],
            recv_sem=recv_sem.at[s - 1],
            device_id=(dest, f),
            device_id_type=MESH,
        )

    for s in range(1, back + 1):

        @pl.when(c - s >= 0)
        def _():
            copy(s, c - s).start()

    out_ref[...] = own_ref[...]
    for s in range(1, back + 1):

        @pl.when(c + s < n_ctx)
        def _():
            copy(s, c).wait_recv()
            out_ref[...] += recv_buf[s - 1].astype(jnp.float32)

    for s in range(1, back + 1):

        @pl.when(c - s >= 0)
        def _():
            copy(s, c - s).wait_send()


def kv_return(own, g, n_ctx, back):
    return pl.pallas_call(
        functools.partial(kv_return_kernel, n_ctx, back),
        out_shape=jax.ShapeDtypeStruct(own.shape, own.dtype),
        in_specs=[pl.BlockSpec(memory_space=pltpu.VMEM)] * 2,
        out_specs=pl.BlockSpec(memory_space=pltpu.VMEM),
        scratch_shapes=[
            pltpu.VMEM(g.shape, g.dtype),
            pltpu.SemaphoreType.DMA((back,)),
            pltpu.SemaphoreType.DMA((back,)),
        ],
        compiler_params=pltpu.CompilerParams(collective_id=1, has_side_effects=True),
    )(own, g)


def peer_barrier(n_f, c, f):
    barrier = pltpu.get_barrier_semaphore()
    for k in range(1, n_f):
        pl.semaphore_signal(barrier, inc=1, device_id=(c, (f + k) % n_f), device_id_type=MESH)
    pl.semaphore_wait(barrier, n_f - 1)


def group_gather_kernel(n_f, x_ref, out_ref, send_sem, recv_sem):
    c = lax.axis_index("ctx")
    f = lax.axis_index("fsdp")
    peer_barrier(n_f, c, f)
    copies = []
    for k in range(1, n_f):
        copy = pltpu.make_async_remote_copy(
            src_ref=x_ref,
            dst_ref=out_ref.at[f],
            send_sem=send_sem.at[k - 1],
            recv_sem=recv_sem.at[k - 1],
            device_id=(c, (f + k) % n_f),
            device_id_type=MESH,
        )
        copy.start()
        copies.append(copy)
    out_ref[f] = x_ref[...]
    for k in range(1, n_f):
        pltpu.make_async_remote_copy(
            src_ref=x_ref,
            dst_ref=out_ref.at[(f + n_f - k) % n_f],
            send_sem=send_sem.at[k - 1],
            recv_sem=recv_sem.at[k - 1],
            device_id=(c, f),
            device_id_type=MESH,
        ).wait_recv()
    for copy in copies:
        copy.wait_send()


def group_gather(x, n_f):
    return pl.pallas_call(
        functools.partial(group_gather_kernel, n_f),
        out_shape=jax.ShapeDtypeStruct((n_f,) + x.shape, x.dtype),
        in_specs=[pl.BlockSpec(memory_space=pltpu.VMEM)],
        out_specs=pl.BlockSpec(memory_space=pltpu.VMEM),
        scratch_shapes=[pltpu.SemaphoreType.DMA((n_f - 1,)), pltpu.SemaphoreType.DMA((n_f - 1,))],
        compiler_params=pltpu.CompilerParams(collective_id=2, has_side_effects=True),
    )(x)


def group_reduce_kernel(n_f, p_ref, out_ref, recv_buf, send_sem, recv_sem):
    c = lax.axis_index("ctx")
    f = lax.axis_index("fsdp")
    peer_barrier(n_f, c, f)
    copies = []
    for k in range(1, n_f):
        dest = (f + k) % n_f
        copy = pltpu.make_async_remote_copy(
            src_ref=p_ref.at[dest],
            dst_ref=recv_buf.at[k - 1],
            send_sem=send_sem.at[k - 1],
            recv_sem=recv_sem.at[k - 1],
            device_id=(c, dest),
            device_id_type=MESH,
        )
        copy.start()
        copies.append(copy)
    out_ref[...] = p_ref[f]
    for k in range(1, n_f):
        copies[k - 1].wait_recv()
        out_ref[...] += recv_buf[k - 1]
    for copy in copies:
        copy.wait_send()


def group_reduce(p, n_f):
    return pl.pallas_call(
        functools.partial(group_reduce_kernel, n_f),
        out_shape=jax.ShapeDtypeStruct(p.shape[1:], p.dtype),
        in_specs=[pl.BlockSpec(memory_space=pltpu.VMEM)],
        out_specs=pl.BlockSpec(memory_space=pltpu.VMEM),
        scratch_shapes=[
            pltpu.VMEM((n_f - 1,) + p.shape[1:], p.dtype),
            pltpu.SemaphoreType.DMA((n_f - 1,)),
            pltpu.SemaphoreType.DMA((n_f - 1,)),
        ],
        compiler_params=pltpu.CompilerParams(collective_id=3, has_side_effects=True),
    )(p)


def pair_barrier(c, partner, across):
    barrier = pltpu.get_barrier_semaphore()
    pl.semaphore_signal(barrier, inc=1, device_id=(c, partner), device_id_type=MESH)
    pl.semaphore_signal(barrier, inc=1, device_id=(c, across), device_id_type=MESH)
    pl.semaphore_wait(barrier, 2)


def quad_ids():
    c = lax.axis_index("ctx")
    f = lax.axis_index("fsdp")
    partner = f + 1 - 2 * (f % 2)
    across = (f + 2) % 4
    diagonal = (partner + 2) % 4
    return c, f, partner, across, diagonal


def quad_gather_kernel(x_ref, out_ref, send_sem, recv_sem):
    c, f, partner, across, diagonal = quad_ids()
    pair_barrier(c, partner, across)

    def copy(src, slot, dest, k):
        return pltpu.make_async_remote_copy(
            src_ref=src,
            dst_ref=out_ref.at[slot],
            send_sem=send_sem.at[k],
            recv_sem=recv_sem.at[slot],
            device_id=(c, dest),
            device_id_type=MESH,
        )

    first = copy(x_ref, f, across, 0)
    first.start()
    own = copy(x_ref, f, partner, 1)
    own.start()
    out_ref[f] = x_ref[...]
    copy(x_ref, across, f, 0).wait_recv()
    relay = copy(out_ref.at[across], across, partner, 2)
    relay.start()
    copy(x_ref, partner, f, 0).wait_recv()
    copy(x_ref, diagonal, f, 0).wait_recv()
    first.wait_send()
    own.wait_send()
    relay.wait_send()


def quad_gather(x):
    return pl.pallas_call(
        quad_gather_kernel,
        out_shape=jax.ShapeDtypeStruct((4,) + x.shape, x.dtype),
        in_specs=[pl.BlockSpec(memory_space=pltpu.VMEM)],
        out_specs=pl.BlockSpec(memory_space=pltpu.VMEM),
        scratch_shapes=[pltpu.SemaphoreType.DMA((3,)), pltpu.SemaphoreType.DMA((4,))],
        compiler_params=pltpu.CompilerParams(collective_id=4, has_side_effects=True),
    )(x)


def quad_reduce_kernel(p_ref, out_ref, near_buf, far_buf, sum_buf, send_sem, recv_sem):
    c, f, partner, across, diagonal = quad_ids()
    pair_barrier(c, partner, across)

    def copy(src, dst, dest, k):
        return pltpu.make_async_remote_copy(
            src_ref=src,
            dst_ref=dst,
            send_sem=send_sem.at[k],
            recv_sem=recv_sem.at[k],
            device_id=(c, dest),
            device_id_type=MESH,
        )

    to_partner = copy(p_ref.at[partner], near_buf.at[0], partner, 0)
    to_partner.start()
    to_diagonal = copy(p_ref.at[diagonal], near_buf.at[1], partner, 1)
    to_diagonal.start()
    to_partner.wait_recv()
    to_diagonal.wait_recv()
    sum_buf[...] = p_ref[across] + near_buf[1]
    to_across = copy(sum_buf, far_buf, across, 2)
    to_across.start()
    out_ref[...] = p_ref[f] + near_buf[0]
    to_across.wait_recv()
    out_ref[...] += far_buf[...]
    to_partner.wait_send()
    to_diagonal.wait_send()
    to_across.wait_send()


def quad_reduce(p):
    block = p.shape[1:]
    return pl.pallas_call(
        quad_reduce_kernel,
        out_shape=jax.ShapeDtypeStruct(block, p.dtype),
        in_specs=[pl.BlockSpec(memory_space=pltpu.VMEM)],
        out_specs=pl.BlockSpec(memory_space=pltpu.VMEM),
        scratch_shapes=[
            pltpu.VMEM((2,) + block, p.dtype),
            pltpu.VMEM(block, p.dtype),
            pltpu.VMEM(block, p.dtype),
            pltpu.SemaphoreType.DMA((3,)),
            pltpu.SemaphoreType.DMA((3,)),
        ],
        compiler_params=pltpu.CompilerParams(collective_id=5, has_side_effects=True),
    )(p)


def fsdp_gather(x, n_f):
    if n_f == 4:
        return quad_gather(x)
    return group_gather(x, n_f)


def fsdp_reduce(p, n_f):
    if n_f == 4:
        return quad_reduce(p)
    return group_reduce(p, n_f)


def body(
    tokens,
    doc_lengths,
    attention_gain,
    query_weight,
    key_weight,
    value_weight,
    output_weight,
    feedforward_gain,
    gate_weight,
    up_weight,
    down_weight,
    cotangent,
):
    n_dev = lax.axis_size(ALL)
    rows = query_weight.shape[0]
    ff_rows = down_weight.shape[0]
    ff = gate_weight.shape[1]
    local_tokens = tokens[0].astype(jnp.float32)
    tok_rows = local_tokens.shape[0]
    stream_len = tok_rows * lax.axis_size("ctx")
    my_first = lax.axis_index("ctx") * tok_rows

    gain_cols = jnp.pad(
        jnp.stack([attention_gain, feedforward_gain], axis=1), ((0, 0), (0, GAIN_PAD - 2))
    )
    att_full = lax.all_gather(
        jnp.concatenate([query_weight, key_weight, value_weight, output_weight, gain_cols], axis=1),
        ALL,
        axis=0,
        tiled=True,
    )
    c_k = D
    c_v = D + KVW
    c_o = D + 2 * KVW
    c_g = 2 * D + 2 * KVW
    query_full = att_full[:, :c_k]
    key_full = att_full[:, c_k:c_v]
    value_full = att_full[:, c_v:c_o]
    qkv_full = att_full[:, :c_o]
    output_full = att_full[:, c_o:c_g]
    gain_one_f = att_full[:, c_g].astype(jnp.float32)
    gain_two_f = att_full[:, c_g + 1].astype(jnp.float32)

    key_docs_all, places_all = document_layout(doc_lengths[0], stream_len)
    query_docs = lax.dynamic_slice_in_dim(key_docs_all, my_first, tok_rows, 0)
    query_positions = lax.dynamic_slice_in_dim(places_all, my_first, tok_rows, 0)
    query_places = my_first + jnp.arange(tok_rows, dtype=jnp.int32)
    group_size = H // KVH
    score_scale = HD ** (-0.5)

    scale_one = rms_scale(local_tokens)
    normed_one = local_tokens * scale_one
    normed_low = (normed_one * gain_one_f).astype(jnp.bfloat16)
    qkv = jnp.dot(normed_low, qkv_full, preferred_element_type=jnp.float32)
    queries = qkv[:, :D]
    keys_new = qkv[:, D : D + KVW]
    values_new = qkv[:, D + KVW :]
    query_low = rotate(queries, query_positions, H, 1.0).astype(jnp.bfloat16)
    key_low = rotate(keys_new, query_positions, KVH, 1.0).astype(jnp.bfloat16)
    value_low = values_new.astype(jnp.bfloat16)

    n_ctx = lax.axis_size("ctx")
    n_f = lax.axis_size("fsdp")
    chunk = ff_rows
    units = n_ctx * chunk
    gu_parts = jnp.transpose(
        jnp.stack([gate_weight, up_weight], axis=1).reshape(rows, 2, n_ctx, n_f, chunk),
        (3, 0, 1, 2, 4),
    )
    gu_parts = lax.all_to_all(gu_parts, "fsdp", 0, 0, tiled=True).reshape(n_f * rows, 2 * units)
    down_rows = D // (2 * n_ctx)
    ff_pack = jnp.concatenate([gu_parts, down_weight.reshape(down_rows, 2 * units)], axis=0)
    ff_pack = ff_pack.at[0, 0].add(att_full[0, 0] * 0)
    ff_stack = lax.all_gather(
        ff_pack,
        "ctx",
        axis=0,
        tiled=False,
    )
    gate_up_tp = ff_stack[:, : n_f * rows].reshape(n_ctx * n_f * rows, 2 * units)
    down_tp = ff_stack[:, n_f * rows :].reshape(n_ctx, ff_rows, D).reshape(units, D)
    max_doc = min(DOC_MOST, KBLK * (stream_len // (2 * KBLK)))
    back = min(-(-(max_doc - 1) // tok_rows), n_ctx - 1)
    win = (back + 1) * tok_rows
    kv_win = kv_share(
        jnp.concatenate([key_low, value_low], axis=1), n_ctx, back
    ).reshape(win, 2 * KVW)
    docs_pad = jnp.concatenate(
        [jnp.full((back * tok_rows,), -1, jnp.int32), key_docs_all.astype(jnp.int32)]
    )
    key_docs = lax.dynamic_slice_in_dim(docs_pad, my_first, win, 0)
    key_places = my_first - back * tok_rows + jnp.arange(win, dtype=jnp.int32)
    key_block = kv_win[:, :KVW].reshape(win, KVH, HD)
    value_block = kv_win[:, KVW:].reshape(win, KVH, HD)
    query_grouped = query_low.reshape(tok_rows, KVH, group_size, HD)
    allowed = (
        (key_docs[None, :] == query_docs[:, None]) & (key_places[None, :] <= query_places[:, None])
    )[:, None, None, :]
    scores = (
        jnp.einsum("qgrd,kgd->qgrk", query_grouped, key_block, preferred_element_type=jnp.float32)
        * score_scale
    )
    scores = jnp.where(allowed, scores, MASKED_SCORE)
    row_max = jnp.max(scores, axis=-1, keepdims=True)
    exponent = jnp.where(allowed, jnp.exp(scores - row_max), 0.0)
    probs = exponent / jnp.sum(exponent, axis=-1, keepdims=True)
    probs_low = probs.astype(jnp.bfloat16)
    attended_sum = jnp.einsum(
        "qgrk,kgd->qgrd", probs_low, value_block, preferred_element_type=jnp.float32
    )
    attended_low = attended_sum.reshape(tok_rows, D).astype(jnp.bfloat16)
    middle = local_tokens + jnp.dot(attended_low, output_full, preferred_element_type=jnp.float32)

    scale_two = rms_scale(middle)
    normed_two = middle * scale_two
    normed_two_low = (normed_two * gain_two_f).astype(jnp.bfloat16)
    group_tokens = n_f * tok_rows
    xn2_all = fsdp_gather(normed_two_low, n_f).reshape(group_tokens, D)
    gate_up = jnp.dot(xn2_all, gate_up_tp, preferred_element_type=jnp.float32)
    gate_pre = gate_up[:, :units]
    up_pre = gate_up[:, units:]
    sigmoid = jax.nn.sigmoid(gate_pre)
    hidden_low = (gate_pre * sigmoid * up_pre).astype(jnp.bfloat16)

    grad_out = cotangent[0]
    grad_all = fsdp_gather(grad_out, n_f).reshape(group_tokens, D)
    down_term = outer_rows(hidden_low, grad_all).astype(jnp.bfloat16)
    hidden_grad = times_transposed(grad_all, down_tp)
    gate_grad = (hidden_grad * up_pre * sigmoid * (1.0 + gate_pre * (1.0 - sigmoid))).astype(
        jnp.bfloat16
    )
    up_grad = (hidden_grad * gate_pre * sigmoid).astype(jnp.bfloat16)
    gate_up_cat = jnp.concatenate([gate_grad, up_grad], axis=1)
    gate_up_term = outer_rows(xn2_all, gate_up_cat)
    grad_pack = jnp.concatenate(
        [
            gate_up_term.astype(jnp.bfloat16).reshape(n_ctx, n_f * rows, 2 * units),
            down_term.reshape(n_ctx, down_rows, 2 * units),
        ],
        axis=1,
    ).reshape(n_ctx * (n_f * rows + down_rows), 2 * units)
    grad_pack, gate_up_cat = lax.optimization_barrier((grad_pack, gate_up_cat))
    grad_sum = lax.psum_scatter(grad_pack, "ctx", scatter_dimension=0, tiled=True)
    down_sum = grad_sum[n_f * rows :].reshape(ff_rows, D)
    gu_sum = lax.all_to_all(grad_sum[: n_f * rows].reshape(n_f, rows, 2 * units), "fsdp", 0, 0, tiled=True)
    ff_sum = jnp.transpose(
        gu_sum.reshape(n_f, rows, 2, n_ctx, chunk), (1, 2, 3, 0, 4)
    ).reshape(rows, 2 * ff)
    normed_two_grad = fsdp_reduce(
        times_transposed(gate_up_cat, gate_up_tp).reshape(n_f, tok_rows, D), n_f
    )
    gain_two_term = jnp.sum(normed_two_grad * normed_two, axis=0)
    scaled_two = normed_two_grad * gain_two_f
    middle_grad = grad_out.astype(jnp.float32) + scale_two * (
        scaled_two - normed_two * jnp.mean(scaled_two * normed_two, axis=-1, keepdims=True)
    )
    branch_grad = middle_grad.astype(jnp.bfloat16)
    attended_grad_low = (
        times_transposed(branch_grad, output_full)
        .astype(jnp.bfloat16)
        .reshape(tok_rows, KVH, group_size, HD)
    )
    row_delta = jnp.sum(
        attended_grad_low.astype(jnp.float32) * attended_sum, axis=-1, keepdims=True
    )
    prob_grad = jnp.einsum(
        "qgrd,kgd->qgrk", attended_grad_low, value_block, preferred_element_type=jnp.float32
    )
    score_grad = (probs * (prob_grad - row_delta)).astype(jnp.bfloat16)
    query_accum = jnp.einsum(
        "qgrk,kgd->qgrd", score_grad, key_block, preferred_element_type=jnp.float32
    )
    key_term = jnp.einsum(
        "qgrk,qgrd->kgd", score_grad, query_grouped, preferred_element_type=jnp.float32
    ).reshape(win, KVW)
    value_term = jnp.einsum(
        "qgrk,qgrd->kgd", probs_low, attended_grad_low, preferred_element_type=jnp.float32
    ).reshape(win, KVW)
    kv_term = jnp.concatenate([key_term, value_term], axis=1).reshape(back + 1, tok_rows, 2 * KVW)
    kv_sum = kv_return(kv_term[back], kv_term[:back].astype(jnp.bfloat16), n_ctx, back)
    key_grad_low = rotate(kv_sum[:, :KVW] * score_scale, query_positions, KVH, -1.0).astype(
        jnp.bfloat16
    )
    value_grad_low = kv_sum[:, KVW:].astype(jnp.bfloat16)
    query_grad_low = rotate(
        query_accum.reshape(tok_rows, D) * score_scale, query_positions, H, -1.0
    ).astype(jnp.bfloat16)
    projection_cat = jnp.concatenate([query_grad_low, key_grad_low, value_grad_low], axis=1)
    normed_grad = times_transposed(projection_cat, qkv_full)
    gain_one_term = jnp.sum(normed_grad * normed_one, axis=0)
    scaled_one = normed_grad * gain_one_f
    tokens_grad = middle_grad + scale_one * (
        scaled_one - normed_one * jnp.mean(scaled_one * normed_one, axis=-1, keepdims=True)
    )
    gain_term_cols = jnp.pad(
        jnp.stack([gain_one_term, gain_two_term], axis=1), ((0, 0), (0, GAIN_PAD - 2))
    )
    attention_pack = jnp.concatenate(
        [
            outer_rows(normed_low, projection_cat).astype(jnp.bfloat16),
            outer_rows(attended_low, branch_grad).astype(jnp.bfloat16),
            gain_term_cols.astype(jnp.bfloat16),
        ],
        axis=1,
    )
    attention_sum = lax.psum_scatter(
        attention_pack, ALL, scatter_dimension=0, tiled=True
    ).astype(jnp.float32)
    late_hidden = hidden_low.at[0, 0].add(attention_pack[0, 0] * 0)
    ff_part = jnp.dot(late_hidden, down_tp, preferred_element_type=jnp.float32)
    layer_out = middle + fsdp_reduce(ff_part.reshape(n_f, tok_rows, D), n_f)
    ff_sum = ff_sum.astype(jnp.float32)
    return (
        layer_out.astype(jnp.bfloat16)[None],
        tokens_grad[None],
        attention_sum[:, c_g],
        attention_sum[:, :c_k],
        attention_sum[:, c_k:c_v],
        attention_sum[:, c_v:c_o],
        attention_sum[:, c_o:c_g],
        attention_sum[:, c_g + 1],
        ff_sum[:, :ff],
        ff_sum[:, ff : 2 * ff],
        down_sum.astype(jnp.float32),
    )


def solution(mesh):
    weight = P(ALL, None)
    stream = P("fsdp", "ctx", None)
    return jax.shard_map(
        body,
        mesh=mesh,
        in_specs=(
            stream,
            P("fsdp", None),
            P(ALL),
            weight,
            weight,
            weight,
            weight,
            P(ALL),
            weight,
            weight,
            weight,
            stream,
        ),
        out_specs=(
            stream,
            stream,
            P(ALL),
            weight,
            weight,
            weight,
            weight,
            P(ALL),
            weight,
            weight,
            weight,
        ),
        check_vma=False,
    )
```

```python
import functools

import jax
import jax.numpy as jnp
from jax import lax
from jax.experimental import pallas as pl
from jax.experimental.pallas import tpu as pltpu
from jax.sharding import PartitionSpec as P

MESH = pl.DeviceIdType.MESH

D = 1536
H = 16
KVH = 8
HD = 96
KBLK = 512
DOC_MOST = 4096
KVW = 768
GAIN_PAD = 128

EPSILON = 1e-05
ROPE_BASE = 100000.0
MASKED_SCORE = -1e30
ALL = ("ctx", "fsdp")


def rms_scale(values):
    return lax.rsqrt(jnp.mean(values * values, axis=-1, keepdims=True) + EPSILON)


def document_layout(lengths, total):
    starts = jnp.cumsum(lengths) - lengths
    places = jnp.arange(total, dtype=jnp.int32)
    inside = places[:, None] >= starts[None, :]
    doc_ids = jnp.sum(inside.astype(jnp.int32), axis=1) - 1
    doc_starts = jnp.max(jnp.where(inside, starts[None, :], 0), axis=1)
    return (doc_ids, places - doc_starts)


def rotate(values, positions, head_count, direction):
    row_count = values.shape[0]
    half_dim = HD // 2
    inverse_freq = ROPE_BASE ** (-(jnp.arange(half_dim).astype(jnp.float32) * (2.0 / HD)))
    angles = positions.astype(jnp.float32)[:, None] * inverse_freq[None, :]
    cosine = jnp.cos(angles)[:, None, :]
    sine_part = direction * jnp.sin(angles)[:, None, :]
    grouped = values.reshape(row_count, head_count, HD)
    former = grouped[:, :, :half_dim]
    latter = grouped[:, :, half_dim:]
    turned = jnp.concatenate(
        [former * cosine - latter * sine_part, latter * cosine + former * sine_part], axis=2
    )
    return turned.reshape(row_count, head_count * HD)


def outer_rows(left, right):
    return lax.dot_general(
        left, right, (((0,), (0,)), ((), ())), preferred_element_type=jnp.float32
    )


def times_transposed(left, right):
    return lax.dot_general(
        left, right, (((1,), (1,)), ((), ())), preferred_element_type=jnp.float32
    )


def neighbour_barrier(n_ctx, back, c, f):
    barrier = pltpu.get_barrier_semaphore()
    for s in range(1, back + 1):
        for peer in ((c + s) % n_ctx, (c + n_ctx - s) % n_ctx):
            pl.semaphore_signal(barrier, inc=1, device_id=(peer, f), device_id_type=MESH)
    pl.semaphore_wait(barrier, 2 * back)


def kv_share_kernel(n_ctx, back, kv_ref, out_ref, send_sem, recv_sem):
    c = lax.axis_index("ctx")
    f = lax.axis_index("fsdp")
    neighbour_barrier(n_ctx, back, c, f)

    def copy(s, dest):
        return pltpu.make_async_remote_copy(
            src_ref=kv_ref,
            dst_ref=out_ref.at[back - s],
            send_sem=send_sem.at[s - 1],
            recv_sem=recv_sem.at[back - s],
            device_id=(dest, f),
            device_id_type=MESH,
        )

    for s in range(1, back + 1):

        @pl.when(c + s < n_ctx)
        def _():
            copy(s, c + s).start()

    out_ref[back] = kv_ref[...]
    for s in range(1, back + 1):

        @pl.when(c - s < 0)
        def _():
            out_ref[back - s] = jnp.zeros(kv_ref.shape, kv_ref.dtype)

    for s in range(1, back + 1):

        @pl.when(c + s < n_ctx)
        def _():
            copy(s, c + s).wait_send()

        @pl.when(c - s >= 0)
        def _():
            copy(s, c).wait_recv()


def kv_share(kv, n_ctx, back):
    return pl.pallas_call(
        functools.partial(kv_share_kernel, n_ctx, back),
        out_shape=jax.ShapeDtypeStruct((back + 1,) + kv.shape, kv.dtype),
        in_specs=[pl.BlockSpec(memory_space=pltpu.VMEM)],
        out_specs=pl.BlockSpec(memory_space=pltpu.VMEM),
        scratch_shapes=[pltpu.SemaphoreType.DMA((back,)), pltpu.SemaphoreType.DMA((back + 1,))],
        compiler_params=pltpu.CompilerParams(collective_id=0, has_side_effects=True),
    )(kv)


def kv_return_kernel(n_ctx, back, own_ref, g_ref, out_ref, recv_buf, send_sem, recv_sem):
    c = lax.axis_index("ctx")
    f = lax.axis_index("fsdp")
    neighbour_barrier(n_ctx, back, c, f)

    def copy(s, dest):
        return pltpu.make_async_remote_copy(
            src_ref=g_ref.at[back - s],
            dst_ref=recv_buf.at[s - 1],
            send_sem=send_sem.at[s - 1],
            recv_sem=recv_sem.at[s - 1],
            device_id=(dest, f),
            device_id_type=MESH,
        )

    for s in range(1, back + 1):

        @pl.when(c - s >= 0)
        def _():
            copy(s, c - s).start()

    out_ref[...] = own_ref[...]
    for s in range(1, back + 1):

        @pl.when(c + s < n_ctx)
        def _():
            copy(s, c).wait_recv()
            out_ref[...] += recv_buf[s - 1].astype(jnp.float32)

    for s in range(1, back + 1):

        @pl.when(c - s >= 0)
        def _():
            copy(s, c - s).wait_send()


def kv_return(own, g, n_ctx, back):
    return pl.pallas_call(
        functools.partial(kv_return_kernel, n_ctx, back),
        out_shape=jax.ShapeDtypeStruct(own.shape, own.dtype),
        in_specs=[pl.BlockSpec(memory_space=pltpu.VMEM), pl.BlockSpec(memory_space=pl.ANY)],
        out_specs=pl.BlockSpec(memory_space=pltpu.VMEM),
        scratch_shapes=[
            pltpu.VMEM(g.shape, g.dtype),
            pltpu.SemaphoreType.DMA((back,)),
            pltpu.SemaphoreType.DMA((back,)),
        ],
        compiler_params=pltpu.CompilerParams(collective_id=1, has_side_effects=True),
    )(own, g)


def peer_barrier(n_f, c, f):
    barrier = pltpu.get_barrier_semaphore()
    for k in range(1, n_f):
        pl.semaphore_signal(barrier, inc=1, device_id=(c, (f + k) % n_f), device_id_type=MESH)
    pl.semaphore_wait(barrier, n_f - 1)


def group_gather_kernel(n_f, x_ref, out_ref, send_sem, recv_sem):
    c = lax.axis_index("ctx")
    f = lax.axis_index("fsdp")
    peer_barrier(n_f, c, f)
    copies = []
    for k in range(1, n_f):
        copy = pltpu.make_async_remote_copy(
            src_ref=x_ref,
            dst_ref=out_ref.at[f],
            send_sem=send_sem.at[k - 1],
            recv_sem=recv_sem.at[k - 1],
            device_id=(c, (f + k) % n_f),
            device_id_type=MESH,
        )
        copy.start()
        copies.append(copy)
    out_ref[f] = x_ref[...]
    for k in range(1, n_f):
        pltpu.make_async_remote_copy(
            src_ref=x_ref,
            dst_ref=out_ref.at[(f + n_f - k) % n_f],
            send_sem=send_sem.at[k - 1],
            recv_sem=recv_sem.at[k - 1],
            device_id=(c, f),
            device_id_type=MESH,
        ).wait_recv()
    for copy in copies:
        copy.wait_send()


def group_gather(x, n_f):
    return pl.pallas_call(
        functools.partial(group_gather_kernel, n_f),
        out_shape=jax.ShapeDtypeStruct((n_f,) + x.shape, x.dtype),
        in_specs=[pl.BlockSpec(memory_space=pltpu.VMEM)],
        out_specs=pl.BlockSpec(memory_space=pltpu.VMEM),
        scratch_shapes=[pltpu.SemaphoreType.DMA((n_f - 1,)), pltpu.SemaphoreType.DMA((n_f - 1,))],
        compiler_params=pltpu.CompilerParams(collective_id=2, has_side_effects=True),
    )(x)


def group_reduce_kernel(n_f, p_ref, out_ref, recv_buf, send_sem, recv_sem):
    c = lax.axis_index("ctx")
    f = lax.axis_index("fsdp")
    peer_barrier(n_f, c, f)
    copies = []
    for k in range(1, n_f):
        dest = (f + k) % n_f
        copy = pltpu.make_async_remote_copy(
            src_ref=p_ref.at[dest],
            dst_ref=recv_buf.at[k - 1],
            send_sem=send_sem.at[k - 1],
            recv_sem=recv_sem.at[k - 1],
            device_id=(c, dest),
            device_id_type=MESH,
        )
        copy.start()
        copies.append(copy)
    out_ref[...] = p_ref[f]
    for k in range(1, n_f):
        copies[k - 1].wait_recv()
        out_ref[...] += recv_buf[k - 1]
    for copy in copies:
        copy.wait_send()


def group_reduce(p, n_f):
    return pl.pallas_call(
        functools.partial(group_reduce_kernel, n_f),
        out_shape=jax.ShapeDtypeStruct(p.shape[1:], p.dtype),
        in_specs=[pl.BlockSpec(memory_space=pltpu.VMEM)],
        out_specs=pl.BlockSpec(memory_space=pltpu.VMEM),
        scratch_shapes=[
            pltpu.VMEM((n_f - 1,) + p.shape[1:], p.dtype),
            pltpu.SemaphoreType.DMA((n_f - 1,)),
            pltpu.SemaphoreType.DMA((n_f - 1,)),
        ],
        compiler_params=pltpu.CompilerParams(collective_id=3, has_side_effects=True),
    )(p)


def pair_barrier(c, partner, across):
    barrier = pltpu.get_barrier_semaphore()
    pl.semaphore_signal(barrier, inc=1, device_id=(c, partner), device_id_type=MESH)
    pl.semaphore_signal(barrier, inc=1, device_id=(c, across), device_id_type=MESH)
    pl.semaphore_wait(barrier, 2)


def quad_ids():
    c = lax.axis_index("ctx")
    f = lax.axis_index("fsdp")
    partner = f + 1 - 2 * (f % 2)
    across = (f + 2) % 4
    diagonal = (partner + 2) % 4
    return c, f, partner, across, diagonal


def quad_gather_kernel(x_ref, out_ref, send_sem, recv_sem):
    c, f, partner, across, diagonal = quad_ids()
    pair_barrier(c, partner, across)

    def copy(src, slot, dest, k):
        return pltpu.make_async_remote_copy(
            src_ref=src,
            dst_ref=out_ref.at[slot],
            send_sem=send_sem.at[k],
            recv_sem=recv_sem.at[slot],
            device_id=(c, dest),
            device_id_type=MESH,
        )

    first = copy(x_ref, f, across, 0)
    first.start()
    own = copy(x_ref, f, partner, 1)
    own.start()
    out_ref[f] = x_ref[...]
    copy(x_ref, across, f, 0).wait_recv()
    relay = copy(out_ref.at[across], across, partner, 2)
    relay.start()
    copy(x_ref, partner, f, 0).wait_recv()
    copy(x_ref, diagonal, f, 0).wait_recv()
    first.wait_send()
    own.wait_send()
    relay.wait_send()


def quad_gather(x):
    return pl.pallas_call(
        quad_gather_kernel,
        out_shape=jax.ShapeDtypeStruct((4,) + x.shape, x.dtype),
        in_specs=[pl.BlockSpec(memory_space=pltpu.VMEM)],
        out_specs=pl.BlockSpec(memory_space=pltpu.VMEM),
        scratch_shapes=[pltpu.SemaphoreType.DMA((3,)), pltpu.SemaphoreType.DMA((4,))],
        compiler_params=pltpu.CompilerParams(collective_id=4, has_side_effects=True),
    )(x)


def quad_reduce_kernel(p_ref, out_ref, near_buf, far_buf, sum_buf, send_sem, recv_sem):
    c, f, partner, across, diagonal = quad_ids()
    pair_barrier(c, partner, across)

    def copy(src, dst, dest, k):
        return pltpu.make_async_remote_copy(
            src_ref=src,
            dst_ref=dst,
            send_sem=send_sem.at[k],
            recv_sem=recv_sem.at[k],
            device_id=(c, dest),
            device_id_type=MESH,
        )

    to_partner = copy(p_ref.at[partner], near_buf.at[0], partner, 0)
    to_partner.start()
    to_diagonal = copy(p_ref.at[diagonal], near_buf.at[1], partner, 1)
    to_diagonal.start()
    to_partner.wait_recv()
    to_diagonal.wait_recv()
    sum_buf[...] = p_ref[across] + near_buf[1]
    to_across = copy(sum_buf, far_buf, across, 2)
    to_across.start()
    out_ref[...] = p_ref[f] + near_buf[0]
    to_across.wait_recv()
    out_ref[...] += far_buf[...]
    to_partner.wait_send()
    to_diagonal.wait_send()
    to_across.wait_send()


def quad_reduce(p):
    block = p.shape[1:]
    return pl.pallas_call(
        quad_reduce_kernel,
        out_shape=jax.ShapeDtypeStruct(block, p.dtype),
        in_specs=[pl.BlockSpec(memory_space=pltpu.VMEM)],
        out_specs=pl.BlockSpec(memory_space=pltpu.VMEM),
        scratch_shapes=[
            pltpu.VMEM((2,) + block, p.dtype),
            pltpu.VMEM(block, p.dtype),
            pltpu.VMEM(block, p.dtype),
            pltpu.SemaphoreType.DMA((3,)),
            pltpu.SemaphoreType.DMA((3,)),
        ],
        compiler_params=pltpu.CompilerParams(collective_id=5, has_side_effects=True),
    )(p)


def fsdp_gather(x, n_f):
    if n_f == 4:
        return quad_gather(x)
    return group_gather(x, n_f)


def fsdp_reduce(p, n_f):
    if n_f == 4:
        return quad_reduce(p)
    return group_reduce(p, n_f)


def body(
    tokens,
    doc_lengths,
    attention_gain,
    query_weight,
    key_weight,
    value_weight,
    output_weight,
    feedforward_gain,
    gate_weight,
    up_weight,
    down_weight,
    cotangent,
):
    n_dev = lax.axis_size(ALL)
    rows = query_weight.shape[0]
    ff_rows = down_weight.shape[0]
    ff = gate_weight.shape[1]
    local_tokens = tokens[0].astype(jnp.float32)
    tok_rows = local_tokens.shape[0]
    stream_len = tok_rows * lax.axis_size("ctx")
    my_first = lax.axis_index("ctx") * tok_rows

    gain_cols = jnp.pad(
        jnp.stack([attention_gain, feedforward_gain], axis=1), ((0, 0), (0, GAIN_PAD - 2))
    )
    att_full = lax.all_gather(
        jnp.concatenate([query_weight, key_weight, value_weight, output_weight, gain_cols], axis=1),
        ALL,
        axis=0,
        tiled=True,
    )
    c_k = D
    c_v = D + KVW
    c_o = D + 2 * KVW
    c_g = 2 * D + 2 * KVW
    query_full = att_full[:, :c_k]
    key_full = att_full[:, c_k:c_v]
    value_full = att_full[:, c_v:c_o]
    qkv_full = att_full[:, :c_o]
    output_full = att_full[:, c_o:c_g]
    gain_one_f = att_full[:, c_g].astype(jnp.float32)
    gain_two_f = att_full[:, c_g + 1].astype(jnp.float32)

    key_docs_all, places_all = document_layout(doc_lengths[0], stream_len)
    query_docs = lax.dynamic_slice_in_dim(key_docs_all, my_first, tok_rows, 0)
    query_positions = lax.dynamic_slice_in_dim(places_all, my_first, tok_rows, 0)
    query_places = my_first + jnp.arange(tok_rows, dtype=jnp.int32)
    group_size = H // KVH
    score_scale = HD ** (-0.5)

    scale_one = rms_scale(local_tokens)
    normed_one = local_tokens * scale_one
    normed_low = (normed_one * gain_one_f).astype(jnp.bfloat16)
    qkv = jnp.dot(normed_low, qkv_full, preferred_element_type=jnp.float32)
    queries = qkv[:, :D]
    keys_new = qkv[:, D : D + KVW]
    values_new = qkv[:, D + KVW :]
    query_low = rotate(queries, query_positions, H, 1.0).astype(jnp.bfloat16)
    key_low = rotate(keys_new, query_positions, KVH, 1.0).astype(jnp.bfloat16)
    value_low = values_new.astype(jnp.bfloat16)

    n_ctx = lax.axis_size("ctx")
    n_f = lax.axis_size("fsdp")
    chunk = ff_rows
    units = n_ctx * chunk
    gu_parts = jnp.transpose(
        jnp.stack([gate_weight, up_weight], axis=1).reshape(rows, 2, n_ctx, n_f, chunk),
        (3, 0, 1, 2, 4),
    )
    gu_parts = lax.all_to_all(gu_parts, "fsdp", 0, 0, tiled=True).reshape(n_f * rows, 2 * units)
    down_rows = D // (2 * n_ctx)
    ff_pack = jnp.concatenate([gu_parts, down_weight.reshape(down_rows, 2 * units)], axis=0)
    ff_pack = ff_pack.at[0, 0].add(att_full[0, 0] * 0)
    ff_stack = lax.all_gather(
        ff_pack,
        "ctx",
        axis=0,
        tiled=False,
    )
    gate_up_tp = ff_stack[:, : n_f * rows].reshape(n_ctx * n_f * rows, 2 * units)
    down_tp = ff_stack[:, n_f * rows :].reshape(n_ctx, ff_rows, D).reshape(units, D)
    max_doc = min(DOC_MOST, KBLK * (stream_len // (2 * KBLK)))
    back = min(-(-(max_doc - 1) // tok_rows), n_ctx - 1)
    win = (back + 1) * tok_rows
    kv_win = kv_share(
        jnp.concatenate([key_low, value_low], axis=1), n_ctx, back
    ).reshape(win, 2 * KVW)
    docs_pad = jnp.concatenate(
        [jnp.full((back * tok_rows,), -1, jnp.int32), key_docs_all.astype(jnp.int32)]
    )
    key_docs = lax.dynamic_slice_in_dim(docs_pad, my_first, win, 0)
    key_places = my_first - back * tok_rows + jnp.arange(win, dtype=jnp.int32)
    key_block = kv_win[:, :KVW].reshape(win, KVH, HD)
    value_block = kv_win[:, KVW:].reshape(win, KVH, HD)
    query_grouped = query_low.reshape(tok_rows, KVH, group_size, HD)
    allowed = (
        (key_docs[None, :] == query_docs[:, None]) & (key_places[None, :] <= query_places[:, None])
    )[:, None, None, :]
    scores = (
        jnp.einsum("qgrd,kgd->qgrk", query_grouped, key_block, preferred_element_type=jnp.float32)
        * score_scale
    )
    scores = jnp.where(allowed, scores, MASKED_SCORE)
    row_max = jnp.max(scores, axis=-1, keepdims=True)
    exponent = jnp.where(allowed, jnp.exp(scores - row_max), 0.0)
    probs = exponent / jnp.sum(exponent, axis=-1, keepdims=True)
    probs_low = probs.astype(jnp.bfloat16)
    attended_sum = jnp.einsum(
        "qgrk,kgd->qgrd", probs_low, value_block, preferred_element_type=jnp.float32
    )
    attended_low = attended_sum.reshape(tok_rows, D).astype(jnp.bfloat16)
    middle = local_tokens + jnp.dot(attended_low, output_full, preferred_element_type=jnp.float32)

    scale_two = rms_scale(middle)
    normed_two = middle * scale_two
    normed_two_low = (normed_two * gain_two_f).astype(jnp.bfloat16)
    group_tokens = n_f * tok_rows
    xn2_all = fsdp_gather(normed_two_low, n_f).reshape(group_tokens, D)
    gate_up = jnp.dot(xn2_all, gate_up_tp, preferred_element_type=jnp.float32)
    gate_pre = gate_up[:, :units]
    up_pre = gate_up[:, units:]
    sigmoid = jax.nn.sigmoid(gate_pre)
    hidden_low = (gate_pre * sigmoid * up_pre).astype(jnp.bfloat16)
    ff_part = jnp.dot(hidden_low, down_tp, preferred_element_type=jnp.float32)

    grad_out = cotangent[0]
    grad_all = fsdp_gather(grad_out, n_f).reshape(group_tokens, D)
    down_term = outer_rows(hidden_low, grad_all).astype(jnp.bfloat16)
    hidden_grad = times_transposed(grad_all, down_tp)
    gate_grad = (hidden_grad * up_pre * sigmoid * (1.0 + gate_pre * (1.0 - sigmoid))).astype(
        jnp.bfloat16
    )
    up_grad = (hidden_grad * gate_pre * sigmoid).astype(jnp.bfloat16)
    gate_up_cat = jnp.concatenate([gate_grad, up_grad], axis=1)
    gate_up_term = outer_rows(xn2_all, gate_up_cat)
    grad_pack = jnp.concatenate(
        [
            gate_up_term.astype(jnp.bfloat16).reshape(n_ctx, n_f * rows, 2 * units),
            down_term.reshape(n_ctx, down_rows, 2 * units),
        ],
        axis=1,
    ).reshape(n_ctx * (n_f * rows + down_rows), 2 * units)
    grad_pack, gate_up_cat = lax.optimization_barrier((grad_pack, gate_up_cat))
    grad_sum = lax.psum_scatter(grad_pack, "ctx", scatter_dimension=0, tiled=True)
    down_sum = grad_sum[n_f * rows :].reshape(ff_rows, D)
    gu_sum = lax.all_to_all(grad_sum[: n_f * rows].reshape(n_f, rows, 2 * units), "fsdp", 0, 0, tiled=True)
    ff_sum = jnp.transpose(
        gu_sum.reshape(n_f, rows, 2, n_ctx, chunk), (1, 2, 3, 0, 4)
    ).reshape(rows, 2 * ff)
    normed_two_grad = fsdp_reduce(
        times_transposed(gate_up_cat, gate_up_tp).reshape(n_f, tok_rows, D), n_f
    )
    gain_two_term = jnp.sum(normed_two_grad * normed_two, axis=0)
    scaled_two = normed_two_grad * gain_two_f
    middle_grad = grad_out.astype(jnp.float32) + scale_two * (
        scaled_two - normed_two * jnp.mean(scaled_two * normed_two, axis=-1, keepdims=True)
    )
    branch_grad = middle_grad.astype(jnp.bfloat16)
    attended_grad_low = (
        times_transposed(branch_grad, output_full)
        .astype(jnp.bfloat16)
        .reshape(tok_rows, KVH, group_size, HD)
    )
    row_delta = jnp.sum(
        attended_grad_low.astype(jnp.float32) * attended_sum, axis=-1, keepdims=True
    )
    prob_grad = jnp.einsum(
        "qgrd,kgd->qgrk", attended_grad_low, value_block, preferred_element_type=jnp.float32
    )
    score_grad = (probs * (prob_grad - row_delta)).astype(jnp.bfloat16)
    query_accum = jnp.einsum(
        "qgrk,kgd->qgrd", score_grad, key_block, preferred_element_type=jnp.float32
    )
    key_term = jnp.einsum(
        "qgrk,qgrd->kgd", score_grad, query_grouped, preferred_element_type=jnp.float32
    ).reshape(win, KVW)
    value_term = jnp.einsum(
        "qgrk,qgrd->kgd", probs_low, attended_grad_low, preferred_element_type=jnp.float32
    ).reshape(win, KVW)
    kv_term = jnp.concatenate([key_term, value_term], axis=1).reshape(back + 1, tok_rows, 2 * KVW)
    kv_sum = kv_return(kv_term[back], kv_term[:back].astype(jnp.bfloat16), n_ctx, back)
    key_grad_low = rotate(kv_sum[:, :KVW] * score_scale, query_positions, KVH, -1.0).astype(
        jnp.bfloat16
    )
    value_grad_low = kv_sum[:, KVW:].astype(jnp.bfloat16)
    query_grad_low = rotate(
        query_accum.reshape(tok_rows, D) * score_scale, query_positions, H, -1.0
    ).astype(jnp.bfloat16)
    projection_cat = jnp.concatenate([query_grad_low, key_grad_low, value_grad_low], axis=1)
    normed_grad = times_transposed(projection_cat, qkv_full)
    gain_one_term = jnp.sum(normed_grad * normed_one, axis=0)
    scaled_one = normed_grad * gain_one_f
    tokens_grad = middle_grad + scale_one * (
        scaled_one - normed_one * jnp.mean(scaled_one * normed_one, axis=-1, keepdims=True)
    )
    gain_term_cols = jnp.pad(
        jnp.stack([gain_one_term, gain_two_term], axis=1), ((0, 0), (0, GAIN_PAD - 2))
    )
    attention_pack = jnp.concatenate(
        [
            outer_rows(normed_low, projection_cat).astype(jnp.bfloat16),
            outer_rows(attended_low, branch_grad).astype(jnp.bfloat16),
            gain_term_cols.astype(jnp.bfloat16),
        ],
        axis=1,
    )
    attention_sum = lax.psum_scatter(
        attention_pack, ALL, scatter_dimension=0, tiled=True
    ).astype(jnp.float32)
    ff_part = ff_part.at[0, 0].add(attention_pack[0, 0].astype(jnp.float32) * 0.0)
    layer_out = middle + fsdp_reduce(ff_part.reshape(n_f, tok_rows, D), n_f)
    ff_sum = ff_sum.astype(jnp.float32)
    return (
        layer_out.astype(jnp.bfloat16)[None],
        tokens_grad[None],
        attention_sum[:, c_g],
        attention_sum[:, :c_k],
        attention_sum[:, c_k:c_v],
        attention_sum[:, c_v:c_o],
        attention_sum[:, c_o:c_g],
        attention_sum[:, c_g + 1],
        ff_sum[:, :ff],
        ff_sum[:, ff : 2 * ff],
        down_sum.astype(jnp.float32),
    )


def solution(mesh):
    weight = P(ALL, None)
    stream = P("fsdp", "ctx", None)
    return jax.shard_map(
        body,
        mesh=mesh,
        in_specs=(
            stream,
            P("fsdp", None),
            P(ALL),
            weight,
            weight,
            weight,
            weight,
            P(ALL),
            weight,
            weight,
            weight,
            stream,
        ),
        out_specs=(
            stream,
            stream,
            P(ALL),
            weight,
            weight,
            weight,
            weight,
            P(ALL),
            weight,
            weight,
            weight,
        ),
        check_vma=False,
    )
```
